32 devices in a mesh: wide: 8 (over y, x, core), narrow: 4 (over z).
Axes of the slice: x: 2, y: 2, z: 4, core: 2. Of those that a mesh axis runs over, the one named last changes fastest.
Arguments:
- layer_in: bfloat16 [16384, 1024], P(('wide', 'narrow')), may hold values from -6 to 6
- value_first: bfloat16 [16384, 1024], P(('wide', 'narrow')), may hold values from -16 to 16
- seg_start: int32 [16], P('wide'), may hold values from 0 to 1, as said below
- gain_one: float32 [1024], replicated, may hold values from 0.5 to 1.5
- w_qkv: bfloat16 [3, 1024, 1024], P(None, 'narrow'), may hold values from -0.1875 to 0.1875
- w_out: bfloat16 [1024, 1024], P('narrow'), may hold values from -0.75 to 0.75
- gain_two: float32 [1024], replicated, may hold values from 0.5 to 1.5
- w_mlp: bfloat16 [1024, 3, 2816], P('wide', None, 'narrow'), may hold values from -0.1875 to 0.1875
- grad_out: bfloat16 [16384, 1024], P(('wide', 'narrow')), may hold values from -6 to 6
Outputs:
- layer_out: bfloat16 [16384, 1024], P(('wide', 'narrow'))
- grad_in: float32 [16384, 1024], P(('wide', 'narrow'))
- grad_value_first: float32 [16384, 1024], P(('wide', 'narrow'))
- grad_gain_one: float32 [1024], replicated
- grad_w_qkv: float32 [3, 1024, 1024], P(None, 'narrow')
- grad_w_out: float32 [1024, 1024], P('narrow')
- grad_gain_two: float32 [1024], replicated
- grad_w_mlp: float32 [1024, 3, 2816], P('wide', None, 'narrow')
- value_norms: float32 [2], replicated
The draws below stay inside these ranges and needn't reach their ends.
Inputs may be any that keep to these rules, and one draw needn't show every extreme that they name: `seg_start`: every packed row of 2 slots begins with 1, and a 0 follows only a 1, so each sequence fills one or two slots.
All inputs are finite; a program needn't handle non-finite values.
Results may differ from the reference program's by a relative error of at most 0.014.
Values may be sent and summed in bfloat16 or wider, within the bound.
A program may use at most 192 MiB of HBM per device.

```python
import jax
import jax.numpy as jnp
from jax import lax

D = 1024
HEADS = 16
HEAD_DIM = 64
FF = 2816
SHORT = 1024
SLOTS = 2
ROW_TOK = 2048
TOKENS = 16384


def draw_seg_start(key, part):
    row_total = TOKENS // ROW_TOK
    coin_flips = jax.random.randint(key, (SLOTS, row_total), 0, 2, dtype=jnp.int32)

    def advance(previous, coin_flip):
        current = jnp.where(previous == 1, coin_flip, 1)
        return (current, current)
    leading = jnp.ones((row_total,), jnp.int32)
    final_state, following = lax.scan(advance, leading, coin_flips[1:])
    slot_table = jnp.concatenate([leading[None, :], following], axis=0)
    return slot_table.T.reshape(row_total * SLOTS)


def draw_value_first(key, part):
    places = jnp.arange(TOKENS, dtype=jnp.float32) / TOKENS
    noise = jax.random.normal(key, (TOKENS, D), jnp.float32)
    ramp_scale = 0.5 + places
    return (noise * ramp_scale[:, None]).astype(jnp.bfloat16)


def levels(rng, shape, cuts, low, high):
    def one(dim, parts):
        steps = jax.random.uniform(jax.random.fold_in(jax.random.fold_in(rng, 6), dim), (parts,), jnp.float32, low / len(cuts), high / len(cuts))
        return jnp.repeat(jnp.exp(steps), shape[dim] // parts).reshape((-1,) + (1,) * (len(shape) - dim - 1))

    factor_of = one(*cuts[0])
    for cut in cuts[1:]:
        factor_of = factor_of * one(*cut)
    return factor_of


def scatter_about(own_key, extent, scale, most, pieces=(), kind=jnp.bfloat16):
    entries = scale * jax.random.normal(own_key, extent, jnp.float32)
    if pieces:
        entries = entries * levels(own_key, extent, pieces, -0.22, 0.18)
    return jnp.clip(entries, -most, most).astype(kind)


def setup_inputs(seed: int = 0) -> dict:
    seeds = jax.random.split(jax.random.key(seed), 10)
    layer_in = scatter_about(seeds[0], (TOKENS, D), 1.0, 6.0, ((0, 32),))
    value_first = draw_value_first(jax.random.fold_in(seeds[9], 71), 0)
    seg_start = draw_seg_start(jax.random.fold_in(seeds[9], 71), 0)
    gain_one = jnp.clip(1.0 + 0.1 * jax.random.normal(seeds[3], (D,), jnp.float32), 0.5, 1.5)
    w_qkv = scatter_about(seeds[4], (3, D, D), D ** -0.5, 0.1875, ((1, 4),))
    w_out = scatter_about(seeds[5], (D, D), (D // 16) ** -0.5, 0.75, ((0, 4),))
    gain_two = jnp.clip(1.0 + 0.1 * jax.random.normal(seeds[6], (D,), jnp.float32), 0.5, 1.5)
    w_mlp = scatter_about(seeds[7], (D, 3, FF), D ** -0.5, 0.1875, ((0, 8), (2, 4)))
    grad_out = scatter_about(seeds[8], (TOKENS, D), 1.0, 6.0, ((0, 32),))
    return dict(layer_in=layer_in, value_first=value_first, seg_start=seg_start, gain_one=gain_one, w_qkv=w_qkv, w_out=w_out, gain_two=gain_two, w_mlp=w_mlp, grad_out=grad_out)


@jax.custom_vjp
def low(v):
    return lax.optimization_barrier(v.astype(jnp.bfloat16)).astype(jnp.float32)

@jax.custom_vjp
def low_back(v):
    return v

def low_keep(v):
    return (low(v), None)

def low_pass(kept, grad):
    return (grad,)

def back_keep(v):
    return (v, None)

def back_low(kept, grad):
    return (low(grad),)
low.defvjp(low_keep, low_pass)
low_back.defvjp(back_keep, back_low)
EPSILON = 1e-06
PRECISE = lax.Precision.HIGHEST

def matmul(left_side, right_side):
    return jnp.dot(left_side, right_side, precision=PRECISE, preferred_element_type=jnp.float32)

def matmul_t(left_side, right_side):
    return lax.dot_general(left_side, right_side, (((1,), (1,)), ((), ())), precision=PRECISE, preferred_element_type=jnp.float32)

def rope_tables(positions):
    half_dim = HEAD_DIM // 2
    frequency = 10000.0 ** (-2.0 * jnp.arange(half_dim, dtype=jnp.float32) / HEAD_DIM)
    angles = positions[:, None] * frequency[None, :]
    return (jnp.cos(angles), jnp.sin(angles))

def rotate(heads_in, cosine, sine_vals):
    half_dim = heads_in.shape[-1] // 2
    first_half = heads_in[..., :half_dim]
    second_half = heads_in[..., half_dim:]
    cos_wide = cosine[:, None, :]
    sin_wide = sine_vals[:, None, :]
    return jnp.concatenate([first_half * cos_wide - second_half * sin_wide, second_half * cos_wide + first_half * sin_wide], axis=-1)

def rms_norm(values, gain_vec):
    inverse = lax.rsqrt(lax.optimization_barrier(jnp.mean(values * values, axis=-1, keepdims=True)) + EPSILON)
    return values * inverse * gain_vec

def attention(query_vals, key_vals, mixed_vals, seg_tok):
    scale = HEAD_DIM ** (-0.5)
    offsets = jnp.arange(SHORT, dtype=jnp.int32)
    spans = jnp.arange(2 * SHORT, dtype=jnp.int32)

    def one_slot(slot_index):
        first_tok = slot_index * SHORT
        key_start = jnp.maximum(slot_index - 1, 0) * SHORT
        q_block = lax.dynamic_slice_in_dim(query_vals, first_tok, SHORT, 0)
        k_block = lax.dynamic_slice_in_dim(key_vals, key_start, 2 * SHORT, 0)
        v_block = lax.dynamic_slice_in_dim(mixed_vals, key_start, 2 * SHORT, 0)
        q_seg = lax.dynamic_slice_in_dim(seg_tok, first_tok, SHORT, 0)
        k_seg = lax.dynamic_slice_in_dim(seg_tok, key_start, 2 * SHORT, 0)
        allowed = ((key_start + spans)[None, :] <= (first_tok + offsets)[:, None]) & (k_seg[None, :] == q_seg[:, None])
        scores = low_back(jnp.einsum('qhd,khd->hqk', q_block, k_block, precision=PRECISE) * scale)
        scores = jnp.where(allowed[None], scores, -1e+30)
        row_max = lax.optimization_barrier(jnp.max(scores, axis=-1, keepdims=True))
        exponent = jnp.exp(scores - row_max)
        weights = low(exponent / lax.optimization_barrier(jnp.sum(exponent, axis=-1, keepdims=True)))
        return jnp.einsum('hqk,khd->qhd', weights, v_block, precision=PRECISE)
    blocks = lax.map(jax.checkpoint(one_slot), jnp.arange(SLOTS, dtype=jnp.int32))
    return blocks.reshape(ROW_TOK, HEADS, HEAD_DIM)

def row_forward(x_row, v_row, gain_a, qkv_w, proj_w, gain_b, mlp_w, seg_tok, cosine, sine_vals):
    shaped = (ROW_TOK, HEADS, HEAD_DIM)
    normed = low(rms_norm(x_row, gain_a))
    query_raw = matmul_t(normed, qkv_w[0])
    key_raw = matmul_t(normed, qkv_w[1])
    own_vals = matmul_t(normed, qkv_w[2])
    query_vals = low(rotate(low_back(query_raw).reshape(shaped), cosine, sine_vals))
    key_vals = low(rotate(low_back(key_raw).reshape(shaped), cosine, sine_vals))
    mixed_vals = low(low_back(0.5 * own_vals + 0.5 * v_row)).reshape(shaped)
    attended = low(low_back(attention(query_vals, key_vals, mixed_vals, seg_tok).reshape(ROW_TOK, D)))
    hidden = x_row + low_back(matmul(attended, proj_w))
    normed_two = low(rms_norm(hidden, gain_b))
    gate_vals = low_back(matmul(normed_two, mlp_w[:, 0, :]))
    up_vals = low_back(matmul(normed_two, mlp_w[:, 1, :]))
    inner_act = low(jax.nn.silu(gate_vals) * up_vals)
    return (hidden + low_back(matmul(inner_act, mlp_w[:, 2, :].T)), own_vals)

def reference(layer_in, value_first, seg_start, gain_one, w_qkv, w_out, gain_two, w_mlp, grad_out):
    row_total = TOKENS // ROW_TOK
    starts = seg_start.reshape(row_total, SLOTS)
    seg_tok = jnp.repeat(jnp.cumsum(starts, axis=1), SHORT, axis=1).astype(jnp.int32)
    positions = ((1 - starts)[:, :, None] * SHORT + jnp.arange(SHORT, dtype=jnp.int32)[None, None, :]).reshape(row_total, ROW_TOK).astype(jnp.float32)
    parameters = (gain_one.astype(jnp.float32), w_qkv.astype(jnp.float32), w_out.astype(jnp.float32), gain_two.astype(jnp.float32), w_mlp.astype(jnp.float32))

    def per_row(totals, inputs):
        x_row, v_row, dy_row, seg_row, pos_row = inputs
        cosine, sine_vals = rope_tables(pos_row)

        def forward(x_in, v_in, gain_a, qkv_w, proj_w, gain_b, mlp_w):
            return row_forward(x_in, v_in, gain_a, qkv_w, proj_w, gain_b, mlp_w, seg_row, cosine, sine_vals)
        outputs, pull, own_vals = jax.vjp(forward, x_row.astype(jnp.float32), v_row.astype(jnp.float32), *parameters, has_aux=True)
        gradients = pull(dy_row.astype(jnp.float32))
        totals = tuple((total + grad for total, grad in zip(totals, gradients[2:])))
        return (totals, (outputs.astype(jnp.bfloat16), gradients[0], gradients[1], jnp.sum(own_vals * own_vals)))
    zero_sums = tuple((jnp.zeros_like(item) for item in parameters))
    totals, (outputs, grad_rows, grad_values, own_sums) = lax.scan(per_row, zero_sums, (layer_in.reshape(row_total, ROW_TOK, D), value_first.reshape(row_total, ROW_TOK, D), grad_out.reshape(row_total, ROW_TOK, D), seg_tok, positions))
    first_vals = value_first.astype(jnp.float32)
    first_sum = jnp.sum(first_vals * first_vals)
    value_norms = jnp.sqrt(jnp.stack([first_sum, jnp.sum(own_sums)]) / (TOKENS * D))
    return (outputs.reshape(TOKENS, D), grad_rows.reshape(TOKENS, D), grad_values.reshape(TOKENS, D), totals[0], totals[1], totals[2], totals[3], totals[4], value_norms)
```

```python
import functools

import jax
import jax.numpy as jnp
from jax import lax
from jax.experimental import pallas as pl
from jax.experimental.pallas import tpu as pltpu
from jax.sharding import Mesh, PartitionSpec as P

HEAD_DIM = 64
EPSILON = 1e-06
BF = jnp.bfloat16
F32 = jnp.float32
AXES = ("hi", "core", "zh", "zq")
MESH = pl.DeviceIdType.MESH
ANY = pl.BlockSpec(memory_space=pl.ANY)
VM = pl.BlockSpec(memory_space=pltpu.VMEM)
VMEM_MAX = 62 << 20
DMA = pltpu.SemaphoreType.DMA


def nn(a, b):
    return lax.dot_general(a, b, (((1,), (0,)), ((), ())), preferred_element_type=F32)


def nt(a, b):
    return lax.dot_general(a, b, (((1,), (1,)), ((), ())), preferred_element_type=F32)


def tn(a, b):
    return lax.dot_general(a, b, (((0,), (0,)), ((), ())), preferred_element_type=F32)


def coords():
    return tuple(lax.axis_index(name) for name in AXES)


def remote(src, dst, send, recv, to):
    return pltpu.make_async_remote_copy(
        src_ref=src, dst_ref=dst, send_sem=send, recv_sem=recv, device_id=to, device_id_type=MESH
    )


def greet_plane(sizes, with_hi):
    hi_n, _, _, nh = sizes
    h, c, r, q = coords()
    barrier = pltpu.get_barrier_semaphore()
    count = 0
    for dc in range(2):
        for dr in range(2):
            for dq in range(nh):
                if dc or dr or dq:
                    to = (h, (c + dc) % 2, (r + dr) % 2, (q + dq) % nh)
                    pl.semaphore_signal(barrier, inc=1, device_id=to, device_id_type=MESH)
                    count += 1
    if with_hi:
        for dh in range(1, hi_n):
            to = ((h + dh) % hi_n, c, r, q)
            pl.semaphore_signal(barrier, inc=1, device_id=to, device_id_type=MESH)
            count += 1
    pl.semaphore_wait(barrier, count)


def rotate_lanes(values, first):
    width = values.shape[1]
    if width < 128:
        return jnp.concatenate([values[:, 32:], values[:, :32]], axis=1)
    return jnp.where(
        first, pltpu.roll(values, width - 32, 1), pltpu.roll(values, 32, 1)
    )


def first_lanes(rows, width):
    lane = lax.broadcasted_iota(jnp.int32, (rows, width), 1)
    return lane % HEAD_DIM < HEAD_DIM // 2


def lane_window(pair, pw, sw):
    return slice(0, sw) if pw == sw else pl.ds(pl.multiple_of(pair * pw, pw), pw)


def tiled(table, width):
    times = width // table.shape[1]
    return table if times == 1 else jnp.concatenate([table] * times, axis=1)


def exchange_kernel(
    sizes, chunks, x, v, w, sg, xa, va, ws, so, xs, wb, sb, vb,
    swap_s, swap_r, peer_s, peer_r, core_s, core_r, w_s, w_r, wh_s, wh_r, sg_s, sg_r, v_s, v_r, loc,
):
    hi_n, _, _, nh = sizes
    n = 2 * nh
    h, c, r, q = coords()
    p = c * nh + q
    partner_p = r * nh + q
    rows = x.shape[0] // chunks
    same = c == r
    other = c != r
    partner = (h, r, c, q)
    mate = (h, 1 - c, r, q)
    greet_plane(sizes, True)

    def part(k):
        return pl.ds(k * rows, rows)

    def swap_x(k):
        return remote(x.at[part(k)], xa.at[partner_p, part(k)], swap_s.at[k], swap_r.at[k], partner)

    def own_arrives(k):
        return remote(x.at[part(k)], xa.at[p, part(k)], swap_s.at[k], swap_r.at[k], partner)

    def push_peer(src, k, dq):
        to = (h, c, r, (q + dq) % nh)
        return remote(src, xa.at[p, part(k)], peer_s.at[dq, k], peer_r.at[dq, k], to)

    def push_mate(src, k, dq):
        block = c * nh + (q + nh - dq) % nh
        return remote(src, xa.at[block, part(k)], core_s.at[dq, k], core_r.at[dq, k], mate)

    def send_w():
        return remote(w.at[h], ws.at[h], w_s, w_r, partner)

    def spread_w(dh):
        to = ((h + dh) % hi_n, c, r, q)
        return remote(ws.at[h], ws.at[h], wh_s.at[dh], wh_r.at[dh], to)

    def send_sg():
        return remote(sg, so, sg_s, sg_r, partner)

    local_x_in = pltpu.make_async_copy(x, xs, loc.at[0])
    local_w_in = pltpu.make_async_copy(w, wb, loc.at[1])
    local_s_in = pltpu.make_async_copy(sg, sb, loc.at[2])
    local_v_in = pltpu.make_async_copy(v.at[p], vb, loc.at[3])
    local_x_out = pltpu.make_async_copy(xs, xa.at[p], loc.at[4])
    local_w_out = pltpu.make_async_copy(wb, ws, loc.at[5])
    local_s_out = pltpu.make_async_copy(sb, so, loc.at[6])
    local_v_out = pltpu.make_async_copy(vb, va.at[p], loc.at[7])

    @pl.when(other)
    def _():
        send_sg().start()
        send_w().start()
        for k in range(chunks):
            swap_x(k).start()

    @pl.when(same)
    def _():
        for k in range(chunks):
            for dq in range(1, nh):
                push_peer(x.at[part(k)], k, dq).start()
            push_mate(x.at[part(k)], k, 0).start()
        local_x_in.start()
        local_w_in.start()
        local_s_in.start()
        local_v_in.start()

    @pl.when(other)
    def _():
        for k in range(chunks):
            own_arrives(k).wait_recv()
            for dq in range(1, nh):
                push_peer(xa.at[p, part(k)], k, dq).start()
            push_mate(xa.at[p, part(k)], k, 0).start()
        send_w().wait_recv()
        for dh in range(1, hi_n):
            spread_w(dh).start()

    @pl.when(same)
    def _():
        local_x_in.wait()
        local_x_out.start()
        local_w_in.wait()
        local_w_out.start()
        local_s_in.wait()
        local_s_out.start()
        local_v_in.wait()
        local_v_out.start()

    def send_v(s):
        to = (h, s // nh, c, s % nh)
        return remote(v.at[s], va.at[r * nh + q], v_s.at[s], v_r.at[r * nh + q], to)

    for s in range(n):
        @pl.when(jnp.logical_or(other, p != s))
        def _():
            send_v(s).start()

    for k in range(chunks):
        for dq in range(1, nh):
            block = c * nh + (q + nh - dq) % nh
            remote(
                x.at[part(k)], xa.at[block, part(k)], peer_s.at[dq, k], peer_r.at[dq, k], mate
            ).wait_recv()
            push_mate(xa.at[block, part(k)], k, dq).start()

    for k in range(chunks):
        for dq in range(nh):
            block = (1 - c) * nh + (q + nh - dq) % nh
            remote(
                x.at[part(k)], xa.at[block, part(k)], core_s.at[dq, k], core_r.at[dq, k], mate
            ).wait_recv()

    @pl.when(other)
    def _():
        send_sg().wait_recv()
        for dh in range(1, hi_n):
            source = (h + hi_n - dh) % hi_n
            remote(ws.at[source], ws.at[source], wh_s.at[dh], wh_r.at[dh], mate).wait_recv()
        send_sg().wait_send()
        send_w().wait_send()
        for dh in range(1, hi_n):
            spread_w(dh).wait_send()
        for k in range(chunks):
            swap_x(k).wait_send()

    for b in range(n):
        @pl.when(jnp.logical_or(other, p != b))
        def _():
            remote(v.at[0], va.at[b], v_s.at[b], v_r.at[b], mate).wait_recv()

    for s in range(n):
        @pl.when(jnp.logical_or(other, p != s))
        def _():
            send_v(s).wait_send()

    for k in range(chunks):
        for dq in range(1, nh):
            push_peer(x.at[part(k)], k, dq).wait_send()
        for dq in range(nh):
            push_mate(x.at[part(k)], k, dq).wait_send()

    @pl.when(same)
    def _():
        local_x_out.wait()
        local_w_out.wait()
        local_s_out.wait()
        local_v_out.wait()


def exchange_inputs(sizes, x, v, w, sg):
    hi_n, _, _, nh = sizes
    n = 2 * nh
    tok, width = x.shape
    sw = v.shape[2]
    chunks = 4 if tok % 64 == 0 else 1
    return pl.pallas_call(
        functools.partial(exchange_kernel, sizes, chunks),
        out_shape=(
            jax.ShapeDtypeStruct((n, tok, width), BF),
            jax.ShapeDtypeStruct((n, tok, sw), BF),
            jax.ShapeDtypeStruct(w.shape, BF),
            jax.ShapeDtypeStruct(sg.shape, F32),
        ),
        in_specs=[ANY] * 4,
        out_specs=(ANY,) * 4,
        scratch_shapes=[
            pltpu.VMEM((tok, width), BF),
            pltpu.VMEM(w.shape, BF),
            pltpu.VMEM(sg.shape, F32),
            pltpu.VMEM((tok, sw), BF),
            DMA((chunks,)), DMA((chunks,)),
            DMA((nh, chunks)), DMA((nh, chunks)),
            DMA((nh, chunks)), DMA((nh, chunks)),
            DMA, DMA,
            DMA((hi_n,)), DMA((hi_n,)),
            DMA, DMA,
            DMA((n,)), DMA((n,)),
            DMA((8,)),
        ],
        name="exchange_inputs",
        compiler_params=pltpu.CompilerParams(collective_id=1, has_side_effects=True),
        cost_estimate=pl.CostEstimate(flops=0, bytes_accessed=160 << 20, transcendentals=0),
    )(x, v, w, sg)


def masked(scores, diagonal, crossing, causal, bias):
    if diagonal:
        return jnp.where(causal, scores, -1e30)
    if crossing:
        return scores + bias
    return scores


def forward_kernel(
    sizes, block, xa, ws, va, g1, cos, sin, bias_ref,
    ai, qo, ko, mo, ao, lse, own, att_s, att_r, loc,
):
    _, _, _, nh = sizes
    n = 2 * nh
    h, c, r, q = coords()
    p = c * nh + q
    row_len, sw = va.shape
    tok = row_len // n
    short = row_len // 2
    pw = cos.shape[1]
    pairs = sw // pw
    halves = pw // HEAD_DIM
    greet_plane(sizes, False)
    br = 256
    own[...] = jnp.zeros_like(own)

    def project(i, carry):
        rows = pl.ds(pl.multiple_of(i * br, br), br)
        xf = xa[rows, :].astype(F32)
        inv = lax.rsqrt(jnp.mean(xf * xf, axis=-1, keepdims=True) + EPSILON)
        normed = (xf * inv * g1[...]).astype(BF)
        raw = nt(normed, ws[...])
        first = first_lanes(br, sw)
        ct = tiled(cos[rows, :], sw)
        st = tiled(sin[rows, :], sw)
        q_raw = raw[:, :sw]
        k_raw = raw[:, sw : 2 * sw]
        own_vals = raw[:, 2 * sw :]
        q_rot = (q_raw * ct + rotate_lanes(q_raw, first) * st).astype(BF)
        qo[rows, :] = (q_rot.astype(F32) * HEAD_DIM**-0.5).astype(BF)
        ko[rows, :] = (k_raw * ct + rotate_lanes(k_raw, first) * st).astype(BF)
        mo[rows, :] = (0.5 * own_vals + 0.5 * va[rows, :].astype(F32)).astype(BF)
        own[...] += jnp.sum((own_vals * own_vals).reshape(br // 8, 8, sw), axis=0)
        return carry

    lax.fori_loop(0, row_len // br, project, 0)

    bias = bias_ref[0:1, 0:1]
    blocks = row_len // block
    per = block // tok
    causal = lax.broadcasted_iota(jnp.int32, (block, block), 0) >= lax.broadcasted_iota(
        jnp.int32, (block, block), 1
    )

    def send(b, pair):
        lanes = lane_window(pair, pw, sw)
        to = (h, b // nh, r, b % nh)
        return remote(
            ao.at[b, :, lanes], ai.at[p, :, lanes], att_s.at[pair, b], att_r.at[pair, p], to
        )

    def keep(pair):
        lanes = lane_window(pair, pw, sw)
        return pltpu.make_async_copy(ao.at[p, :, lanes], ai.at[p, :, lanes], loc.at[pair])

    def pair_step(pair, carry):
        lanes = lane_window(pair, pw, sw)
        for i in range(blocks):
            outs = []
            rows = pl.ds(i * block, block)
            for half in range(halves):
                cols = slice(half * HEAD_DIM, (half + 1) * HEAD_DIM)
                qh = qo[rows, lanes][:, cols]
                score = []
                for j in range(i + 1):
                    kj = ko[pl.ds(j * block, block), lanes][:, cols]
                    crossing = i * block >= short and j * block < short
                    score.append(masked(nt(qh, kj), i == j, crossing, causal, bias))
                top = functools.reduce(
                    jnp.maximum, [jnp.max(s, axis=-1, keepdims=True) for s in score]
                )
                total = 0.0
                acc = 0.0
                for j in range(i + 1):
                    e = jnp.exp(score[j] - top)
                    total = total + jnp.sum(e, axis=-1, keepdims=True)
                    vj = mo[pl.ds(j * block, block), lanes][:, cols]
                    acc = acc + nn(e.astype(BF), vj)
                outs.append(acc / total)
                lse[pair, rows, half : half + 1] = top + jnp.log(total)
            out = (jnp.concatenate(outs, axis=1) if halves > 1 else outs[0]).astype(BF)
            for t in range(per):
                b = i * per + t
                ao[b, :, lanes] = out[t * tok : (t + 1) * tok]

                @pl.when(p != b)
                def _():
                    send(b, pair).start()

        keep(pair).start()
        return carry

    lax.fori_loop(0, pairs, pair_step, 0)

    def drain(pair, carry):
        lanes = lane_window(pair, pw, sw)
        for b in range(n):
            @pl.when(p != b)
            def _():
                send(b, pair).wait_send()
                remote(
                    ao.at[b, :, lanes], ai.at[b, :, lanes], att_s.at[pair, b], att_r.at[pair, b],
                    (h, 1 - c, r, q),
                ).wait_recv()
        keep(pair).wait()
        return carry

    lax.fori_loop(0, pairs, drain, 0)


def attention_forward(sizes, xa, ws, va, g1, cos, sin, bias):
    _, _, _, nh = sizes
    n = 2 * nh
    row_len, sw = va.shape
    tok = row_len // n
    pw = cos.shape[1]
    pairs = sw // pw
    block = max(tok, 512)
    flops = 2 * row_len * xa.shape[1] * 3 * sw + 2 * row_len * row_len * sw
    return pl.pallas_call(
        functools.partial(forward_kernel, sizes, block),
        out_shape=(
            jax.ShapeDtypeStruct((n, tok, sw), BF),
            jax.ShapeDtypeStruct((row_len, sw), BF),
            jax.ShapeDtypeStruct((row_len, sw), BF),
            jax.ShapeDtypeStruct((row_len, sw), BF),
            jax.ShapeDtypeStruct((n, tok, sw), BF),
            jax.ShapeDtypeStruct((pairs, row_len, pw // HEAD_DIM), F32),
            jax.ShapeDtypeStruct((8, sw), F32),
        ),
        in_specs=[VM] * 7,
        out_specs=(ANY,) + (VM,) * 6,
        scratch_shapes=[DMA((pairs, n)), DMA((pairs, n)), DMA((pairs,))],
        name="attention_forward",
        compiler_params=pltpu.CompilerParams(
            collective_id=2, has_side_effects=True, vmem_limit_bytes=VMEM_MAX
        ),
        cost_estimate=pl.CostEstimate(
            flops=4 * flops, bytes_accessed=16 << 20, transcendentals=row_len * row_len * sw // 128
        ),
    )(xa, ws, va, g1, cos, sin, bias)


def mlp_kernel(
    p_ref, x, ai, dy, g2, wo, wm, lo, gh, ga, dwm, dwo, gg2, hid, n2, acc_o, acc_g
):
    step = pl.program_id(0)
    n = ai.shape[0]
    wide = wm.shape[0]
    width = x.shape[2]
    dw = width // wide

    @pl.when(step == 0)
    def _():
        total = x[0].astype(F32)
        for s in range(n):
            total = total + nn(ai[s], wo[s])
        hid[...] = total
        inv = lax.rsqrt(jnp.mean(total * total, axis=-1, keepdims=True) + EPSILON)
        n2[...] = (total * inv * g2[...]).astype(BF)
        acc_o[...] = jnp.zeros_like(acc_o)
        acc_g[...] = jnp.zeros_like(acc_g)

    def weight(j):
        return jnp.concatenate([wm[w, 0, j] for w in range(wide)], axis=1)

    def put(j, grad):
        low = grad.astype(BF)
        for w in range(wide):
            dwm[w, 0, j] = low[:, w * dw : (w + 1) * dw]

    gate = nt(n2[...], weight(0))
    up = nt(n2[...], weight(1))
    sig = jax.nn.sigmoid(gate)
    silu = gate * sig
    inner = (silu * up).astype(BF)
    grad_inner = nt(dy[...], weight(2))
    grad_gate = (grad_inner * up * sig * (1.0 + gate * (1.0 - sig))).astype(BF)
    grad_up = (grad_inner * silu).astype(BF)
    acc_o[...] += nn(inner, weight(2))
    acc_g[...] += nn(grad_gate, weight(0)) + nn(grad_up, weight(1))
    put(0, tn(grad_gate, n2[...]))
    put(1, tn(grad_up, n2[...]))
    put(2, tn(inner, dy[...]))

    @pl.when(step == pl.num_programs(0) - 1)
    def _():
        hidden = hid[...]
        lo[...] = (hidden + acc_o[...]).astype(BF)
        inv = lax.rsqrt(jnp.mean(hidden * hidden, axis=-1, keepdims=True) + EPSILON)
        grad_n = acc_g[...]
        gg2[...] = jnp.sum((grad_n * hidden * inv).reshape(-1, 8, width), axis=0)
        scaled = grad_n * g2[...]
        dot = jnp.sum(scaled * hidden, axis=-1, keepdims=True)
        grad_h = dy[...].astype(F32) + scaled * inv - hidden * (inv * inv * inv * dot / width)
        gh[...] = grad_h
        low = grad_h.astype(BF)
        for s in range(n):
            ga[s] = nt(low, wo[s]).astype(BF)
            dwo[s] = tn(ai[s], low).astype(BF)


def feed_forward(place, xa, ai, dy, g2, wo, wm):
    n, tok, sw = ai.shape
    width = dy.shape[1]
    wide, _, _, ffs, dw = wm.shape

    def whole(*shape):
        return pl.BlockSpec(shape, lambda i, p: (0,) * len(shape))

    chunk = pl.BlockSpec((wide, 1, 3, ffs, dw), lambda i, p: (0, i, 0, 0, 0))
    return pl.pallas_call(
        mlp_kernel,
        out_shape=(
            jax.ShapeDtypeStruct((tok, width), BF),
            jax.ShapeDtypeStruct((tok, width), F32),
            jax.ShapeDtypeStruct((n, tok, sw), BF),
            jax.ShapeDtypeStruct(wm.shape, BF),
            jax.ShapeDtypeStruct((n, sw, width), BF),
            jax.ShapeDtypeStruct((8, width), F32),
        ),
        grid_spec=pltpu.PrefetchScalarGridSpec(
            num_scalar_prefetch=1,
            grid=(n,),
            in_specs=[
                pl.BlockSpec((1, tok, width), lambda i, p: (p[0], 0, 0)),
                whole(n, tok, sw),
                whole(tok, width),
                whole(1, width),
                whole(n, sw, width),
                chunk,
            ],
            out_specs=(
                whole(tok, width),
                whole(tok, width),
                whole(n, tok, sw),
                chunk,
                whole(n, sw, width),
                whole(8, width),
            ),
            scratch_shapes=[
                pltpu.VMEM((tok, width), F32),
                pltpu.VMEM((tok, width), BF),
                pltpu.VMEM((tok, width), F32),
                pltpu.VMEM((tok, width), F32),
            ],
        ),
        name="feed_forward",
        compiler_params=pltpu.CompilerParams(
            dimension_semantics=("arbitrary",), vmem_limit_bytes=VMEM_MAX
        ),
        cost_estimate=pl.CostEstimate(
            flops=18 * tok * width * ffs * n, bytes_accessed=40 << 20, transcendentals=tok * ffs * n
        ),
    )(place, xa, ai, dy, g2, wo, wm)


def backward_kernel(
    sizes, block, ga, xa, ws, g1, cos, sin, bias_ref, qi, ki, mi, ao, lse, gh,
    gv, gi, dwq, gg1,
    do, normed, dq, dk, dv, dcat, gow, gnp, rcv, rcv2, gis,
    do_s, do_r, gv_s, gv_r, co_s, co_r, pe_s, pe_r, gi_s, gi_r, loc,
):
    _, _, _, nh = sizes
    n = 2 * nh
    h, c, r, q = coords()
    p = c * nh + q
    row_len, sw = qi.shape
    width = xa.shape[1]
    tok = row_len // n
    short = row_len // 2
    pw = cos.shape[1]
    pairs = sw // pw
    halves = pw // HEAD_DIM
    same = c == r
    mate = (h, 1 - c, r, q)
    greet_plane(sizes, False)

    def send_do(s):
        to = (h, s // nh, r, s % nh)
        return remote(ga.at[s], do.at[p], do_s.at[s], do_r.at[p], to)

    keep_do = pltpu.make_async_copy(ga.at[p], do.at[p], loc.at[0])
    for s in range(n):
        @pl.when(p != s)
        def _():
            send_do(s).start()

    keep_do.start()
    br = 256

    def norm(i, carry):
        rows = pl.ds(pl.multiple_of(i * br, br), br)
        xf = xa[rows, :].astype(F32)
        inv = lax.rsqrt(jnp.mean(xf * xf, axis=-1, keepdims=True) + EPSILON)
        normed[rows, :] = (xf * inv * g1[...]).astype(BF)
        return carry

    lax.fori_loop(0, row_len // br, norm, 0)
    keep_do.wait()
    for s in range(n):
        @pl.when(p != s)
        def _():
            remote(ga.at[s], do.at[s], do_s.at[s], do_r.at[s], mate).wait_recv()
            send_do(s).wait_send()

    bias = bias_ref[0:1, 0:1]
    blocks = row_len // block
    per = block // tok
    causal = lax.broadcasted_iota(jnp.int32, (block, block), 0) >= lax.broadcasted_iota(
        jnp.int32, (block, block), 1
    )

    def send_gv(b, pair):
        lanes = lane_window(pair, pw, sw)
        to = (h, r, b // nh, b % nh)
        return remote(
            gow.at[b, :, lanes], gv.at[p, :, lanes], gv_s.at[pair, b], gv_r.at[pair, p], to
        )

    def keep_gv(pair):
        lanes = lane_window(pair, pw, sw)
        return pltpu.make_async_copy(gow.at[p, :, lanes], gv.at[p, :, lanes], loc.at[1 + pair])

    def pair_step(pair, carry):
        lanes = lane_window(pair, pw, sw)
        dk[...] = jnp.zeros_like(dk)
        dv[...] = jnp.zeros_like(dv)
        for i in range(blocks):
            rows = pl.ds(i * block, block)
            pieces = [[] for _ in range(i + 1)]
            dq_parts = []
            do_rows = [do[i * per + t, :, lanes] for t in range(per)]
            do_i = do_rows[0] if per == 1 else jnp.concatenate(do_rows, axis=0)
            ao_rows = [ao[i * per + t, :, lanes] for t in range(per)]
            ao_i = ao_rows[0] if per == 1 else jnp.concatenate(ao_rows, axis=0)
            product = do_i.astype(F32) * ao_i.astype(F32)
            for half in range(halves):
                cols = slice(half * HEAD_DIM, (half + 1) * HEAD_DIM)
                qh = qi[rows, lanes][:, cols]
                doh = do_i[:, cols]
                delta = jnp.sum(product[:, cols], axis=-1, keepdims=True)
                level = lse[pair, rows, half : half + 1]
                acc = 0.0
                for j in range(i + 1):
                    kj = ki[pl.ds(j * block, block), lanes][:, cols]
                    vj = mi[pl.ds(j * block, block), lanes][:, cols]
                    crossing = i * block >= short and j * block < short
                    score = masked(nt(qh, kj), i == j, crossing, causal, bias)
                    prob = jnp.exp(score - level)
                    grad_prob = nt(doh, vj)
                    grad_score = (prob * (grad_prob - delta)).astype(BF)
                    acc = acc + nn(grad_score, kj)
                    pieces[j].append((tn(grad_score, qh), tn(prob.astype(BF), doh)))
                dq_parts.append(acc * HEAD_DIM**-0.5)
            dq[rows, :] = dq_parts[0] if halves == 1 else jnp.concatenate(dq_parts, axis=1)
            for j in range(i + 1):
                at = pl.ds(j * block, block)
                if halves == 1:
                    dk[at, :] += pieces[j][0][0]
                    dv[at, :] += pieces[j][0][1]
                else:
                    dk[at, :] += jnp.concatenate([t[0] for t in pieces[j]], axis=1)
                    dv[at, :] += jnp.concatenate([t[1] for t in pieces[j]], axis=1)
        first = first_lanes(br, pw)

        def finish(i, inner_carry):
            rows = pl.ds(pl.multiple_of(i * br, br), br)
            ct = cos[rows, :]
            st = sin[rows, :]
            a = dq[rows, :]
            b = dk[rows, :]
            dcat[0, rows, lanes] = (a * ct - rotate_lanes(a, first) * st).astype(BF)
            dcat[1, rows, lanes] = (b * ct - rotate_lanes(b, first) * st).astype(BF)
            dcat[2, rows, lanes] = (0.5 * dv[rows, :].astype(BF).astype(F32)).astype(BF)
            return inner_carry

        lax.fori_loop(0, row_len // br, finish, 0)
        for b in range(n):
            gow[b, :, lanes] = dcat[2, pl.ds(b * tok, tok), lanes]

            @pl.when(jnp.logical_or(c != r, p != b))
            def _():
                send_gv(b, pair).start()

        @pl.when(same)
        def _():
            keep_gv(pair).start()

        return carry

    lax.fori_loop(0, pairs, pair_step, 0)

    ck = min(256, tok)
    half_rows = row_len // 2
    n_half = half_rows // ck
    n_blk = tok // ck

    def partial(base, k):
        rows = pl.ds(pl.multiple_of(base + k * ck, ck), ck)
        total = nn(dcat[0, rows, :], ws[:sw, :])
        for t in range(1, 3):
            total = total + nn(dcat[t, rows, :], ws[t * sw : (t + 1) * sw, :])
        gnp[rows, :] = total.astype(BF)

    def to_mate(k):
        rows = pl.ds(pl.multiple_of((1 - c) * half_rows + k * ck, ck), ck)
        return remote(gnp.at[rows], rcv.at[pl.ds(k * ck, ck)], co_s.at[k], co_r.at[k], mate)

    for k in range(n_half):
        partial((1 - c) * half_rows, k)
        to_mate(k).start()

    def own_rows(d):
        return ((q + d) % nh) * tok

    def to_peer(d, k):
        rows = pl.ds(pl.multiple_of(c * half_rows + own_rows(d) + k * ck, ck), ck)
        to = (h, c, r, (q + d) % nh)
        return remote(
            gnp.at[rows], rcv2.at[d - 1, pl.ds(k * ck, ck)], pe_s.at[d, k], pe_r.at[d, k], to
        )

    for d in range(1, nh + 1):
        for k in range(n_blk):
            partial(c * half_rows + own_rows(d), k)

    for k in range(n_half):
        to_mate(k).wait_recv()

    def added(d, k):
        rows = pl.ds(pl.multiple_of(c * half_rows + own_rows(d) + k * ck, ck), ck)
        theirs = pl.ds(pl.multiple_of(own_rows(d) + k * ck, ck), ck)
        return rows, gnp[rows, :].astype(F32) + rcv[theirs, :].astype(F32)

    for d in range(1, nh):
        for k in range(n_blk):
            rows, total = added(d, k)
            gnp[rows, :] = total.astype(BF)
            to_peer(d, k).start()

    for t in range(3):
        dwq[t * sw : (t + 1) * sw, :] = tn(dcat[t], normed[...]).astype(BF)

    partner = (h, r, c, q)
    gg1[...] = jnp.zeros_like(gg1)

    def send_gi(k):
        rows = pl.ds(k * ck, ck)
        return remote(gis.at[rows], gi.at[rows], gi_s.at[k], gi_r.at[k], partner)

    def keep_gi(k):
        rows = pl.ds(k * ck, ck)
        return pltpu.make_async_copy(gis.at[rows], gi.at[rows], gi_s.at[k])

    for k in range(n_blk):
        for d in range(1, nh):
            to_peer(d, k).wait_recv()
        _, grad_n = added(0, k)
        for d in range(1, nh):
            grad_n = grad_n + rcv2[d - 1, pl.ds(k * ck, ck), :].astype(F32)
        here = pl.ds(pl.multiple_of(p * tok + k * ck, ck), ck)
        xf = xa[here, :].astype(F32)
        inv = lax.rsqrt(jnp.mean(xf * xf, axis=-1, keepdims=True) + EPSILON)
        gg1[...] += jnp.sum((grad_n * xf * inv).reshape(-1, 8, width), axis=0)
        scaled = grad_n * g1[...]
        dot = jnp.sum(scaled * xf, axis=-1, keepdims=True)
        rows = pl.ds(k * ck, ck)
        gis[rows, :] = (
            gh[rows, :] + scaled * inv - xf * (inv * inv * inv * dot / width)
        ).astype(BF)

        @pl.when(c != r)
        def _():
            send_gi(k).start()

        @pl.when(same)
        def _():
            keep_gi(k).start()

    for k in range(n_blk):
        @pl.when(c != r)
        def _():
            send_gi(k).wait_send()
            send_gi(k).wait_recv()

        @pl.when(same)
        def _():
            keep_gi(k).wait()

    for k in range(n_half):
        to_mate(k).wait_send()
    for d in range(1, nh):
        for k in range(n_blk):
            to_peer(d, k).wait_send()

    def drain(pair, carry):
        lanes = lane_window(pair, pw, sw)
        for b in range(n):
            @pl.when(jnp.logical_or(c != r, p != b))
            def _():
                send_gv(b, pair).wait_send()
                remote(
                    gow.at[b, :, lanes], gv.at[b, :, lanes], gv_s.at[pair, b], gv_r.at[pair, b], mate
                ).wait_recv()

        @pl.when(same)
        def _():
            keep_gv(pair).wait()

        return carry

    lax.fori_loop(0, pairs, drain, 0)


def attention_backward(sizes, ga, xa, ws, g1, cos, sin, bias, qi, ki, mi, ao, lse, gh):
    _, _, _, nh = sizes
    n, tok, sw = ga.shape
    row_len, width = xa.shape
    pw = cos.shape[1]
    pairs = sw // pw
    block = max(tok, 512)
    ck = min(256, tok)
    n_half = row_len // 2 // ck
    n_blk = tok // ck
    return pl.pallas_call(
        functools.partial(backward_kernel, sizes, block),
        out_shape=(
            jax.ShapeDtypeStruct((n, tok, sw), BF),
            jax.ShapeDtypeStruct((tok, width), BF),
            jax.ShapeDtypeStruct((3 * sw, width), BF),
            jax.ShapeDtypeStruct((8, width), F32),
        ),
        in_specs=[ANY] + [VM] * 12,
        out_specs=(ANY, ANY, VM, VM),
        scratch_shapes=[
            pltpu.VMEM((n, tok, sw), BF),
            pltpu.VMEM((row_len, width), BF),
            pltpu.VMEM((row_len, pw), F32),
            pltpu.VMEM((row_len, pw), F32),
            pltpu.VMEM((row_len, pw), F32),
            pltpu.VMEM((3, row_len, sw), BF),
            pltpu.VMEM((n, tok, sw), BF),
            pltpu.VMEM((row_len, width), BF),
            pltpu.VMEM((row_len // 2, width), BF),
            pltpu.VMEM((max(nh - 1, 1), tok, width), BF),
            pltpu.VMEM((tok, width), BF),
            DMA((n,)), DMA((n,)),
            DMA((pairs, n)), DMA((pairs, n)),
            DMA((n_half,)), DMA((n_half,)),
            DMA((nh, n_blk)), DMA((nh, n_blk)),
            DMA((n_blk,)), DMA((n_blk,)),
            DMA((1 + pairs,)),
        ],
        name="attention_backward",
        compiler_params=pltpu.CompilerParams(
            collective_id=3, has_side_effects=True, vmem_limit_bytes=VMEM_MAX
        ),
        cost_estimate=pl.CostEstimate(
            flops=60 << 30, bytes_accessed=24 << 20, transcendentals=row_len * row_len * sw // 128
        ),
    )(ga, xa, ws, g1, cos, sin, bias, qi, ki, mi, ao, lse, gh)


def per_device(sizes, layer_in, value_first, seg_start, gain_one, w_qkv, w_out, gain_two, w_mlp, grad_out):
    hi_n, _, _, nh = sizes
    n = 2 * nh
    wide = 2 * hi_n
    tok, width = layer_in.shape
    sw = w_qkv.shape[1]
    ffs = w_mlp.shape[2]
    dw = w_mlp.shape[0]
    row_len = n * tok
    short = row_len // seg_start.shape[0]
    h, c, r, q = coords()
    place = (c * nh + q).astype(jnp.int32)

    w_mlp_t = jnp.transpose(w_mlp, (1, 2, 0)).reshape(3 * ffs, dw)
    wm = lax.all_gather(w_mlp_t, AXES, axis=0, tiled=False).reshape(wide, n, 3, ffs, dw)
    wo = lax.all_gather(w_out, ("zh", "zq"), axis=0, tiled=False)

    swap = [
        (((a * 2 + b) * 2 + d) * nh + e, ((a * 2 + d) * 2 + b) * nh + e)
        for a in range(hi_n)
        for b in range(2)
        for d in range(2)
        for e in range(nh)
    ]
    v_cut = value_first.reshape(tok, n, sw).transpose(1, 0, 2)
    sg = jnp.full((8, 128), seg_start[1].astype(F32))
    w_cut = w_qkv.reshape(hi_n, 3 * sw // hi_n, width)
    xa, va, ws, so = exchange_inputs(sizes, layer_in, v_cut, w_cut, sg)
    ws = ws.reshape(3 * sw, width)
    dy = lax.ppermute(grad_out, AXES, swap)

    joined = 1.0 - so[0, 0]
    index = jnp.arange(row_len, dtype=jnp.int32)
    slot = index // short
    positions = (index - slot * short).astype(F32) + jnp.where(slot == 1, joined * short, 0.0)
    pw = min(sw, 128)
    half_dim = HEAD_DIM // 2
    frequency = 10000.0 ** (-2.0 * jnp.arange(half_dim, dtype=F32) / HEAD_DIM)
    angles = positions[:, None] * frequency[None, :]
    cosine, sine = jnp.cos(angles), jnp.sin(angles)
    times = pw // HEAD_DIM
    cos = jnp.concatenate([cosine, cosine] * times, axis=1)
    sin = jnp.concatenate([-sine, sine] * times, axis=1)
    bias = (1.0 - joined) * jnp.full((8, 128), -1e30, F32)

    g1 = gain_one.reshape(1, width)
    g2 = gain_two.reshape(1, width)
    xr = xa.reshape(row_len, width)
    ai, qo, ko, mo, ao, lse, own = attention_forward(
        sizes, xr, ws, va.reshape(row_len, sw), g1, cos, sin, bias
    )
    lo, gh, ga, dwm, dwo, gg2 = feed_forward(place.reshape(1), xa, ai, dy, g2, wo, wm)
    layer_out = lax.ppermute(lo, AXES, swap)

    dwm = lax.psum_scatter(dwm, ("hi", "core"), scatter_dimension=0, tiled=True)
    dwm = lax.psum_scatter(dwm, ("zh", "zq"), scatter_dimension=1, tiled=True)
    grad_w_mlp = jnp.transpose(dwm.reshape(3, ffs, dw).astype(F32), (2, 0, 1))
    dwo = lax.psum_scatter(dwo, ("zh", "zq"), scatter_dimension=0, tiled=True)
    grad_w_out = lax.psum(dwo.reshape(sw, width), ("hi", "core")).astype(F32)

    gv, gi, dwq, gg1 = attention_backward(
        sizes, ga, xr, ws, g1, cos, sin, bias, qo, ko, mo, ao, lse, gh
    )
    grad_value_first = gv.transpose(1, 0, 2).reshape(tok, width).astype(F32)
    grad_in = gi.astype(F32)

    dwq = lax.psum_scatter(dwq, ("hi", "zh"), scatter_dimension=0, tiled=True)
    dwq = lax.all_gather(dwq, ("core", "hi", "zh"), axis=0, tiled=False)
    dwq = dwq.reshape(2, 3 * sw, width)
    grad_w_qkv = lax.dynamic_index_in_dim(dwq, r, 0, keepdims=False)
    grad_w_qkv = grad_w_qkv.reshape(3, sw, width).astype(F32)

    first_f = value_first.astype(F32)
    sums = jnp.concatenate(
        [
            jnp.sum(gg1, axis=0),
            jnp.sum(gg2, axis=0),
            jnp.sum(first_f * first_f).reshape(1),
            jnp.sum(own).reshape(1),
        ]
    )
    sums = lax.psum(sums, AXES)
    entries = tok * width * wide * n
    value_norms = jnp.sqrt(sums[2 * width :] / entries)
    return (
        layer_out,
        grad_in,
        grad_value_first,
        sums[:width],
        grad_w_qkv,
        grad_w_out,
        sums[width : 2 * width],
        grad_w_mlp,
        value_norms,
    )


def solution(mesh):
    wide, narrow = mesh.shape["wide"], mesh.shape["narrow"]
    sizes = (wide // 2, 2, 2, narrow // 2)
    fine = Mesh(mesh.devices.reshape(sizes), AXES)
    w_axes, n_axes = ("hi", "core"), ("zh", "zq")
    rows = P(AXES, None)
    return jax.shard_map(
        functools.partial(per_device, sizes),
        mesh=fine,
        in_specs=(
            rows,
            rows,
            P(w_axes),
            P(),
            P(None, n_axes, None),
            P(n_axes, None),
            P(),
            P(w_axes, None, n_axes),
            rows,
        ),
        out_specs=(
            rows,
            rows,
            rows,
            P(),
            P(None, n_axes, None),
            P(n_axes, None),
            P(),
            P(w_axes, None, n_axes),
            P(),
        ),
        check_vma=False,
    )
```

```python
import functools

import jax
import jax.numpy as jnp
from jax import lax
from jax.experimental import pallas as pl
from jax.experimental.pallas import tpu as pltpu
from jax.sharding import Mesh, PartitionSpec as P

HEAD_DIM = 64
EPSILON = 1e-06
BF = jnp.bfloat16
F32 = jnp.float32
AXES = ("hi", "core", "zh", "zq")
MESH = pl.DeviceIdType.MESH
ANY = pl.BlockSpec(memory_space=pl.ANY)
VM = pl.BlockSpec(memory_space=pltpu.VMEM)
VMEM_MAX = 62 << 20
DMA = pltpu.SemaphoreType.DMA


def nn(a, b):
    return lax.dot_general(a, b, (((1,), (0,)), ((), ())), preferred_element_type=F32)


def nt(a, b):
    return lax.dot_general(a, b, (((1,), (1,)), ((), ())), preferred_element_type=F32)


def tn(a, b):
    return lax.dot_general(a, b, (((0,), (0,)), ((), ())), preferred_element_type=F32)


def coords():
    return tuple(lax.axis_index(name) for name in AXES)


def remote(src, dst, send, recv, to):
    return pltpu.make_async_remote_copy(
        src_ref=src, dst_ref=dst, send_sem=send, recv_sem=recv, device_id=to, device_id_type=MESH
    )


def greet_plane(sizes, with_hi):
    hi_n, _, _, nh = sizes
    h, c, r, q = coords()
    barrier = pltpu.get_barrier_semaphore()
    count = 0
    for dc in range(2):
        for dr in range(2):
            for dq in range(nh):
                if dc or dr or dq:
                    to = (h, (c + dc) % 2, (r + dr) % 2, (q + dq) % nh)
                    pl.semaphore_signal(barrier, inc=1, device_id=to, device_id_type=MESH)
                    count += 1
    if with_hi:
        for dh in range(1, hi_n):
            to = ((h + dh) % hi_n, c, r, q)
            pl.semaphore_signal(barrier, inc=1, device_id=to, device_id_type=MESH)
            count += 1
    pl.semaphore_wait(barrier, count)


def rotate_lanes(values, first):
    width = values.shape[1]
    if width < 128:
        return jnp.concatenate([values[:, 32:], values[:, :32]], axis=1)
    return jnp.where(
        first, pltpu.roll(values, width - 32, 1), pltpu.roll(values, 32, 1)
    )


def first_lanes(rows, width):
    lane = lax.broadcasted_iota(jnp.int32, (rows, width), 1)
    return lane % HEAD_DIM < HEAD_DIM // 2


def lane_window(pair, pw, sw):
    return slice(0, sw) if pw == sw else pl.ds(pl.multiple_of(pair * pw, pw), pw)


def tiled(table, width):
    times = width // table.shape[1]
    return table if times == 1 else jnp.concatenate([table] * times, axis=1)


def exchange_kernel(
    sizes, chunks, x, v, w, sg, xa, va, ws, so, xs, wb, sb, vb,
    swap_s, swap_r, peer_s, peer_r, core_s, core_r, w_s, w_r, wh_s, wh_r, sg_s, sg_r, v_s, v_r, loc,
):
    hi_n, _, _, nh = sizes
    n = 2 * nh
    h, c, r, q = coords()
    p = c * nh + q
    partner_p = r * nh + q
    rows = x.shape[0] // chunks
    same = c == r
    other = c != r
    partner = (h, r, c, q)
    mate = (h, 1 - c, r, q)
    greet_plane(sizes, True)

    def part(k):
        return pl.ds(k * rows, rows)

    def swap_x(k):
        return remote(x.at[part(k)], xa.at[partner_p, part(k)], swap_s.at[k], swap_r.at[k], partner)

    def own_arrives(k):
        return remote(x.at[part(k)], xa.at[p, part(k)], swap_s.at[k], swap_r.at[k], partner)

    def push_peer(src, k, dq):
        to = (h, c, r, (q + dq) % nh)
        return remote(src, xa.at[p, part(k)], peer_s.at[dq, k], peer_r.at[dq, k], to)

    def push_mate(src, k, dq):
        block = c * nh + (q + nh - dq) % nh
        return remote(src, xa.at[block, part(k)], core_s.at[dq, k], core_r.at[dq, k], mate)

    def send_w():
        return remote(w.at[h], ws.at[h], w_s, w_r, partner)

    def spread_w(dh):
        to = ((h + dh) % hi_n, c, r, q)
        return remote(ws.at[h], ws.at[h], wh_s.at[dh], wh_r.at[dh], to)

    def send_sg():
        return remote(sg, so, sg_s, sg_r, partner)

    local_x_in = pltpu.make_async_copy(x, xs, loc.at[0])
    local_w_in = pltpu.make_async_copy(w, wb, loc.at[1])
    local_s_in = pltpu.make_async_copy(sg, sb, loc.at[2])
    local_v_in = pltpu.make_async_copy(v.at[p], vb, loc.at[3])
    local_x_out = pltpu.make_async_copy(xs, xa.at[p], loc.at[4])
    local_w_out = pltpu.make_async_copy(wb, ws, loc.at[5])
    local_s_out = pltpu.make_async_copy(sb, so, loc.at[6])
    local_v_out = pltpu.make_async_copy(vb, va.at[p], loc.at[7])

    @pl.when(other)
    def _():
        send_sg().start()
        send_w().start()
        for k in range(chunks):
            swap_x(k).start()

    @pl.when(same)
    def _():
        for k in range(chunks):
            for dq in range(1, nh):
                push_peer(x.at[part(k)], k, dq).start()
            push_mate(x.at[part(k)], k, 0).start()
        local_x_in.start()
        local_w_in.start()
        local_s_in.start()
        local_v_in.start()

    @pl.when(other)
    def _():
        for k in range(chunks):
            own_arrives(k).wait_recv()
            for dq in range(1, nh):
                push_peer(xa.at[p, part(k)], k, dq).start()
            push_mate(xa.at[p, part(k)], k, 0).start()
        send_w().wait_recv()
        for dh in range(1, hi_n):
            spread_w(dh).start()

    @pl.when(same)
    def _():
        local_x_in.wait()
        local_x_out.start()
        local_w_in.wait()
        local_w_out.start()
        local_s_in.wait()
        local_s_out.start()
        local_v_in.wait()
        local_v_out.start()

    def send_v(s):
        to = (h, s // nh, c, s % nh)
        return remote(v.at[s], va.at[r * nh + q], v_s.at[s], v_r.at[r * nh + q], to)

    for s in range(n):
        @pl.when(jnp.logical_or(other, p != s))
        def _():
            send_v(s).start()

    for k in range(chunks):
        for dq in range(1, nh):
            block = c * nh + (q + nh - dq) % nh
            remote(
                x.at[part(k)], xa.at[block, part(k)], peer_s.at[dq, k], peer_r.at[dq, k], mate
            ).wait_recv()
            push_mate(xa.at[block, part(k)], k, dq).start()

    for k in range(chunks):
        for dq in range(nh):
            block = (1 - c) * nh + (q + nh - dq) % nh
            remote(
                x.at[part(k)], xa.at[block, part(k)], core_s.at[dq, k], core_r.at[dq, k], mate
            ).wait_recv()

    @pl.when(other)
    def _():
        send_sg().wait_recv()
        for dh in range(1, hi_n):
            source = (h + hi_n - dh) % hi_n
            remote(ws.at[source], ws.at[source], wh_s.at[dh], wh_r.at[dh], mate).wait_recv()
        send_sg().wait_send()
        send_w().wait_send()
        for dh in range(1, hi_n):
            spread_w(dh).wait_send()
        for k in range(chunks):
            swap_x(k).wait_send()

    for b in range(n):
        @pl.when(jnp.logical_or(other, p != b))
        def _():
            remote(v.at[0], va.at[b], v_s.at[b], v_r.at[b], mate).wait_recv()

    for s in range(n):
        @pl.when(jnp.logical_or(other, p != s))
        def _():
            send_v(s).wait_send()

    for k in range(chunks):
        for dq in range(1, nh):
            push_peer(x.at[part(k)], k, dq).wait_send()
        for dq in range(nh):
            push_mate(x.at[part(k)], k, dq).wait_send()

    @pl.when(same)
    def _():
        local_x_out.wait()
        local_w_out.wait()
        local_s_out.wait()
        local_v_out.wait()


def exchange_inputs(sizes, x, v, w, sg):
    hi_n, _, _, nh = sizes
    n = 2 * nh
    tok, width = x.shape
    sw = v.shape[2]
    chunks = 4 if tok % 64 == 0 else 1
    return pl.pallas_call(
        functools.partial(exchange_kernel, sizes, chunks),
        out_shape=(
            jax.ShapeDtypeStruct((n, tok, width), BF),
            jax.ShapeDtypeStruct((n, tok, sw), BF),
            jax.ShapeDtypeStruct(w.shape, BF),
            jax.ShapeDtypeStruct(sg.shape, F32),
        ),
        in_specs=[ANY] * 4,
        out_specs=(ANY,) * 4,
        scratch_shapes=[
            pltpu.VMEM((tok, width), BF),
            pltpu.VMEM(w.shape, BF),
            pltpu.VMEM(sg.shape, F32),
            pltpu.VMEM((tok, sw), BF),
            DMA((chunks,)), DMA((chunks,)),
            DMA((nh, chunks)), DMA((nh, chunks)),
            DMA((nh, chunks)), DMA((nh, chunks)),
            DMA, DMA,
            DMA((hi_n,)), DMA((hi_n,)),
            DMA, DMA,
            DMA((n,)), DMA((n,)),
            DMA((8,)),
        ],
        name="exchange_inputs",
        compiler_params=pltpu.CompilerParams(collective_id=1, has_side_effects=True),
        cost_estimate=pl.CostEstimate(flops=0, bytes_accessed=160 << 20, transcendentals=0),
    )(x, v, w, sg)


def masked(scores, diagonal, crossing, causal, bias):
    if diagonal:
        return jnp.where(causal, scores, -1e30)
    if crossing:
        return scores + bias
    return scores


def forward_kernel(
    sizes, block, xa, ws, va, g1, cos, sin, bias_ref,
    ai, qo, ko, mo, ao, lse, own, att_s, att_r, loc,
):
    _, _, _, nh = sizes
    n = 2 * nh
    h, c, r, q = coords()
    p = c * nh + q
    row_len, sw = va.shape
    tok = row_len // n
    short = row_len // 2
    pw = cos.shape[1]
    pairs = sw // pw
    halves = pw // HEAD_DIM
    greet_plane(sizes, False)
    br = 256
    own[...] = jnp.zeros_like(own)

    def project(i, carry):
        rows = pl.ds(pl.multiple_of(i * br, br), br)
        xf = xa[rows, :].astype(F32)
        inv = lax.rsqrt(jnp.mean(xf * xf, axis=-1, keepdims=True) + EPSILON)
        normed = (xf * inv * g1[...]).astype(BF)
        raw = nt(normed, ws[...])
        first = first_lanes(br, sw)
        ct = tiled(cos[rows, :], sw)
        st = tiled(sin[rows, :], sw)
        q_raw = raw[:, :sw]
        k_raw = raw[:, sw : 2 * sw]
        own_vals = raw[:, 2 * sw :]
        q_rot = (q_raw * ct + rotate_lanes(q_raw, first) * st).astype(BF)
        qo[rows, :] = (q_rot.astype(F32) * HEAD_DIM**-0.5).astype(BF)
        ko[rows, :] = (k_raw * ct + rotate_lanes(k_raw, first) * st).astype(BF)
        mo[rows, :] = (0.5 * own_vals + 0.5 * va[rows, :].astype(F32)).astype(BF)
        own[...] += jnp.sum((own_vals * own_vals).reshape(br // 8, 8, sw), axis=0)
        return carry

    lax.fori_loop(0, row_len // br, project, 0)

    bias = bias_ref[0:1, 0:1]
    blocks = row_len // block
    per = block // tok
    causal = lax.broadcasted_iota(jnp.int32, (block, block), 0) >= lax.broadcasted_iota(
        jnp.int32, (block, block), 1
    )

    def send(b, pair):
        lanes = lane_window(pair, pw, sw)
        to = (h, b // nh, r, b % nh)
        return remote(
            ao.at[b, :, lanes], ai.at[p, :, lanes], att_s.at[pair, b], att_r.at[pair, p], to
        )

    def keep(pair):
        lanes = lane_window(pair, pw, sw)
        return pltpu.make_async_copy(ao.at[p, :, lanes], ai.at[p, :, lanes], loc.at[pair])

    def pair_step(pair, carry):
        lanes = lane_window(pair, pw, sw)
        for i in range(blocks):
            outs = []
            rows = pl.ds(i * block, block)
            for half in range(halves):
                cols = slice(half * HEAD_DIM, (half + 1) * HEAD_DIM)
                qh = qo[rows, lanes][:, cols]
                score = []
                for j in range(i + 1):
                    kj = ko[pl.ds(j * block, block), lanes][:, cols]
                    crossing = i * block >= short and j * block < short
                    score.append(masked(nt(qh, kj), i == j, crossing, causal, bias))
                top = functools.reduce(
                    jnp.maximum, [jnp.max(s, axis=-1, keepdims=True) for s in score]
                )
                total = 0.0
                acc = 0.0
                for j in range(i + 1):
                    e = jnp.exp(score[j] - top)
                    total = total + jnp.sum(e, axis=-1, keepdims=True)
                    vj = mo[pl.ds(j * block, block), lanes][:, cols]
                    acc = acc + nn(e.astype(BF), vj)
                outs.append(acc / total)
                lse[pair, rows, half : half + 1] = top + jnp.log(total)
            out = (jnp.concatenate(outs, axis=1) if halves > 1 else outs[0]).astype(BF)
            for t in range(per):
                b = i * per + t
                ao[b, :, lanes] = out[t * tok : (t + 1) * tok]

                @pl.when(p != b)
                def _():
                    send(b, pair).start()

        keep(pair).start()
        return carry

    lax.fori_loop(0, pairs, pair_step, 0)

    def drain(pair, carry):
        lanes = lane_window(pair, pw, sw)
        for b in range(n):
            @pl.when(p != b)
            def _():
                send(b, pair).wait_send()
                remote(
                    ao.at[b, :, lanes], ai.at[b, :, lanes], att_s.at[pair, b], att_r.at[pair, b],
                    (h, 1 - c, r, q),
                ).wait_recv()
        keep(pair).wait()
        return carry

    lax.fori_loop(0, pairs, drain, 0)


def attention_forward(sizes, xa, ws, va, g1, cos, sin, bias):
    _, _, _, nh = sizes
    n = 2 * nh
    row_len, sw = va.shape
    tok = row_len // n
    pw = cos.shape[1]
    pairs = sw // pw
    block = max(tok, 512)
    flops = 2 * row_len * xa.shape[1] * 3 * sw + 2 * row_len * row_len * sw
    return pl.pallas_call(
        functools.partial(forward_kernel, sizes, block),
        out_shape=(
            jax.ShapeDtypeStruct((n, tok, sw), BF),
            jax.ShapeDtypeStruct((row_len, sw), BF),
            jax.ShapeDtypeStruct((row_len, sw), BF),
            jax.ShapeDtypeStruct((row_len, sw), BF),
            jax.ShapeDtypeStruct((n, tok, sw), BF),
            jax.ShapeDtypeStruct((pairs, row_len, pw // HEAD_DIM), F32),
            jax.ShapeDtypeStruct((8, sw), F32),
        ),
        in_specs=[VM] * 7,
        out_specs=(ANY,) + (VM,) * 6,
        scratch_shapes=[DMA((pairs, n)), DMA((pairs, n)), DMA((pairs,))],
        name="attention_forward",
        compiler_params=pltpu.CompilerParams(
            collective_id=2, has_side_effects=True, vmem_limit_bytes=VMEM_MAX
        ),
        cost_estimate=pl.CostEstimate(
            flops=4 * flops, bytes_accessed=16 << 20, transcendentals=row_len * row_len * sw // 128
        ),
    )(xa, ws, va, g1, cos, sin, bias)


def mlp_kernel(
    xa, ai, dy, g2, wo, wm, lo, gh, ga, dsum, dosum, gg2,
    x, hid, n2, acc_o, acc_g, buf, rcv, bo, rcvo, x_s, buf_s, buf_r, bo_s, bo_r,
):
    step = pl.program_id(0)
    n = ai.shape[0]
    wide = wm.shape[0]
    width = x.shape[1]
    dw = width // wide
    hi_n = wide // 2
    rw = bo.shape[3]
    h, c, r, q = coords()
    own_x = pltpu.make_async_copy(xa.at[c * (n // 2) + q], x, x_s)
    mate = (h, 1 - c, r, q)
    slot = step % 2
    last = n - 1

    def to_mate(at):
        return remote(buf.at[at, 1 - c], rcv.at[at], buf_s.at[at], buf_r.at[at], mate)

    def out_to_mate():
        return remote(bo.at[1 - c], rcvo, bo_s, bo_r, mate)

    @pl.when(step == 0)
    def _():
        own_x.start()
        barrier = pltpu.get_barrier_semaphore()
        pl.semaphore_signal(barrier, inc=1, device_id=mate, device_id_type=MESH)
        pl.semaphore_wait(barrier, 1)
        own_x.wait()
        total = x[...].astype(F32)
        for s in range(n):
            total = total + nn(ai[s], wo[s])
        hid[...] = total
        inv = lax.rsqrt(jnp.mean(total * total, axis=-1, keepdims=True) + EPSILON)
        n2[...] = (total * inv * g2[...]).astype(BF)
        acc_o[...] = jnp.zeros_like(acc_o)
        acc_g[...] = jnp.zeros_like(acc_g)

    @pl.when(step < n)
    def _():
        @pl.when(step > 1)
        def _():
            to_mate(slot).wait_send()

        def weight(j):
            return jnp.concatenate([wm[w, 0, j] for w in range(wide)], axis=1)

        def put(j, grad):
            low = grad.astype(BF)
            for w in range(wide):
                buf[slot, w % 2, w // 2, j] = low[:, w * dw : (w + 1) * dw]

        gate = nt(n2[...], weight(0))
        up = nt(n2[...], weight(1))
        sig = jax.nn.sigmoid(gate)
        silu = gate * sig
        inner = (silu * up).astype(BF)
        grad_inner = nt(dy[...], weight(2))
        grad_gate = (grad_inner * up * sig * (1.0 + gate * (1.0 - sig))).astype(BF)
        grad_up = (grad_inner * silu).astype(BF)
        acc_o[...] += nn(inner, weight(2))
        acc_g[...] += nn(grad_gate, weight(0)) + nn(grad_up, weight(1))
        put(0, tn(grad_gate, n2[...]))
        put(1, tn(grad_up, n2[...]))
        put(2, tn(inner, dy[...]))

    @pl.when(step == last)
    def _():
        hidden = hid[...]
        lo[...] = (hidden + acc_o[...]).astype(BF)
        inv = lax.rsqrt(jnp.mean(hidden * hidden, axis=-1, keepdims=True) + EPSILON)
        grad_n = acc_g[...]
        gg2[...] = jnp.sum((grad_n * hidden * inv).reshape(-1, 8, width), axis=0)
        scaled = grad_n * g2[...]
        dot = jnp.sum(scaled * hidden, axis=-1, keepdims=True)
        grad_h = dy[...].astype(F32) + scaled * inv - hidden * (inv * inv * inv * dot / width)
        gh[...] = grad_h
        low = grad_h.astype(BF)
        for s in range(n):
            ga[s] = nt(low, wo[s]).astype(BF)
            grad_wo = tn(ai[s], low).astype(BF)
            for w in range(wide):
                bo[w % 2, w // 2, s] = grad_wo[w * rw : (w + 1) * rw]

    @pl.when(step > 0)
    def _():
        before = (step + 1) % 2
        to_mate(before).wait_recv()
        for a in range(hi_n):
            for j in range(3):
                total = buf[before, c, a, j].astype(F32) + rcv[before, a, j].astype(F32)
                dsum[a, 0, j] = total.astype(BF)

    @pl.when(step < n)
    def _():
        to_mate(slot).start()

    @pl.when(step == last)
    def _():
        out_to_mate().start()

    @pl.when(step == n)
    def _():
        out_to_mate().wait_recv()
        for a in range(hi_n):
            for s in range(n):
                total = bo[c, a, s].astype(F32) + rcvo[a, s].astype(F32)
                dosum[a, s] = total.astype(BF)
        out_to_mate().wait_send()
        to_mate(0).wait_send()
        if n > 1:
            to_mate(1).wait_send()


def feed_forward(xa, ai, dy, g2, wo, wm):
    n, tok, sw = ai.shape
    width = dy.shape[1]
    wide, _, _, ffs, dw = wm.shape
    hi_n = wide // 2
    rw = sw // wide

    def whole(*shape):
        return pl.BlockSpec(shape, lambda i: (0,) * len(shape))

    def fixed(*shape):
        return pl.BlockSpec(
            shape, lambda i: (0,) * len(shape), pipeline_mode=pl.Buffered(1)
        )

    return pl.pallas_call(
        mlp_kernel,
        out_shape=(
            jax.ShapeDtypeStruct((tok, width), BF),
            jax.ShapeDtypeStruct((tok, width), F32),
            jax.ShapeDtypeStruct((n, tok, sw), BF),
            jax.ShapeDtypeStruct((hi_n, n, 3, ffs, dw), BF),
            jax.ShapeDtypeStruct((hi_n, n, rw, width), BF),
            jax.ShapeDtypeStruct((8, width), F32),
        ),
        grid_spec=pl.GridSpec(
            grid=(n + 1,),
            in_specs=[
                ANY,
                fixed(n, tok, sw),
                fixed(tok, width),
                fixed(1, width),
                fixed(n, sw, width),
                pl.BlockSpec(
                    (wide, 1, 3, ffs, dw), lambda i: (0, jnp.minimum(i, n - 1), 0, 0, 0)
                ),
            ],
            out_specs=(
                whole(tok, width),
                whole(tok, width),
                whole(n, tok, sw),
                pl.BlockSpec(
                    (hi_n, 1, 3, ffs, dw), lambda i: (0, jnp.maximum(i - 1, 0), 0, 0, 0)
                ),
                whole(hi_n, n, rw, width),
                whole(8, width),
            ),
            scratch_shapes=[
                pltpu.VMEM((tok, width), BF),
                pltpu.VMEM((tok, width), F32),
                pltpu.VMEM((tok, width), BF),
                pltpu.VMEM((tok, width), F32),
                pltpu.VMEM((tok, width), F32),
                pltpu.VMEM((2, 2, hi_n, 3, ffs, dw), BF),
                pltpu.VMEM((2, hi_n, 3, ffs, dw), BF),
                pltpu.VMEM((2, hi_n, n, rw, width), BF),
                pltpu.VMEM((hi_n, n, rw, width), BF),
                DMA, DMA((2,)), DMA((2,)), DMA, DMA,
            ],
        ),
        name="feed_forward",
        compiler_params=pltpu.CompilerParams(
            dimension_semantics=("arbitrary",),
            collective_id=4,
            has_side_effects=True,
            vmem_limit_bytes=VMEM_MAX,
        ),
        cost_estimate=pl.CostEstimate(
            flops=18 * tok * width * ffs * n, bytes_accessed=40 << 20, transcendentals=tok * ffs * n
        ),
    )(xa, ai, dy, g2, wo, wm)


def backward_kernel(
    sizes, block, ga, ds, dos, lo, xa, ws, g1, cos, sin, bias_ref, qi, ki, mi, ao, lse, gh,
    gv, gi, dwq, gg1, lo_in, rx, rxo, zr, zo,
    do, normed, dq, dk, dv, dcat, gow, gnp, rcv, rcv2, gis, part, zs, zos, do_part,
    do_s, do_r, gv_s, gv_r, co_s, co_r, pe_s, pe_r, gi_s, gi_r, loc,
    rx_s, rx_r, rxo_s, rxo_r, lo_s, lo_r, ld, z_s, z_r, zo_s, zo_r,
):
    hi_n, _, _, nh = sizes
    n = 2 * nh
    h, c, r, q = coords()
    p = c * nh + q
    row_len, sw = qi.shape
    width = xa.shape[1]
    tok = row_len // n
    short = row_len // 2
    pw = cos.shape[1]
    pairs = sw // pw
    halves = pw // HEAD_DIM
    same = c == r
    mate = (h, 1 - c, r, q)
    swap_to = (h, r, c, q)
    zed = r * nh + q
    greet_plane(sizes, True)

    def over_hi(dh, i):
        to = (h + dh) % hi_n
        return remote(
            ds.at[to, i], rx.at[dh - 1, i], rx_s.at[dh, i], rx_r.at[dh, i], (to, c, r, q)
        )

    def out_over_hi(dh):
        to = (h + dh) % hi_n
        return remote(dos.at[to], rxo.at[dh - 1], rxo_s.at[dh], rxo_r.at[dh], (to, c, r, q))

    def send_lo():
        return remote(lo, lo_in, lo_s, lo_r, swap_to)

    def over_z(i):
        return remote(zs.at[i], zr.at[zed], z_s.at[i], z_r.at[zed], (h, c, i // nh, i % nh))

    def out_over_z(i):
        return remote(zos.at[i], zo.at[zed], zo_s.at[i], zo_r.at[zed], (h, c, i // nh, i % nh))

    def keep_z(i):
        return pltpu.make_async_copy(zs.at[i], zr.at[i], z_s.at[i])

    def keep_out_z(i):
        return pltpu.make_async_copy(zos.at[i], zo.at[i], zo_s.at[i])

    def load_chunk(i):
        copies = [pltpu.make_async_copy(ds.at[h, i], part.at[0], ld.at[0])]
        for dh in range(1, hi_n):
            copies.append(pltpu.make_async_copy(rx.at[dh - 1, i], part.at[dh], ld.at[dh]))
        return copies

    def reduce_chunk(i):
        for dh in range(1, hi_n):
            over_hi(dh, i).wait_recv()
        for copy in load_chunk(i):
            copy.start()
        for copy in load_chunk(i):
            copy.wait()
        for j in range(3):
            total = part[0, j].astype(F32)
            for dh in range(1, hi_n):
                total = total + part[dh, j].astype(F32)
            zs[i, j] = total.astype(BF)

        @pl.when(zed != i)
        def _():
            over_z(i).start()

        @pl.when(zed == i)
        def _():
            keep_z(i).start()

    own_out = pltpu.make_async_copy(dos.at[h], zos, ld.at[0])

    def reduce_out():
        own_out.start()
        own_out.wait()
        for dh in range(1, hi_n):
            out_over_hi(dh).wait_recv()
            copy = pltpu.make_async_copy(rxo.at[dh - 1], do_part, ld.at[dh])
            copy.start()
            copy.wait()
            zos[...] = (zos[...].astype(F32) + do_part[...].astype(F32)).astype(BF)
        for i in range(n):
            @pl.when(zed != i)
            def _():
                out_over_z(i).start()

            @pl.when(zed == i)
            def _():
                keep_out_z(i).start()

    @pl.when(c != r)
    def _():
        send_lo().start()

    for dh in range(1, hi_n):
        out_over_hi(dh).start()

    def send_do(s):
        to = (h, s // nh, r, s % nh)
        return remote(ga.at[s], do.at[p], do_s.at[s], do_r.at[p], to)

    keep_do = pltpu.make_async_copy(ga.at[p], do.at[p], loc.at[0])
    for s in range(n):
        @pl.when(p != s)
        def _():
            send_do(s).start()

    keep_do.start()
    for i in range(n):
        for dh in range(1, hi_n):
            over_hi(dh, i).start()
    br = 256

    def norm(i, carry):
        rows = pl.ds(pl.multiple_of(i * br, br), br)
        xf = xa[rows, :].astype(F32)
        inv = lax.rsqrt(jnp.mean(xf * xf, axis=-1, keepdims=True) + EPSILON)
        normed[rows, :] = (xf * inv * g1[...]).astype(BF)
        return carry

    lax.fori_loop(0, row_len // br, norm, 0)
    keep_do.wait()
    for s in range(n):
        @pl.when(p != s)
        def _():
            remote(ga.at[s], do.at[s], do_s.at[s], do_r.at[s], mate).wait_recv()
            send_do(s).wait_send()

    bias = bias_ref[0:1, 0:1]
    blocks = row_len // block
    per = block // tok
    causal = lax.broadcasted_iota(jnp.int32, (block, block), 0) >= lax.broadcasted_iota(
        jnp.int32, (block, block), 1
    )

    def send_gv(b, pair):
        lanes = lane_window(pair, pw, sw)
        to = (h, r, b // nh, b % nh)
        return remote(
            gow.at[b, :, lanes], gv.at[p, :, lanes], gv_s.at[pair, b], gv_r.at[pair, p], to
        )

    def keep_gv(pair):
        lanes = lane_window(pair, pw, sw)
        return pltpu.make_async_copy(gow.at[p, :, lanes], gv.at[p, :, lanes], loc.at[1 + pair])

    def pair_step(pair, carry):
        lanes = lane_window(pair, pw, sw)
        dk[...] = jnp.zeros_like(dk)
        dv[...] = jnp.zeros_like(dv)
        for i in range(blocks):
            rows = pl.ds(i * block, block)
            pieces = [[] for _ in range(i + 1)]
            dq_parts = []
            do_rows = [do[i * per + t, :, lanes] for t in range(per)]
            do_i = do_rows[0] if per == 1 else jnp.concatenate(do_rows, axis=0)
            ao_rows = [ao[i * per + t, :, lanes] for t in range(per)]
            ao_i = ao_rows[0] if per == 1 else jnp.concatenate(ao_rows, axis=0)
            product = do_i.astype(F32) * ao_i.astype(F32)
            for half in range(halves):
                cols = slice(half * HEAD_DIM, (half + 1) * HEAD_DIM)
                qh = qi[rows, lanes][:, cols]
                doh = do_i[:, cols]
                delta = jnp.sum(product[:, cols], axis=-1, keepdims=True)
                level = lse[pair, rows, half : half + 1]
                acc = 0.0
                for j in range(i + 1):
                    kj = ki[pl.ds(j * block, block), lanes][:, cols]
                    vj = mi[pl.ds(j * block, block), lanes][:, cols]
                    crossing = i * block >= short and j * block < short
                    score = masked(nt(qh, kj), i == j, crossing, causal, bias)
                    prob = jnp.exp(score - level)
                    grad_prob = nt(doh, vj)
                    grad_score = (prob * (grad_prob - delta)).astype(BF)
                    acc = acc + nn(grad_score, kj)
                    pieces[j].append((tn(grad_score, qh), tn(prob.astype(BF), doh)))
                dq_parts.append(acc * HEAD_DIM**-0.5)
            dq[rows, :] = dq_parts[0] if halves == 1 else jnp.concatenate(dq_parts, axis=1)
            for j in range(i + 1):
                at = pl.ds(j * block, block)
                if halves == 1:
                    dk[at, :] += pieces[j][0][0]
                    dv[at, :] += pieces[j][0][1]
                else:
                    dk[at, :] += jnp.concatenate([t[0] for t in pieces[j]], axis=1)
                    dv[at, :] += jnp.concatenate([t[1] for t in pieces[j]], axis=1)
        first = first_lanes(br, pw)

        def finish(i, inner_carry):
            rows = pl.ds(pl.multiple_of(i * br, br), br)
            ct = cos[rows, :]
            st = sin[rows, :]
            a = dq[rows, :]
            b = dk[rows, :]
            dcat[0, rows, lanes] = (a * ct - rotate_lanes(a, first) * st).astype(BF)
            dcat[1, rows, lanes] = (b * ct - rotate_lanes(b, first) * st).astype(BF)
            dcat[2, rows, lanes] = (0.5 * dv[rows, :].astype(BF).astype(F32)).astype(BF)
            return inner_carry

        lax.fori_loop(0, row_len // br, finish, 0)
        for b in range(n):
            gow[b, :, lanes] = dcat[2, pl.ds(b * tok, tok), lanes]

            @pl.when(jnp.logical_or(c != r, p != b))
            def _():
                send_gv(b, pair).start()

        @pl.when(same)
        def _():
            keep_gv(pair).start()

        return carry

    lax.fori_loop(0, pairs, pair_step, 0)
    reduce_out()
    for i in range(n - 1):
        reduce_chunk(i)

    ck = min(256, tok)
    half_rows = row_len // 2
    n_half = half_rows // ck
    n_blk = tok // ck

    def partial(base, k):
        rows = pl.ds(pl.multiple_of(base + k * ck, ck), ck)
        total = nn(dcat[0, rows, :], ws[:sw, :])
        for t in range(1, 3):
            total = total + nn(dcat[t, rows, :], ws[t * sw : (t + 1) * sw, :])
        gnp[rows, :] = total.astype(BF)

    def to_mate(k):
        rows = pl.ds(pl.multiple_of((1 - c) * half_rows + k * ck, ck), ck)
        return remote(gnp.at[rows], rcv.at[pl.ds(k * ck, ck)], co_s.at[k], co_r.at[k], mate)

    for k in range(n_half):
        partial((1 - c) * half_rows, k)
        to_mate(k).start()

    def own_rows(d):
        return ((q + d) % nh) * tok

    def to_peer(d, k):
        rows = pl.ds(pl.multiple_of(c * half_rows + own_rows(d) + k * ck, ck), ck)
        to = (h, c, r, (q + d) % nh)
        return remote(
            gnp.at[rows], rcv2.at[d - 1, pl.ds(k * ck, ck)], pe_s.at[d, k], pe_r.at[d, k], to
        )

    for d in range(1, nh + 1):
        for k in range(n_blk):
            partial(c * half_rows + own_rows(d), k)

    for k in range(n_half):
        to_mate(k).wait_recv()

    def added(d, k):
        rows = pl.ds(pl.multiple_of(c * half_rows + own_rows(d) + k * ck, ck), ck)
        theirs = pl.ds(pl.multiple_of(own_rows(d) + k * ck, ck), ck)
        return rows, gnp[rows, :].astype(F32) + rcv[theirs, :].astype(F32)

    for d in range(1, nh):
        for k in range(n_blk):
            rows, total = added(d, k)
            gnp[rows, :] = total.astype(BF)
            to_peer(d, k).start()

    for t in range(3):
        dwq[t * sw : (t + 1) * sw, :] = tn(dcat[t], normed[...]).astype(BF)

    reduce_chunk(n - 1)
    partner = swap_to
    gg1[...] = jnp.zeros_like(gg1)

    def send_gi(k):
        rows = pl.ds(k * ck, ck)
        return remote(gis.at[rows], gi.at[rows], gi_s.at[k], gi_r.at[k], partner)

    def keep_gi(k):
        rows = pl.ds(k * ck, ck)
        return pltpu.make_async_copy(gis.at[rows], gi.at[rows], gi_s.at[k])

    for k in range(n_blk):
        for d in range(1, nh):
            to_peer(d, k).wait_recv()
        _, grad_n = added(0, k)
        for d in range(1, nh):
            grad_n = grad_n + rcv2[d - 1, pl.ds(k * ck, ck), :].astype(F32)
        here = pl.ds(pl.multiple_of(p * tok + k * ck, ck), ck)
        xf = xa[here, :].astype(F32)
        inv = lax.rsqrt(jnp.mean(xf * xf, axis=-1, keepdims=True) + EPSILON)
        gg1[...] += jnp.sum((grad_n * xf * inv).reshape(-1, 8, width), axis=0)
        scaled = grad_n * g1[...]
        dot = jnp.sum(scaled * xf, axis=-1, keepdims=True)
        rows = pl.ds(k * ck, ck)
        gis[rows, :] = (
            gh[rows, :] + scaled * inv - xf * (inv * inv * inv * dot / width)
        ).astype(BF)

        @pl.when(c != r)
        def _():
            send_gi(k).start()

        @pl.when(same)
        def _():
            keep_gi(k).start()

    for k in range(n_blk):
        @pl.when(c != r)
        def _():
            send_gi(k).wait_send()
            send_gi(k).wait_recv()

        @pl.when(same)
        def _():
            keep_gi(k).wait()

    for k in range(n_half):
        to_mate(k).wait_send()
    for d in range(1, nh):
        for k in range(n_blk):
            to_peer(d, k).wait_send()

    def drain(pair, carry):
        lanes = lane_window(pair, pw, sw)
        for b in range(n):
            @pl.when(jnp.logical_or(c != r, p != b))
            def _():
                send_gv(b, pair).wait_send()
                remote(
                    gow.at[b, :, lanes], gv.at[b, :, lanes], gv_s.at[pair, b], gv_r.at[pair, b], mate
                ).wait_recv()

        @pl.when(same)
        def _():
            keep_gv(pair).wait()

        return carry

    lax.fori_loop(0, pairs, drain, 0)

    @pl.when(c != r)
    def _():
        send_lo().wait_send()
        send_lo().wait_recv()

    for dh in range(1, hi_n):
        out_over_hi(dh).wait_send()
        for i in range(n):
            over_hi(dh, i).wait_send()
    for i in range(n):
        @pl.when(zed != i)
        def _():
            over_z(i).wait_send()
            out_over_z(i).wait_send()
            remote(zs.at[i], zr.at[i], z_s.at[i], z_r.at[i], mate).wait_recv()
            remote(zos.at[i], zo.at[i], zo_s.at[i], zo_r.at[i], mate).wait_recv()

        @pl.when(zed == i)
        def _():
            keep_z(i).wait()
            keep_out_z(i).wait()


def attention_backward(sizes, ga, ds, dos, lo, xa, ws, g1, cos, sin, bias, qi, ki, mi, ao, lse, gh):
    _, _, _, nh = sizes
    n, tok, sw = ga.shape
    row_len, width = xa.shape
    pw = cos.shape[1]
    pairs = sw // pw
    block = max(tok, 512)
    ck = min(256, tok)
    n_half = row_len // 2 // ck
    n_blk = tok // ck
    hi_n = sizes[0]
    _, _, _, ffs, dw = ds.shape
    rw = dos.shape[2]
    others = max(hi_n - 1, 1)
    return pl.pallas_call(
        functools.partial(backward_kernel, sizes, block),
        out_shape=(
            jax.ShapeDtypeStruct((n, tok, sw), BF),
            jax.ShapeDtypeStruct((tok, width), BF),
            jax.ShapeDtypeStruct((3 * sw, width), BF),
            jax.ShapeDtypeStruct((8, width), F32),
            jax.ShapeDtypeStruct((tok, width), BF),
            jax.ShapeDtypeStruct((others, n, 3, ffs, dw), BF),
            jax.ShapeDtypeStruct((others, n, rw, width), BF),
            jax.ShapeDtypeStruct((n, 3, ffs, dw), BF),
            jax.ShapeDtypeStruct((n, rw, width), BF),
        ),
        in_specs=[ANY] * 4 + [VM] * 12,
        out_specs=(ANY, ANY, VM, VM) + (ANY,) * 5,
        scratch_shapes=[
            pltpu.VMEM((n, tok, sw), BF),
            pltpu.VMEM((row_len, width), BF),
            pltpu.VMEM((row_len, pw), F32),
            pltpu.VMEM((row_len, pw), F32),
            pltpu.VMEM((row_len, pw), F32),
            pltpu.VMEM((3, row_len, sw), BF),
            pltpu.VMEM((n, tok, sw), BF),
            pltpu.VMEM((row_len, width), BF),
            pltpu.VMEM((row_len // 2, width), BF),
            pltpu.VMEM((max(nh - 1, 1), tok, width), BF),
            pltpu.VMEM((tok, width), BF),
            pltpu.VMEM((hi_n, 3, ffs, dw), BF),
            pltpu.VMEM((n, 3, ffs, dw), BF),
            pltpu.VMEM((n, rw, width), BF),
            pltpu.VMEM((n, rw, width), BF),
            DMA((n,)), DMA((n,)),
            DMA((pairs, n)), DMA((pairs, n)),
            DMA((n_half,)), DMA((n_half,)),
            DMA((nh, n_blk)), DMA((nh, n_blk)),
            DMA((n_blk,)), DMA((n_blk,)),
            DMA((1 + pairs,)),
            DMA((hi_n, n)), DMA((hi_n, n)),
            DMA((hi_n,)), DMA((hi_n,)),
            DMA, DMA,
            DMA((hi_n,)),
            DMA((n,)), DMA((n,)),
            DMA((n,)), DMA((n,)),
        ],
        name="attention_backward",
        compiler_params=pltpu.CompilerParams(
            collective_id=3, has_side_effects=True, vmem_limit_bytes=VMEM_MAX
        ),
        cost_estimate=pl.CostEstimate(
            flops=60 << 30, bytes_accessed=24 << 20, transcendentals=row_len * row_len * sw // 128
        ),
    )(ga, ds, dos, lo, xa, ws, g1, cos, sin, bias, qi, ki, mi, ao, lse, gh)


def finish_kernel(
    sizes, dwq, sm, zo, fin, og, total,
    r1, s1, r2, s2, own, mine,
    a_s, a_r, b_s, b_r, c_s, c_r, d_s, d_r, e_s, e_r, f_s, f_r, m_s, m_r,
):
    hi_n, _, _, nh = sizes
    n = 2 * nh
    h, c, r, q = coords()
    wide = 2 * hi_n
    w = 2 * h + c
    mate = (h, 1 - c, r, q)
    same = c == r
    barrier = pltpu.get_barrier_semaphore()
    count = 0
    for dh in range(hi_n):
        for dc in range(2):
            if dh or dc:
                to = ((h + dh) % hi_n, (c + dc) % 2, r, q)
                pl.semaphore_signal(barrier, inc=1, device_id=to, device_id_type=MESH)
                count += 1
    for dc in range(2):
        for dz in range(1, n):
            to = (h, (c + dc) % 2, ((r * nh + q + dz) % n) // nh, ((r * nh + q + dz) % n) % nh)
            pl.semaphore_signal(barrier, inc=1, device_id=to, device_id_type=MESH)
            count += 1
    pl.semaphore_wait(barrier, count)

    def hi_part(dh):
        to = (h + dh) % hi_n
        return remote(dwq.at[to], r1.at[dh - 1], a_s.at[dh], a_r.at[dh], (to, c, r, q))

    def hi_small(dh):
        to = ((h + dh) % hi_n, c, r, q)
        return remote(sm, s1.at[h], b_s.at[dh], b_r.at[dh], to)

    for dh in range(1, hi_n):
        hi_small(dh).start()
    for dh in range(1, hi_n):
        hi_part(dh).start()

    out_rows = zo[0].astype(F32)
    for i in range(1, n):
        out_rows = out_rows + zo[i].astype(F32)
    own[...] = out_rows.astype(BF)
    og[w] = own[...]

    def plane_out(dh, dc):
        to = ((h + dh) % hi_n, (c + dc) % 2, r, q)
        return remote(own, og.at[w], c_s.at[dh, dc], c_r.at[dh, dc], to)

    for dh in range(hi_n):
        for dc in range(2):
            if dh or dc:
                plane_out(dh, dc).start()

    s1[h] = sm[...]
    for dh in range(1, hi_n):
        source = (h + hi_n - dh) % hi_n
        remote(sm, s1.at[source], b_s.at[dh], b_r.at[dh], mate).wait_recv()
    small = s1[0]
    for i in range(1, hi_n):
        small = small + s1[i]
    spot = c * n + r * nh + q
    s2[spot] = small

    def plane_small(k):
        dc, dz = k // n, k % n
        z = (r * nh + q + dz) % n
        to = (h, (c + dc) % 2, z // nh, z % nh)
        return remote(s2.at[spot], s2.at[spot], d_s.at[k], d_r.at[k], to)

    def small_arrives(k):
        dc, dz = k // n, k % n
        source = ((c + dc) % 2) * n + (r * nh + q + n - dz) % n
        return remote(s2.at[source], s2.at[source], d_s.at[k], d_r.at[k], mate)

    for k in range(1, 2 * n):
        plane_small(k).start()

    part = dwq[h].astype(F32)
    for dh in range(1, hi_n):
        hi_part(dh).wait_recv()
        part = part + r1[dh - 1].astype(F32)
    mine[...] = part.astype(BF)
    across = remote(mine, r2, e_s, e_r, (h, c, 1 - r, q))

    @pl.when(c != r)
    def _():
        across.start()

    def spread(dh):
        to = ((h + dh) % hi_n, c, r, q)
        return remote(fin.at[h], fin.at[h], f_s.at[dh], f_r.at[dh], to)

    def share(dh):
        block = (h + hi_n - dh) % hi_n
        return remote(fin.at[block], fin.at[block], m_s.at[dh], m_r.at[dh], mate)

    @pl.when(same)
    def _():
        across.wait_recv()
        fin[h] = (mine[...].astype(F32) + r2[...].astype(F32)).astype(BF)
        for dh in range(1, hi_n):
            spread(dh).start()
        share(0).start()
        for dh in range(1, hi_n):
            block = (h + hi_n - dh) % hi_n
            remote(fin.at[h], fin.at[block], f_s.at[dh], f_r.at[dh], mate).wait_recv()
            share(dh).start()

    for k in range(1, 2 * n):
        small_arrives(k).wait_recv()
    whole = s2[0]
    for k in range(1, 2 * n):
        whole = whole + s2[k]
    total[...] = whole

    @pl.when(c != r)
    def _():
        for dh in range(hi_n):
            share(dh).wait_recv()
        across.wait_send()

    @pl.when(same)
    def _():
        for dh in range(1, hi_n):
            spread(dh).wait_send()
        for dh in range(hi_n):
            share(dh).wait_send()

    for dh in range(hi_n):
        for dc in range(2):
            if dh or dc:
                theirs = 2 * ((h + hi_n - dh) % hi_n) + (c + dc) % 2
                remote(own, og.at[theirs], c_s.at[dh, dc], c_r.at[dh, dc], mate).wait_recv()
                plane_out(dh, dc).wait_send()
    for dh in range(1, hi_n):
        hi_small(dh).wait_send()
        hi_part(dh).wait_send()
    for k in range(1, 2 * n):
        plane_small(k).wait_send()


def finish(sizes, dwq, sm, zo):
    hi_n, _, _, nh = sizes
    n = 2 * nh
    wide = 2 * hi_n
    others = max(hi_n - 1, 1)
    rw, width = zo.shape[1:]
    return pl.pallas_call(
        functools.partial(finish_kernel, sizes),
        out_shape=(
            jax.ShapeDtypeStruct(dwq.shape, BF),
            jax.ShapeDtypeStruct((wide, rw, width), BF),
            jax.ShapeDtypeStruct(sm.shape, F32),
        ),
        in_specs=[VM] * 3,
        out_specs=(VM,) * 3,
        scratch_shapes=[
            pltpu.VMEM((others,) + dwq.shape[1:], BF),
            pltpu.VMEM((hi_n,) + sm.shape, F32),
            pltpu.VMEM(dwq.shape[1:], BF),
            pltpu.VMEM((2 * n,) + sm.shape, F32),
            pltpu.VMEM((rw, width), BF),
            pltpu.VMEM(dwq.shape[1:], BF),
            DMA((hi_n,)), DMA((hi_n,)),
            DMA((hi_n,)), DMA((hi_n,)),
            DMA((hi_n, 2)), DMA((hi_n, 2)),
            DMA((2 * n,)), DMA((2 * n,)),
            DMA, DMA,
            DMA((hi_n,)), DMA((hi_n,)),
            DMA((hi_n,)), DMA((hi_n,)),
        ],
        name="finish",
        compiler_params=pltpu.CompilerParams(
            collective_id=5, has_side_effects=True, vmem_limit_bytes=VMEM_MAX
        ),
    )(dwq, sm, zo)


def per_device(sizes, layer_in, value_first, seg_start, gain_one, w_qkv, w_out, gain_two, w_mlp, grad_out):
    hi_n, _, _, nh = sizes
    n = 2 * nh
    wide = 2 * hi_n
    tok, width = layer_in.shape
    sw = w_qkv.shape[1]
    ffs = w_mlp.shape[2]
    dw = w_mlp.shape[0]
    row_len = n * tok
    short = row_len // seg_start.shape[0]
    h, c, r, q = coords()

    w_mlp_t = jnp.transpose(w_mlp, (1, 2, 0)).reshape(3 * ffs, dw)
    wm = lax.all_gather(w_mlp_t, AXES, axis=0, tiled=False).reshape(wide, n, 3, ffs, dw)
    wo = lax.all_gather(w_out, ("zh", "zq"), axis=0, tiled=False)

    swap = [
        (((a * 2 + b) * 2 + d) * nh + e, ((a * 2 + d) * 2 + b) * nh + e)
        for a in range(hi_n)
        for b in range(2)
        for d in range(2)
        for e in range(nh)
    ]
    v_cut = value_first.reshape(tok, n, sw).transpose(1, 0, 2)
    sg = jnp.full((8, 128), seg_start[1].astype(F32))
    w_cut = w_qkv.reshape(hi_n, 3 * sw // hi_n, width)
    xa, va, ws, so = exchange_inputs(sizes, layer_in, v_cut, w_cut, sg)
    ws = ws.reshape(3 * sw, width)
    dy = lax.ppermute(grad_out, AXES, swap)

    joined = 1.0 - so[0, 0]
    index = jnp.arange(row_len, dtype=jnp.int32)
    slot = index // short
    positions = (index - slot * short).astype(F32) + jnp.where(slot == 1, joined * short, 0.0)
    pw = min(sw, 128)
    half_dim = HEAD_DIM // 2
    frequency = 10000.0 ** (-2.0 * jnp.arange(half_dim, dtype=F32) / HEAD_DIM)
    angles = positions[:, None] * frequency[None, :]
    cosine, sine = jnp.cos(angles), jnp.sin(angles)
    times = pw // HEAD_DIM
    cos = jnp.concatenate([cosine, cosine] * times, axis=1)
    sin = jnp.concatenate([-sine, sine] * times, axis=1)
    bias = (1.0 - joined) * jnp.full((8, 128), -1e30, F32)

    g1 = gain_one.reshape(1, width)
    g2 = gain_two.reshape(1, width)
    xr = xa.reshape(row_len, width)
    ai, qo, ko, mo, ao, lse, own = attention_forward(
        sizes, xr, ws, va.reshape(row_len, sw), g1, cos, sin, bias
    )
    lo, gh, ga, ds, dos, gg2 = feed_forward(xa, ai, dy, g2, wo, wm)
    gv, gi, dwq, gg1, lo_in, _, _, zr, zo = attention_backward(
        sizes, ga, ds, dos, lo, xr, ws, g1, cos, sin, bias, qo, ko, mo, ao, lse, gh
    )
    first_f = value_first.astype(F32)
    lane = jnp.arange(width)
    third = jnp.where(
        lane == 0, jnp.sum(first_f * first_f), jnp.where(lane == 1, jnp.sum(own), 0.0)
    )
    small = jnp.stack([jnp.sum(gg1, axis=0), jnp.sum(gg2, axis=0), third] + [jnp.zeros_like(third)] * 5)
    fin, og, sums = finish(sizes, dwq.reshape(hi_n, 3 * sw // hi_n, width), small, zo)

    layer_out = jnp.where(c == r, lo, lo_in)
    grad_value_first = gv.transpose(1, 0, 2).reshape(tok, width).astype(F32)
    grad_in = gi.astype(F32)
    grad_w_mlp = jnp.transpose(jnp.sum(zr.astype(F32), axis=0), (2, 0, 1))
    grad_w_out = og.reshape(sw, width).astype(F32)
    grad_w_qkv = fin.reshape(3, sw, width).astype(F32)
    entries = tok * width * wide * n
    value_norms = jnp.sqrt(sums[2, :2] / entries)
    return (
        layer_out,
        grad_in,
        grad_value_first,
        sums[0],
        grad_w_qkv,
        grad_w_out,
        sums[1],
        grad_w_mlp,
        value_norms,
    )


def solution(mesh):
    wide, narrow = mesh.shape["wide"], mesh.shape["narrow"]
    sizes = (wide // 2, 2, 2, narrow // 2)
    fine = Mesh(mesh.devices.reshape(sizes), AXES)
    w_axes, n_axes = ("hi", "core"), ("zh", "zq")
    rows = P(AXES, None)
    return jax.shard_map(
        functools.partial(per_device, sizes),
        mesh=fine,
        in_specs=(
            rows,
            rows,
            P(w_axes),
            P(),
            P(None, n_axes, None),
            P(n_axes, None),
            P(),
            P(w_axes, None, n_axes),
            rows,
        ),
        out_specs=(
            rows,
            rows,
            rows,
            P(),
            P(None, n_axes, None),
            P(n_axes, None),
            P(),
            P(w_axes, None, n_axes),
            P(),
        ),
        check_vma=False,
    )
```

```python
import functools

import jax
import jax.numpy as jnp
import numpy as np
from jax import lax
from jax.experimental import pallas as pl
from jax.experimental.pallas import tpu as pltpu
from jax.sharding import Mesh, PartitionSpec as P

HEAD_DIM = 64
EPSILON = 1e-06
BF = jnp.bfloat16
F32 = jnp.float32
AXES = ("hi", "core", "zh", "zq")
MESH = pl.DeviceIdType.MESH
ANY = pl.BlockSpec(memory_space=pl.ANY)
VM = pl.BlockSpec(memory_space=pltpu.VMEM)
VMEM_MAX = 62 << 20
DMA = pltpu.SemaphoreType.DMA


def nn(a, b):
    return lax.dot_general(a, b, (((1,), (0,)), ((), ())), preferred_element_type=F32)


def nt(a, b):
    return lax.dot_general(a, b, (((1,), (1,)), ((), ())), preferred_element_type=F32)


def tn(a, b):
    return lax.dot_general(a, b, (((0,), (0,)), ((), ())), preferred_element_type=F32)


def coords():
    return tuple(lax.axis_index(name) for name in AXES)


def remote(src, dst, send, recv, to):
    return pltpu.make_async_remote_copy(
        src_ref=src, dst_ref=dst, send_sem=send, recv_sem=recv, device_id=to, device_id_type=MESH
    )


def greet_plane(sizes, with_hi):
    hi_n, _, _, nh = sizes
    h, c, r, q = coords()
    barrier = pltpu.get_barrier_semaphore()
    count = 0
    for dc in range(2):
        for dr in range(2):
            for dq in range(nh):
                if dc or dr or dq:
                    to = (h, (c + dc) % 2, (r + dr) % 2, (q + dq) % nh)
                    pl.semaphore_signal(barrier, inc=1, device_id=to, device_id_type=MESH)
                    count += 1
    if with_hi:
        for dh in range(1, hi_n):
            to = ((h + dh) % hi_n, c, r, q)
            pl.semaphore_signal(barrier, inc=1, device_id=to, device_id_type=MESH)
            count += 1
    pl.semaphore_wait(barrier, count)


def rotate_lanes(values, first):
    width = values.shape[1]
    if width < 128:
        return jnp.concatenate([values[:, 32:], values[:, :32]], axis=1)
    return jnp.where(
        first, pltpu.roll(values, width - 32, 1), pltpu.roll(values, 32, 1)
    )


def first_lanes(rows, width):
    lane = lax.broadcasted_iota(jnp.int32, (rows, width), 1)
    return lane % HEAD_DIM < HEAD_DIM // 2


def lane_window(pair, pw, sw):
    return slice(0, sw) if pw == sw else pl.ds(pl.multiple_of(pair * pw, pw), pw)


def rope_rows(lo_c, lo_s, hi_c, hi_s, flag, i, rows):
    step = lo_c.shape[0]
    half = hi_c.shape[0] // 2
    cos, sin = [], []
    for u in range(rows // step):
        k = i * (rows // step) + u
        far, near = pl.ds(k, 1), pl.ds(k % half, 1)
        ch = hi_c[near, :] * flag + hi_c[far, :] * (1.0 - flag)
        sh = hi_s[near, :] * flag + hi_s[far, :] * (1.0 - flag)
        cos.append(lo_c[...] * ch - lo_s[...] * sh)
        sin.append(lo_s[...] * ch + lo_c[...] * sh)
    cos = jnp.concatenate(cos, axis=0)
    sin = jnp.concatenate(sin, axis=0)
    return cos, jnp.where(first_lanes(rows, cos.shape[1]), -sin, sin)


def rope_parts(row_len, pw):
    half = HEAD_DIM // 2
    frequency = 10000.0 ** (-2.0 * np.arange(half) / HEAD_DIM)
    frequency = np.tile(frequency, pw // half)[None, :]
    lo = np.arange(64)[:, None] * frequency
    hi = 64.0 * np.arange(row_len // 64)[:, None] * frequency
    return tuple(jnp.asarray(t, F32) for t in (np.cos(lo), np.sin(lo), np.cos(hi), np.sin(hi)))


def columns_of(ref, s, sw):
    if len(ref.shape) == 3:
        return ref.at[s]
    start = s * sw if isinstance(s, int) else pl.multiple_of(s * sw, sw)
    return ref.at[:, pl.ds(start, sw)]


def tiled(table, width):
    times = width // table.shape[1]
    return table if times == 1 else jnp.concatenate([table] * times, axis=1)


def exchange_kernel(
    sizes, chunks, x, w, sg, wt, wo, xa, ws, so, g1, cross, oz,
    xs, wb, sb, tb, ob,
    swap_s, swap_r, peer_s, peer_r, core_s, core_r, w_s, w_r, wh_s, wh_r, sg_s, sg_r, loc,
    oz_s, oz_r, gp_s, gp_r, gh_s, gh_r, cr_s, cr_r,
):
    hi_n, _, _, nh = sizes
    n = 2 * nh
    h, c, r, q = coords()
    p = c * nh + q
    zed = r * nh + q
    partner_p = r * nh + q
    rows = x.shape[0] // chunks
    same = c == r
    other = c != r
    partner = (h, r, c, q)
    mate = (h, 1 - c, r, q)
    greet_plane(sizes, True)

    def part(k):
        return pl.ds(k * rows, rows)

    def swap_x(k):
        return remote(x.at[part(k)], xa.at[partner_p, part(k)], swap_s.at[k], swap_r.at[k], partner)

    def own_arrives(k):
        return remote(x.at[part(k)], xa.at[p, part(k)], swap_s.at[k], swap_r.at[k], partner)

    def push_peer(src, k, dq):
        to = (h, c, r, (q + dq) % nh)
        return remote(src, xa.at[p, part(k)], peer_s.at[dq, k], peer_r.at[dq, k], to)

    def push_mate(src, k, dq):
        block = c * nh + (q + nh - dq) % nh
        return remote(src, xa.at[block, part(k)], core_s.at[dq, k], core_r.at[dq, k], mate)

    def send_w():
        return remote(w.at[h], ws.at[h], w_s, w_r, partner)

    def spread_w(dh):
        to = ((h + dh) % hi_n, c, r, q)
        return remote(ws.at[h], ws.at[h], wh_s.at[dh], wh_r.at[dh], to)

    def send_sg():
        return remote(sg, so, sg_s, sg_r, partner)

    def shard_peer(dq):
        to = (h, c, r, (q + dq) % nh)
        return remote(wt, g1.at[h, (nh - dq) % nh], gp_s.at[dq], gp_r.at[dq], to)

    def shard_hi(src, dh, t):
        to = ((h + dh) % hi_n, c, r, q)
        return remote(src, g1.at[h, t], gh_s.at[dh, t], gh_r.at[dh, t], to)

    def shard_cross():
        return remote(wt, cross, cr_s, cr_r, (h, c, 1 - r, q))

    def rows_z(dz):
        z = (zed + dz) % n
        return remote(
            wo.at[2 * h + c], oz.at[zed], oz_s.at[dz], oz_r.at[dz], (h, c, z // nh, z % nh)
        )

    def from_hi(dh):
        return (h + hi_n - dh) % hi_n

    local = [
        (pltpu.make_async_copy(wt, tb, loc.at[0]), pltpu.make_async_copy(tb, g1.at[h, 0], loc.at[5])),
        (
            pltpu.make_async_copy(wo.at[2 * h + c], ob, loc.at[1]),
            pltpu.make_async_copy(ob, oz.at[zed], loc.at[6]),
        ),
    ]
    local_same = [
        (pltpu.make_async_copy(x, xs, loc.at[2]), pltpu.make_async_copy(xs, xa.at[p], loc.at[7])),
        (pltpu.make_async_copy(w, wb, loc.at[3]), pltpu.make_async_copy(wb, ws, loc.at[8])),
        (pltpu.make_async_copy(sg, sb, loc.at[4]), pltpu.make_async_copy(sb, so, loc.at[9])),
    ]

    @pl.when(other)
    def _():
        send_sg().start()
        send_w().start()
        for k in range(chunks):
            swap_x(k).start()

    @pl.when(same)
    def _():
        for k in range(chunks):
            for dq in range(1, nh):
                push_peer(x.at[part(k)], k, dq).start()
            push_mate(x.at[part(k)], k, 0).start()
        for get, _ in local_same:
            get.start()

    for dq in range(1, nh):
        shard_peer(dq).start()
    for dh in range(1, hi_n):
        shard_hi(wt, dh, 0).start()
    for dz in range(1, n):
        rows_z(dz).start()
    shard_cross().start()
    for get, _ in local:
        get.start()

    @pl.when(other)
    def _():
        send_w().wait_recv()
        for dh in range(1, hi_n):
            spread_w(dh).start()

    for dq in range(1, nh):
        remote(wt, g1.at[h, (nh - dq) % nh], gp_s.at[dq], gp_r.at[dq], mate).wait_recv()
        t = (nh - dq) % nh
        for dh in range(1, hi_n):
            shard_hi(g1.at[h, t], dh, t).start()

    @pl.when(other)
    def _():
        for k in range(chunks):
            own_arrives(k).wait_recv()
            for dq in range(1, nh):
                push_peer(xa.at[p, part(k)], k, dq).start()
            push_mate(xa.at[p, part(k)], k, 0).start()

    for get, put in local:
        get.wait()
        put.start()

    @pl.when(same)
    def _():
        for get, put in local_same:
            get.wait()
            put.start()

    for k in range(chunks):
        for dq in range(1, nh):
            block = c * nh + (q + nh - dq) % nh
            remote(
                x.at[part(k)], xa.at[block, part(k)], peer_s.at[dq, k], peer_r.at[dq, k], mate
            ).wait_recv()
            push_mate(xa.at[block, part(k)], k, dq).start()

    for k in range(chunks):
        for dq in range(nh):
            block = (1 - c) * nh + (q + nh - dq) % nh
            remote(
                x.at[part(k)], xa.at[block, part(k)], core_s.at[dq, k], core_r.at[dq, k], mate
            ).wait_recv()

    @pl.when(other)
    def _():
        send_sg().wait_recv()
        for dh in range(1, hi_n):
            source = from_hi(dh)
            remote(ws.at[source], ws.at[source], wh_s.at[dh], wh_r.at[dh], mate).wait_recv()
        send_sg().wait_send()
        send_w().wait_send()
        for dh in range(1, hi_n):
            spread_w(dh).wait_send()
        for k in range(chunks):
            swap_x(k).wait_send()

    for k in range(chunks):
        for dq in range(1, nh):
            push_peer(x.at[part(k)], k, dq).wait_send()
        for dq in range(nh):
            push_mate(x.at[part(k)], k, dq).wait_send()

    @pl.when(same)
    def _():
        for _, put in local_same:
            put.wait()

    for dq in range(1, nh):
        shard_peer(dq).wait_send()
    for dz in range(1, n):
        z = (zed + n - dz) % n
        remote(wo.at[0], oz.at[z], oz_s.at[dz], oz_r.at[dz], mate).wait_recv()
        rows_z(dz).wait_send()
    for t in range(nh):
        for dh in range(1, hi_n):
            shard_hi(wt, dh, t).wait_send()
            remote(wt, g1.at[from_hi(dh), t], gh_s.at[dh, t], gh_r.at[dh, t], mate).wait_recv()
    shard_cross().wait_recv()
    shard_cross().wait_send()
    for _, put in local:
        put.wait()


def exchange_inputs(sizes, x, w, sg, wt, wo):
    hi_n, _, _, nh = sizes
    n = 2 * nh
    tok, width = x.shape
    chunks = 4 if tok % 64 == 0 else 1
    return pl.pallas_call(
        functools.partial(exchange_kernel, sizes, chunks),
        out_shape=(
            jax.ShapeDtypeStruct((n, tok, width), BF),
            jax.ShapeDtypeStruct(w.shape, BF),
            jax.ShapeDtypeStruct(sg.shape, F32),
            jax.ShapeDtypeStruct((hi_n, nh) + wt.shape, BF),
            jax.ShapeDtypeStruct(wt.shape, BF),
            jax.ShapeDtypeStruct((n,) + wo.shape[1:], BF),
        ),
        in_specs=[ANY] * 5,
        out_specs=(ANY,) * 6,
        scratch_shapes=[
            pltpu.VMEM((tok, width), BF),
            pltpu.VMEM(w.shape, BF),
            pltpu.VMEM(sg.shape, F32),
            pltpu.VMEM(wt.shape, BF),
            pltpu.VMEM(wo.shape[1:], BF),
            DMA((chunks,)), DMA((chunks,)),
            DMA((nh, chunks)), DMA((nh, chunks)),
            DMA((nh, chunks)), DMA((nh, chunks)),
            DMA, DMA,
            DMA((hi_n,)), DMA((hi_n,)),
            DMA, DMA,
            DMA((10,)),
            DMA((n,)), DMA((n,)),
            DMA((nh,)), DMA((nh,)),
            DMA((hi_n, nh)), DMA((hi_n, nh)),
            DMA, DMA,
        ],
        name="exchange_inputs",
        compiler_params=pltpu.CompilerParams(collective_id=1, has_side_effects=True),
        cost_estimate=pl.CostEstimate(flops=0, bytes_accessed=160 << 20, transcendentals=0),
    )(x, w, sg, wt, wo)


def masked(scores, diagonal, crossing, causal, bias):
    if diagonal:
        return jnp.where(causal, scores, -1e30)
    if crossing:
        return scores + bias
    return scores


def forward_kernel(
    sizes, block, v, gout, cross, oz, xa, ws, g1, lo_c, lo_s, hi_c, hi_s, seg,
    ai, dy_in, g2, oh, qo, ko, mo, ao, lse, own,
    va, own_rows, tb, ob,
    att_s, att_r, loc, v_s, v_r, dy_s, dy_r, gp_s, gp_r, gh_s, gh_r, oh_s, oh_r, lc,
):
    hi_n, _, _, nh = sizes
    n = 2 * nh
    h, c, r, q = coords()
    p = c * nh + q
    row_len, sw = qo.shape
    tok = row_len // n
    short = row_len // 2
    pw = lo_c.shape[1]
    pairs = sw // pw
    halves = pw // HEAD_DIM
    mate = (h, 1 - c, r, q)
    other = c != r
    greet_plane(sizes, True)

    def send_v(s):
        to = (h, s // nh, c, s % nh)
        spot = r * nh + q
        return remote(columns_of(v, s, sw), va.at[spot], v_s.at[s], v_r.at[spot], to)

    def send_dy():
        return remote(gout, dy_in, dy_s, dy_r, (h, r, c, q))

    def shard_peer(dq):
        to = (h, c, r, (q + dq) % nh)
        return remote(cross, g2.at[h, (nh - dq) % nh], gp_s.at[dq], gp_r.at[dq], to)

    def shard_hi(src, dh, t):
        to = ((h + dh) % hi_n, c, r, q)
        return remote(src, g2.at[h, t], gh_s.at[dh, t], gh_r.at[dh, t], to)

    def rows_hi(dh):
        to = ((h + dh) % hi_n, c, r, q)
        return remote(oz, oh.at[h], oh_s.at[dh], oh_r.at[dh], to)

    def from_hi(dh):
        return (h + hi_n - dh) % hi_n

    keep_v = pltpu.make_async_copy(columns_of(v, p, sw), va.at[p], lc.at[0])
    local = [
        (pltpu.make_async_copy(cross, tb, lc.at[1]), pltpu.make_async_copy(tb, g2.at[h, 0], lc.at[3])),
        (pltpu.make_async_copy(oz, ob, lc.at[2]), pltpu.make_async_copy(ob, oh.at[h], lc.at[4])),
    ]
    for s in range(n):
        @pl.when(jnp.logical_or(other, p != s))
        def _():
            send_v(s).start()

    @pl.when(c == r)
    def _():
        keep_v.start()

    for dq in range(1, nh):
        shard_peer(dq).start()
    for dh in range(1, hi_n):
        rows_hi(dh).start()
        shard_hi(cross, dh, 0).start()

    @pl.when(other)
    def _():
        send_dy().start()

    for get, _ in local:
        get.start()

    br = 256
    own[...] = jnp.zeros_like(own)
    flag = seg[0:1, 0:1]

    def project(i, carry):
        rows = pl.ds(pl.multiple_of(i * br, br), br)
        xf = xa[rows, :].astype(F32)
        inv = lax.rsqrt(jnp.mean(xf * xf, axis=-1, keepdims=True) + EPSILON)
        normed = (xf * inv * g1[...]).astype(BF)
        raw = nt(normed, ws[...])
        first = first_lanes(br, sw)
        ct, st = rope_rows(lo_c, lo_s, hi_c, hi_s, flag, i, br)
        ct, st = tiled(ct, sw), tiled(st, sw)
        q_raw = raw[:, :sw]
        k_raw = raw[:, sw : 2 * sw]
        own_vals = raw[:, 2 * sw :]
        q_rot = (q_raw * ct + rotate_lanes(q_raw, first) * st).astype(BF)
        qo[rows, :] = (q_rot.astype(F32) * HEAD_DIM**-0.5).astype(BF)
        ko[rows, :] = (k_raw * ct + rotate_lanes(k_raw, first) * st).astype(BF)
        own_rows[rows, :] = own_vals
        own[...] += jnp.sum((own_vals * own_vals).reshape(br // 8, 8, sw), axis=0)
        return carry

    lax.fori_loop(0, row_len // br, project, 0)

    for get, put in local:
        get.wait()
        put.start()
    for dq in range(1, nh):
        t = (nh - dq) % nh
        remote(cross, g2.at[h, t], gp_s.at[dq], gp_r.at[dq], mate).wait_recv()
        for dh in range(1, hi_n):
            shard_hi(g2.at[h, t], dh, t).start()

    for b in range(n):
        @pl.when(jnp.logical_or(other, p != b))
        def _():
            remote(columns_of(v, 0, sw), va.at[b], v_s.at[b], v_r.at[b], mate).wait_recv()

    @pl.when(c == r)
    def _():
        keep_v.wait()

    for b in range(n):
        rows = pl.ds(b * tok, tok)
        mo[rows, :] = (0.5 * own_rows[rows, :] + 0.5 * va[b].astype(F32)).astype(BF)

    bias = flag * -1e30
    blocks = row_len // block
    per = block // tok
    causal = lax.broadcasted_iota(jnp.int32, (block, block), 0) >= lax.broadcasted_iota(
        jnp.int32, (block, block), 1
    )

    def send(b, pair):
        lanes = lane_window(pair, pw, sw)
        to = (h, b // nh, r, b % nh)
        return remote(
            ao.at[b, :, lanes], ai.at[p, :, lanes], att_s.at[pair, b], att_r.at[pair, p], to
        )

    def keep(pair):
        lanes = lane_window(pair, pw, sw)
        return pltpu.make_async_copy(ao.at[p, :, lanes], ai.at[p, :, lanes], loc.at[pair])

    def pair_step(pair, carry):
        lanes = lane_window(pair, pw, sw)
        for i in range(blocks):
            outs = []
            rows = pl.ds(i * block, block)
            for half in range(halves):
                cols = slice(half * HEAD_DIM, (half + 1) * HEAD_DIM)
                qh = qo[rows, lanes][:, cols]
                score = []
                for j in range(i + 1):
                    kj = ko[pl.ds(j * block, block), lanes][:, cols]
                    crossing = i * block >= short and j * block < short
                    score.append(masked(nt(qh, kj), i == j, crossing, causal, bias))
                top = functools.reduce(
                    jnp.maximum, [jnp.max(s, axis=-1, keepdims=True) for s in score]
                )
                total = 0.0
                acc = 0.0
                for j in range(i + 1):
                    e = jnp.exp(score[j] - top)
                    total = total + jnp.sum(e, axis=-1, keepdims=True)
                    vj = mo[pl.ds(j * block, block), lanes][:, cols]
                    acc = acc + nn(e.astype(BF), vj)
                outs.append(acc / total)
                lse[pair, rows, half : half + 1] = top + jnp.log(total)
            out = (jnp.concatenate(outs, axis=1) if halves > 1 else outs[0]).astype(BF)
            for t in range(per):
                b = i * per + t
                ao[b, :, lanes] = out[t * tok : (t + 1) * tok]

                @pl.when(p != b)
                def _():
                    send(b, pair).start()

        keep(pair).start()
        return carry

    lax.fori_loop(0, pairs, pair_step, 0)

    def drain(pair, carry):
        lanes = lane_window(pair, pw, sw)
        for b in range(n):
            @pl.when(p != b)
            def _():
                send(b, pair).wait_send()
                remote(
                    ao.at[b, :, lanes], ai.at[b, :, lanes], att_s.at[pair, b], att_r.at[pair, b],
                    (h, 1 - c, r, q),
                ).wait_recv()
        keep(pair).wait()
        return carry

    lax.fori_loop(0, pairs, drain, 0)

    for s in range(n):
        @pl.when(jnp.logical_or(other, p != s))
        def _():
            send_v(s).wait_send()

    for dq in range(1, nh):
        shard_peer(dq).wait_send()
    for dh in range(1, hi_n):
        rows_hi(dh).wait_send()
        remote(oz, oh.at[from_hi(dh)], oh_s.at[dh], oh_r.at[dh], mate).wait_recv()
        for t in range(nh):
            shard_hi(cross, dh, t).wait_send()
            remote(cross, g2.at[from_hi(dh), t], gh_s.at[dh, t], gh_r.at[dh, t], mate).wait_recv()

    @pl.when(other)
    def _():
        send_dy().wait_send()
        send_dy().wait_recv()

    for _, put in local:
        put.wait()


def attention_forward(sizes, v, gout, cross, oz, xa, ws, g1, tables, seg):
    hi_n, _, _, nh = sizes
    n = 2 * nh
    row_len, width = xa.shape
    sw = ws.shape[0] // 3
    tok = row_len // n
    pw = tables[0].shape[1]
    pairs = sw // pw
    block = max(tok, 512)
    flops = 2 * row_len * width * 3 * sw + 2 * row_len * row_len * sw
    return pl.pallas_call(
        functools.partial(forward_kernel, sizes, block),
        out_shape=(
            jax.ShapeDtypeStruct((n, tok, sw), BF),
            jax.ShapeDtypeStruct((tok, width), BF),
            jax.ShapeDtypeStruct((hi_n, nh) + cross.shape, BF),
            jax.ShapeDtypeStruct((hi_n,) + oz.shape, BF),
            jax.ShapeDtypeStruct((row_len, sw), BF),
            jax.ShapeDtypeStruct((row_len, sw), BF),
            jax.ShapeDtypeStruct((row_len, sw), BF),
            jax.ShapeDtypeStruct((n, tok, sw), BF),
            jax.ShapeDtypeStruct((pairs, row_len, pw // HEAD_DIM), F32),
            jax.ShapeDtypeStruct((8, sw), F32),
        ),
        in_specs=[ANY] * 4 + [VM] * 8,
        out_specs=(ANY,) * 4 + (VM,) * 6,
        scratch_shapes=[
            pltpu.VMEM((n, tok, sw), BF),
            pltpu.VMEM((row_len, sw), F32),
            pltpu.VMEM(cross.shape, BF),
            pltpu.VMEM(oz.shape, BF),
            DMA((pairs, n)), DMA((pairs, n)), DMA((pairs,)),
            DMA((n,)), DMA((n,)),
            DMA, DMA,
            DMA((nh,)), DMA((nh,)),
            DMA((hi_n, nh)), DMA((hi_n, nh)),
            DMA((hi_n,)), DMA((hi_n,)),
            DMA((5,)),
        ],
        name="attention_forward",
        compiler_params=pltpu.CompilerParams(
            collective_id=2, has_side_effects=True, vmem_limit_bytes=VMEM_MAX
        ),
        cost_estimate=pl.CostEstimate(
            flops=4 * flops, bytes_accessed=16 << 20, transcendentals=row_len * row_len * sw // 128
        ),
    )(v, gout, cross, oz, xa, ws, g1, *tables, seg)


def mlp_kernel(
    xa, gout, dy_in, near, far, oh, ai, g2, lo, gh, ga, dsum, dosum, gg2, theirs,
    x, dy, hid, n2, acc_o, acc_g, buf, rcv, bo, rcvo, wm, wo, oa, ob,
    x_s, buf_s, buf_r, bo_s, bo_r, ld, th_s, th_r, o_s, o_r,
):
    step = pl.program_id(0)
    n = ai.shape[0]
    nh = n // 2
    hi_n = wm.shape[2]
    wide = 2 * hi_n
    width = x.shape[1]
    dw = width // wide
    rw = bo.shape[3]
    h, c, r, q = coords()
    own_dy = pltpu.make_async_copy(gout, dy, ld.at[4])
    swapped_dy = pltpu.make_async_copy(dy_in, dy, ld.at[4])
    own_o = pltpu.make_async_copy(oh, oa, ld.at[5])

    def block_of(t):
        return near.at[:, t] if t < nh else far.at[:, t - nh]

    def give(t):
        return remote(block_of(t), theirs.at[t], th_s.at[t], th_r.at[t], (h, 1 - c, r, q))

    def give_o():
        return remote(oh, ob, o_s, o_r, (h, 1 - c, r, q))

    def load_own(src, at):
        return pltpu.make_async_copy(src, wm.at[at, c], ld.at[at])

    def load_theirs(t, at):
        return pltpu.make_async_copy(theirs.at[t], wm.at[at, 1 - c], ld.at[2 + at])
    own_x = pltpu.make_async_copy(xa.at[c * (n // 2) + q], x, x_s)
    mate = (h, 1 - c, r, q)
    slot = step % 2
    last = n - 1

    def to_mate(at):
        return remote(buf.at[at, 1 - c], rcv.at[at], buf_s.at[at], buf_r.at[at], mate)

    def out_to_mate():
        return remote(bo.at[1 - c], rcvo, bo_s, bo_r, mate)

    @pl.when(step == 0)
    def _():
        own_x.start()
        own_o.start()
        load_own(near.at[:, 0], 0).start()

        @pl.when(c == r)
        def _():
            own_dy.start()

        @pl.when(c != r)
        def _():
            swapped_dy.start()

        barrier = pltpu.get_barrier_semaphore()
        pl.semaphore_signal(barrier, inc=1, device_id=mate, device_id_type=MESH)
        pl.semaphore_wait(barrier, 1)
        give_o().start()
        for t in range(n):
            give(t).start()
        own_x.wait()
        own_o.wait()
        own_dy.wait()
        give_o().wait_recv()
        for s in range(n):
            for w in range(wide):
                wo[s, w * rw : (w + 1) * rw] = jnp.where(c == w % 2, oa[w // 2, s], ob[w // 2, s])
        give(0).wait_recv()
        load_theirs(0, 0).start()
        total = x[...].astype(F32)
        for s in range(n):
            total = total + nn(ai[s], wo[s])
        hid[...] = total
        inv = lax.rsqrt(jnp.mean(total * total, axis=-1, keepdims=True) + EPSILON)
        n2[...] = (total * inv * g2[...]).astype(BF)
        acc_o[...] = jnp.zeros_like(acc_o)
        acc_g[...] = jnp.zeros_like(acc_g)

    @pl.when(step < n)
    def _():
        @pl.when(step > 1)
        def _():
            to_mate(slot).wait_send()

        load_own(near.at[:, 0], slot).wait()
        load_theirs(0, slot).wait()

        def weight(j):
            return jnp.concatenate([wm[slot, w % 2, w // 2, j] for w in range(wide)], axis=1)

        def put(j, grad):
            low = grad.astype(BF)
            for w in range(wide):
                buf[slot, w % 2, w // 2, j] = low[:, w * dw : (w + 1) * dw]

        gate = nt(n2[...], weight(0))
        up = nt(n2[...], weight(1))
        sig = jax.nn.sigmoid(gate)
        silu = gate * sig
        inner = (silu * up).astype(BF)
        grad_inner = nt(dy[...], weight(2))
        for t in range(1, n):
            @pl.when(step == t - 1)
            def _():
                load_own(block_of(t), t % 2).start()
                give(t).wait_recv()
                load_theirs(t, t % 2).start()

        grad_gate = (grad_inner * up * sig * (1.0 + gate * (1.0 - sig))).astype(BF)
        grad_up = (grad_inner * silu).astype(BF)
        acc_o[...] += nn(inner, weight(2))
        acc_g[...] += nn(grad_gate, weight(0)) + nn(grad_up, weight(1))
        put(0, tn(grad_gate, n2[...]))
        put(1, tn(grad_up, n2[...]))
        put(2, tn(inner, dy[...]))

    @pl.when(step == last)
    def _():
        hidden = hid[...]
        lo[...] = (hidden + acc_o[...]).astype(BF)
        inv = lax.rsqrt(jnp.mean(hidden * hidden, axis=-1, keepdims=True) + EPSILON)
        grad_n = acc_g[...]
        gg2[...] = jnp.sum((grad_n * hidden * inv).reshape(-1, 8, width), axis=0)
        scaled = grad_n * g2[...]
        dot = jnp.sum(scaled * hidden, axis=-1, keepdims=True)
        grad_h = dy[...].astype(F32) + scaled * inv - hidden * (inv * inv * inv * dot / width)
        gh[...] = grad_h
        low = grad_h.astype(BF)
        for s in range(n):
            ga[s] = nt(low, wo[s]).astype(BF)
            grad_wo = tn(ai[s], low).astype(BF)
            for w in range(wide):
                bo[w % 2, w // 2, s] = grad_wo[w * rw : (w + 1) * rw]

    @pl.when(step > 0)
    def _():
        before = (step + 1) % 2
        to_mate(before).wait_recv()
        for a in range(hi_n):
            for j in range(3):
                total = buf[before, c, a, j].astype(F32) + rcv[before, a, j].astype(F32)
                dsum[a, 0, j] = total.astype(BF)

    @pl.when(step < n)
    def _():
        to_mate(slot).start()

    @pl.when(step == last)
    def _():
        out_to_mate().start()

    @pl.when(step == n)
    def _():
        out_to_mate().wait_recv()
        for a in range(hi_n):
            for s in range(n):
                total = bo[c, a, s].astype(F32) + rcvo[a, s].astype(F32)
                dosum[a, s] = total.astype(BF)
        out_to_mate().wait_send()
        to_mate(0).wait_send()
        to_mate(1).wait_send()
        give_o().wait_send()
        for t in range(n):
            give(t).wait_send()


def feed_forward(xa, gout, dy_in, near, far, oh, ai, g2):
    n, tok, sw = ai.shape
    width = gout.shape[1]
    hi_n, _, _, ffs, dw = near.shape
    wide = 2 * hi_n
    rw = sw // wide

    def whole(*shape):
        return pl.BlockSpec(shape, lambda i: (0,) * len(shape))

    def fixed(*shape):
        return pl.BlockSpec(
            shape, lambda i: (0,) * len(shape), pipeline_mode=pl.Buffered(1)
        )

    return pl.pallas_call(
        mlp_kernel,
        out_shape=(
            jax.ShapeDtypeStruct((tok, width), BF),
            jax.ShapeDtypeStruct((tok, width), F32),
            jax.ShapeDtypeStruct((n, tok, sw), BF),
            jax.ShapeDtypeStruct((hi_n, n, 3, ffs, dw), BF),
            jax.ShapeDtypeStruct((hi_n, n, rw, width), BF),
            jax.ShapeDtypeStruct((8, width), F32),
            jax.ShapeDtypeStruct((n, hi_n, 3, ffs, dw), BF),
        ),
        grid_spec=pl.GridSpec(
            grid=(n + 1,),
            in_specs=[ANY] * 6 + [fixed(n, tok, sw), fixed(1, width)],
            out_specs=(
                whole(tok, width),
                whole(tok, width),
                whole(n, tok, sw),
                pl.BlockSpec(
                    (hi_n, 1, 3, ffs, dw), lambda i: (0, jnp.maximum(i - 1, 0), 0, 0, 0)
                ),
                whole(hi_n, n, rw, width),
                whole(8, width),
                ANY,
            ),
            scratch_shapes=[
                pltpu.VMEM((tok, width), BF),
                pltpu.VMEM((tok, width), BF),
                pltpu.VMEM((tok, width), F32),
                pltpu.VMEM((tok, width), BF),
                pltpu.VMEM((tok, width), F32),
                pltpu.VMEM((tok, width), F32),
                pltpu.VMEM((2, 2, hi_n, 3, ffs, dw), BF),
                pltpu.VMEM((2, hi_n, 3, ffs, dw), BF),
                pltpu.VMEM((2, hi_n, n, rw, width), BF),
                pltpu.VMEM((hi_n, n, rw, width), BF),
                pltpu.VMEM((2, 2, hi_n, 3, ffs, dw), BF),
                pltpu.VMEM((n, sw, width), BF),
                pltpu.VMEM((hi_n, n, rw, width), BF),
                pltpu.VMEM((hi_n, n, rw, width), BF),
                DMA, DMA((2,)), DMA((2,)), DMA, DMA,
                DMA((6,)), DMA((n,)), DMA((n,)), DMA, DMA,
            ],
        ),
        name="feed_forward",
        compiler_params=pltpu.CompilerParams(
            dimension_semantics=("arbitrary",),
            collective_id=4,
            has_side_effects=True,
            vmem_limit_bytes=VMEM_MAX,
        ),
        cost_estimate=pl.CostEstimate(
            flops=18 * tok * width * ffs * n, bytes_accessed=40 << 20, transcendentals=tok * ffs * n
        ),
    )(xa, gout, dy_in, near, far, oh, ai, g2)


def backward_kernel(
    sizes, block, ga, ds, dos, lo, xa, ws, g1, lo_c, lo_s, hi_c, hi_s, seg, qi, ki, mi, ao, lse, gh,
    gv, gi, dwq, gg1, lo_in, rx, rxo, zr, zo,
    do, normed, dq, dk, dv, dcat, gow, gnp, rcv, rcv2, gis, part, zs, zos, do_part,
    do_s, do_r, gv_s, gv_r, co_s, co_r, pe_s, pe_r, gi_s, gi_r, loc,
    rx_s, rx_r, rxo_s, rxo_r, ly_s, ly_r, ld, z_s, z_r, zo_s, zo_r,
):
    hi_n, _, _, nh = sizes
    n = 2 * nh
    h, c, r, q = coords()
    p = c * nh + q
    row_len, sw = qi.shape
    width = xa.shape[1]
    tok = row_len // n
    short = row_len // 2
    pw = lo_c.shape[1]
    pairs = sw // pw
    halves = pw // HEAD_DIM
    same = c == r
    mate = (h, 1 - c, r, q)
    swap_to = (h, r, c, q)
    zed = r * nh + q
    greet_plane(sizes, True)

    def over_hi(dh, i):
        to = (h + dh) % hi_n
        return remote(
            ds.at[to, i], rx.at[dh - 1, i], rx_s.at[dh, i], rx_r.at[dh, i], (to, c, r, q)
        )

    def out_over_hi(dh):
        to = (h + dh) % hi_n
        return remote(dos.at[to], rxo.at[dh - 1], rxo_s.at[dh], rxo_r.at[dh], (to, c, r, q))

    def send_lo():
        return remote(lo, lo_in, ly_s, ly_r, swap_to)

    def over_z(t):
        to = (h, c, (r + t // nh) % 2, (q + t % nh) % nh)
        return remote(zs.at[t], zr.at[zed], z_s.at[t], z_r.at[zed], to)

    def out_over_z(i):
        return remote(zos.at[i], zo.at[zed], zo_s.at[i], zo_r.at[zed], (h, c, i // nh, i % nh))

    def keep_z():
        return pltpu.make_async_copy(zs.at[0], zr.at[zed], z_s.at[0])

    def keep_out_z(i):
        return pltpu.make_async_copy(zos.at[i], zo.at[i], zo_s.at[i])

    def load_chunk(i):
        copies = [pltpu.make_async_copy(ds.at[h, i], part.at[0], ld.at[0])]
        for dh in range(1, hi_n):
            copies.append(pltpu.make_async_copy(rx.at[dh - 1, i], part.at[dh], ld.at[dh]))
        return copies

    def reduce_chunk(i):
        for dh in range(1, hi_n):
            over_hi(dh, i).wait_recv()
        for copy in load_chunk(i):
            copy.start()
        for copy in load_chunk(i):
            copy.wait()
        for j in range(3):
            total = part[0, j].astype(F32)
            for dh in range(1, hi_n):
                total = total + part[dh, j].astype(F32)
            zs[i, j] = total.astype(BF)

        if i:
            over_z(i).start()
        else:
            keep_z().start()

    own_out = pltpu.make_async_copy(dos.at[h], zos, ld.at[0])

    def reduce_out():
        own_out.start()
        own_out.wait()
        for dh in range(1, hi_n):
            out_over_hi(dh).wait_recv()
            copy = pltpu.make_async_copy(rxo.at[dh - 1], do_part, ld.at[dh])
            copy.start()
            copy.wait()
            zos[...] = (zos[...].astype(F32) + do_part[...].astype(F32)).astype(BF)
        for i in range(n):
            @pl.when(zed != i)
            def _():
                out_over_z(i).start()

            @pl.when(zed == i)
            def _():
                keep_out_z(i).start()

    @pl.when(c != r)
    def _():
        send_lo().start()

    for dh in range(1, hi_n):
        out_over_hi(dh).start()

    def send_do(s):
        to = (h, s // nh, r, s % nh)
        return remote(ga.at[s], do.at[p], do_s.at[s], do_r.at[p], to)

    keep_do = pltpu.make_async_copy(ga.at[p], do.at[p], loc.at[0])
    for s in range(n):
        @pl.when(p != s)
        def _():
            send_do(s).start()

    keep_do.start()
    for i in range(n):
        for dh in range(1, hi_n):
            over_hi(dh, i).start()
    br = 256

    def norm(i, carry):
        rows = pl.ds(pl.multiple_of(i * br, br), br)
        xf = xa[rows, :].astype(F32)
        inv = lax.rsqrt(jnp.mean(xf * xf, axis=-1, keepdims=True) + EPSILON)
        normed[rows, :] = (xf * inv * g1[...]).astype(BF)
        return carry

    lax.fori_loop(0, row_len // br, norm, 0)
    keep_do.wait()
    for s in range(n):
        @pl.when(p != s)
        def _():
            remote(ga.at[s], do.at[s], do_s.at[s], do_r.at[s], mate).wait_recv()
            send_do(s).wait_send()

    flag = seg[0:1, 0:1]
    bias = flag * -1e30
    blocks = row_len // block
    per = block // tok
    causal = lax.broadcasted_iota(jnp.int32, (block, block), 0) >= lax.broadcasted_iota(
        jnp.int32, (block, block), 1
    )

    def gv_at(s, pair):
        if len(gv.shape) == 3:
            return gv.at[s]
        return gv.at[:, pl.ds(pl.multiple_of(s * sw + pair * pw, pw), pw)]

    def send_gv(b, pair):
        lanes = lane_window(pair, pw, sw)
        to = (h, r, b // nh, b % nh)
        return remote(
            gow.at[b, :, lanes], gv_at(p, pair), gv_s.at[pair, b], gv_r.at[pair, p], to
        )

    def keep_gv(pair):
        lanes = lane_window(pair, pw, sw)
        return pltpu.make_async_copy(gow.at[p, :, lanes], gv_at(p, pair), loc.at[1 + pair])

    def pair_step(pair, carry):
        lanes = lane_window(pair, pw, sw)
        dk[...] = jnp.zeros_like(dk)
        dv[...] = jnp.zeros_like(dv)
        for i in range(blocks):
            rows = pl.ds(i * block, block)
            pieces = [[] for _ in range(i + 1)]
            dq_parts = []
            do_rows = [do[i * per + t, :, lanes] for t in range(per)]
            do_i = do_rows[0] if per == 1 else jnp.concatenate(do_rows, axis=0)
            ao_rows = [ao[i * per + t, :, lanes] for t in range(per)]
            ao_i = ao_rows[0] if per == 1 else jnp.concatenate(ao_rows, axis=0)
            product = do_i.astype(F32) * ao_i.astype(F32)
            for half in range(halves):
                cols = slice(half * HEAD_DIM, (half + 1) * HEAD_DIM)
                qh = qi[rows, lanes][:, cols]
                doh = do_i[:, cols]
                delta = jnp.sum(product[:, cols], axis=-1, keepdims=True)
                level = lse[pair, rows, half : half + 1]
                acc = 0.0
                for j in range(i + 1):
                    kj = ki[pl.ds(j * block, block), lanes][:, cols]
                    vj = mi[pl.ds(j * block, block), lanes][:, cols]
                    crossing = i * block >= short and j * block < short
                    score = masked(nt(qh, kj), i == j, crossing, causal, bias)
                    prob = jnp.exp(score - level)
                    grad_prob = nt(doh, vj)
                    grad_score = (prob * (grad_prob - delta)).astype(BF)
                    acc = acc + nn(grad_score, kj)
                    pieces[j].append((tn(grad_score, qh), tn(prob.astype(BF), doh)))
                dq_parts.append(acc * HEAD_DIM**-0.5)
            dq[rows, :] = dq_parts[0] if halves == 1 else jnp.concatenate(dq_parts, axis=1)
            for j in range(i + 1):
                at = pl.ds(j * block, block)
                if halves == 1:
                    dk[at, :] += pieces[j][0][0]
                    dv[at, :] += pieces[j][0][1]
                else:
                    dk[at, :] += jnp.concatenate([t[0] for t in pieces[j]], axis=1)
                    dv[at, :] += jnp.concatenate([t[1] for t in pieces[j]], axis=1)
        first = first_lanes(br, pw)

        def finish(i, inner_carry):
            rows = pl.ds(pl.multiple_of(i * br, br), br)
            ct, st = rope_rows(lo_c, lo_s, hi_c, hi_s, flag, i, br)
            a = dq[rows, :]
            b = dk[rows, :]
            dcat[0, rows, lanes] = (a * ct - rotate_lanes(a, first) * st).astype(BF)
            dcat[1, rows, lanes] = (b * ct - rotate_lanes(b, first) * st).astype(BF)
            dcat[2, rows, lanes] = (0.5 * dv[rows, :].astype(BF).astype(F32)).astype(BF)
            return inner_carry

        lax.fori_loop(0, row_len // br, finish, 0)
        for b in range(n):
            gow[b, :, lanes] = dcat[2, pl.ds(b * tok, tok), lanes]

            @pl.when(jnp.logical_or(c != r, p != b))
            def _():
                send_gv(b, pair).start()

        @pl.when(same)
        def _():
            keep_gv(pair).start()

        return carry

    lax.fori_loop(0, pairs, pair_step, 0)
    reduce_out()
    for i in range(n - 1):
        reduce_chunk(i)

    ck = min(256, tok)
    half_rows = row_len // 2
    n_half = half_rows // ck
    n_blk = tok // ck

    def partial(base, k):
        rows = pl.ds(pl.multiple_of(base + k * ck, ck), ck)
        total = nn(dcat[0, rows, :], ws[:sw, :])
        for t in range(1, 3):
            total = total + nn(dcat[t, rows, :], ws[t * sw : (t + 1) * sw, :])
        gnp[rows, :] = total.astype(BF)

    def to_mate(k):
        rows = pl.ds(pl.multiple_of((1 - c) * half_rows + k * ck, ck), ck)
        return remote(gnp.at[rows], rcv.at[pl.ds(k * ck, ck)], co_s.at[k], co_r.at[k], mate)

    for k in range(n_half):
        partial((1 - c) * half_rows, k)
        to_mate(k).start()

    def own_rows(d):
        return ((q + d) % nh) * tok

    def to_peer(d, k):
        rows = pl.ds(pl.multiple_of(c * half_rows + own_rows(d) + k * ck, ck), ck)
        to = (h, c, r, (q + d) % nh)
        return remote(
            gnp.at[rows], rcv2.at[d - 1, pl.ds(k * ck, ck)], pe_s.at[d, k], pe_r.at[d, k], to
        )

    for d in range(1, nh + 1):
        for k in range(n_blk):
            partial(c * half_rows + own_rows(d), k)

    for k in range(n_half):
        to_mate(k).wait_recv()

    def added(d, k):
        rows = pl.ds(pl.multiple_of(c * half_rows + own_rows(d) + k * ck, ck), ck)
        theirs = pl.ds(pl.multiple_of(own_rows(d) + k * ck, ck), ck)
        return rows, gnp[rows, :].astype(F32) + rcv[theirs, :].astype(F32)

    for d in range(1, nh):
        for k in range(n_blk):
            rows, total = added(d, k)
            gnp[rows, :] = total.astype(BF)
            to_peer(d, k).start()

    for t in range(3):
        dwq[t * sw : (t + 1) * sw, :] = tn(dcat[t], normed[...]).astype(BF)

    reduce_chunk(n - 1)
    partner = swap_to
    gg1[...] = jnp.zeros_like(gg1)

    def send_gi(k):
        rows = pl.ds(k * ck, ck)
        return remote(gis.at[rows], gi.at[rows], gi_s.at[k], gi_r.at[k], partner)

    def keep_gi(k):
        rows = pl.ds(k * ck, ck)
        return pltpu.make_async_copy(gis.at[rows], gi.at[rows], gi_s.at[k])

    for k in range(n_blk):
        for d in range(1, nh):
            to_peer(d, k).wait_recv()
        _, grad_n = added(0, k)
        for d in range(1, nh):
            grad_n = grad_n + rcv2[d - 1, pl.ds(k * ck, ck), :].astype(F32)
        here = pl.ds(pl.multiple_of(p * tok + k * ck, ck), ck)
        xf = xa[here, :].astype(F32)
        inv = lax.rsqrt(jnp.mean(xf * xf, axis=-1, keepdims=True) + EPSILON)
        gg1[...] += jnp.sum((grad_n * xf * inv).reshape(-1, 8, width), axis=0)
        scaled = grad_n * g1[...]
        dot = jnp.sum(scaled * xf, axis=-1, keepdims=True)
        rows = pl.ds(k * ck, ck)
        gis[rows, :] = (
            gh[rows, :] + scaled * inv - xf * (inv * inv * inv * dot / width)
        ).astype(BF)

        @pl.when(c != r)
        def _():
            send_gi(k).start()

        @pl.when(same)
        def _():
            keep_gi(k).start()

    for k in range(n_blk):
        @pl.when(c != r)
        def _():
            send_gi(k).wait_send()
            send_gi(k).wait_recv()

        @pl.when(same)
        def _():
            keep_gi(k).wait()

    for k in range(n_half):
        to_mate(k).wait_send()
    for d in range(1, nh):
        for k in range(n_blk):
            to_peer(d, k).wait_send()

    def drain(pair, carry):
        lanes = lane_window(pair, pw, sw)
        for b in range(n):
            @pl.when(jnp.logical_or(c != r, p != b))
            def _():
                send_gv(b, pair).wait_send()
                remote(
                    gow.at[b, :, lanes], gv_at(b, pair), gv_s.at[pair, b], gv_r.at[pair, b], mate
                ).wait_recv()

        @pl.when(same)
        def _():
            keep_gv(pair).wait()

        return carry

    lax.fori_loop(0, pairs, drain, 0)

    @pl.when(c != r)
    def _():
        send_lo().wait_send()
        send_lo().wait_recv()

    for dh in range(1, hi_n):
        out_over_hi(dh).wait_send()
        for i in range(n):
            over_hi(dh, i).wait_send()
    for i in range(n):
        @pl.when(zed != i)
        def _():
            out_over_z(i).wait_send()
            remote(zs.at[i], zr.at[i], z_s.at[i], z_r.at[i], mate).wait_recv()
            remote(zos.at[i], zo.at[i], zo_s.at[i], zo_r.at[i], mate).wait_recv()

        @pl.when(zed == i)
        def _():
            keep_out_z(i).wait()

    keep_z().wait()
    for t in range(1, n):
        over_z(t).wait_send()


def attention_backward(sizes, ga, ds, dos, lo, xa, ws, g1, tables, seg, qi, ki, mi, ao, lse, gh):
    _, _, _, nh = sizes
    n, tok, sw = ga.shape
    row_len, width = xa.shape
    pw = tables[0].shape[1]
    pairs = sw // pw
    block = max(tok, 512)
    ck = min(256, tok)
    n_half = row_len // 2 // ck
    n_blk = tok // ck
    hi_n = sizes[0]
    _, _, _, ffs, dw = ds.shape
    rw = dos.shape[2]
    others = max(hi_n - 1, 1)
    return pl.pallas_call(
        functools.partial(backward_kernel, sizes, block),
        out_shape=(
            jax.ShapeDtypeStruct((n, tok, sw) if sw % 128 else (tok, width), BF),
            jax.ShapeDtypeStruct((tok, width), BF),
            jax.ShapeDtypeStruct((3 * sw, width), BF),
            jax.ShapeDtypeStruct((8, width), F32),
            jax.ShapeDtypeStruct((tok, width), BF),
            jax.ShapeDtypeStruct((others, n, 3, ffs, dw), BF),
            jax.ShapeDtypeStruct((others, n, rw, width), BF),
            jax.ShapeDtypeStruct((n, 3, ffs, dw), BF),
            jax.ShapeDtypeStruct((n, rw, width), BF),
        ),
        in_specs=[ANY] * 4 + [VM] * 14,
        out_specs=(ANY, ANY, VM, VM) + (ANY,) * 5,
        scratch_shapes=[
            pltpu.VMEM((n, tok, sw), BF),
            pltpu.VMEM((row_len, width), BF),
            pltpu.VMEM((row_len, pw), F32),
            pltpu.VMEM((row_len, pw), F32),
            pltpu.VMEM((row_len, pw), F32),
            pltpu.VMEM((3, row_len, sw), BF),
            pltpu.VMEM((n, tok, sw), BF),
            pltpu.VMEM((row_len, width), BF),
            pltpu.VMEM((row_len // 2, width), BF),
            pltpu.VMEM((max(nh - 1, 1), tok, width), BF),
            pltpu.VMEM((tok, width), BF),
            pltpu.VMEM((hi_n, 3, ffs, dw), BF),
            pltpu.VMEM((n, 3, ffs, dw), BF),
            pltpu.VMEM((n, rw, width), BF),
            pltpu.VMEM((n, rw, width), BF),
            DMA((n,)), DMA((n,)),
            DMA((pairs, n)), DMA((pairs, n)),
            DMA((n_half,)), DMA((n_half,)),
            DMA((nh, n_blk)), DMA((nh, n_blk)),
            DMA((n_blk,)), DMA((n_blk,)),
            DMA((1 + pairs,)),
            DMA((hi_n, n)), DMA((hi_n, n)),
            DMA((hi_n,)), DMA((hi_n,)),
            DMA, DMA,
            DMA((hi_n,)),
            DMA((n,)), DMA((n,)),
            DMA((n,)), DMA((n,)),
        ],
        name="attention_backward",
        compiler_params=pltpu.CompilerParams(
            collective_id=3, has_side_effects=True, vmem_limit_bytes=VMEM_MAX
        ),
        cost_estimate=pl.CostEstimate(
            flops=60 << 30, bytes_accessed=24 << 20, transcendentals=row_len * row_len * sw // 128
        ),
    )(ga, ds, dos, lo, xa, ws, g1, *tables, seg, qi, ki, mi, ao, lse, gh)


def finish_kernel(
    sizes, dwq, sm, zo, fin, og, total,
    r1, s1, r2, s2, own, mine,
    a_s, a_r, b_s, b_r, c_s, c_r, d_s, d_r, e_s, e_r, f_s, f_r, m_s, m_r,
):
    hi_n, _, _, nh = sizes
    n = 2 * nh
    h, c, r, q = coords()
    wide = 2 * hi_n
    w = 2 * h + c
    mate = (h, 1 - c, r, q)
    same = c == r
    barrier = pltpu.get_barrier_semaphore()
    count = 0
    for dh in range(hi_n):
        for dc in range(2):
            if dh or dc:
                to = ((h + dh) % hi_n, (c + dc) % 2, r, q)
                pl.semaphore_signal(barrier, inc=1, device_id=to, device_id_type=MESH)
                count += 1
    for dc in range(2):
        for dz in range(1, n):
            to = (h, (c + dc) % 2, ((r * nh + q + dz) % n) // nh, ((r * nh + q + dz) % n) % nh)
            pl.semaphore_signal(barrier, inc=1, device_id=to, device_id_type=MESH)
            count += 1
    pl.semaphore_wait(barrier, count)

    def hi_part(dh):
        to = (h + dh) % hi_n
        return remote(dwq.at[to], r1.at[dh - 1], a_s.at[dh], a_r.at[dh], (to, c, r, q))

    def hi_small(dh):
        to = ((h + dh) % hi_n, c, r, q)
        return remote(sm, s1.at[h], b_s.at[dh], b_r.at[dh], to)

    for dh in range(1, hi_n):
        hi_small(dh).start()
    for dh in range(1, hi_n):
        hi_part(dh).start()

    out_rows = zo[0].astype(F32)
    for i in range(1, n):
        out_rows = out_rows + zo[i].astype(F32)
    own[...] = out_rows.astype(BF)
    og[w] = own[...]

    def plane_out(dh, dc):
        to = ((h + dh) % hi_n, (c + dc) % 2, r, q)
        return remote(own, og.at[w], c_s.at[dh, dc], c_r.at[dh, dc], to)

    for dh in range(hi_n):
        for dc in range(2):
            if dh or dc:
                plane_out(dh, dc).start()

    s1[h] = sm[...]
    for dh in range(1, hi_n):
        source = (h + hi_n - dh) % hi_n
        remote(sm, s1.at[source], b_s.at[dh], b_r.at[dh], mate).wait_recv()
    small = s1[0]
    for i in range(1, hi_n):
        small = small + s1[i]
    spot = c * n + r * nh + q
    s2[spot] = small

    def plane_small(k):
        dc, dz = k // n, k % n
        z = (r * nh + q + dz) % n
        to = (h, (c + dc) % 2, z // nh, z % nh)
        return remote(s2.at[spot], s2.at[spot], d_s.at[k], d_r.at[k], to)

    def small_arrives(k):
        dc, dz = k // n, k % n
        source = ((c + dc) % 2) * n + (r * nh + q + n - dz) % n
        return remote(s2.at[source], s2.at[source], d_s.at[k], d_r.at[k], mate)

    for k in range(1, 2 * n):
        plane_small(k).start()

    part = dwq[h].astype(F32)
    for dh in range(1, hi_n):
        hi_part(dh).wait_recv()
        part = part + r1[dh - 1].astype(F32)
    mine[...] = part.astype(BF)
    across = remote(mine, r2, e_s, e_r, (h, c, 1 - r, q))

    @pl.when(c != r)
    def _():
        across.start()

    def spread(dh):
        to = ((h + dh) % hi_n, c, r, q)
        return remote(fin.at[h], fin.at[h], f_s.at[dh], f_r.at[dh], to)

    def share(dh):
        block = (h + hi_n - dh) % hi_n
        return remote(fin.at[block], fin.at[block], m_s.at[dh], m_r.at[dh], mate)

    @pl.when(same)
    def _():
        across.wait_recv()
        fin[h] = (mine[...].astype(F32) + r2[...].astype(F32)).astype(BF)
        for dh in range(1, hi_n):
            spread(dh).start()
        share(0).start()
        for dh in range(1, hi_n):
            block = (h + hi_n - dh) % hi_n
            remote(fin.at[h], fin.at[block], f_s.at[dh], f_r.at[dh], mate).wait_recv()
            share(dh).start()

    for k in range(1, 2 * n):
        small_arrives(k).wait_recv()
    whole = s2[0]
    for k in range(1, 2 * n):
        whole = whole + s2[k]
    total[...] = whole

    @pl.when(c != r)
    def _():
        for dh in range(hi_n):
            share(dh).wait_recv()
        across.wait_send()

    @pl.when(same)
    def _():
        for dh in range(1, hi_n):
            spread(dh).wait_send()
        for dh in range(hi_n):
            share(dh).wait_send()

    for dh in range(hi_n):
        for dc in range(2):
            if dh or dc:
                theirs = 2 * ((h + hi_n - dh) % hi_n) + (c + dc) % 2
                remote(own, og.at[theirs], c_s.at[dh, dc], c_r.at[dh, dc], mate).wait_recv()
                plane_out(dh, dc).wait_send()
    for dh in range(1, hi_n):
        hi_small(dh).wait_send()
        hi_part(dh).wait_send()
    for k in range(1, 2 * n):
        plane_small(k).wait_send()


def finish(sizes, dwq, sm, zo):
    hi_n, _, _, nh = sizes
    n = 2 * nh
    wide = 2 * hi_n
    others = max(hi_n - 1, 1)
    rw, width = zo.shape[1:]
    return pl.pallas_call(
        functools.partial(finish_kernel, sizes),
        out_shape=(
            jax.ShapeDtypeStruct(dwq.shape, BF),
            jax.ShapeDtypeStruct((wide, rw, width), BF),
            jax.ShapeDtypeStruct(sm.shape, F32),
        ),
        in_specs=[VM] * 3,
        out_specs=(VM,) * 3,
        scratch_shapes=[
            pltpu.VMEM((others,) + dwq.shape[1:], BF),
            pltpu.VMEM((hi_n,) + sm.shape, F32),
            pltpu.VMEM(dwq.shape[1:], BF),
            pltpu.VMEM((2 * n,) + sm.shape, F32),
            pltpu.VMEM((rw, width), BF),
            pltpu.VMEM(dwq.shape[1:], BF),
            DMA((hi_n,)), DMA((hi_n,)),
            DMA((hi_n,)), DMA((hi_n,)),
            DMA((hi_n, 2)), DMA((hi_n, 2)),
            DMA((2 * n,)), DMA((2 * n,)),
            DMA, DMA,
            DMA((hi_n,)), DMA((hi_n,)),
            DMA((hi_n,)), DMA((hi_n,)),
        ],
        name="finish",
        compiler_params=pltpu.CompilerParams(
            collective_id=5, has_side_effects=True, vmem_limit_bytes=VMEM_MAX
        ),
    )(dwq, sm, zo)


def per_device(sizes, layer_in, value_first, seg_start, gain_one, w_qkv, w_out, gain_two, w_mlp, grad_out):
    hi_n, _, _, nh = sizes
    n = 2 * nh
    wide = 2 * hi_n
    tok, width = layer_in.shape
    sw = w_qkv.shape[1]
    row_len = n * tok
    h, c, r, q = coords()

    w_mlp_t = jnp.transpose(w_mlp, (1, 2, 0))
    sg = jnp.full((8, 128), seg_start[1].astype(F32))
    w_cut = w_qkv.reshape(hi_n, 3 * sw // hi_n, width)
    wo_cut = w_out.reshape(wide, sw // wide, width)
    v_cut = value_first.reshape(tok, n, sw).transpose(1, 0, 2) if sw % 128 else value_first
    xa, ws, so, near, cross, oz = exchange_inputs(sizes, layer_in, w_cut, sg, w_mlp_t, wo_cut)
    ws = ws.reshape(3 * sw, width)

    tables = rope_parts(row_len, min(sw, 128))
    g1 = gain_one.reshape(1, width)
    g2 = gain_two.reshape(1, width)
    xr = xa.reshape(row_len, width)
    ai, dy_in, far, oh, qo, ko, mo, ao, lse, own = attention_forward(
        sizes, v_cut, grad_out, cross, oz, xr, ws, g1, tables, so
    )
    lo, gh, ga, ds, dos, gg2, _ = feed_forward(xa, grad_out, dy_in, near, far, oh, ai, g2)
    gv, gi, dwq, gg1, lo_in, _, _, zr, zo = attention_backward(
        sizes, ga, ds, dos, lo, xr, ws, g1, tables, so, qo, ko, mo, ao, lse, gh
    )
    first_f = value_first.astype(F32)
    lane = jnp.arange(width)
    third = jnp.where(
        lane == 0, jnp.sum(first_f * first_f), jnp.where(lane == 1, jnp.sum(own), 0.0)
    )
    small = jnp.stack([jnp.sum(gg1, axis=0), jnp.sum(gg2, axis=0), third] + [jnp.zeros_like(third)] * 5)
    fin, og, sums = finish(sizes, dwq.reshape(hi_n, 3 * sw // hi_n, width), small, zo)

    layer_out = jnp.where(c == r, lo, lo_in)
    grad_value_first = (gv.transpose(1, 0, 2).reshape(tok, width) if sw % 128 else gv).astype(F32)
    grad_in = gi.astype(F32)
    grad_w_mlp = jnp.transpose(jnp.sum(zr.astype(F32), axis=0), (2, 0, 1))
    grad_w_out = og.reshape(sw, width).astype(F32)
    grad_w_qkv = fin.reshape(3, sw, width).astype(F32)
    entries = tok * width * wide * n
    value_norms = jnp.sqrt(sums[2, :2] / entries)
    return (
        layer_out,
        grad_in,
        grad_value_first,
        sums[0],
        grad_w_qkv,
        grad_w_out,
        sums[1],
        grad_w_mlp,
        value_norms,
    )


def solution(mesh):
    wide, narrow = mesh.shape["wide"], mesh.shape["narrow"]
    sizes = (wide // 2, 2, 2, narrow // 2)
    fine = Mesh(mesh.devices.reshape(sizes), AXES)
    w_axes, n_axes = ("hi", "core"), ("zh", "zq")
    rows = P(AXES, None)
    return jax.shard_map(
        functools.partial(per_device, sizes),
        mesh=fine,
        in_specs=(
            rows,
            rows,
            P(w_axes),
            P(),
            P(None, n_axes, None),
            P(n_axes, None),
            P(),
            P(w_axes, None, n_axes),
            rows,
        ),
        out_specs=(
            rows,
            rows,
            rows,
            P(),
            P(None, n_axes, None),
            P(n_axes, None),
            P(),
            P(w_axes, None, n_axes),
            P(),
        ),
        check_vma=False,
    )
```

```python
import functools

import jax
import jax.numpy as jnp
import numpy as np
from jax import lax
from jax.experimental import pallas as pl
from jax.experimental.pallas import tpu as pltpu
from jax.sharding import Mesh, PartitionSpec as P

HEAD_DIM = 64
EPSILON = 1e-06
BF = jnp.bfloat16
F32 = jnp.float32
AXES = ("hi", "core", "zh", "zq")
MESH = pl.DeviceIdType.MESH
ANY = pl.BlockSpec(memory_space=pl.ANY)
VM = pl.BlockSpec(memory_space=pltpu.VMEM)
VMEM_MAX = 62 << 20
DMA = pltpu.SemaphoreType.DMA


def nn(a, b):
    return lax.dot_general(a, b, (((1,), (0,)), ((), ())), preferred_element_type=F32)


def nt(a, b):
    return lax.dot_general(a, b, (((1,), (1,)), ((), ())), preferred_element_type=F32)


def tn(a, b):
    return lax.dot_general(a, b, (((0,), (0,)), ((), ())), preferred_element_type=F32)


def coords():
    return tuple(lax.axis_index(name) for name in AXES)


def remote(src, dst, send, recv, to):
    return pltpu.make_async_remote_copy(
        src_ref=src, dst_ref=dst, send_sem=send, recv_sem=recv, device_id=to, device_id_type=MESH
    )


def greet_plane(sizes, with_hi, cores=1):
    hi_n, _, _, nh = sizes
    h, c, r, q = coords()
    barrier = pltpu.get_barrier_semaphore()
    count = 0
    for dc in range(2):
        for dr in range(2):
            for dq in range(nh):
                if dc or dr or dq:
                    to = (h, (c + dc) % 2, (r + dr) % 2, (q + dq) % nh)
                    pl.semaphore_signal(barrier, inc=1, device_id=to, device_id_type=MESH)
                    count += 1
    if with_hi:
        for dh in range(1, hi_n):
            for dc in range(cores):
                to = ((h + dh) % hi_n, (c + dc) % 2, r, q)
                pl.semaphore_signal(barrier, inc=1, device_id=to, device_id_type=MESH)
                count += 1
    pl.semaphore_wait(barrier, count)


def rotate_lanes(values, first):
    width = values.shape[1]
    if width < 128:
        return jnp.concatenate([values[:, 32:], values[:, :32]], axis=1)
    return jnp.where(
        first, pltpu.roll(values, width - 32, 1), pltpu.roll(values, 32, 1)
    )


def first_lanes(rows, width):
    lane = lax.broadcasted_iota(jnp.int32, (rows, width), 1)
    return lane % HEAD_DIM < HEAD_DIM // 2


def lane_window(pair, pw, sw):
    return slice(0, sw) if pw == sw else pl.ds(pl.multiple_of(pair * pw, pw), pw)


def rope_rows(lo_c, lo_s, hi_c, hi_s, flag, i, rows):
    step = lo_c.shape[0]
    half = hi_c.shape[0] // 2
    cos, sin = [], []
    for u in range(rows // step):
        k = i * (rows // step) + u
        far, near = pl.ds(k, 1), pl.ds(k % half, 1)
        ch = hi_c[near, :] * flag + hi_c[far, :] * (1.0 - flag)
        sh = hi_s[near, :] * flag + hi_s[far, :] * (1.0 - flag)
        cos.append(lo_c[...] * ch - lo_s[...] * sh)
        sin.append(lo_s[...] * ch + lo_c[...] * sh)
    cos = jnp.concatenate(cos, axis=0)
    sin = jnp.concatenate(sin, axis=0)
    return cos, jnp.where(first_lanes(rows, cos.shape[1]), -sin, sin)


def rope_parts(row_len, pw):
    half = HEAD_DIM // 2
    frequency = 10000.0 ** (-2.0 * np.arange(half) / HEAD_DIM)
    frequency = np.tile(frequency, pw // half)[None, :]
    lo = np.arange(64)[:, None] * frequency
    hi = 64.0 * np.arange(row_len // 64)[:, None] * frequency
    return tuple(jnp.asarray(t, F32) for t in (np.cos(lo), np.sin(lo), np.cos(hi), np.sin(hi)))


def columns_of(ref, s, sw):
    if len(ref.shape) == 3:
        return ref.at[s]
    start = s * sw if isinstance(s, int) else pl.multiple_of(s * sw, sw)
    return ref.at[:, pl.ds(start, sw)]


def tiled(table, width):
    times = width // table.shape[1]
    return table if times == 1 else jnp.concatenate([table] * times, axis=1)


def exchange_kernel(
    sizes, chunks, x, w, sg, wt, wo, xa, ws, so, g1, cross, oz,
    xs, wb, sb, tb, ob,
    swap_s, swap_r, peer_s, peer_r, core_s, core_r, w_s, w_r, wh_s, wh_r, sg_s, sg_r, loc,
    oz_s, oz_r, gp_s, gp_r, gh_s, gh_r, cr_s, cr_r,
):
    hi_n, _, _, nh = sizes
    n = 2 * nh
    h, c, r, q = coords()
    p = c * nh + q
    zed = r * nh + q
    partner_p = r * nh + q
    rows = x.shape[0] // chunks
    same = c == r
    other = c != r
    partner = (h, r, c, q)
    mate = (h, 1 - c, r, q)
    greet_plane(sizes, True)

    def part(k):
        return pl.ds(k * rows, rows)

    def swap_x(k):
        return remote(x.at[part(k)], xa.at[partner_p, part(k)], swap_s.at[k], swap_r.at[k], partner)

    def own_arrives(k):
        return remote(x.at[part(k)], xa.at[p, part(k)], swap_s.at[k], swap_r.at[k], partner)

    def push_peer(src, k, dq):
        to = (h, c, r, (q + dq) % nh)
        return remote(src, xa.at[p, part(k)], peer_s.at[dq, k], peer_r.at[dq, k], to)

    def push_mate(src, k, dq):
        block = c * nh + (q + nh - dq) % nh
        return remote(src, xa.at[block, part(k)], core_s.at[dq, k], core_r.at[dq, k], mate)

    def send_w():
        return remote(w.at[h], ws.at[h], w_s, w_r, partner)

    def spread_w(dh):
        to = ((h + dh) % hi_n, c, r, q)
        return remote(ws.at[h], ws.at[h], wh_s.at[dh], wh_r.at[dh], to)

    def send_sg():
        return remote(sg, so, sg_s, sg_r, partner)

    def shard_peer(dq):
        to = (h, c, r, (q + dq) % nh)
        return remote(wt, g1.at[h, (nh - dq) % nh], gp_s.at[dq], gp_r.at[dq], to)

    def shard_hi(src, dh, t):
        to = ((h + dh) % hi_n, c, r, q)
        return remote(src, g1.at[h, t], gh_s.at[dh, t], gh_r.at[dh, t], to)

    def shard_cross():
        return remote(wt, cross, cr_s, cr_r, (h, c, 1 - r, q))

    def rows_z(dz):
        z = (zed + dz) % n
        return remote(
            wo.at[2 * h + c], oz.at[zed], oz_s.at[dz], oz_r.at[dz], (h, c, z // nh, z % nh)
        )

    def from_hi(dh):
        return (h + hi_n - dh) % hi_n

    local = [
        (pltpu.make_async_copy(wt, tb, loc.at[0]), pltpu.make_async_copy(tb, g1.at[h, 0], loc.at[5])),
        (
            pltpu.make_async_copy(wo.at[2 * h + c], ob, loc.at[1]),
            pltpu.make_async_copy(ob, oz.at[zed], loc.at[6]),
        ),
    ]
    local_same = [
        (pltpu.make_async_copy(x, xs, loc.at[2]), pltpu.make_async_copy(xs, xa.at[p], loc.at[7])),
        (pltpu.make_async_copy(w, wb, loc.at[3]), pltpu.make_async_copy(wb, ws, loc.at[8])),
        (pltpu.make_async_copy(sg, sb, loc.at[4]), pltpu.make_async_copy(sb, so, loc.at[9])),
    ]

    @pl.when(other)
    def _():
        send_sg().start()
        send_w().start()
        for k in range(chunks):
            swap_x(k).start()

    @pl.when(same)
    def _():
        for k in range(chunks):
            for dq in range(1, nh):
                push_peer(x.at[part(k)], k, dq).start()
            push_mate(x.at[part(k)], k, 0).start()
        for get, _ in local_same:
            get.start()

    for dq in range(1, nh):
        shard_peer(dq).start()
    for dh in range(1, hi_n):
        shard_hi(wt, dh, 0).start()
    for dz in range(1, n):
        rows_z(dz).start()
    shard_cross().start()
    for get, _ in local:
        get.start()

    @pl.when(other)
    def _():
        send_w().wait_recv()
        for dh in range(1, hi_n):
            spread_w(dh).start()

    for dq in range(1, nh):
        remote(wt, g1.at[h, (nh - dq) % nh], gp_s.at[dq], gp_r.at[dq], mate).wait_recv()
        t = (nh - dq) % nh
        for dh in range(1, hi_n):
            shard_hi(g1.at[h, t], dh, t).start()

    @pl.when(other)
    def _():
        for k in range(chunks):
            own_arrives(k).wait_recv()
            for dq in range(1, nh):
                push_peer(xa.at[p, part(k)], k, dq).start()
            push_mate(xa.at[p, part(k)], k, 0).start()

    for get, put in local:
        get.wait()
        put.start()

    @pl.when(same)
    def _():
        for get, put in local_same:
            get.wait()
            put.start()

    for k in range(chunks):
        for dq in range(1, nh):
            block = c * nh + (q + nh - dq) % nh
            remote(
                x.at[part(k)], xa.at[block, part(k)], peer_s.at[dq, k], peer_r.at[dq, k], mate
            ).wait_recv()
            push_mate(xa.at[block, part(k)], k, dq).start()

    for k in range(chunks):
        for dq in range(nh):
            block = (1 - c) * nh + (q + nh - dq) % nh
            remote(
                x.at[part(k)], xa.at[block, part(k)], core_s.at[dq, k], core_r.at[dq, k], mate
            ).wait_recv()

    @pl.when(other)
    def _():
        send_sg().wait_recv()
        for dh in range(1, hi_n):
            source = from_hi(dh)
            remote(ws.at[source], ws.at[source], wh_s.at[dh], wh_r.at[dh], mate).wait_recv()
        send_sg().wait_send()
        send_w().wait_send()
        for dh in range(1, hi_n):
            spread_w(dh).wait_send()
        for k in range(chunks):
            swap_x(k).wait_send()

    for k in range(chunks):
        for dq in range(1, nh):
            push_peer(x.at[part(k)], k, dq).wait_send()
        for dq in range(nh):
            push_mate(x.at[part(k)], k, dq).wait_send()

    @pl.when(same)
    def _():
        for _, put in local_same:
            put.wait()

    for dq in range(1, nh):
        shard_peer(dq).wait_send()
    for dz in range(1, n):
        z = (zed + n - dz) % n
        remote(wo.at[0], oz.at[z], oz_s.at[dz], oz_r.at[dz], mate).wait_recv()
        rows_z(dz).wait_send()
    for t in range(nh):
        for dh in range(1, hi_n):
            shard_hi(wt, dh, t).wait_send()
            remote(wt, g1.at[from_hi(dh), t], gh_s.at[dh, t], gh_r.at[dh, t], mate).wait_recv()
    shard_cross().wait_recv()
    shard_cross().wait_send()
    for _, put in local:
        put.wait()


def exchange_inputs(sizes, x, w, sg, wt, wo):
    hi_n, _, _, nh = sizes
    n = 2 * nh
    tok, width = x.shape
    chunks = 4 if tok % 64 == 0 else 1
    return pl.pallas_call(
        functools.partial(exchange_kernel, sizes, chunks),
        out_shape=(
            jax.ShapeDtypeStruct((n, tok, width), BF),
            jax.ShapeDtypeStruct(w.shape, BF),
            jax.ShapeDtypeStruct(sg.shape, F32),
            jax.ShapeDtypeStruct((hi_n, nh) + wt.shape, BF),
            jax.ShapeDtypeStruct(wt.shape, BF),
            jax.ShapeDtypeStruct((n,) + wo.shape[1:], BF),
        ),
        in_specs=[ANY] * 5,
        out_specs=(ANY,) * 6,
        scratch_shapes=[
            pltpu.VMEM((tok, width), BF),
            pltpu.VMEM(w.shape, BF),
            pltpu.VMEM(sg.shape, F32),
            pltpu.VMEM(wt.shape, BF),
            pltpu.VMEM(wo.shape[1:], BF),
            DMA((chunks,)), DMA((chunks,)),
            DMA((nh, chunks)), DMA((nh, chunks)),
            DMA((nh, chunks)), DMA((nh, chunks)),
            DMA, DMA,
            DMA((hi_n,)), DMA((hi_n,)),
            DMA, DMA,
            DMA((10,)),
            DMA((n,)), DMA((n,)),
            DMA((nh,)), DMA((nh,)),
            DMA((hi_n, nh)), DMA((hi_n, nh)),
            DMA, DMA,
        ],
        name="exchange_inputs",
        compiler_params=pltpu.CompilerParams(collective_id=1, has_side_effects=True),
        cost_estimate=pl.CostEstimate(flops=0, bytes_accessed=160 << 20, transcendentals=0),
    )(x, w, sg, wt, wo)


def masked(scores, diagonal, crossing, causal, bias):
    if diagonal:
        return jnp.where(causal, scores, -1e30)
    if crossing:
        return scores + bias
    return scores


def forward_kernel(
    sizes, block, v, gout, cross, oz, xa, ws, g1, lo_c, lo_s, hi_c, hi_s, seg,
    ai, dy_in, g2, oh, qo, ko, mo, ao, lse, own, vsq,
    va, own_rows, tb, ob,
    att_s, att_r, loc, v_s, v_r, dy_s, dy_r, gp_s, gp_r, gh_s, gh_r, oh_s, oh_r, lc,
):
    hi_n, _, _, nh = sizes
    n = 2 * nh
    h, c, r, q = coords()
    p = c * nh + q
    row_len, sw = qo.shape
    tok = row_len // n
    short = row_len // 2
    pw = lo_c.shape[1]
    pairs = sw // pw
    halves = pw // HEAD_DIM
    mate = (h, 1 - c, r, q)
    other = c != r
    greet_plane(sizes, True)

    def send_v(s):
        to = (h, s // nh, c, s % nh)
        spot = r * nh + q
        return remote(columns_of(v, s, sw), va.at[spot], v_s.at[s], v_r.at[spot], to)

    def send_dy():
        return remote(gout, dy_in, dy_s, dy_r, (h, r, c, q))

    def shard_peer(dq):
        to = (h, c, r, (q + dq) % nh)
        return remote(cross, g2.at[h, (nh - dq) % nh], gp_s.at[dq], gp_r.at[dq], to)

    def shard_hi(src, dh, t):
        to = ((h + dh) % hi_n, c, r, q)
        return remote(src, g2.at[h, t], gh_s.at[dh, t], gh_r.at[dh, t], to)

    def rows_hi(dh):
        to = ((h + dh) % hi_n, c, r, q)
        return remote(oz, oh.at[h], oh_s.at[dh], oh_r.at[dh], to)

    def from_hi(dh):
        return (h + hi_n - dh) % hi_n

    keep_v = pltpu.make_async_copy(columns_of(v, p, sw), va.at[p], lc.at[0])
    local = [
        (pltpu.make_async_copy(cross, tb, lc.at[1]), pltpu.make_async_copy(tb, g2.at[h, 0], lc.at[3])),
        (pltpu.make_async_copy(oz, ob, lc.at[2]), pltpu.make_async_copy(ob, oh.at[h], lc.at[4])),
    ]
    for s in range(n):
        @pl.when(jnp.logical_or(other, p != s))
        def _():
            send_v(s).start()

    @pl.when(c == r)
    def _():
        keep_v.start()

    for dq in range(1, nh):
        shard_peer(dq).start()
    for dh in range(1, hi_n):
        rows_hi(dh).start()
        shard_hi(cross, dh, 0).start()

    @pl.when(other)
    def _():
        send_dy().start()

    for get, _ in local:
        get.start()

    br = 256
    own[...] = jnp.zeros_like(own)
    vsq[...] = jnp.zeros_like(vsq)
    flag = seg[0:1, 0:1]

    def project(i, carry):
        rows = pl.ds(pl.multiple_of(i * br, br), br)
        xf = xa[rows, :].astype(F32)
        inv = lax.rsqrt(jnp.mean(xf * xf, axis=-1, keepdims=True) + EPSILON)
        normed = (xf * inv * g1[...]).astype(BF)
        raw = nt(normed, ws[...])
        first = first_lanes(br, sw)
        ct, st = rope_rows(lo_c, lo_s, hi_c, hi_s, flag, i, br)
        ct, st = tiled(ct, sw), tiled(st, sw)
        q_raw = raw[:, :sw]
        k_raw = raw[:, sw : 2 * sw]
        own_vals = raw[:, 2 * sw :]
        q_rot = (q_raw * ct + rotate_lanes(q_raw, first) * st).astype(BF)
        qo[rows, :] = (q_rot.astype(F32) * HEAD_DIM**-0.5).astype(BF)
        ko[rows, :] = (k_raw * ct + rotate_lanes(k_raw, first) * st).astype(BF)
        own_rows[rows, :] = own_vals
        own[...] += jnp.sum((own_vals * own_vals).reshape(br // 8, 8, sw), axis=0)
        return carry

    lax.fori_loop(0, row_len // br, project, 0)

    for get, put in local:
        get.wait()
        put.start()
    for dq in range(1, nh):
        t = (nh - dq) % nh
        remote(cross, g2.at[h, t], gp_s.at[dq], gp_r.at[dq], mate).wait_recv()
        for dh in range(1, hi_n):
            shard_hi(g2.at[h, t], dh, t).start()

    for b in range(n):
        @pl.when(jnp.logical_or(other, p != b))
        def _():
            remote(columns_of(v, 0, sw), va.at[b], v_s.at[b], v_r.at[b], mate).wait_recv()

    @pl.when(c == r)
    def _():
        keep_v.wait()

    for b in range(n):
        rows = pl.ds(b * tok, tok)
        values = va[b].astype(F32)
        vsq[...] += jnp.sum((values * values).reshape(tok // 8, 8, sw), axis=0)
        mo[rows, :] = (0.5 * own_rows[rows, :] + 0.5 * values).astype(BF)

    bias = flag * -1e30
    blocks = row_len // block
    per = block // tok
    causal = lax.broadcasted_iota(jnp.int32, (block, block), 0) >= lax.broadcasted_iota(
        jnp.int32, (block, block), 1
    )

    def send(b, pair):
        lanes = lane_window(pair, pw, sw)
        to = (h, b // nh, r, b % nh)
        return remote(
            ao.at[b, :, lanes], ai.at[p, :, lanes], att_s.at[pair, b], att_r.at[pair, p], to
        )

    def keep(pair):
        lanes = lane_window(pair, pw, sw)
        return pltpu.make_async_copy(ao.at[p, :, lanes], ai.at[p, :, lanes], loc.at[pair])

    def pair_step(pair, carry):
        lanes = lane_window(pair, pw, sw)
        for i in range(blocks):
            outs = []
            rows = pl.ds(i * block, block)
            for half in range(halves):
                cols = slice(half * HEAD_DIM, (half + 1) * HEAD_DIM)
                qh = qo[rows, lanes][:, cols]
                score = []
                for j in range(i + 1):
                    kj = ko[pl.ds(j * block, block), lanes][:, cols]
                    crossing = i * block >= short and j * block < short
                    score.append(masked(nt(qh, kj), i == j, crossing, causal, bias))
                top = functools.reduce(
                    jnp.maximum, [jnp.max(s, axis=-1, keepdims=True) for s in score]
                )
                total = 0.0
                acc = 0.0
                for j in range(i + 1):
                    e = jnp.exp(score[j] - top)
                    total = total + jnp.sum(e, axis=-1, keepdims=True)
                    vj = mo[pl.ds(j * block, block), lanes][:, cols]
                    acc = acc + nn(e.astype(BF), vj)
                outs.append(acc / total)
                lse[pair, rows, half : half + 1] = top + jnp.log(total)
            out = (jnp.concatenate(outs, axis=1) if halves > 1 else outs[0]).astype(BF)
            for t in range(per):
                b = i * per + t
                ao[b, :, lanes] = out[t * tok : (t + 1) * tok]

                @pl.when(p != b)
                def _():
                    send(b, pair).start()

        keep(pair).start()
        return carry

    lax.fori_loop(0, pairs, pair_step, 0)

    def drain(pair, carry):
        lanes = lane_window(pair, pw, sw)
        for b in range(n):
            @pl.when(p != b)
            def _():
                send(b, pair).wait_send()
                remote(
                    ao.at[b, :, lanes], ai.at[b, :, lanes], att_s.at[pair, b], att_r.at[pair, b],
                    (h, 1 - c, r, q),
                ).wait_recv()
        keep(pair).wait()
        return carry

    lax.fori_loop(0, pairs, drain, 0)

    for s in range(n):
        @pl.when(jnp.logical_or(other, p != s))
        def _():
            send_v(s).wait_send()

    for dq in range(1, nh):
        shard_peer(dq).wait_send()
    for dh in range(1, hi_n):
        rows_hi(dh).wait_send()
        remote(oz, oh.at[from_hi(dh)], oh_s.at[dh], oh_r.at[dh], mate).wait_recv()
        for t in range(nh):
            shard_hi(cross, dh, t).wait_send()
            remote(cross, g2.at[from_hi(dh), t], gh_s.at[dh, t], gh_r.at[dh, t], mate).wait_recv()

    @pl.when(other)
    def _():
        send_dy().wait_send()
        send_dy().wait_recv()

    for _, put in local:
        put.wait()


def attention_forward(sizes, v, gout, cross, oz, xa, ws, g1, tables, seg):
    hi_n, _, _, nh = sizes
    n = 2 * nh
    row_len, width = xa.shape
    sw = ws.shape[0] // 3
    tok = row_len // n
    pw = tables[0].shape[1]
    pairs = sw // pw
    block = max(tok, 512)
    flops = 2 * row_len * width * 3 * sw + 2 * row_len * row_len * sw
    return pl.pallas_call(
        functools.partial(forward_kernel, sizes, block),
        out_shape=(
            jax.ShapeDtypeStruct((n, tok, sw), BF),
            jax.ShapeDtypeStruct((tok, width), BF),
            jax.ShapeDtypeStruct((hi_n, nh) + cross.shape, BF),
            jax.ShapeDtypeStruct((hi_n,) + oz.shape, BF),
            jax.ShapeDtypeStruct((row_len, sw), BF),
            jax.ShapeDtypeStruct((row_len, sw), BF),
            jax.ShapeDtypeStruct((row_len, sw), BF),
            jax.ShapeDtypeStruct((n, tok, sw), BF),
            jax.ShapeDtypeStruct((pairs, row_len, pw // HEAD_DIM), F32),
            jax.ShapeDtypeStruct((8, sw), F32),
            jax.ShapeDtypeStruct((8, sw), F32),
        ),
        in_specs=[ANY] * 4 + [VM] * 8,
        out_specs=(ANY,) * 4 + (VM,) * 7,
        scratch_shapes=[
            pltpu.VMEM((n, tok, sw), BF),
            pltpu.VMEM((row_len, sw), F32),
            pltpu.VMEM(cross.shape, BF),
            pltpu.VMEM(oz.shape, BF),
            DMA((pairs, n)), DMA((pairs, n)), DMA((pairs,)),
            DMA((n,)), DMA((n,)),
            DMA, DMA,
            DMA((nh,)), DMA((nh,)),
            DMA((hi_n, nh)), DMA((hi_n, nh)),
            DMA((hi_n,)), DMA((hi_n,)),
            DMA((5,)),
        ],
        name="attention_forward",
        compiler_params=pltpu.CompilerParams(
            collective_id=2, has_side_effects=True, vmem_limit_bytes=VMEM_MAX
        ),
        cost_estimate=pl.CostEstimate(
            flops=4 * flops, bytes_accessed=16 << 20, transcendentals=row_len * row_len * sw // 128
        ),
    )(v, gout, cross, oz, xa, ws, g1, *tables, seg)


def mlp_kernel(
    xa, gout, dy_in, near, far, oh, ai, g2, lo, gh, ga, dsum, dosum, gg2, theirs,
    x, dy, hid, n2, acc_o, acc_g, buf, rcv, bo, rcvo, wm, wo, oa, ob,
    x_s, buf_s, buf_r, bo_s, bo_r, ld, th_s, th_r, o_s, o_r,
):
    step = pl.program_id(0)
    n = ai.shape[0]
    nh = n // 2
    hi_n = wm.shape[2]
    wide = 2 * hi_n
    width = x.shape[1]
    dw = width // wide
    rw = bo.shape[3]
    h, c, r, q = coords()
    own_dy = pltpu.make_async_copy(gout, dy, ld.at[4])
    swapped_dy = pltpu.make_async_copy(dy_in, dy, ld.at[4])
    own_o = pltpu.make_async_copy(oh, oa, ld.at[5])

    def block_of(t):
        return near.at[:, t] if t < nh else far.at[:, t - nh]

    def give(t):
        return remote(block_of(t), theirs.at[t], th_s.at[t], th_r.at[t], (h, 1 - c, r, q))

    def give_o():
        return remote(oh, ob, o_s, o_r, (h, 1 - c, r, q))

    def load_own(src, at):
        return pltpu.make_async_copy(src, wm.at[at, c], ld.at[at])

    def load_theirs(t, at):
        return pltpu.make_async_copy(theirs.at[t], wm.at[at, 1 - c], ld.at[2 + at])
    own_x = pltpu.make_async_copy(xa.at[c * (n // 2) + q], x, x_s)
    mate = (h, 1 - c, r, q)
    slot = step % 2
    last = n - 1

    def to_mate(at):
        return remote(buf.at[at, 1 - c], rcv.at[at], buf_s.at[at], buf_r.at[at], mate)

    def out_to_mate():
        return remote(bo.at[1 - c], rcvo, bo_s, bo_r, mate)

    @pl.when(step == 0)
    def _():
        own_x.start()
        own_o.start()
        load_own(near.at[:, 0], 0).start()

        @pl.when(c == r)
        def _():
            own_dy.start()

        @pl.when(c != r)
        def _():
            swapped_dy.start()

        barrier = pltpu.get_barrier_semaphore()
        pl.semaphore_signal(barrier, inc=1, device_id=mate, device_id_type=MESH)
        pl.semaphore_wait(barrier, 1)
        give_o().start()
        for t in range(n):
            give(t).start()
        own_x.wait()
        own_o.wait()
        own_dy.wait()
        give_o().wait_recv()
        for s in range(n):
            for w in range(wide):
                wo[s, w * rw : (w + 1) * rw] = jnp.where(c == w % 2, oa[w // 2, s], ob[w // 2, s])
        give(0).wait_recv()
        load_theirs(0, 0).start()
        total = x[...].astype(F32)
        for s in range(n):
            total = total + nn(ai[s], wo[s])
        hid[...] = total
        inv = lax.rsqrt(jnp.mean(total * total, axis=-1, keepdims=True) + EPSILON)
        n2[...] = (total * inv * g2[...]).astype(BF)
        acc_o[...] = jnp.zeros_like(acc_o)
        acc_g[...] = jnp.zeros_like(acc_g)

    @pl.when(step < n)
    def _():
        @pl.when(step > 1)
        def _():
            to_mate(slot).wait_send()

        load_own(near.at[:, 0], slot).wait()
        load_theirs(0, slot).wait()

        def weight(j):
            return jnp.concatenate([wm[slot, w % 2, w // 2, j] for w in range(wide)], axis=1)

        def put(j, grad):
            low = grad.astype(BF)
            for w in range(wide):
                buf[slot, w % 2, w // 2, j] = low[:, w * dw : (w + 1) * dw]

        gate = nt(n2[...], weight(0))
        up = nt(n2[...], weight(1))
        sig = jax.nn.sigmoid(gate)
        silu = gate * sig
        inner = (silu * up).astype(BF)
        grad_inner = nt(dy[...], weight(2))
        for t in range(1, n):
            @pl.when(step == t - 1)
            def _():
                load_own(block_of(t), t % 2).start()
                give(t).wait_recv()
                load_theirs(t, t % 2).start()

        grad_gate = (grad_inner * up * sig * (1.0 + gate * (1.0 - sig))).astype(BF)
        grad_up = (grad_inner * silu).astype(BF)
        acc_o[...] += nn(inner, weight(2))
        acc_g[...] += nn(grad_gate, weight(0)) + nn(grad_up, weight(1))
        put(0, tn(grad_gate, n2[...]))
        put(1, tn(grad_up, n2[...]))
        put(2, tn(inner, dy[...]))

    @pl.when(step == last)
    def _():
        hidden = hid[...]
        lo[...] = (hidden + acc_o[...]).astype(BF)
        inv = lax.rsqrt(jnp.mean(hidden * hidden, axis=-1, keepdims=True) + EPSILON)
        grad_n = acc_g[...]
        gg2[...] = jnp.sum((grad_n * hidden * inv).reshape(-1, 8, width), axis=0)
        scaled = grad_n * g2[...]
        dot = jnp.sum(scaled * hidden, axis=-1, keepdims=True)
        grad_h = dy[...].astype(F32) + scaled * inv - hidden * (inv * inv * inv * dot / width)
        gh[...] = grad_h
        low = grad_h.astype(BF)
        for s in range(n):
            ga[s] = nt(low, wo[s]).astype(BF)
            grad_wo = tn(ai[s], low).astype(BF)
            for w in range(wide):
                bo[w % 2, w // 2, s] = grad_wo[w * rw : (w + 1) * rw]

    @pl.when(step > 0)
    def _():
        before = (step + 1) % 2
        to_mate(before).wait_recv()
        for a in range(hi_n):
            for j in range(3):
                total = buf[before, c, a, j].astype(F32) + rcv[before, a, j].astype(F32)
                dsum[a, 0, j] = total.astype(BF)

    @pl.when(step < n)
    def _():
        to_mate(slot).start()

    @pl.when(step == last)
    def _():
        out_to_mate().start()

    @pl.when(step == n)
    def _():
        out_to_mate().wait_recv()
        for a in range(hi_n):
            for s in range(n):
                total = bo[c, a, s].astype(F32) + rcvo[a, s].astype(F32)
                dosum[a, s] = total.astype(BF)
        out_to_mate().wait_send()
        to_mate(0).wait_send()
        to_mate(1).wait_send()
        give_o().wait_send()
        for t in range(n):
            give(t).wait_send()


def feed_forward(xa, gout, dy_in, near, far, oh, ai, g2):
    n, tok, sw = ai.shape
    width = gout.shape[1]
    hi_n, _, _, ffs, dw = near.shape
    wide = 2 * hi_n
    rw = sw // wide

    def whole(*shape):
        return pl.BlockSpec(shape, lambda i: (0,) * len(shape))

    def fixed(*shape):
        return pl.BlockSpec(
            shape, lambda i: (0,) * len(shape), pipeline_mode=pl.Buffered(1)
        )

    return pl.pallas_call(
        mlp_kernel,
        out_shape=(
            jax.ShapeDtypeStruct((tok, width), BF),
            jax.ShapeDtypeStruct((tok, width), F32),
            jax.ShapeDtypeStruct((n, tok, sw), BF),
            jax.ShapeDtypeStruct((hi_n, n, 3, ffs, dw), BF),
            jax.ShapeDtypeStruct((hi_n, n, rw, width), BF),
            jax.ShapeDtypeStruct((8, width), F32),
            jax.ShapeDtypeStruct((n, hi_n, 3, ffs, dw), BF),
        ),
        grid_spec=pl.GridSpec(
            grid=(n + 1,),
            in_specs=[ANY] * 6 + [fixed(n, tok, sw), fixed(1, width)],
            out_specs=(
                whole(tok, width),
                whole(tok, width),
                whole(n, tok, sw),
                pl.BlockSpec(
                    (hi_n, 1, 3, ffs, dw), lambda i: (0, jnp.maximum(i - 1, 0), 0, 0, 0)
                ),
                whole(hi_n, n, rw, width),
                whole(8, width),
                ANY,
            ),
            scratch_shapes=[
                pltpu.VMEM((tok, width), BF),
                pltpu.VMEM((tok, width), BF),
                pltpu.VMEM((tok, width), F32),
                pltpu.VMEM((tok, width), BF),
                pltpu.VMEM((tok, width), F32),
                pltpu.VMEM((tok, width), F32),
                pltpu.VMEM((2, 2, hi_n, 3, ffs, dw), BF),
                pltpu.VMEM((2, hi_n, 3, ffs, dw), BF),
                pltpu.VMEM((2, hi_n, n, rw, width), BF),
                pltpu.VMEM((hi_n, n, rw, width), BF),
                pltpu.VMEM((2, 2, hi_n, 3, ffs, dw), BF),
                pltpu.VMEM((n, sw, width), BF),
                pltpu.VMEM((hi_n, n, rw, width), BF),
                pltpu.VMEM((hi_n, n, rw, width), BF),
                DMA, DMA((2,)), DMA((2,)), DMA, DMA,
                DMA((6,)), DMA((n,)), DMA((n,)), DMA, DMA,
            ],
        ),
        name="feed_forward",
        compiler_params=pltpu.CompilerParams(
            dimension_semantics=("arbitrary",),
            collective_id=4,
            has_side_effects=True,
            vmem_limit_bytes=VMEM_MAX,
        ),
        cost_estimate=pl.CostEstimate(
            flops=18 * tok * width * ffs * n, bytes_accessed=40 << 20, transcendentals=tok * ffs * n
        ),
    )(xa, gout, dy_in, near, far, oh, ai, g2)


def backward_kernel(
    sizes, block, ga, ds, dos, lo, xa, ws, g1, lo_c, lo_s, hi_c, hi_s, seg, qi, ki, mi, ao, lse, gh,
    gg2, squares, values_sq,
    gv, gi, fin, og, total_small, lo_in, rx, rxo, zr,
    do, normed, dq, dk, dv, dcat, gow, gnp, rcv, rcv2, gis, part, zs, zos, do_part,
    dwq, gg1, zo, sm, s1, s2, r1, r2, own, mine,
    do_s, do_r, gv_s, gv_r, co_s, co_r, pe_s, pe_r, gi_s, gi_r, loc,
    rx_s, rx_r, rxo_s, rxo_r, ly_s, ly_r, ld, z_s, z_r, zo_s, zo_r,
    a_s, a_r, b_s, b_r, c_s, c_r, d_s, d_r, e_s, e_r, f_s, f_r, m_s, m_r,
):
    hi_n, _, _, nh = sizes
    n = 2 * nh
    h, c, r, q = coords()
    p = c * nh + q
    row_len, sw = qi.shape
    width = xa.shape[1]
    tok = row_len // n
    short = row_len // 2
    pw = lo_c.shape[1]
    pairs = sw // pw
    halves = pw // HEAD_DIM
    same = c == r
    mate = (h, 1 - c, r, q)
    swap_to = (h, r, c, q)
    zed = r * nh + q
    greet_plane(sizes, True, 2)

    order = list(range(nh, n)) + list(range(1, nh)) + [0]

    def over_hi(dh, i):
        to = (h + dh) % hi_n
        return remote(
            ds.at[to, i], rx.at[dh - 1, i], rx_s.at[dh, i], rx_r.at[dh, i], (to, c, r, q)
        )

    def out_over_hi(dh):
        to = (h + dh) % hi_n
        return remote(dos.at[to], rxo.at[dh - 1], rxo_s.at[dh], rxo_r.at[dh], (to, c, r, q))

    def send_lo():
        return remote(lo, lo_in, ly_s, ly_r, swap_to)

    def over_z(t):
        to = (h, c, (r + t // nh) % 2, (q + t % nh) % nh)
        return remote(zs.at[t], zr.at[zed], z_s.at[t], z_r.at[zed], to)

    def out_over_z(i):
        return remote(zos.at[i], zo.at[zed], zo_s.at[i], zo_r.at[zed], (h, c, i // nh, i % nh))

    def keep_z():
        return pltpu.make_async_copy(zs.at[0], zr.at[zed], z_s.at[0])

    def keep_out_z(i):
        return pltpu.make_async_copy(zos.at[i], zo.at[i], zo_s.at[i])

    def load_chunk(i):
        copies = [pltpu.make_async_copy(ds.at[h, i], part.at[0], ld.at[0])]
        for dh in range(1, hi_n):
            copies.append(pltpu.make_async_copy(rx.at[dh - 1, i], part.at[dh], ld.at[dh]))
        return copies

    def reduce_chunk(i):
        for dh in range(1, hi_n):
            over_hi(dh, i).wait_recv()
        for copy in load_chunk(i):
            copy.start()
        for copy in load_chunk(i):
            copy.wait()
        for j in range(3):
            total = part[0, j].astype(F32)
            for dh in range(1, hi_n):
                total = total + part[dh, j].astype(F32)
            zs[i, j] = total.astype(BF)

        if i:
            over_z(i).start()
        else:
            keep_z().start()

    own_out = pltpu.make_async_copy(dos.at[h], zos, ld.at[0])

    def reduce_out():
        own_out.start()
        own_out.wait()
        for dh in range(1, hi_n):
            out_over_hi(dh).wait_recv()
            copy = pltpu.make_async_copy(rxo.at[dh - 1], do_part, ld.at[dh])
            copy.start()
            copy.wait()
            zos[...] = (zos[...].astype(F32) + do_part[...].astype(F32)).astype(BF)
        for i in range(n):
            @pl.when(zed != i)
            def _():
                out_over_z(i).start()

            @pl.when(zed == i)
            def _():
                keep_out_z(i).start()

    def send_do(s, pair):
        lanes = lane_window(pair, pw, sw)
        to = (h, s // nh, r, s % nh)
        return remote(
            ga.at[s, :, lanes], do.at[p, :, lanes], do_s.at[pair, s], do_r.at[pair, p], to
        )

    def do_arrives(s, pair):
        lanes = lane_window(pair, pw, sw)
        return remote(
            ga.at[s, :, lanes], do.at[s, :, lanes], do_s.at[pair, s], do_r.at[pair, s], mate
        )

    keep_do = pltpu.make_async_copy(ga.at[p], do.at[p], loc.at[0])
    for pair in range(pairs):
        for s in range(n):
            @pl.when(p != s)
            def _():
                send_do(s, pair).start()

    keep_do.start()
    for dh in range(1, hi_n):
        out_over_hi(dh).start()
    for i in order:
        for dh in range(1, hi_n):
            over_hi(dh, i).start()

    @pl.when(c != r)
    def _():
        send_lo().start()

    br = 256

    def norm(i, carry):
        rows = pl.ds(pl.multiple_of(i * br, br), br)
        xf = xa[rows, :].astype(F32)
        inv = lax.rsqrt(jnp.mean(xf * xf, axis=-1, keepdims=True) + EPSILON)
        normed[rows, :] = (xf * inv * g1[...]).astype(BF)
        return carry

    lax.fori_loop(0, row_len // br, norm, 0)
    keep_do.wait()

    flag = seg[0:1, 0:1]
    bias = flag * -1e30
    blocks = row_len // block
    per = block // tok
    causal = lax.broadcasted_iota(jnp.int32, (block, block), 0) >= lax.broadcasted_iota(
        jnp.int32, (block, block), 1
    )

    def gv_at(s, pair):
        if len(gv.shape) == 3:
            return gv.at[s]
        return gv.at[:, pl.ds(pl.multiple_of(s * sw + pair * pw, pw), pw)]

    def send_gv(b, pair):
        lanes = lane_window(pair, pw, sw)
        to = (h, r, b // nh, b % nh)
        return remote(
            gow.at[b, :, lanes], gv_at(p, pair), gv_s.at[pair, b], gv_r.at[pair, p], to
        )

    def keep_gv(pair):
        lanes = lane_window(pair, pw, sw)
        return pltpu.make_async_copy(gow.at[p, :, lanes], gv_at(p, pair), loc.at[1 + pair])

    def early(pair, i):
        if pairs < 2 or blocks < 4:
            return 0

        @pl.when(pair == 0)
        def _():
            if i == blocks - 2:
                reduce_out()
                reduce_chunk(order[0])

        @pl.when(pair == 1)
        def _():
            if i == 1:
                reduce_chunk(order[1])

        return 2

    def pair_step(pair, carry):
        for s in range(n):
            @pl.when(p != s)
            def _():
                do_arrives(s, pair).wait_recv()

        lanes = lane_window(pair, pw, sw)
        dk[...] = jnp.zeros_like(dk)
        dv[...] = jnp.zeros_like(dv)
        for i in range(blocks):
            rows = pl.ds(i * block, block)
            pieces = [[] for _ in range(i + 1)]
            dq_parts = []
            do_rows = [do[i * per + t, :, lanes] for t in range(per)]
            do_i = do_rows[0] if per == 1 else jnp.concatenate(do_rows, axis=0)
            ao_rows = [ao[i * per + t, :, lanes] for t in range(per)]
            ao_i = ao_rows[0] if per == 1 else jnp.concatenate(ao_rows, axis=0)
            product = do_i.astype(F32) * ao_i.astype(F32)
            for half in range(halves):
                cols = slice(half * HEAD_DIM, (half + 1) * HEAD_DIM)
                qh = qi[rows, lanes][:, cols]
                doh = do_i[:, cols]
                delta = jnp.sum(product[:, cols], axis=-1, keepdims=True)
                level = lse[pair, rows, half : half + 1]
                acc = 0.0
                for j in range(i + 1):
                    kj = ki[pl.ds(j * block, block), lanes][:, cols]
                    vj = mi[pl.ds(j * block, block), lanes][:, cols]
                    crossing = i * block >= short and j * block < short
                    score = masked(nt(qh, kj), i == j, crossing, causal, bias)
                    prob = jnp.exp(score - level)
                    grad_prob = nt(doh, vj)
                    grad_score = (prob * (grad_prob - delta)).astype(BF)
                    acc = acc + nn(grad_score, kj)
                    pieces[j].append((tn(grad_score, qh), tn(prob.astype(BF), doh)))
                dq_parts.append(acc * HEAD_DIM**-0.5)
            dq[rows, :] = dq_parts[0] if halves == 1 else jnp.concatenate(dq_parts, axis=1)
            for j in range(i + 1):
                at = pl.ds(j * block, block)
                if halves == 1:
                    dk[at, :] += pieces[j][0][0]
                    dv[at, :] += pieces[j][0][1]
                else:
                    dk[at, :] += jnp.concatenate([t[0] for t in pieces[j]], axis=1)
                    dv[at, :] += jnp.concatenate([t[1] for t in pieces[j]], axis=1)
            early(pair, i)
        first = first_lanes(br, pw)

        def finish(i, inner_carry):
            rows = pl.ds(pl.multiple_of(i * br, br), br)
            ct, st = rope_rows(lo_c, lo_s, hi_c, hi_s, flag, i, br)
            a = dq[rows, :]
            b = dk[rows, :]
            dcat[0, rows, lanes] = (a * ct - rotate_lanes(a, first) * st).astype(BF)
            dcat[1, rows, lanes] = (b * ct - rotate_lanes(b, first) * st).astype(BF)
            dcat[2, rows, lanes] = (0.5 * dv[rows, :].astype(BF).astype(F32)).astype(BF)
            return inner_carry

        lax.fori_loop(0, row_len // br, finish, 0)
        for b in range(n):
            gow[b, :, lanes] = dcat[2, pl.ds(b * tok, tok), lanes]

            @pl.when(jnp.logical_or(c != r, p != b))
            def _():
                send_gv(b, pair).start()

        @pl.when(same)
        def _():
            keep_gv(pair).start()

        return carry

    lax.fori_loop(0, pairs, pair_step, 0)
    rest = order[2:] if pairs > 1 and blocks > 3 else order
    if len(rest) == n:
        reduce_out()

    ck = min(256, tok)
    half_rows = row_len // 2
    n_half = half_rows // ck
    n_blk = tok // ck

    def partial(base, k):
        rows = pl.ds(pl.multiple_of(base + k * ck, ck), ck)
        total = nn(dcat[0, rows, :], ws[:sw, :])
        for t in range(1, 3):
            total = total + nn(dcat[t, rows, :], ws[t * sw : (t + 1) * sw, :])
        gnp[rows, :] = total.astype(BF)

    def to_mate(k):
        rows = pl.ds(pl.multiple_of((1 - c) * half_rows + k * ck, ck), ck)
        return remote(gnp.at[rows], rcv.at[pl.ds(k * ck, ck)], co_s.at[k], co_r.at[k], mate)

    for k in range(n_half):
        partial((1 - c) * half_rows, k)
        to_mate(k).start()

    def own_rows(d):
        return ((q + d) % nh) * tok

    def to_peer(d, k):
        rows = pl.ds(pl.multiple_of(c * half_rows + own_rows(d) + k * ck, ck), ck)
        to = (h, c, r, (q + d) % nh)
        return remote(
            gnp.at[rows], rcv2.at[d - 1, pl.ds(k * ck, ck)], pe_s.at[d, k], pe_r.at[d, k], to
        )

    for d in range(1, nh + 1):
        for k in range(n_blk):
            partial(c * half_rows + own_rows(d), k)

    for k in range(n_half):
        to_mate(k).wait_recv()

    def added(d, k):
        rows = pl.ds(pl.multiple_of(c * half_rows + own_rows(d) + k * ck, ck), ck)
        theirs = pl.ds(pl.multiple_of(own_rows(d) + k * ck, ck), ck)
        return rows, gnp[rows, :].astype(F32) + rcv[theirs, :].astype(F32)

    for d in range(1, nh):
        for k in range(n_blk):
            rows, total = added(d, k)
            gnp[rows, :] = total.astype(BF)
            to_peer(d, k).start()

    w = 2 * h + c

    def plane_out(dh, dc):
        to = ((h + dh) % hi_n, (c + dc) % 2, r, q)
        return remote(own, og.at[w], c_s.at[dh, dc], c_r.at[dh, dc], to)

    for i in range(n):
        @pl.when(zed != i)
        def _():
            remote(zos.at[i], zo.at[i], zo_s.at[i], zo_r.at[i], mate).wait_recv()

        @pl.when(zed == i)
        def _():
            keep_out_z(i).wait()

    out_rows = zo[0].astype(F32)
    for i in range(1, n):
        out_rows = out_rows + zo[i].astype(F32)
    own[...] = out_rows.astype(BF)
    og[w] = own[...]
    for dh in range(hi_n):
        for dc in range(2):
            if dh or dc:
                plane_out(dh, dc).start()

    cut = 3 * sw // hi_n

    def hi_part(dh):
        to = (h + dh) % hi_n
        return remote(dwq.at[to], r1.at[dh - 1], a_s.at[dh], a_r.at[dh], (to, c, r, q))

    for t in range(3):
        grad = tn(dcat[t], normed[...]).astype(BF)
        for i in range(hi_n):
            begin, end = max(t * sw, i * cut), min((t + 1) * sw, (i + 1) * cut)
            if begin < end:
                dwq[i, begin - i * cut : end - i * cut, :] = grad[begin - t * sw : end - t * sw]
    for dh in range(1, hi_n):
        hi_part(dh).start()

    for i in rest[:-1]:
        reduce_chunk(i)

    partner = swap_to
    gg1[...] = jnp.zeros_like(gg1)

    def send_gi(k):
        rows = pl.ds(k * ck, ck)
        return remote(gis.at[rows], gi.at[rows], gi_s.at[k], gi_r.at[k], partner)

    def keep_gi(k):
        rows = pl.ds(k * ck, ck)
        return pltpu.make_async_copy(gis.at[rows], gi.at[rows], gi_s.at[k])

    for k in range(n_blk):
        for d in range(1, nh):
            to_peer(d, k).wait_recv()
        _, grad_n = added(0, k)
        for d in range(1, nh):
            grad_n = grad_n + rcv2[d - 1, pl.ds(k * ck, ck), :].astype(F32)
        here = pl.ds(pl.multiple_of(p * tok + k * ck, ck), ck)
        xf = xa[here, :].astype(F32)
        inv = lax.rsqrt(jnp.mean(xf * xf, axis=-1, keepdims=True) + EPSILON)
        gg1[...] += jnp.sum((grad_n * xf * inv).reshape(-1, 8, width), axis=0)
        scaled = grad_n * g1[...]
        dot = jnp.sum(scaled * xf, axis=-1, keepdims=True)
        rows = pl.ds(k * ck, ck)
        gis[rows, :] = (
            gh[rows, :] + scaled * inv - xf * (inv * inv * inv * dot / width)
        ).astype(BF)

        @pl.when(c != r)
        def _():
            send_gi(k).start()

        @pl.when(same)
        def _():
            keep_gi(k).start()

    def hi_small(dh):
        to = ((h + dh) % hi_n, c, r, q)
        return remote(sm, s1.at[h], b_s.at[dh], b_r.at[dh], to)

    sm[...] = jnp.zeros_like(sm)
    sm[0:1, :] = jnp.sum(gg1[...], axis=0, keepdims=True)
    sm[1:2, :] = jnp.sum(gg2[...], axis=0, keepdims=True)
    sm[2:3, :sw] = jnp.sum(values_sq[...], axis=0, keepdims=True)
    sm[3:4, :sw] = jnp.sum(squares[...], axis=0, keepdims=True)
    for dh in range(1, hi_n):
        hi_small(dh).start()
    s1[h] = sm[...]
    reduce_chunk(rest[-1])
    for dh in range(1, hi_n):
        source = (h + hi_n - dh) % hi_n
        remote(sm, s1.at[source], b_s.at[dh], b_r.at[dh], mate).wait_recv()
    small = s1[0]
    for i in range(1, hi_n):
        small = small + s1[i]
    spot = c * n + zed
    s2[spot] = small

    def plane_small(k):
        dc, dz = k // n, k % n
        z = (zed + dz) % n
        to = (h, (c + dc) % 2, z // nh, z % nh)
        return remote(s2.at[spot], s2.at[spot], d_s.at[k], d_r.at[k], to)

    def small_arrives(k):
        dc, dz = k // n, k % n
        source = ((c + dc) % 2) * n + (zed + n - dz) % n
        return remote(s2.at[source], s2.at[source], d_s.at[k], d_r.at[k], mate)

    for k in range(1, 2 * n):
        plane_small(k).start()

    part_sum = dwq[h].astype(F32)
    for dh in range(1, hi_n):
        hi_part(dh).wait_recv()
        part_sum = part_sum + r1[dh - 1].astype(F32)
    mine[...] = part_sum.astype(BF)
    across = remote(mine, r2, e_s, e_r, (h, c, 1 - r, q))

    @pl.when(c != r)
    def _():
        across.start()

    for k in range(1, 2 * n):
        small_arrives(k).wait_recv()
    whole = s2[0]
    for k in range(1, 2 * n):
        whole = whole + s2[k]
    total_small[...] = whole

    def spread(dh):
        to = ((h + dh) % hi_n, c, r, q)
        return remote(fin.at[h], fin.at[h], f_s.at[dh], f_r.at[dh], to)

    def share(dh):
        source = (h + hi_n - dh) % hi_n
        return remote(fin.at[source], fin.at[source], m_s.at[dh], m_r.at[dh], mate)

    @pl.when(same)
    def _():
        across.wait_recv()
        fin[h] = (mine[...].astype(F32) + r2[...].astype(F32)).astype(BF)
        for dh in range(1, hi_n):
            spread(dh).start()
        share(0).start()
        for dh in range(1, hi_n):
            source = (h + hi_n - dh) % hi_n
            remote(fin.at[h], fin.at[source], f_s.at[dh], f_r.at[dh], mate).wait_recv()
            share(dh).start()

    @pl.when(c != r)
    def _():
        for dh in range(hi_n):
            share(dh).wait_recv()
        across.wait_send()

    @pl.when(same)
    def _():
        for dh in range(1, hi_n):
            spread(dh).wait_send()
        for dh in range(hi_n):
            share(dh).wait_send()

    for k in range(n_blk):
        @pl.when(c != r)
        def _():
            send_gi(k).wait_send()
            send_gi(k).wait_recv()

        @pl.when(same)
        def _():
            keep_gi(k).wait()

    for k in range(n_half):
        to_mate(k).wait_send()
    for d in range(1, nh):
        for k in range(n_blk):
            to_peer(d, k).wait_send()
    for dh in range(hi_n):
        for dc in range(2):
            if dh or dc:
                theirs = 2 * ((h + hi_n - dh) % hi_n) + (c + dc) % 2
                remote(own, og.at[theirs], c_s.at[dh, dc], c_r.at[dh, dc], mate).wait_recv()
                plane_out(dh, dc).wait_send()
    for dh in range(1, hi_n):
        hi_small(dh).wait_send()
        hi_part(dh).wait_send()
    for k in range(1, 2 * n):
        plane_small(k).wait_send()

    def drain(pair, carry):
        lanes = lane_window(pair, pw, sw)
        for b in range(n):
            @pl.when(p != b)
            def _():
                send_do(b, pair).wait_send()

            @pl.when(jnp.logical_or(c != r, p != b))
            def _():
                send_gv(b, pair).wait_send()
                remote(
                    gow.at[b, :, lanes], gv_at(b, pair), gv_s.at[pair, b], gv_r.at[pair, b], mate
                ).wait_recv()

        @pl.when(same)
        def _():
            keep_gv(pair).wait()

        return carry

    lax.fori_loop(0, pairs, drain, 0)

    @pl.when(c != r)
    def _():
        send_lo().wait_send()
        send_lo().wait_recv()

    for dh in range(1, hi_n):
        out_over_hi(dh).wait_send()
        for i in range(n):
            over_hi(dh, i).wait_send()
    for i in range(n):
        @pl.when(zed != i)
        def _():
            out_over_z(i).wait_send()
            remote(zs.at[i], zr.at[i], z_s.at[i], z_r.at[i], mate).wait_recv()

    keep_z().wait()
    for t in range(1, n):
        over_z(t).wait_send()


def attention_backward(sizes, ga, ds, dos, lo, xa, ws, g1, tables, seg, *saved):
    _, _, _, nh = sizes
    n, tok, sw = ga.shape
    row_len, width = xa.shape
    pw = tables[0].shape[1]
    pairs = sw // pw
    block = max(tok, 512)
    ck = min(256, tok)
    n_half = row_len // 2 // ck
    n_blk = tok // ck
    hi_n = sizes[0]
    _, _, _, ffs, dw = ds.shape
    rw = dos.shape[2]
    others = max(hi_n - 1, 1)
    cut = 3 * sw // hi_n
    return pl.pallas_call(
        functools.partial(backward_kernel, sizes, block),
        out_shape=(
            jax.ShapeDtypeStruct((n, tok, sw) if sw % 128 else (tok, width), BF),
            jax.ShapeDtypeStruct((tok, width), BF),
            jax.ShapeDtypeStruct((hi_n, cut, width), BF),
            jax.ShapeDtypeStruct((2 * hi_n, rw, width), BF),
            jax.ShapeDtypeStruct((8, width), F32),
            jax.ShapeDtypeStruct((tok, width), BF),
            jax.ShapeDtypeStruct((others, n, 3, ffs, dw), BF),
            jax.ShapeDtypeStruct((others, n, rw, width), BF),
            jax.ShapeDtypeStruct((n, 3, ffs, dw), BF),
        ),
        in_specs=[ANY] * 4 + [VM] * 17,
        out_specs=(ANY, ANY, VM, VM, VM) + (ANY,) * 4,
        scratch_shapes=[
            pltpu.VMEM((n, tok, sw), BF),
            pltpu.VMEM((row_len, width), BF),
            pltpu.VMEM((row_len, pw), F32),
            pltpu.VMEM((row_len, pw), F32),
            pltpu.VMEM((row_len, pw), F32),
            pltpu.VMEM((3, row_len, sw), BF),
            pltpu.VMEM((n, tok, sw), BF),
            pltpu.VMEM((row_len, width), BF),
            pltpu.VMEM((row_len // 2, width), BF),
            pltpu.VMEM((max(nh - 1, 1), tok, width), BF),
            pltpu.VMEM((tok, width), BF),
            pltpu.VMEM((hi_n, 3, ffs, dw), BF),
            pltpu.VMEM((n, 3, ffs, dw), BF),
            pltpu.VMEM((n, rw, width), BF),
            pltpu.VMEM((n, rw, width), BF),
            pltpu.VMEM((hi_n, cut, width), BF),
            pltpu.VMEM((8, width), F32),
            pltpu.VMEM((n, rw, width), BF),
            pltpu.VMEM((8, width), F32),
            pltpu.VMEM((hi_n, 8, width), F32),
            pltpu.VMEM((2 * n, 8, width), F32),
            pltpu.VMEM((others, cut, width), BF),
            pltpu.VMEM((cut, width), BF),
            pltpu.VMEM((rw, width), BF),
            pltpu.VMEM((cut, width), BF),
            DMA((pairs, n)), DMA((pairs, n)),
            DMA((pairs, n)), DMA((pairs, n)),
            DMA((n_half,)), DMA((n_half,)),
            DMA((nh, n_blk)), DMA((nh, n_blk)),
            DMA((n_blk,)), DMA((n_blk,)),
            DMA((1 + pairs,)),
            DMA((hi_n, n)), DMA((hi_n, n)),
            DMA((hi_n,)), DMA((hi_n,)),
            DMA, DMA,
            DMA((hi_n,)),
            DMA((n,)), DMA((n,)),
            DMA((n,)), DMA((n,)),
            DMA((hi_n,)), DMA((hi_n,)),
            DMA((hi_n,)), DMA((hi_n,)),
            DMA((hi_n, 2)), DMA((hi_n, 2)),
            DMA((2 * n,)), DMA((2 * n,)),
            DMA, DMA,
            DMA((hi_n,)), DMA((hi_n,)),
            DMA((hi_n,)), DMA((hi_n,)),
        ],
        name="attention_backward",
        compiler_params=pltpu.CompilerParams(
            collective_id=3, has_side_effects=True, vmem_limit_bytes=VMEM_MAX
        ),
        cost_estimate=pl.CostEstimate(
            flops=60 << 30, bytes_accessed=24 << 20, transcendentals=row_len * row_len * sw // 128
        ),
    )(ga, ds, dos, lo, xa, ws, g1, *tables, seg, *saved)


def per_device(sizes, layer_in, value_first, seg_start, gain_one, w_qkv, w_out, gain_two, w_mlp, grad_out):
    hi_n, _, _, nh = sizes
    n = 2 * nh
    wide = 2 * hi_n
    tok, width = layer_in.shape
    sw = w_qkv.shape[1]
    row_len = n * tok
    h, c, r, q = coords()

    w_mlp_t = jnp.transpose(w_mlp, (1, 2, 0))
    sg = jnp.full((8, 128), seg_start[1].astype(F32))
    w_cut = w_qkv.reshape(hi_n, 3 * sw // hi_n, width)
    wo_cut = w_out.reshape(wide, sw // wide, width)
    v_cut = value_first.reshape(tok, n, sw).transpose(1, 0, 2) if sw % 128 else value_first
    xa, ws, so, near, cross, oz = exchange_inputs(sizes, layer_in, w_cut, sg, w_mlp_t, wo_cut)
    ws = ws.reshape(3 * sw, width)

    tables = rope_parts(row_len, min(sw, 128))
    g1 = gain_one.reshape(1, width)
    g2 = gain_two.reshape(1, width)
    xr = xa.reshape(row_len, width)
    ai, dy_in, far, oh, qo, ko, mo, ao, lse, squares, values_sq = attention_forward(
        sizes, v_cut, grad_out, cross, oz, xr, ws, g1, tables, so
    )
    lo, gh, ga, ds, dos, gg2, _ = feed_forward(xa, grad_out, dy_in, near, far, oh, ai, g2)
    gv, gi, fin, og, sums, lo_in, _, _, zr = attention_backward(
        sizes, ga, ds, dos, lo, xr, ws, g1, tables, so, qo, ko, mo, ao, lse, gh, gg2, squares, values_sq
    )

    layer_out = jnp.where(c == r, lo, lo_in)
    grad_value_first = (gv.transpose(1, 0, 2).reshape(tok, width) if sw % 128 else gv).astype(F32)
    grad_in = gi.astype(F32)
    grad_w_mlp = jnp.transpose(jnp.sum(zr.astype(F32), axis=0), (2, 0, 1))
    grad_w_out = og.reshape(sw, width).astype(F32)
    grad_w_qkv = fin.reshape(3, sw, width).astype(F32)
    entries = tok * width * wide * n
    value_norms = jnp.sqrt(jnp.sum(sums[2:4], axis=1) / entries)
    return (
        layer_out,
        grad_in,
        grad_value_first,
        sums[0],
        grad_w_qkv,
        grad_w_out,
        sums[1],
        grad_w_mlp,
        value_norms,
    )


def solution(mesh):
    wide, narrow = mesh.shape["wide"], mesh.shape["narrow"]
    sizes = (wide // 2, 2, 2, narrow // 2)
    fine = Mesh(mesh.devices.reshape(sizes), AXES)
    w_axes, n_axes = ("hi", "core"), ("zh", "zq")
    rows = P(AXES, None)
    return jax.shard_map(
        functools.partial(per_device, sizes),
        mesh=fine,
        in_specs=(
            rows,
            rows,
            P(w_axes),
            P(),
            P(None, n_axes, None),
            P(n_axes, None),
            P(),
            P(w_axes, None, n_axes),
            rows,
        ),
        out_specs=(
            rows,
            rows,
            rows,
            P(),
            P(None, n_axes, None),
            P(n_axes, None),
            P(),
            P(w_axes, None, n_axes),
            P(),
        ),
        check_vma=False,
    )
```

```python
import functools

import jax
import jax.numpy as jnp
import numpy as np
from jax import lax
from jax.experimental import pallas as pl
from jax.experimental.pallas import tpu as pltpu
from jax.sharding import Mesh, PartitionSpec as P

HEAD_DIM = 64
EPSILON = 1e-06
BF = jnp.bfloat16
F32 = jnp.float32
AXES = ("hi", "core", "zh", "zq")
MESH = pl.DeviceIdType.MESH
ANY = pl.BlockSpec(memory_space=pl.ANY)
VM = pl.BlockSpec(memory_space=pltpu.VMEM)
VMEM_MAX = 62 << 20
DMA = pltpu.SemaphoreType.DMA


def nn(a, b):
    return lax.dot_general(a, b, (((1,), (0,)), ((), ())), preferred_element_type=F32)


def nt(a, b):
    return lax.dot_general(a, b, (((1,), (1,)), ((), ())), preferred_element_type=F32)


def tn(a, b):
    return lax.dot_general(a, b, (((0,), (0,)), ((), ())), preferred_element_type=F32)


def coords():
    return tuple(lax.axis_index(name) for name in AXES)


def remote(src, dst, send, recv, to):
    return pltpu.make_async_remote_copy(
        src_ref=src, dst_ref=dst, send_sem=send, recv_sem=recv, device_id=to, device_id_type=MESH
    )


def greet_plane(sizes, with_hi, cores=1):
    hi_n, _, _, nh = sizes
    h, c, r, q = coords()
    barrier = pltpu.get_barrier_semaphore()
    count = 0
    for dc in range(2):
        for dr in range(2):
            for dq in range(nh):
                if dc or dr or dq:
                    to = (h, (c + dc) % 2, (r + dr) % 2, (q + dq) % nh)
                    pl.semaphore_signal(barrier, inc=1, device_id=to, device_id_type=MESH)
                    count += 1
    if with_hi:
        for dh in range(1, hi_n):
            for dc in range(cores):
                to = ((h + dh) % hi_n, (c + dc) % 2, r, q)
                pl.semaphore_signal(barrier, inc=1, device_id=to, device_id_type=MESH)
                count += 1
    pl.semaphore_wait(barrier, count)


def rotate_lanes(values, first):
    width = values.shape[1]
    if width < 128:
        return jnp.concatenate([values[:, 32:], values[:, :32]], axis=1)
    return jnp.where(
        first, pltpu.roll(values, width - 32, 1), pltpu.roll(values, 32, 1)
    )


def first_lanes(rows, width):
    lane = lax.broadcasted_iota(jnp.int32, (rows, width), 1)
    return lane % HEAD_DIM < HEAD_DIM // 2


def lane_window(pair, pw, sw):
    return slice(0, sw) if pw == sw else pl.ds(pl.multiple_of(pair * pw, pw), pw)


def rope_rows(lo_c, lo_s, hi_c, hi_s, flag, i, rows):
    step = lo_c.shape[0]
    half = hi_c.shape[0] // 2
    cos, sin = [], []
    for u in range(rows // step):
        k = i * (rows // step) + u
        far, near = pl.ds(k, 1), pl.ds(k % half, 1)
        ch = hi_c[near, :] * flag + hi_c[far, :] * (1.0 - flag)
        sh = hi_s[near, :] * flag + hi_s[far, :] * (1.0 - flag)
        cos.append(lo_c[...] * ch - lo_s[...] * sh)
        sin.append(lo_s[...] * ch + lo_c[...] * sh)
    cos = jnp.concatenate(cos, axis=0)
    sin = jnp.concatenate(sin, axis=0)
    return cos, jnp.where(first_lanes(rows, cos.shape[1]), -sin, sin)


def rope_parts(row_len, pw):
    half = HEAD_DIM // 2
    frequency = 10000.0 ** (-2.0 * np.arange(half) / HEAD_DIM)
    frequency = np.tile(frequency, pw // half)[None, :]
    lo = np.arange(64)[:, None] * frequency
    hi = 64.0 * np.arange(row_len // 64)[:, None] * frequency
    return tuple(jnp.asarray(t, F32) for t in (np.cos(lo), np.sin(lo), np.cos(hi), np.sin(hi)))


def columns_of(ref, s, start, size, sw):
    if len(ref.shape) == 3:
        return ref.at[s]
    start = s * sw + start
    start = start if isinstance(start, int) else pl.multiple_of(start, size)
    return ref.at[:, pl.ds(start, size)]


def tiled(table, width):
    times = width // table.shape[1]
    return table if times == 1 else jnp.concatenate([table] * times, axis=1)


def exchange_kernel(
    sizes, chunks, x, w, sg, wt, wo, xa, ws, so, g1, cross, oz,
    xs, wb, sb, tb, ob,
    swap_s, swap_r, peer_s, peer_r, core_s, core_r, w_s, w_r, wh_s, wh_r, sg_s, sg_r, loc,
    oz_s, oz_r, gp_s, gp_r, gh_s, gh_r, cr_s, cr_r,
):
    hi_n, _, _, nh = sizes
    n = 2 * nh
    h, c, r, q = coords()
    p = c * nh + q
    zed = r * nh + q
    partner_p = r * nh + q
    rows = x.shape[0] // chunks
    same = c == r
    other = c != r
    partner = (h, r, c, q)
    mate = (h, 1 - c, r, q)
    greet_plane(sizes, True)

    def part(k):
        return pl.ds(k * rows, rows)

    def swap_x(k):
        return remote(x.at[part(k)], xa.at[partner_p, part(k)], swap_s.at[k], swap_r.at[k], partner)

    def own_arrives(k):
        return remote(x.at[part(k)], xa.at[p, part(k)], swap_s.at[k], swap_r.at[k], partner)

    def push_peer(src, k, dq):
        to = (h, c, r, (q + dq) % nh)
        return remote(src, xa.at[p, part(k)], peer_s.at[dq, k], peer_r.at[dq, k], to)

    def push_mate(src, k, dq):
        block = c * nh + (q + nh - dq) % nh
        return remote(src, xa.at[block, part(k)], core_s.at[dq, k], core_r.at[dq, k], mate)

    def send_w():
        return remote(w.at[h], ws.at[h], w_s, w_r, partner)

    def spread_w(dh):
        to = ((h + dh) % hi_n, c, r, q)
        return remote(ws.at[h], ws.at[h], wh_s.at[dh], wh_r.at[dh], to)

    def send_sg():
        return remote(sg, so, sg_s, sg_r, partner)

    def shard_peer(dq):
        to = (h, c, r, (q + dq) % nh)
        return remote(wt, g1.at[h, (nh - dq) % nh], gp_s.at[dq], gp_r.at[dq], to)

    def shard_hi(src, dh, t):
        to = ((h + dh) % hi_n, c, r, q)
        return remote(src, g1.at[h, t], gh_s.at[dh, t], gh_r.at[dh, t], to)

    def shard_cross():
        return remote(wt, cross, cr_s, cr_r, (h, c, 1 - r, q))

    def rows_z(dz):
        z = (zed + dz) % n
        return remote(
            wo.at[2 * h + c], oz.at[zed], oz_s.at[dz], oz_r.at[dz], (h, c, z // nh, z % nh)
        )

    def from_hi(dh):
        return (h + hi_n - dh) % hi_n

    local = [
        (pltpu.make_async_copy(wt, tb, loc.at[0]), pltpu.make_async_copy(tb, g1.at[h, 0], loc.at[5])),
        (
            pltpu.make_async_copy(wo.at[2 * h + c], ob, loc.at[1]),
            pltpu.make_async_copy(ob, oz.at[zed], loc.at[6]),
        ),
    ]
    local_same = [
        (pltpu.make_async_copy(x, xs, loc.at[2]), pltpu.make_async_copy(xs, xa.at[p], loc.at[7])),
        (pltpu.make_async_copy(w, wb, loc.at[3]), pltpu.make_async_copy(wb, ws, loc.at[8])),
        (pltpu.make_async_copy(sg, sb, loc.at[4]), pltpu.make_async_copy(sb, so, loc.at[9])),
    ]

    @pl.when(other)
    def _():
        send_sg().start()
        send_w().start()
        for k in range(chunks):
            swap_x(k).start()

    @pl.when(same)
    def _():
        for k in range(chunks):
            for dq in range(1, nh):
                push_peer(x.at[part(k)], k, dq).start()
            push_mate(x.at[part(k)], k, 0).start()
        for get, _ in local_same:
            get.start()

    for dq in range(1, nh):
        shard_peer(dq).start()
    for dh in range(1, hi_n):
        shard_hi(wt, dh, 0).start()
    for dz in range(1, n):
        rows_z(dz).start()
    shard_cross().start()
    for get, _ in local:
        get.start()

    @pl.when(other)
    def _():
        send_w().wait_recv()
        for dh in range(1, hi_n):
            spread_w(dh).start()

    for dq in range(1, nh):
        remote(wt, g1.at[h, (nh - dq) % nh], gp_s.at[dq], gp_r.at[dq], mate).wait_recv()
        t = (nh - dq) % nh
        for dh in range(1, hi_n):
            shard_hi(g1.at[h, t], dh, t).start()

    @pl.when(other)
    def _():
        for k in range(chunks):
            own_arrives(k).wait_recv()
            for dq in range(1, nh):
                push_peer(xa.at[p, part(k)], k, dq).start()
            push_mate(xa.at[p, part(k)], k, 0).start()

    for get, put in local:
        get.wait()
        put.start()

    @pl.when(same)
    def _():
        for get, put in local_same:
            get.wait()
            put.start()

    for k in range(chunks):
        for dq in range(1, nh):
            block = c * nh + (q + nh - dq) % nh
            remote(
                x.at[part(k)], xa.at[block, part(k)], peer_s.at[dq, k], peer_r.at[dq, k], mate
            ).wait_recv()
            push_mate(xa.at[block, part(k)], k, dq).start()

    for k in range(chunks):
        for dq in range(nh):
            block = (1 - c) * nh + (q + nh - dq) % nh
            remote(
                x.at[part(k)], xa.at[block, part(k)], core_s.at[dq, k], core_r.at[dq, k], mate
            ).wait_recv()

    @pl.when(other)
    def _():
        send_sg().wait_recv()
        for dh in range(1, hi_n):
            source = from_hi(dh)
            remote(ws.at[source], ws.at[source], wh_s.at[dh], wh_r.at[dh], mate).wait_recv()
        send_sg().wait_send()
        send_w().wait_send()
        for dh in range(1, hi_n):
            spread_w(dh).wait_send()
        for k in range(chunks):
            swap_x(k).wait_send()

    for k in range(chunks):
        for dq in range(1, nh):
            push_peer(x.at[part(k)], k, dq).wait_send()
        for dq in range(nh):
            push_mate(x.at[part(k)], k, dq).wait_send()

    @pl.when(same)
    def _():
        for _, put in local_same:
            put.wait()

    for dq in range(1, nh):
        shard_peer(dq).wait_send()
    for dz in range(1, n):
        z = (zed + n - dz) % n
        remote(wo.at[0], oz.at[z], oz_s.at[dz], oz_r.at[dz], mate).wait_recv()
        rows_z(dz).wait_send()
    for t in range(nh):
        for dh in range(1, hi_n):
            shard_hi(wt, dh, t).wait_send()
            remote(wt, g1.at[from_hi(dh), t], gh_s.at[dh, t], gh_r.at[dh, t], mate).wait_recv()
    shard_cross().wait_recv()
    shard_cross().wait_send()
    for _, put in local:
        put.wait()


def exchange_inputs(sizes, x, w, sg, wt, wo):
    hi_n, _, _, nh = sizes
    n = 2 * nh
    tok, width = x.shape
    chunks = 4 if tok % 64 == 0 else 1
    return pl.pallas_call(
        functools.partial(exchange_kernel, sizes, chunks),
        out_shape=(
            jax.ShapeDtypeStruct((n, tok, width), BF),
            jax.ShapeDtypeStruct(w.shape, BF),
            jax.ShapeDtypeStruct(sg.shape, F32),
            jax.ShapeDtypeStruct((hi_n, nh) + wt.shape, BF),
            jax.ShapeDtypeStruct(wt.shape, BF),
            jax.ShapeDtypeStruct((n,) + wo.shape[1:], BF),
        ),
        in_specs=[ANY] * 5,
        out_specs=(ANY,) * 6,
        scratch_shapes=[
            pltpu.VMEM((tok, width), BF),
            pltpu.VMEM(w.shape, BF),
            pltpu.VMEM(sg.shape, F32),
            pltpu.VMEM(wt.shape, BF),
            pltpu.VMEM(wo.shape[1:], BF),
            DMA((chunks,)), DMA((chunks,)),
            DMA((nh, chunks)), DMA((nh, chunks)),
            DMA((nh, chunks)), DMA((nh, chunks)),
            DMA, DMA,
            DMA((hi_n,)), DMA((hi_n,)),
            DMA, DMA,
            DMA((10,)),
            DMA((n,)), DMA((n,)),
            DMA((nh,)), DMA((nh,)),
            DMA((hi_n, nh)), DMA((hi_n, nh)),
            DMA, DMA,
        ],
        name="exchange_inputs",
        compiler_params=pltpu.CompilerParams(collective_id=1, has_side_effects=True),
        cost_estimate=pl.CostEstimate(flops=0, bytes_accessed=160 << 20, transcendentals=0),
    )(x, w, sg, wt, wo)


def masked(scores, diagonal, crossing, causal, bias):
    if diagonal:
        return jnp.where(causal, scores, -1e30)
    if crossing:
        return scores + bias
    return scores


def forward_kernel(
    sizes, block, v, gout, cross, oz, xa, ws, g1, lo_c, lo_s, hi_c, hi_s, seg,
    ai, dy_in, g2, late, oh, qo, ko, mo, ao, lse, own, vsq,
    va, own_rows, tb, ob,
    att_s, att_r, loc, v_s, v_r, dy_s, dy_r, gp_s, gp_r, gh_s, gh_r, oh_s, oh_r, lc,
):
    hi_n, _, _, nh = sizes
    n = 2 * nh
    h, c, r, q = coords()
    p = c * nh + q
    row_len, sw = qo.shape
    tok = row_len // n
    short = row_len // 2
    pw = lo_c.shape[1]
    pairs = sw // pw
    halves = pw // HEAD_DIM
    mate = (h, 1 - c, r, q)
    other = c != r
    greet_plane(sizes, True)

    def send_v(s, pair):
        lanes = lane_window(pair, pw, sw)
        to = (h, s // nh, c, s % nh)
        spot = r * nh + q
        return remote(
            columns_of(v, s, pair * pw, pw, sw), va.at[spot, :, lanes],
            v_s.at[pair, s], v_r.at[pair, spot], to,
        )

    def v_arrives(b, pair):
        lanes = lane_window(pair, pw, sw)
        return remote(
            columns_of(v, 0, 0, pw, sw), va.at[b, :, lanes], v_s.at[pair, b], v_r.at[pair, b], mate
        )

    def send_dy():
        return remote(gout, dy_in, dy_s, dy_r, (h, r, c, q))

    def shard_hi(dh):
        to = ((h + dh) % hi_n, c, r, q)
        return remote(cross, g2.at[h], gh_s.at[dh], gh_r.at[dh], to)

    def late_peer(dq):
        to = (h, c, r, (q + dq) % nh)
        return remote(cross, late.at[nh - dq - 1], gp_s.at[dq], gp_r.at[dq], to)

    def rows_hi(dh):
        to = ((h + dh) % hi_n, c, r, q)
        return remote(oz, oh.at[h], oh_s.at[dh], oh_r.at[dh], to)

    def from_hi(dh):
        return (h + hi_n - dh) % hi_n

    keep_v = pltpu.make_async_copy(columns_of(v, p, 0, sw, sw), va.at[p], lc.at[0])
    local = [
        (pltpu.make_async_copy(cross, tb, lc.at[1]), pltpu.make_async_copy(tb, g2.at[h], lc.at[3])),
        (pltpu.make_async_copy(oz, ob, lc.at[2]), pltpu.make_async_copy(ob, oh.at[h], lc.at[4])),
    ]
    for pair in range(pairs):
        for s in range(n):
            @pl.when(jnp.logical_or(other, p != s))
            def _():
                send_v(s, pair).start()

    @pl.when(c == r)
    def _():
        keep_v.start()

    for dh in range(1, hi_n):
        shard_hi(dh).start()
    for dh in range(1, hi_n):
        rows_hi(dh).start()
    for dq in range(1, nh):
        late_peer(dq).start()

    @pl.when(other)
    def _():
        send_dy().start()

    for get, _ in local:
        get.start()

    br = 256
    own[...] = jnp.zeros_like(own)
    flag = seg[0:1, 0:1]

    def project(i, carry):
        rows = pl.ds(pl.multiple_of(i * br, br), br)
        xf = xa[rows, :].astype(F32)
        inv = lax.rsqrt(jnp.mean(xf * xf, axis=-1, keepdims=True) + EPSILON)
        normed = (xf * inv * g1[...]).astype(BF)
        raw = nt(normed, ws[...])
        first = first_lanes(br, sw)
        ct, st = rope_rows(lo_c, lo_s, hi_c, hi_s, flag, i, br)
        ct, st = tiled(ct, sw), tiled(st, sw)
        q_raw = raw[:, :sw]
        k_raw = raw[:, sw : 2 * sw]
        own_vals = raw[:, 2 * sw :]
        q_rot = (q_raw * ct + rotate_lanes(q_raw, first) * st).astype(BF)
        qo[rows, :] = (q_rot.astype(F32) * HEAD_DIM**-0.5).astype(BF)
        ko[rows, :] = (k_raw * ct + rotate_lanes(k_raw, first) * st).astype(BF)
        own_rows[rows, :] = own_vals
        own[...] += jnp.sum((own_vals * own_vals).reshape(br // 8, 8, sw), axis=0)
        return carry

    lax.fori_loop(0, row_len // br, project, 0)

    for get, put in local:
        get.wait()
        put.start()
    @pl.when(c == r)
    def _():
        keep_v.wait()

    bias = flag * -1e30
    blocks = row_len // block
    per = block // tok
    causal = lax.broadcasted_iota(jnp.int32, (block, block), 0) >= lax.broadcasted_iota(
        jnp.int32, (block, block), 1
    )

    def send(b, pair):
        lanes = lane_window(pair, pw, sw)
        to = (h, b // nh, r, b % nh)
        return remote(
            ao.at[b, :, lanes], ai.at[p, :, lanes], att_s.at[pair, b], att_r.at[pair, p], to
        )

    def keep(pair):
        lanes = lane_window(pair, pw, sw)
        return pltpu.make_async_copy(ao.at[p, :, lanes], ai.at[p, :, lanes], loc.at[pair])

    def pair_step(pair, carry):
        lanes = lane_window(pair, pw, sw)
        for b in range(n):
            @pl.when(jnp.logical_or(other, p != b))
            def _():
                v_arrives(b, pair).wait_recv()

        sums = 0.0
        for b in range(n):
            rows = pl.ds(b * tok, tok)
            values = va[b, :, lanes].astype(F32)
            sums = sums + jnp.sum((values * values).reshape(tok // 8, 8, pw), axis=0)
            mo[rows, lanes] = (0.5 * own_rows[rows, lanes] + 0.5 * values).astype(BF)
        vsq[:, lanes] = sums
        for i in range(blocks):
            outs = []
            rows = pl.ds(i * block, block)
            for half in range(halves):
                cols = slice(half * HEAD_DIM, (half + 1) * HEAD_DIM)
                qh = qo[rows, lanes][:, cols]
                score = []
                for j in range(i + 1):
                    kj = ko[pl.ds(j * block, block), lanes][:, cols]
                    crossing = i * block >= short and j * block < short
                    score.append(masked(nt(qh, kj), i == j, crossing, causal, bias))
                top = functools.reduce(
                    jnp.maximum, [jnp.max(s, axis=-1, keepdims=True) for s in score]
                )
                total = 0.0
                acc = 0.0
                for j in range(i + 1):
                    e = jnp.exp(score[j] - top)
                    total = total + jnp.sum(e, axis=-1, keepdims=True)
                    vj = mo[pl.ds(j * block, block), lanes][:, cols]
                    acc = acc + nn(e.astype(BF), vj)
                outs.append(acc / total)
                lse[pair, rows, half : half + 1] = top + jnp.log(total)
            out = (jnp.concatenate(outs, axis=1) if halves > 1 else outs[0]).astype(BF)
            for t in range(per):
                b = i * per + t
                ao[b, :, lanes] = out[t * tok : (t + 1) * tok]

                @pl.when(p != b)
                def _():
                    send(b, pair).start()

        keep(pair).start()
        return carry

    lax.fori_loop(0, pairs, pair_step, 0)

    def drain(pair, carry):
        lanes = lane_window(pair, pw, sw)
        for b in range(n):
            @pl.when(p != b)
            def _():
                send(b, pair).wait_send()
                remote(
                    ao.at[b, :, lanes], ai.at[b, :, lanes], att_s.at[pair, b], att_r.at[pair, b],
                    (h, 1 - c, r, q),
                ).wait_recv()
        keep(pair).wait()
        return carry

    lax.fori_loop(0, pairs, drain, 0)

    for pair in range(pairs):
        for s in range(n):
            @pl.when(jnp.logical_or(other, p != s))
            def _():
                send_v(s, pair).wait_send()

    for dh in range(1, hi_n):
        rows_hi(dh).wait_send()
        remote(oz, oh.at[from_hi(dh)], oh_s.at[dh], oh_r.at[dh], mate).wait_recv()
        shard_hi(dh).wait_send()
        remote(cross, g2.at[from_hi(dh)], gh_s.at[dh], gh_r.at[dh], mate).wait_recv()
    for dq in range(1, nh):
        late_peer(dq).wait_send()
        late_peer(dq).wait_recv()

    @pl.when(other)
    def _():
        send_dy().wait_send()
        send_dy().wait_recv()

    for _, put in local:
        put.wait()


def attention_forward(sizes, v, gout, cross, oz, xa, ws, g1, tables, seg):
    hi_n, _, _, nh = sizes
    n = 2 * nh
    row_len, width = xa.shape
    sw = ws.shape[0] // 3
    tok = row_len // n
    pw = tables[0].shape[1]
    pairs = sw // pw
    block = max(tok, 512)
    flops = 2 * row_len * width * 3 * sw + 2 * row_len * row_len * sw
    return pl.pallas_call(
        functools.partial(forward_kernel, sizes, block),
        out_shape=(
            jax.ShapeDtypeStruct((n, tok, sw), BF),
            jax.ShapeDtypeStruct((tok, width), BF),
            jax.ShapeDtypeStruct((hi_n,) + cross.shape, BF),
            jax.ShapeDtypeStruct((max(nh - 1, 1),) + cross.shape, BF),
            jax.ShapeDtypeStruct((hi_n,) + oz.shape, BF),
            jax.ShapeDtypeStruct((row_len, sw), BF),
            jax.ShapeDtypeStruct((row_len, sw), BF),
            jax.ShapeDtypeStruct((row_len, sw), BF),
            jax.ShapeDtypeStruct((n, tok, sw), BF),
            jax.ShapeDtypeStruct((pairs, row_len, pw // HEAD_DIM), F32),
            jax.ShapeDtypeStruct((8, sw), F32),
            jax.ShapeDtypeStruct((8, sw), F32),
        ),
        in_specs=[ANY] * 4 + [VM] * 8,
        out_specs=(ANY,) * 5 + (VM,) * 7,
        scratch_shapes=[
            pltpu.VMEM((n, tok, sw), BF),
            pltpu.VMEM((row_len, sw), F32),
            pltpu.VMEM(cross.shape, BF),
            pltpu.VMEM(oz.shape, BF),
            DMA((pairs, n)), DMA((pairs, n)), DMA((pairs,)),
            DMA((pairs, n)), DMA((pairs, n)),
            DMA, DMA,
            DMA((nh,)), DMA((nh,)),
            DMA((hi_n,)), DMA((hi_n,)),
            DMA((hi_n,)), DMA((hi_n,)),
            DMA((5,)),
        ],
        name="attention_forward",
        compiler_params=pltpu.CompilerParams(
            collective_id=2, has_side_effects=True, vmem_limit_bytes=VMEM_MAX
        ),
        cost_estimate=pl.CostEstimate(
            flops=4 * flops, bytes_accessed=16 << 20, transcendentals=row_len * row_len * sw // 128
        ),
    )(v, gout, cross, oz, xa, ws, g1, *tables, seg)


def mlp_kernel(
    xa, gout, dy_in, near, far, lp, oh, ai, g2, lo, gh, ga, dsum, dosum, gg2, theirs, late,
    x, dy, hid, n2, acc_o, acc_g, buf, rcv, bo, rcvo, wm, wo, oa, ob,
    x_s, buf_s, buf_r, bo_s, bo_r, ld, th_s, th_r, o_s, o_r, gh_s, gh_r,
):
    step = pl.program_id(0)
    n = ai.shape[0]
    nh = n // 2
    hi_n = wm.shape[2]
    wide = 2 * hi_n
    width = x.shape[1]
    dw = width // wide
    rw = bo.shape[3]
    h, c, r, q = coords()
    own_dy = pltpu.make_async_copy(gout, dy, ld.at[4])
    swapped_dy = pltpu.make_async_copy(dy_in, dy, ld.at[4])
    own_o = pltpu.make_async_copy(oh, oa, ld.at[5])

    mate = (h, 1 - c, r, q)

    def block_of(t):
        return near.at[:, t] if t < nh else far

    def give(t):
        return remote(block_of(t), theirs.at[t], th_s.at[t, 0], th_r.at[t, 0], mate)

    def late_hi(t, dh):
        to = ((h + dh) % hi_n, c, r, q)
        u = t - nh - 1
        return remote(lp.at[u], late.at[h, u], gh_s.at[u, dh], gh_r.at[u, dh], to)

    def late_piece(t, dh):
        return late.at[(h + hi_n - dh) % hi_n, t - nh - 1] if dh else lp.at[t - nh - 1]

    def late_arrives(t, dh):
        u = t - nh - 1
        return remote(lp.at[u], late_piece(t, dh), gh_s.at[u, dh], gh_r.at[u, dh], mate)

    def give_late(t, dh):
        source = (h + hi_n - dh) % hi_n
        return remote(
            late_piece(t, dh), theirs.at[t, source], th_s.at[t, dh], th_r.at[t, dh], mate
        )

    def load_late(t, dh):
        source = (h + hi_n - dh) % hi_n
        return pltpu.make_async_copy(late_piece(t, dh), wm.at[t % 2, c, source], ld.at[t % 2])

    def give_o():
        return remote(oh, ob, o_s, o_r, (h, 1 - c, r, q))

    def load_own(src, at):
        return pltpu.make_async_copy(src, wm.at[at, c], ld.at[at])

    def load_theirs(t, at):
        return pltpu.make_async_copy(theirs.at[t], wm.at[at, 1 - c], ld.at[2 + at])
    own_x = pltpu.make_async_copy(xa.at[c * (n // 2) + q], x, x_s)
    slot = step % 2
    last = n - 1

    def to_mate(at):
        return remote(buf.at[at, 1 - c], rcv.at[at], buf_s.at[at], buf_r.at[at], mate)

    def out_to_mate():
        return remote(bo.at[1 - c], rcvo, bo_s, bo_r, mate)

    @pl.when(step == 0)
    def _():
        own_x.start()
        own_o.start()
        load_own(near.at[:, 0], 0).start()

        @pl.when(c == r)
        def _():
            own_dy.start()

        @pl.when(c != r)
        def _():
            swapped_dy.start()

        barrier = pltpu.get_barrier_semaphore()
        friends = [mate]
        friends += [((h + dh) % hi_n, c, r, q) for dh in range(1, hi_n)]
        for to in friends:
            pl.semaphore_signal(barrier, inc=1, device_id=to, device_id_type=MESH)
        pl.semaphore_wait(barrier, len(friends))
        for t in range(nh + 1, n):
            for dh in range(1, hi_n):
                late_hi(t, dh).start()
        give_o().start()
        for t in range(nh + 1):
            give(t).start()
        for t in range(nh + 1, n):
            give_late(t, 0).start()
        own_x.wait()
        own_o.wait()
        own_dy.wait()
        give_o().wait_recv()
        for s in range(n):
            for w in range(wide):
                wo[s, w * rw : (w + 1) * rw] = jnp.where(c == w % 2, oa[w // 2, s], ob[w // 2, s])
        give(0).wait_recv()
        load_theirs(0, 0).start()
        hid[...] = x[...].astype(F32)

        def project(s, carry):
            hid[...] += nn(ai[s], wo[s])
            return carry

        lax.fori_loop(0, n, project, 0)
        total = hid[...]
        inv = lax.rsqrt(jnp.mean(total * total, axis=-1, keepdims=True) + EPSILON)
        n2[...] = (total * inv * g2[...]).astype(BF)
        acc_o[...] = jnp.zeros_like(acc_o)
        acc_g[...] = jnp.zeros_like(acc_g)

    @pl.when(step < n)
    def _():
        @pl.when(step > 1)
        def _():
            to_mate(slot).wait_send()

        load_own(near.at[:, 0], slot).wait()
        load_theirs(0, slot).wait()

        def weight(j):
            return jnp.concatenate([wm[slot, w % 2, w // 2, j] for w in range(wide)], axis=1)

        def put(j, grad):
            low = grad.astype(BF)
            for w in range(wide):
                buf[slot, w % 2, w // 2, j] = low[:, w * dw : (w + 1) * dw]

        gate = nt(n2[...], weight(0))
        up = nt(n2[...], weight(1))
        sig = jax.nn.sigmoid(gate)
        silu = gate * sig
        inner = (silu * up).astype(BF)
        grad_inner = nt(dy[...], weight(2))
        for t in range(1, nh + 1):
            @pl.when(step == t - 1)
            def _():
                load_own(block_of(t), t % 2).start()
                give(t).wait_recv()
                load_theirs(t, t % 2).start()

        for t in range(nh + 1, n):
            @pl.when(step == t - 1)
            def _():
                load_late(t, 0).start()
                for dh in range(1, hi_n):
                    late_arrives(t, dh).wait_recv()
                    give_late(t, dh).start()
                    load_late(t, dh).start()

        grad_gate = (grad_inner * up * sig * (1.0 + gate * (1.0 - sig))).astype(BF)
        grad_up = (grad_inner * silu).astype(BF)
        acc_o[...] += nn(inner, weight(2))
        acc_g[...] += nn(grad_gate, weight(0)) + nn(grad_up, weight(1))
        put(0, tn(grad_gate, n2[...]))
        put(1, tn(grad_up, n2[...]))
        put(2, tn(inner, dy[...]))

    @pl.when(step == last)
    def _():
        hidden = hid[...]
        lo[...] = (hidden + acc_o[...]).astype(BF)
        inv = lax.rsqrt(jnp.mean(hidden * hidden, axis=-1, keepdims=True) + EPSILON)
        grad_n = acc_g[...]
        gg2[...] = jnp.sum((grad_n * hidden * inv).reshape(-1, 8, width), axis=0)
        scaled = grad_n * g2[...]
        dot = jnp.sum(scaled * hidden, axis=-1, keepdims=True)
        grad_h = dy[...].astype(F32) + scaled * inv - hidden * (inv * inv * inv * dot / width)
        gh[...] = grad_h
        low = grad_h.astype(BF)

        def project_back(s, carry):
            ga[s] = nt(low, wo[s]).astype(BF)
            grad_wo = tn(ai[s], low).astype(BF)
            for w in range(wide):
                bo[w % 2, w // 2, s] = grad_wo[w * rw : (w + 1) * rw]
            return carry

        lax.fori_loop(0, n, project_back, 0)

    @pl.when(step > 0)
    def _():
        before = (step + 1) % 2
        to_mate(before).wait_recv()
        for a in range(hi_n):
            for j in range(3):
                total = buf[before, c, a, j].astype(F32) + rcv[before, a, j].astype(F32)
                dsum[a, 0, j] = total.astype(BF)

    for t in range(nh + 1, n):
        @pl.when(step == t - 1)
        def _():
            for dh in range(hi_n):
                give_late(t, dh).wait_recv()
            load_theirs(t, t % 2).start()

    @pl.when(step < n)
    def _():
        to_mate(slot).start()

    @pl.when(step == last)
    def _():
        out_to_mate().start()

    @pl.when(step == n)
    def _():
        out_to_mate().wait_recv()
        for a in range(hi_n):
            for s in range(n):
                total = bo[c, a, s].astype(F32) + rcvo[a, s].astype(F32)
                dosum[a, s] = total.astype(BF)
        out_to_mate().wait_send()
        to_mate(0).wait_send()
        to_mate(1).wait_send()
        give_o().wait_send()
        for t in range(nh + 1):
            give(t).wait_send()
        for t in range(nh + 1, n):
            for dh in range(hi_n):
                give_late(t, dh).wait_send()
            for dh in range(1, hi_n):
                late_hi(t, dh).wait_send()


def feed_forward(xa, gout, dy_in, near, far, lp, oh, ai, g2):
    n, tok, sw = ai.shape
    nh = n // 2
    width = gout.shape[1]
    hi_n, _, _, ffs, dw = near.shape
    wide = 2 * hi_n
    rw = sw // wide

    def whole(*shape):
        return pl.BlockSpec(shape, lambda i: (0,) * len(shape))

    def fixed(*shape):
        return pl.BlockSpec(
            shape, lambda i: (0,) * len(shape), pipeline_mode=pl.Buffered(1)
        )

    return pl.pallas_call(
        mlp_kernel,
        out_shape=(
            jax.ShapeDtypeStruct((tok, width), BF),
            jax.ShapeDtypeStruct((tok, width), F32),
            jax.ShapeDtypeStruct((n, tok, sw), BF),
            jax.ShapeDtypeStruct((hi_n, n, 3, ffs, dw), BF),
            jax.ShapeDtypeStruct((hi_n, n, rw, width), BF),
            jax.ShapeDtypeStruct((8, width), F32),
            jax.ShapeDtypeStruct((n, hi_n, 3, ffs, dw), BF),
            jax.ShapeDtypeStruct((hi_n, max(nh - 1, 1), 3, ffs, dw), BF),
        ),
        grid_spec=pl.GridSpec(
            grid=(n + 1,),
            in_specs=[ANY] * 7 + [fixed(n, tok, sw), fixed(1, width)],
            out_specs=(
                whole(tok, width),
                whole(tok, width),
                whole(n, tok, sw),
                pl.BlockSpec(
                    (hi_n, 1, 3, ffs, dw), lambda i: (0, jnp.maximum(i - 1, 0), 0, 0, 0)
                ),
                whole(hi_n, n, rw, width),
                whole(8, width),
                ANY,
                ANY,
            ),
            scratch_shapes=[
                pltpu.VMEM((tok, width), BF),
                pltpu.VMEM((tok, width), BF),
                pltpu.VMEM((tok, width), F32),
                pltpu.VMEM((tok, width), BF),
                pltpu.VMEM((tok, width), F32),
                pltpu.VMEM((tok, width), F32),
                pltpu.VMEM((2, 2, hi_n, 3, ffs, dw), BF),
                pltpu.VMEM((2, hi_n, 3, ffs, dw), BF),
                pltpu.VMEM((2, hi_n, n, rw, width), BF),
                pltpu.VMEM((hi_n, n, rw, width), BF),
                pltpu.VMEM((2, 2, hi_n, 3, ffs, dw), BF),
                pltpu.VMEM((n, sw, width), BF),
                pltpu.VMEM((hi_n, n, rw, width), BF),
                pltpu.VMEM((hi_n, n, rw, width), BF),
                DMA, DMA((2,)), DMA((2,)), DMA, DMA,
                DMA((6,)), DMA((n, hi_n)), DMA((n, hi_n)), DMA, DMA,
                DMA((max(nh - 1, 1), hi_n)), DMA((max(nh - 1, 1), hi_n)),
            ],
        ),
        name="feed_forward",
        compiler_params=pltpu.CompilerParams(
            dimension_semantics=("arbitrary",),
            collective_id=4,
            has_side_effects=True,
            vmem_limit_bytes=VMEM_MAX,
        ),
        cost_estimate=pl.CostEstimate(
            flops=18 * tok * width * ffs * n, bytes_accessed=40 << 20, transcendentals=tok * ffs * n
        ),
    )(xa, gout, dy_in, near, far, lp, oh, ai, g2)


def backward_kernel(
    sizes, block, ga, ds, dos, lo, xa, ws, g1, lo_c, lo_s, hi_c, hi_s, seg, qi, ki, mi, ao, lse, gh,
    gg2, squares, values_sq,
    gv, gi, fin, og, total_small, lo_in, rx, rxo, zr,
    do, normed, dq, dk, dv, dcat, gow, gnp, rcv, rcv2, gis, part, zs, zos, do_part,
    dwq, gg1, zo, sm, s1, s2, r1, r2, own, mine,
    do_s, do_r, gv_s, gv_r, co_s, co_r, pe_s, pe_r, gi_s, gi_r, loc,
    rx_s, rx_r, rxo_s, rxo_r, ly_s, ly_r, ld, z_s, z_r, zo_s, zo_r,
    a_s, a_r, b_s, b_r, c_s, c_r, d_s, d_r, e_s, e_r, f_s, f_r, m_s, m_r,
):
    hi_n, _, _, nh = sizes
    n = 2 * nh
    h, c, r, q = coords()
    p = c * nh + q
    row_len, sw = qi.shape
    width = xa.shape[1]
    tok = row_len // n
    short = row_len // 2
    pw = lo_c.shape[1]
    pairs = sw // pw
    halves = pw // HEAD_DIM
    same = c == r
    mate = (h, 1 - c, r, q)
    swap_to = (h, r, c, q)
    zed = r * nh + q
    greet_plane(sizes, True, 2)

    order = list(range(nh, n)) + list(range(1, nh)) + [0]

    def over_hi(dh, i):
        to = (h + dh) % hi_n
        return remote(
            ds.at[to, i], rx.at[dh - 1, i], rx_s.at[dh, i], rx_r.at[dh, i], (to, c, r, q)
        )

    def out_over_hi(dh):
        to = (h + dh) % hi_n
        return remote(dos.at[to], rxo.at[dh - 1], rxo_s.at[dh], rxo_r.at[dh], (to, c, r, q))

    def send_lo():
        return remote(lo, lo_in, ly_s, ly_r, swap_to)

    def over_z(t):
        to = (h, c, (r + t // nh) % 2, (q + t % nh) % nh)
        return remote(zs.at[t], zr.at[zed], z_s.at[t], z_r.at[zed], to)

    def out_over_z(i):
        return remote(zos.at[i], zo.at[zed], zo_s.at[i], zo_r.at[zed], (h, c, i // nh, i % nh))

    def keep_z():
        return pltpu.make_async_copy(zs.at[0], zr.at[zed], z_s.at[0])

    def keep_out_z(i):
        return pltpu.make_async_copy(zos.at[i], zo.at[i], zo_s.at[i])

    def load_chunk(i):
        copies = [pltpu.make_async_copy(ds.at[h, i], part.at[0], ld.at[0])]
        for dh in range(1, hi_n):
            copies.append(pltpu.make_async_copy(rx.at[dh - 1, i], part.at[dh], ld.at[dh]))
        return copies

    def reduce_chunk(i):
        for dh in range(1, hi_n):
            over_hi(dh, i).wait_recv()
        for copy in load_chunk(i):
            copy.start()
        for copy in load_chunk(i):
            copy.wait()

        def add(j, carry):
            total = part[0, j].astype(F32)
            for dh in range(1, hi_n):
                total = total + part[dh, j].astype(F32)
            zs[i, j] = total.astype(BF)
            return carry

        lax.fori_loop(0, 3, add, 0)
        if i:
            over_z(i).start()
        else:
            keep_z().start()

    own_out = pltpu.make_async_copy(dos.at[h], zos, ld.at[0])

    def reduce_out():
        own_out.start()
        own_out.wait()
        for dh in range(1, hi_n):
            out_over_hi(dh).wait_recv()
            copy = pltpu.make_async_copy(rxo.at[dh - 1], do_part, ld.at[dh])
            copy.start()
            copy.wait()
            zos[...] = (zos[...].astype(F32) + do_part[...].astype(F32)).astype(BF)
        for i in range(n):
            @pl.when(zed != i)
            def _():
                out_over_z(i).start()

            @pl.when(zed == i)
            def _():
                keep_out_z(i).start()

    def send_do(s, pair):
        lanes = lane_window(pair, pw, sw)
        to = (h, s // nh, r, s % nh)
        return remote(
            ga.at[s, :, lanes], do.at[p, :, lanes], do_s.at[pair, s], do_r.at[pair, p], to
        )

    def do_arrives(s, pair):
        lanes = lane_window(pair, pw, sw)
        return remote(
            ga.at[s, :, lanes], do.at[s, :, lanes], do_s.at[pair, s], do_r.at[pair, s], mate
        )

    keep_do = pltpu.make_async_copy(ga.at[p], do.at[p], loc.at[0])
    for pair in range(pairs):
        for s in range(n):
            @pl.when(p != s)
            def _():
                send_do(s, pair).start()

    keep_do.start()
    for dh in range(1, hi_n):
        out_over_hi(dh).start()
    for i in order:
        for dh in range(1, hi_n):
            over_hi(dh, i).start()

    @pl.when(c != r)
    def _():
        send_lo().start()

    br = 256

    def norm(i, carry):
        rows = pl.ds(pl.multiple_of(i * br, br), br)
        xf = xa[rows, :].astype(F32)
        inv = lax.rsqrt(jnp.mean(xf * xf, axis=-1, keepdims=True) + EPSILON)
        normed[rows, :] = (xf * inv * g1[...]).astype(BF)
        return carry

    lax.fori_loop(0, row_len // br, norm, 0)
    keep_do.wait()

    flag = seg[0:1, 0:1]
    bias = flag * -1e30
    blocks = row_len // block
    per = block // tok
    causal = lax.broadcasted_iota(jnp.int32, (block, block), 0) >= lax.broadcasted_iota(
        jnp.int32, (block, block), 1
    )

    def gv_at(s, pair):
        if len(gv.shape) == 3:
            return gv.at[s]
        return gv.at[:, pl.ds(pl.multiple_of(s * sw + pair * pw, pw), pw)]

    def send_gv(b, pair):
        lanes = lane_window(pair, pw, sw)
        to = (h, r, b // nh, b % nh)
        return remote(
            gow.at[b, :, lanes], gv_at(p, pair), gv_s.at[pair, b], gv_r.at[pair, p], to
        )

    def keep_gv(pair):
        lanes = lane_window(pair, pw, sw)
        return pltpu.make_async_copy(gow.at[p, :, lanes], gv_at(p, pair), loc.at[1 + pair])

    def early(pair, i):
        if pairs < 2 or blocks < 4:
            return 0

        @pl.when(pair == 0)
        def _():
            if i == blocks - 2:
                reduce_out()
                reduce_chunk(order[0])

        @pl.when(pair == 1)
        def _():
            if i == 1:
                reduce_chunk(order[1])

        return 2

    def pair_step(pair, carry):
        for s in range(n):
            @pl.when(p != s)
            def _():
                do_arrives(s, pair).wait_recv()

        lanes = lane_window(pair, pw, sw)
        dk[...] = jnp.zeros_like(dk)
        dv[...] = jnp.zeros_like(dv)
        for i in range(blocks):
            rows = pl.ds(i * block, block)
            pieces = [[] for _ in range(i + 1)]
            dq_parts = []
            do_rows = [do[i * per + t, :, lanes] for t in range(per)]
            do_i = do_rows[0] if per == 1 else jnp.concatenate(do_rows, axis=0)
            ao_rows = [ao[i * per + t, :, lanes] for t in range(per)]
            ao_i = ao_rows[0] if per == 1 else jnp.concatenate(ao_rows, axis=0)
            product = do_i.astype(F32) * ao_i.astype(F32)
            for half in range(halves):
                cols = slice(half * HEAD_DIM, (half + 1) * HEAD_DIM)
                qh = qi[rows, lanes][:, cols]
                doh = do_i[:, cols]
                delta = jnp.sum(product[:, cols], axis=-1, keepdims=True)
                level = lse[pair, rows, half : half + 1]
                acc = 0.0
                for j in range(i + 1):
                    kj = ki[pl.ds(j * block, block), lanes][:, cols]
                    vj = mi[pl.ds(j * block, block), lanes][:, cols]
                    crossing = i * block >= short and j * block < short
                    score = masked(nt(qh, kj), i == j, crossing, causal, bias)
                    prob = jnp.exp(score - level)
                    grad_prob = nt(doh, vj)
                    grad_score = (prob * (grad_prob - delta)).astype(BF)
                    acc = acc + nn(grad_score, kj)
                    pieces[j].append((tn(grad_score, qh), tn(prob.astype(BF), doh)))
                dq_parts.append(acc * HEAD_DIM**-0.5)
            dq[rows, :] = dq_parts[0] if halves == 1 else jnp.concatenate(dq_parts, axis=1)
            for j in range(i + 1):
                at = pl.ds(j * block, block)
                if halves == 1:
                    dk[at, :] += pieces[j][0][0]
                    dv[at, :] += pieces[j][0][1]
                else:
                    dk[at, :] += jnp.concatenate([t[0] for t in pieces[j]], axis=1)
                    dv[at, :] += jnp.concatenate([t[1] for t in pieces[j]], axis=1)
            early(pair, i)
        first = first_lanes(br, pw)

        def finish(i, inner_carry):
            rows = pl.ds(pl.multiple_of(i * br, br), br)
            ct, st = rope_rows(lo_c, lo_s, hi_c, hi_s, flag, i, br)
            a = dq[rows, :]
            b = dk[rows, :]
            dcat[0, rows, lanes] = (a * ct - rotate_lanes(a, first) * st).astype(BF)
            dcat[1, rows, lanes] = (b * ct - rotate_lanes(b, first) * st).astype(BF)
            dcat[2, rows, lanes] = (0.5 * dv[rows, :].astype(BF).astype(F32)).astype(BF)
            return inner_carry

        lax.fori_loop(0, row_len // br, finish, 0)
        for b in range(n):
            gow[b, :, lanes] = dcat[2, pl.ds(b * tok, tok), lanes]

            @pl.when(jnp.logical_or(c != r, p != b))
            def _():
                send_gv(b, pair).start()

        @pl.when(same)
        def _():
            keep_gv(pair).start()

        return carry

    lax.fori_loop(0, pairs, pair_step, 0)
    rest = order[2:] if pairs > 1 and blocks > 3 else order
    if len(rest) == n:
        reduce_out()

    ck = min(256, tok)
    half_rows = row_len // 2
    n_half = half_rows // ck
    n_blk = tok // ck

    def partial(base, k):
        rows = pl.ds(pl.multiple_of(base + k * ck, ck), ck)
        total = nn(dcat[0, rows, :], ws[:sw, :])
        for t in range(1, 3):
            total = total + nn(dcat[t, rows, :], ws[t * sw : (t + 1) * sw, :])
        gnp[rows, :] = total.astype(BF)

    def to_mate(k):
        rows = pl.ds(pl.multiple_of((1 - c) * half_rows + k * ck, ck), ck)
        here = pl.ds(pl.multiple_of(k * ck, ck), ck)
        return remote(gnp.at[rows], rcv.at[here], co_s.at[k], co_r.at[k], mate)

    def first_half(k, carry):
        partial((1 - c) * half_rows, k)
        to_mate(k).start()
        return carry

    lax.fori_loop(0, n_half, first_half, 0)

    def own_rows(d):
        return ((q + d) % nh) * tok

    def to_peer(d, k):
        rows = pl.ds(pl.multiple_of(c * half_rows + own_rows(d) + k * ck, ck), ck)
        to = (h, c, r, (q + d) % nh)
        here = pl.ds(pl.multiple_of(k * ck, ck), ck)
        return remote(gnp.at[rows], rcv2.at[d - 1, here], pe_s.at[d, k], pe_r.at[d, k], to)

    def second_half(u, carry):
        partial(c * half_rows + own_rows(1 + u // n_blk), u % n_blk)
        return carry

    lax.fori_loop(0, nh * n_blk, second_half, 0)

    for k in range(n_half):
        to_mate(k).wait_recv()

    def added(d, k):
        rows = pl.ds(pl.multiple_of(c * half_rows + own_rows(d) + k * ck, ck), ck)
        theirs = pl.ds(pl.multiple_of(own_rows(d) + k * ck, ck), ck)
        return rows, gnp[rows, :].astype(F32) + rcv[theirs, :].astype(F32)

    def pass_on(u, carry):
        d, k = 1 + u // n_blk, u % n_blk
        rows, total = added(d, k)
        gnp[rows, :] = total.astype(BF)
        to_peer(d, k).start()
        return carry

    lax.fori_loop(0, (nh - 1) * n_blk, pass_on, 0)

    w = 2 * h + c

    def plane_out(dh, dc):
        to = ((h + dh) % hi_n, (c + dc) % 2, r, q)
        return remote(own, og.at[w], c_s.at[dh, dc], c_r.at[dh, dc], to)

    for i in range(n):
        @pl.when(zed != i)
        def _():
            remote(zos.at[i], zo.at[i], zo_s.at[i], zo_r.at[i], mate).wait_recv()

        @pl.when(zed == i)
        def _():
            keep_out_z(i).wait()

    out_rows = zo[0].astype(F32)
    for i in range(1, n):
        out_rows = out_rows + zo[i].astype(F32)
    own[...] = out_rows.astype(BF)
    og[w] = own[...]
    for dh in range(hi_n):
        for dc in range(2):
            if dh or dc:
                plane_out(dh, dc).start()

    cut = 3 * sw // hi_n

    def hi_part(dh):
        to = (h + dh) % hi_n
        return remote(dwq.at[to], r1.at[dh - 1], a_s.at[dh], a_r.at[dh], (to, c, r, q))

    for t in range(3):
        grad = tn(dcat[t], normed[...]).astype(BF)
        for i in range(hi_n):
            begin, end = max(t * sw, i * cut), min((t + 1) * sw, (i + 1) * cut)
            if begin < end:
                dwq[i, begin - i * cut : end - i * cut, :] = grad[begin - t * sw : end - t * sw]
    for dh in range(1, hi_n):
        hi_part(dh).start()

    for i in rest[:-1]:
        reduce_chunk(i)

    partner = swap_to
    gg1[...] = jnp.zeros_like(gg1)

    def send_gi(k):
        rows = pl.ds(pl.multiple_of(k * ck, ck), ck)
        return remote(gis.at[rows], gi.at[rows], gi_s.at[k], gi_r.at[k], partner)

    def keep_gi(k):
        rows = pl.ds(pl.multiple_of(k * ck, ck), ck)
        return pltpu.make_async_copy(gis.at[rows], gi.at[rows], gi_s.at[k])

    def last_sums(k, carry):
        rows = pl.ds(pl.multiple_of(k * ck, ck), ck)
        for d in range(1, nh):
            to_peer(d, k).wait_recv()
        _, grad_n = added(0, k)
        for d in range(1, nh):
            grad_n = grad_n + rcv2[d - 1, rows, :].astype(F32)
        here = pl.ds(pl.multiple_of(p * tok + k * ck, ck), ck)
        xf = xa[here, :].astype(F32)
        inv = lax.rsqrt(jnp.mean(xf * xf, axis=-1, keepdims=True) + EPSILON)
        gg1[...] += jnp.sum((grad_n * xf * inv).reshape(-1, 8, width), axis=0)
        scaled = grad_n * g1[...]
        dot = jnp.sum(scaled * xf, axis=-1, keepdims=True)
        gis[rows, :] = (
            gh[rows, :] + scaled * inv - xf * (inv * inv * inv * dot / width)
        ).astype(BF)

        @pl.when(c != r)
        def _():
            send_gi(k).start()

        @pl.when(same)
        def _():
            keep_gi(k).start()

        return carry

    lax.fori_loop(0, n_blk, last_sums, 0)

    def hi_small(dh):
        to = ((h + dh) % hi_n, c, r, q)
        return remote(sm, s1.at[h], b_s.at[dh], b_r.at[dh], to)

    sm[...] = jnp.zeros_like(sm)
    sm[0:1, :] = jnp.sum(gg1[...], axis=0, keepdims=True)
    sm[1:2, :] = jnp.sum(gg2[...], axis=0, keepdims=True)
    sm[2:3, :sw] = jnp.sum(values_sq[...], axis=0, keepdims=True)
    sm[3:4, :sw] = jnp.sum(squares[...], axis=0, keepdims=True)
    for dh in range(1, hi_n):
        hi_small(dh).start()
    s1[h] = sm[...]
    reduce_chunk(rest[-1])
    for dh in range(1, hi_n):
        source = (h + hi_n - dh) % hi_n
        remote(sm, s1.at[source], b_s.at[dh], b_r.at[dh], mate).wait_recv()
    small = s1[0]
    for i in range(1, hi_n):
        small = small + s1[i]
    spot = c * n + zed
    s2[spot] = small

    def plane_small(k):
        dc, dz = k // n, k % n
        z = (zed + dz) % n
        to = (h, (c + dc) % 2, z // nh, z % nh)
        return remote(s2.at[spot], s2.at[spot], d_s.at[k], d_r.at[k], to)

    def small_arrives(k):
        dc, dz = k // n, k % n
        source = ((c + dc) % 2) * n + (zed + n - dz) % n
        return remote(s2.at[source], s2.at[source], d_s.at[k], d_r.at[k], mate)

    for k in range(1, 2 * n):
        plane_small(k).start()

    part_sum = dwq[h].astype(F32)
    for dh in range(1, hi_n):
        hi_part(dh).wait_recv()
        part_sum = part_sum + r1[dh - 1].astype(F32)
    mine[...] = part_sum.astype(BF)
    across = remote(mine, r2, e_s, e_r, (h, c, 1 - r, q))

    @pl.when(c != r)
    def _():
        across.start()

    for k in range(1, 2 * n):
        small_arrives(k).wait_recv()
    whole = s2[0]
    for k in range(1, 2 * n):
        whole = whole + s2[k]
    total_small[...] = whole

    def spread(dh):
        to = ((h + dh) % hi_n, c, r, q)
        return remote(fin.at[h], fin.at[h], f_s.at[dh], f_r.at[dh], to)

    def share(dh):
        source = (h + hi_n - dh) % hi_n
        return remote(fin.at[source], fin.at[source], m_s.at[dh], m_r.at[dh], mate)

    @pl.when(same)
    def _():
        across.wait_recv()
        fin[h] = (mine[...].astype(F32) + r2[...].astype(F32)).astype(BF)
        for dh in range(1, hi_n):
            spread(dh).start()
        share(0).start()
        for dh in range(1, hi_n):
            source = (h + hi_n - dh) % hi_n
            remote(fin.at[h], fin.at[source], f_s.at[dh], f_r.at[dh], mate).wait_recv()
            share(dh).start()

    @pl.when(c != r)
    def _():
        for dh in range(hi_n):
            share(dh).wait_recv()
        across.wait_send()

    @pl.when(same)
    def _():
        for dh in range(1, hi_n):
            spread(dh).wait_send()
        for dh in range(hi_n):
            share(dh).wait_send()

    for k in range(n_blk):
        @pl.when(c != r)
        def _():
            send_gi(k).wait_send()
            send_gi(k).wait_recv()

        @pl.when(same)
        def _():
            keep_gi(k).wait()

    for k in range(n_half):
        to_mate(k).wait_send()
    for d in range(1, nh):
        for k in range(n_blk):
            to_peer(d, k).wait_send()
    for dh in range(hi_n):
        for dc in range(2):
            if dh or dc:
                theirs = 2 * ((h + hi_n - dh) % hi_n) + (c + dc) % 2
                remote(own, og.at[theirs], c_s.at[dh, dc], c_r.at[dh, dc], mate).wait_recv()
                plane_out(dh, dc).wait_send()
    for dh in range(1, hi_n):
        hi_small(dh).wait_send()
        hi_part(dh).wait_send()
    for k in range(1, 2 * n):
        plane_small(k).wait_send()

    def drain(pair, carry):
        lanes = lane_window(pair, pw, sw)
        for b in range(n):
            @pl.when(p != b)
            def _():
                send_do(b, pair).wait_send()

            @pl.when(jnp.logical_or(c != r, p != b))
            def _():
                send_gv(b, pair).wait_send()
                remote(
                    gow.at[b, :, lanes], gv_at(b, pair), gv_s.at[pair, b], gv_r.at[pair, b], mate
                ).wait_recv()

        @pl.when(same)
        def _():
            keep_gv(pair).wait()

        return carry

    lax.fori_loop(0, pairs, drain, 0)

    @pl.when(c != r)
    def _():
        send_lo().wait_send()
        send_lo().wait_recv()

    for dh in range(1, hi_n):
        out_over_hi(dh).wait_send()
        for i in range(n):
            over_hi(dh, i).wait_send()
    for i in range(n):
        @pl.when(zed != i)
        def _():
            out_over_z(i).wait_send()
            remote(zs.at[i], zr.at[i], z_s.at[i], z_r.at[i], mate).wait_recv()

    keep_z().wait()
    for t in range(1, n):
        over_z(t).wait_send()


def attention_backward(sizes, ga, ds, dos, lo, xa, ws, g1, tables, seg, *saved):
    _, _, _, nh = sizes
    n, tok, sw = ga.shape
    row_len, width = xa.shape
    pw = tables[0].shape[1]
    pairs = sw // pw
    block = max(tok, 512)
    ck = min(256, tok)
    n_half = row_len // 2 // ck
    n_blk = tok // ck
    hi_n = sizes[0]
    _, _, _, ffs, dw = ds.shape
    rw = dos.shape[2]
    others = max(hi_n - 1, 1)
    cut = 3 * sw // hi_n
    return pl.pallas_call(
        functools.partial(backward_kernel, sizes, block),
        out_shape=(
            jax.ShapeDtypeStruct((n, tok, sw) if sw % 128 else (tok, width), BF),
            jax.ShapeDtypeStruct((tok, width), BF),
            jax.ShapeDtypeStruct((hi_n, cut, width), BF),
            jax.ShapeDtypeStruct((2 * hi_n, rw, width), BF),
            jax.ShapeDtypeStruct((8, width), F32),
            jax.ShapeDtypeStruct((tok, width), BF),
            jax.ShapeDtypeStruct((others, n, 3, ffs, dw), BF),
            jax.ShapeDtypeStruct((others, n, rw, width), BF),
            jax.ShapeDtypeStruct((n, 3, ffs, dw), BF),
        ),
        in_specs=[ANY] * 4 + [VM] * 17,
        out_specs=(ANY, ANY, VM, VM, VM) + (ANY,) * 4,
        scratch_shapes=[
            pltpu.VMEM((n, tok, sw), BF),
            pltpu.VMEM((row_len, width), BF),
            pltpu.VMEM((row_len, pw), F32),
            pltpu.VMEM((row_len, pw), F32),
            pltpu.VMEM((row_len, pw), F32),
            pltpu.VMEM((3, row_len, sw), BF),
            pltpu.VMEM((n, tok, sw), BF),
            pltpu.VMEM((row_len, width), BF),
            pltpu.VMEM((row_len // 2, width), BF),
            pltpu.VMEM((max(nh - 1, 1), tok, width), BF),
            pltpu.VMEM((tok, width), BF),
            pltpu.VMEM((hi_n, 3, ffs, dw), BF),
            pltpu.VMEM((n, 3, ffs, dw), BF),
            pltpu.VMEM((n, rw, width), BF),
            pltpu.VMEM((n, rw, width), BF),
            pltpu.VMEM((hi_n, cut, width), BF),
            pltpu.VMEM((8, width), F32),
            pltpu.VMEM((n, rw, width), BF),
            pltpu.VMEM((8, width), F32),
            pltpu.VMEM((hi_n, 8, width), F32),
            pltpu.VMEM((2 * n, 8, width), F32),
            pltpu.VMEM((others, cut, width), BF),
            pltpu.VMEM((cut, width), BF),
            pltpu.VMEM((rw, width), BF),
            pltpu.VMEM((cut, width), BF),
            DMA((pairs, n)), DMA((pairs, n)),
            DMA((pairs, n)), DMA((pairs, n)),
            DMA((n_half,)), DMA((n_half,)),
            DMA((nh, n_blk)), DMA((nh, n_blk)),
            DMA((n_blk,)), DMA((n_blk,)),
            DMA((1 + pairs,)),
            DMA((hi_n, n)), DMA((hi_n, n)),
            DMA((hi_n,)), DMA((hi_n,)),
            DMA, DMA,
            DMA((hi_n,)),
            DMA((n,)), DMA((n,)),
            DMA((n,)), DMA((n,)),
            DMA((hi_n,)), DMA((hi_n,)),
            DMA((hi_n,)), DMA((hi_n,)),
            DMA((hi_n, 2)), DMA((hi_n, 2)),
            DMA((2 * n,)), DMA((2 * n,)),
            DMA, DMA,
            DMA((hi_n,)), DMA((hi_n,)),
            DMA((hi_n,)), DMA((hi_n,)),
        ],
        name="attention_backward",
        compiler_params=pltpu.CompilerParams(
            collective_id=3, has_side_effects=True, vmem_limit_bytes=VMEM_MAX
        ),
        cost_estimate=pl.CostEstimate(
            flops=60 << 30, bytes_accessed=24 << 20, transcendentals=row_len * row_len * sw // 128
        ),
    )(ga, ds, dos, lo, xa, ws, g1, *tables, seg, *saved)


def per_device(sizes, layer_in, value_first, seg_start, gain_one, w_qkv, w_out, gain_two, w_mlp, grad_out):
    hi_n, _, _, nh = sizes
    n = 2 * nh
    wide = 2 * hi_n
    tok, width = layer_in.shape
    sw = w_qkv.shape[1]
    row_len = n * tok
    h, c, r, q = coords()

    w_mlp_t = jnp.transpose(w_mlp, (1, 2, 0))
    sg = jnp.full((8, 128), seg_start[1].astype(F32))
    w_cut = w_qkv.reshape(hi_n, 3 * sw // hi_n, width)
    wo_cut = w_out.reshape(wide, sw // wide, width)
    v_cut = value_first.reshape(tok, n, sw).transpose(1, 0, 2) if sw % 128 else value_first
    xa, ws, so, near, cross, oz = exchange_inputs(sizes, layer_in, w_cut, sg, w_mlp_t, wo_cut)
    ws = ws.reshape(3 * sw, width)

    tables = rope_parts(row_len, min(sw, 128))
    g1 = gain_one.reshape(1, width)
    g2 = gain_two.reshape(1, width)
    xr = xa.reshape(row_len, width)
    ai, dy_in, far, late, oh, qo, ko, mo, ao, lse, squares, values_sq = attention_forward(
        sizes, v_cut, grad_out, cross, oz, xr, ws, g1, tables, so
    )
    lo, gh, ga, ds, dos, gg2, _, _ = feed_forward(xa, grad_out, dy_in, near, far, late, oh, ai, g2)
    gv, gi, fin, og, sums, lo_in, _, _, zr = attention_backward(
        sizes, ga, ds, dos, lo, xr, ws, g1, tables, so, qo, ko, mo, ao, lse, gh, gg2, squares, values_sq
    )

    layer_out = jnp.where(c == r, lo, lo_in)
    grad_value_first = (gv.transpose(1, 0, 2).reshape(tok, width) if sw % 128 else gv).astype(F32)
    grad_in = gi.astype(F32)
    grad_w_mlp = jnp.transpose(jnp.sum(zr.astype(F32), axis=0), (2, 0, 1))
    grad_w_out = og.reshape(sw, width).astype(F32)
    grad_w_qkv = fin.reshape(3, sw, width).astype(F32)
    entries = tok * width * wide * n
    value_norms = jnp.sqrt(jnp.sum(sums[2:4], axis=1) / entries)
    return (
        layer_out,
        grad_in,
        grad_value_first,
        sums[0],
        grad_w_qkv,
        grad_w_out,
        sums[1],
        grad_w_mlp,
        value_norms,
    )


def solution(mesh):
    wide, narrow = mesh.shape["wide"], mesh.shape["narrow"]
    sizes = (wide // 2, 2, 2, narrow // 2)
    fine = Mesh(mesh.devices.reshape(sizes), AXES)
    w_axes, n_axes = ("hi", "core"), ("zh", "zq")
    rows = P(AXES, None)
    return jax.shard_map(
        functools.partial(per_device, sizes),
        mesh=fine,
        in_specs=(
            rows,
            rows,
            P(w_axes),
            P(),
            P(None, n_axes, None),
            P(n_axes, None),
            P(),
            P(w_axes, None, n_axes),
            rows,
        ),
        out_specs=(
            rows,
            rows,
            rows,
            P(),
            P(None, n_axes, None),
            P(n_axes, None),
            P(),
            P(w_axes, None, n_axes),
            P(),
        ),
        check_vma=False,
    )
```

```python
import functools

import jax
import jax.numpy as jnp
import numpy as np
from jax import lax
from jax.experimental import pallas as pl
from jax.experimental.pallas import tpu as pltpu
from jax.sharding import Mesh, PartitionSpec as P

HEAD_DIM = 64
EPSILON = 1e-06
BF = jnp.bfloat16
F32 = jnp.float32
AXES = ("hi", "core", "zh", "zq")
MESH = pl.DeviceIdType.MESH
ANY = pl.BlockSpec(memory_space=pl.ANY)
VM = pl.BlockSpec(memory_space=pltpu.VMEM)
VMEM_MAX = 62 << 20
DMA = pltpu.SemaphoreType.DMA


def nn(a, b):
    return lax.dot_general(a, b, (((1,), (0,)), ((), ())), preferred_element_type=F32)


def nt(a, b):
    return lax.dot_general(a, b, (((1,), (1,)), ((), ())), preferred_element_type=F32)


def tn(a, b):
    return lax.dot_general(a, b, (((0,), (0,)), ((), ())), preferred_element_type=F32)


def coords():
    return tuple(lax.axis_index(name) for name in AXES)


def remote(src, dst, send, recv, to):
    return pltpu.make_async_remote_copy(
        src_ref=src, dst_ref=dst, send_sem=send, recv_sem=recv, device_id=to, device_id_type=MESH
    )


def greet_plane(sizes, with_hi, cores=1):
    hi_n, _, _, nh = sizes
    h, c, r, q = coords()
    barrier = pltpu.get_barrier_semaphore()
    count = 0
    for dc in range(2):
        for dr in range(2):
            for dq in range(nh):
                if dc or dr or dq:
                    to = (h, (c + dc) % 2, (r + dr) % 2, (q + dq) % nh)
                    pl.semaphore_signal(barrier, inc=1, device_id=to, device_id_type=MESH)
                    count += 1
    if with_hi:
        for dh in range(1, hi_n):
            for dc in range(cores):
                to = ((h + dh) % hi_n, (c + dc) % 2, r, q)
                pl.semaphore_signal(barrier, inc=1, device_id=to, device_id_type=MESH)
                count += 1
    pl.semaphore_wait(barrier, count)


def rotate_lanes(values, first):
    width = values.shape[1]
    if width < 128:
        return jnp.concatenate([values[:, 32:], values[:, :32]], axis=1)
    return jnp.where(
        first, pltpu.roll(values, width - 32, 1), pltpu.roll(values, 32, 1)
    )


def first_lanes(rows, width):
    lane = lax.broadcasted_iota(jnp.int32, (rows, width), 1)
    return lane % HEAD_DIM < HEAD_DIM // 2


def lane_window(pair, pw, sw):
    return slice(0, sw) if pw == sw else pl.ds(pl.multiple_of(pair * pw, pw), pw)


def rope_rows(lo_c, lo_s, hi_c, hi_s, flag, i, rows):
    step = lo_c.shape[0]
    half = hi_c.shape[0] // 2
    cos, sin = [], []
    for u in range(rows // step):
        k = i * (rows // step) + u
        far, near = pl.ds(k, 1), pl.ds(k % half, 1)
        ch = hi_c[near, :] * flag + hi_c[far, :] * (1.0 - flag)
        sh = hi_s[near, :] * flag + hi_s[far, :] * (1.0 - flag)
        cos.append(lo_c[...] * ch - lo_s[...] * sh)
        sin.append(lo_s[...] * ch + lo_c[...] * sh)
    cos = jnp.concatenate(cos, axis=0)
    sin = jnp.concatenate(sin, axis=0)
    return cos, jnp.where(first_lanes(rows, cos.shape[1]), -sin, sin)


def rope_parts(row_len, pw):
    half = HEAD_DIM // 2
    frequency = 10000.0 ** (-2.0 * np.arange(half) / HEAD_DIM)
    frequency = np.tile(frequency, pw // half)[None, :]
    lo = np.arange(64)[:, None] * frequency
    hi = 64.0 * np.arange(row_len // 64)[:, None] * frequency
    return tuple(jnp.asarray(t, F32) for t in (np.cos(lo), np.sin(lo), np.cos(hi), np.sin(hi)))


def columns_of(ref, s, start, size, sw):
    if len(ref.shape) == 3:
        return ref.at[s]
    start = s * sw + start
    start = start if isinstance(start, int) else pl.multiple_of(start, size)
    return ref.at[:, pl.ds(start, size)]


def tiled(table, width):
    times = width // table.shape[1]
    return table if times == 1 else jnp.concatenate([table] * times, axis=1)


def exchange_kernel(
    sizes, chunks, x, w, sg, wt, wo, xa, ws, so, g1, cross, oz,
    xs, wb, sb, tb, ob,
    swap_s, swap_r, peer_s, peer_r, core_s, core_r, w_s, w_r, wh_s, wh_r, sg_s, sg_r, loc,
    oz_s, oz_r, gp_s, gp_r, gh_s, gh_r, cr_s, cr_r,
):
    hi_n, _, _, nh = sizes
    n = 2 * nh
    h, c, r, q = coords()
    p = c * nh + q
    zed = r * nh + q
    partner_p = r * nh + q
    rows = x.shape[0] // chunks
    same = c == r
    other = c != r
    partner = (h, r, c, q)
    mate = (h, 1 - c, r, q)
    greet_plane(sizes, True)

    def part(k):
        return pl.ds(k * rows, rows)

    def swap_x(k):
        return remote(x.at[part(k)], xa.at[partner_p, part(k)], swap_s.at[k], swap_r.at[k], partner)

    def own_arrives(k):
        return remote(x.at[part(k)], xa.at[p, part(k)], swap_s.at[k], swap_r.at[k], partner)

    def push_peer(src, k, dq):
        to = (h, c, r, (q + dq) % nh)
        return remote(src, xa.at[p, part(k)], peer_s.at[dq, k], peer_r.at[dq, k], to)

    def push_mate(src, k, dq):
        block = c * nh + (q + nh - dq) % nh
        return remote(src, xa.at[block, part(k)], core_s.at[dq, k], core_r.at[dq, k], mate)

    def send_w():
        return remote(w.at[h], ws.at[h], w_s, w_r, partner)

    def spread_w(dh):
        to = ((h + dh) % hi_n, c, r, q)
        return remote(ws.at[h], ws.at[h], wh_s.at[dh], wh_r.at[dh], to)

    def send_sg():
        return remote(sg, so, sg_s, sg_r, partner)

    def shard_peer(dq):
        to = (h, c, r, (q + dq) % nh)
        return remote(wt, g1.at[h, (nh - dq) % nh], gp_s.at[dq], gp_r.at[dq], to)

    def shard_hi(src, dh, t):
        to = ((h + dh) % hi_n, c, r, q)
        return remote(src, g1.at[h, t], gh_s.at[dh, t], gh_r.at[dh, t], to)

    def shard_cross():
        return remote(wt, cross, cr_s, cr_r, (h, c, 1 - r, q))

    def rows_z(dz):
        z = (zed + dz) % n
        return remote(
            wo.at[2 * h + c], oz.at[zed], oz_s.at[dz], oz_r.at[dz], (h, c, z // nh, z % nh)
        )

    def from_hi(dh):
        return (h + hi_n - dh) % hi_n

    local = [
        (pltpu.make_async_copy(wt, tb, loc.at[0]), pltpu.make_async_copy(tb, g1.at[h, 0], loc.at[5])),
        (
            pltpu.make_async_copy(wo.at[2 * h + c], ob, loc.at[1]),
            pltpu.make_async_copy(ob, oz.at[zed], loc.at[6]),
        ),
    ]
    local_same = [
        (pltpu.make_async_copy(x, xs, loc.at[2]), pltpu.make_async_copy(xs, xa.at[p], loc.at[7])),
        (pltpu.make_async_copy(w, wb, loc.at[3]), pltpu.make_async_copy(wb, ws, loc.at[8])),
        (pltpu.make_async_copy(sg, sb, loc.at[4]), pltpu.make_async_copy(sb, so, loc.at[9])),
    ]

    @pl.when(other)
    def _():
        send_sg().start()
        send_w().start()
        for k in range(chunks):
            swap_x(k).start()

    @pl.when(same)
    def _():
        for k in range(chunks):
            for dq in range(1, nh):
                push_peer(x.at[part(k)], k, dq).start()
            push_mate(x.at[part(k)], k, 0).start()
        for get, _ in local_same:
            get.start()

    for dq in range(1, nh):
        shard_peer(dq).start()
    for dh in range(1, hi_n):
        shard_hi(wt, dh, 0).start()
    for dz in range(1, n):
        rows_z(dz).start()
    shard_cross().start()
    for get, _ in local:
        get.start()

    @pl.when(other)
    def _():
        send_w().wait_recv()
        for dh in range(1, hi_n):
            spread_w(dh).start()

    for dq in range(1, nh):
        remote(wt, g1.at[h, (nh - dq) % nh], gp_s.at[dq], gp_r.at[dq], mate).wait_recv()
        t = (nh - dq) % nh
        for dh in range(1, hi_n):
            shard_hi(g1.at[h, t], dh, t).start()

    @pl.when(other)
    def _():
        for k in range(chunks):
            own_arrives(k).wait_recv()
            for dq in range(1, nh):
                push_peer(xa.at[p, part(k)], k, dq).start()
            push_mate(xa.at[p, part(k)], k, 0).start()

    for get, put in local:
        get.wait()
        put.start()

    @pl.when(same)
    def _():
        for get, put in local_same:
            get.wait()
            put.start()

    for k in range(chunks):
        for dq in range(1, nh):
            block = c * nh + (q + nh - dq) % nh
            remote(
                x.at[part(k)], xa.at[block, part(k)], peer_s.at[dq, k], peer_r.at[dq, k], mate
            ).wait_recv()
            push_mate(xa.at[block, part(k)], k, dq).start()

    for k in range(chunks):
        for dq in range(nh):
            block = (1 - c) * nh + (q + nh - dq) % nh
            remote(
                x.at[part(k)], xa.at[block, part(k)], core_s.at[dq, k], core_r.at[dq, k], mate
            ).wait_recv()

    @pl.when(other)
    def _():
        send_sg().wait_recv()
        for dh in range(1, hi_n):
            source = from_hi(dh)
            remote(ws.at[source], ws.at[source], wh_s.at[dh], wh_r.at[dh], mate).wait_recv()
        send_sg().wait_send()
        send_w().wait_send()
        for dh in range(1, hi_n):
            spread_w(dh).wait_send()
        for k in range(chunks):
            swap_x(k).wait_send()

    for k in range(chunks):
        for dq in range(1, nh):
            push_peer(x.at[part(k)], k, dq).wait_send()
        for dq in range(nh):
            push_mate(x.at[part(k)], k, dq).wait_send()

    @pl.when(same)
    def _():
        for _, put in local_same:
            put.wait()

    for dq in range(1, nh):
        shard_peer(dq).wait_send()
    for dz in range(1, n):
        z = (zed + n - dz) % n
        remote(wo.at[0], oz.at[z], oz_s.at[dz], oz_r.at[dz], mate).wait_recv()
        rows_z(dz).wait_send()
    for t in range(nh):
        for dh in range(1, hi_n):
            shard_hi(wt, dh, t).wait_send()
            remote(wt, g1.at[from_hi(dh), t], gh_s.at[dh, t], gh_r.at[dh, t], mate).wait_recv()
    shard_cross().wait_recv()
    shard_cross().wait_send()
    for _, put in local:
        put.wait()


def exchange_inputs(sizes, x, w, sg, wt, wo):
    hi_n, _, _, nh = sizes
    n = 2 * nh
    tok, width = x.shape
    chunks = 4 if tok % 64 == 0 else 1
    return pl.pallas_call(
        functools.partial(exchange_kernel, sizes, chunks),
        out_shape=(
            jax.ShapeDtypeStruct((n, tok, width), BF),
            jax.ShapeDtypeStruct(w.shape, BF),
            jax.ShapeDtypeStruct(sg.shape, F32),
            jax.ShapeDtypeStruct((hi_n, nh) + wt.shape, BF),
            jax.ShapeDtypeStruct(wt.shape, BF),
            jax.ShapeDtypeStruct((n,) + wo.shape[1:], BF),
        ),
        in_specs=[ANY] * 5,
        out_specs=(ANY,) * 6,
        scratch_shapes=[
            pltpu.VMEM((tok, width), BF),
            pltpu.VMEM(w.shape, BF),
            pltpu.VMEM(sg.shape, F32),
            pltpu.VMEM(wt.shape, BF),
            pltpu.VMEM(wo.shape[1:], BF),
            DMA((chunks,)), DMA((chunks,)),
            DMA((nh, chunks)), DMA((nh, chunks)),
            DMA((nh, chunks)), DMA((nh, chunks)),
            DMA, DMA,
            DMA((hi_n,)), DMA((hi_n,)),
            DMA, DMA,
            DMA((10,)),
            DMA((n,)), DMA((n,)),
            DMA((nh,)), DMA((nh,)),
            DMA((hi_n, nh)), DMA((hi_n, nh)),
            DMA, DMA,
        ],
        name="exchange_inputs",
        compiler_params=pltpu.CompilerParams(collective_id=1, has_side_effects=True),
        cost_estimate=pl.CostEstimate(flops=0, bytes_accessed=160 << 20, transcendentals=0),
    )(x, w, sg, wt, wo)


def masked(scores, diagonal, crossing, causal, bias):
    if diagonal:
        return jnp.where(causal, scores, -1e30)
    if crossing:
        return scores + bias
    return scores


def forward_kernel(
    sizes, block, v, gout, cross, oz, xa, ws, g1, lo_c, lo_s, hi_c, hi_s, seg,
    ai, dy_in, g2, late, oh, qo, ko, mo, ao, lse, own, vsq,
    va, own_rows, tb, ob,
    att_s, att_r, loc, v_s, v_r, dy_s, dy_r, gp_s, gp_r, gh_s, gh_r, oh_s, oh_r, lc,
):
    hi_n, _, _, nh = sizes
    n = 2 * nh
    h, c, r, q = coords()
    p = c * nh + q
    row_len, sw = qo.shape
    tok = row_len // n
    short = row_len // 2
    pw = lo_c.shape[1]
    pairs = sw // pw
    halves = pw // HEAD_DIM
    mate = (h, 1 - c, r, q)
    other = c != r
    greet_plane(sizes, True)

    def send_v(s, pair):
        lanes = lane_window(pair, pw, sw)
        to = (h, s // nh, c, s % nh)
        spot = r * nh + q
        return remote(
            columns_of(v, s, pair * pw, pw, sw), va.at[spot, :, lanes],
            v_s.at[pair, s], v_r.at[pair, spot], to,
        )

    def v_arrives(b, pair):
        lanes = lane_window(pair, pw, sw)
        return remote(
            columns_of(v, 0, 0, pw, sw), va.at[b, :, lanes], v_s.at[pair, b], v_r.at[pair, b], mate
        )

    def send_dy():
        return remote(gout, dy_in, dy_s, dy_r, (h, r, c, q))

    def shard_hi(dh):
        to = ((h + dh) % hi_n, c, r, q)
        return remote(cross, g2.at[h], gh_s.at[dh], gh_r.at[dh], to)

    def late_peer(dq):
        to = (h, c, r, (q + dq) % nh)
        return remote(cross, late.at[nh - dq - 1], gp_s.at[dq], gp_r.at[dq], to)

    def rows_hi(dh):
        to = ((h + dh) % hi_n, c, r, q)
        return remote(oz, oh.at[h], oh_s.at[dh], oh_r.at[dh], to)

    def from_hi(dh):
        return (h + hi_n - dh) % hi_n

    keep_v = pltpu.make_async_copy(columns_of(v, p, 0, sw, sw), va.at[p], lc.at[0])
    local = [
        (pltpu.make_async_copy(cross, tb, lc.at[1]), pltpu.make_async_copy(tb, g2.at[h], lc.at[3])),
        (pltpu.make_async_copy(oz, ob, lc.at[2]), pltpu.make_async_copy(ob, oh.at[h], lc.at[4])),
    ]
    for pair in range(pairs):
        for s in range(n):
            @pl.when(jnp.logical_or(other, p != s))
            def _():
                send_v(s, pair).start()

    @pl.when(c == r)
    def _():
        keep_v.start()

    for dh in range(1, hi_n):
        shard_hi(dh).start()
    for dh in range(1, hi_n):
        rows_hi(dh).start()
    for dq in range(1, nh):
        late_peer(dq).start()

    @pl.when(other)
    def _():
        send_dy().start()

    for get, _ in local:
        get.start()

    br = 256
    own[...] = jnp.zeros_like(own)
    flag = seg[0:1, 0:1]

    def project(i, carry):
        rows = pl.ds(pl.multiple_of(i * br, br), br)
        xf = xa[rows, :].astype(F32)
        inv = lax.rsqrt(jnp.mean(xf * xf, axis=-1, keepdims=True) + EPSILON)
        normed = (xf * inv * g1[...]).astype(BF)
        raw = nt(normed, ws[...])
        first = first_lanes(br, sw)
        ct, st = rope_rows(lo_c, lo_s, hi_c, hi_s, flag, i, br)
        ct, st = tiled(ct, sw), tiled(st, sw)
        q_raw = raw[:, :sw]
        k_raw = raw[:, sw : 2 * sw]
        own_vals = raw[:, 2 * sw :]
        q_rot = (q_raw * ct + rotate_lanes(q_raw, first) * st).astype(BF)
        qo[rows, :] = (q_rot.astype(F32) * HEAD_DIM**-0.5).astype(BF)
        ko[rows, :] = (k_raw * ct + rotate_lanes(k_raw, first) * st).astype(BF)
        own_rows[rows, :] = own_vals
        own[...] += jnp.sum((own_vals * own_vals).reshape(br // 8, 8, sw), axis=0)
        return carry

    lax.fori_loop(0, row_len // br, project, 0)

    for get, put in local:
        get.wait()
        put.start()
    @pl.when(c == r)
    def _():
        keep_v.wait()

    bias = flag * -1e30
    blocks = row_len // block
    per = block // tok
    causal = lax.broadcasted_iota(jnp.int32, (block, block), 0) >= lax.broadcasted_iota(
        jnp.int32, (block, block), 1
    )

    def send(b, pair):
        lanes = lane_window(pair, pw, sw)
        to = (h, b // nh, r, b % nh)
        return remote(
            ao.at[b, :, lanes], ai.at[p, :, lanes], att_s.at[pair, b], att_r.at[pair, p], to
        )

    def keep(pair):
        lanes = lane_window(pair, pw, sw)
        return pltpu.make_async_copy(ao.at[p, :, lanes], ai.at[p, :, lanes], loc.at[pair])

    def pair_step(pair, carry):
        lanes = lane_window(pair, pw, sw)
        for b in range(n):
            @pl.when(jnp.logical_or(other, p != b))
            def _():
                v_arrives(b, pair).wait_recv()

        sums = 0.0
        for b in range(n):
            rows = pl.ds(b * tok, tok)
            values = va[b, :, lanes].astype(F32)
            sums = sums + jnp.sum((values * values).reshape(tok // 8, 8, pw), axis=0)
            mo[rows, lanes] = (0.5 * own_rows[rows, lanes] + 0.5 * values).astype(BF)
        vsq[:, lanes] = sums
        for i in range(blocks):
            outs = []
            rows = pl.ds(i * block, block)
            for half in range(halves):
                cols = slice(half * HEAD_DIM, (half + 1) * HEAD_DIM)
                qh = qo[rows, lanes][:, cols]
                score = []
                for j in range(i + 1):
                    kj = ko[pl.ds(j * block, block), lanes][:, cols]
                    crossing = i * block >= short and j * block < short
                    score.append(masked(nt(qh, kj), i == j, crossing, causal, bias))
                top = functools.reduce(
                    jnp.maximum, [jnp.max(s, axis=-1, keepdims=True) for s in score]
                )
                total = 0.0
                acc = 0.0
                for j in range(i + 1):
                    e = jnp.exp(score[j] - top)
                    total = total + jnp.sum(e, axis=-1, keepdims=True)
                    vj = mo[pl.ds(j * block, block), lanes][:, cols]
                    acc = acc + nn(e.astype(BF), vj)
                outs.append(acc / total)
                lse[pair, rows, half : half + 1] = top + jnp.log(total)
            out = (jnp.concatenate(outs, axis=1) if halves > 1 else outs[0]).astype(BF)
            for t in range(per):
                b = i * per + t
                ao[b, :, lanes] = out[t * tok : (t + 1) * tok]

                @pl.when(p != b)
                def _():
                    send(b, pair).start()

        keep(pair).start()
        return carry

    lax.fori_loop(0, pairs, pair_step, 0)

    def drain(pair, carry):
        lanes = lane_window(pair, pw, sw)
        for b in range(n):
            @pl.when(p != b)
            def _():
                send(b, pair).wait_send()
                remote(
                    ao.at[b, :, lanes], ai.at[b, :, lanes], att_s.at[pair, b], att_r.at[pair, b],
                    (h, 1 - c, r, q),
                ).wait_recv()
        keep(pair).wait()
        return carry

    lax.fori_loop(0, pairs, drain, 0)

    for pair in range(pairs):
        for s in range(n):
            @pl.when(jnp.logical_or(other, p != s))
            def _():
                send_v(s, pair).wait_send()

    for dh in range(1, hi_n):
        rows_hi(dh).wait_send()
        remote(oz, oh.at[from_hi(dh)], oh_s.at[dh], oh_r.at[dh], mate).wait_recv()
        shard_hi(dh).wait_send()
        remote(cross, g2.at[from_hi(dh)], gh_s.at[dh], gh_r.at[dh], mate).wait_recv()
    for dq in range(1, nh):
        late_peer(dq).wait_send()
        late_peer(dq).wait_recv()

    @pl.when(other)
    def _():
        send_dy().wait_send()
        send_dy().wait_recv()

    for _, put in local:
        put.wait()


def attention_forward(sizes, v, gout, cross, oz, xa, ws, g1, tables, seg):
    hi_n, _, _, nh = sizes
    n = 2 * nh
    row_len, width = xa.shape
    sw = ws.shape[0] // 3
    tok = row_len // n
    pw = tables[0].shape[1]
    pairs = sw // pw
    block = max(tok, 512)
    flops = 2 * row_len * width * 3 * sw + 2 * row_len * row_len * sw
    return pl.pallas_call(
        functools.partial(forward_kernel, sizes, block),
        out_shape=(
            jax.ShapeDtypeStruct((n, tok, sw), BF),
            jax.ShapeDtypeStruct((tok, width), BF),
            jax.ShapeDtypeStruct((hi_n,) + cross.shape, BF),
            jax.ShapeDtypeStruct((max(nh - 1, 1),) + cross.shape, BF),
            jax.ShapeDtypeStruct((hi_n,) + oz.shape, BF),
            jax.ShapeDtypeStruct((row_len, sw), BF),
            jax.ShapeDtypeStruct((row_len, sw), BF),
            jax.ShapeDtypeStruct((row_len, sw), BF),
            jax.ShapeDtypeStruct((n, tok, sw), BF),
            jax.ShapeDtypeStruct((pairs, row_len, pw // HEAD_DIM), F32),
            jax.ShapeDtypeStruct((8, sw), F32),
            jax.ShapeDtypeStruct((8, sw), F32),
        ),
        in_specs=[ANY] * 4 + [VM] * 8,
        out_specs=(ANY,) * 5 + (VM,) * 7,
        scratch_shapes=[
            pltpu.VMEM((n, tok, sw), BF),
            pltpu.VMEM((row_len, sw), F32),
            pltpu.VMEM(cross.shape, BF),
            pltpu.VMEM(oz.shape, BF),
            DMA((pairs, n)), DMA((pairs, n)), DMA((pairs,)),
            DMA((pairs, n)), DMA((pairs, n)),
            DMA, DMA,
            DMA((nh,)), DMA((nh,)),
            DMA((hi_n,)), DMA((hi_n,)),
            DMA((hi_n,)), DMA((hi_n,)),
            DMA((5,)),
        ],
        name="attention_forward",
        compiler_params=pltpu.CompilerParams(
            collective_id=2, has_side_effects=True, vmem_limit_bytes=VMEM_MAX
        ),
        cost_estimate=pl.CostEstimate(
            flops=4 * flops, bytes_accessed=16 << 20, transcendentals=row_len * row_len * sw // 128
        ),
    )(v, gout, cross, oz, xa, ws, g1, *tables, seg)


def mlp_kernel(
    xa, gout, dy_in, near, far, lp, oh, ai, g2, lo, gh, ga, dsum, dosum, gg2, theirs, late, rx0,
    x, dy, hid, n2, acc_o, acc_g, buf, rcv, bo, rcvo, wm, wo, oa, ob, first,
    x_s, buf_s, buf_r, bo_s, bo_r, ld, th_s, th_r, o_s, o_r, gh_s, gh_r, fi_s, fi_r,
):
    step = pl.program_id(0)
    n = ai.shape[0]
    nh = n // 2
    hi_n = wm.shape[2]
    wide = 2 * hi_n
    width = x.shape[1]
    dw = width // wide
    rw = bo.shape[3]
    h, c, r, q = coords()
    own_dy = pltpu.make_async_copy(gout, dy, ld.at[4])
    swapped_dy = pltpu.make_async_copy(dy_in, dy, ld.at[4])
    own_o = pltpu.make_async_copy(oh, oa, ld.at[5])

    mate = (h, 1 - c, r, q)

    def block_of(t):
        return near.at[:, t] if t < nh else far

    def give(t):
        return remote(block_of(t), theirs.at[t], th_s.at[t, 0], th_r.at[t, 0], mate)

    def late_hi(t, dh):
        to = ((h + dh) % hi_n, c, r, q)
        u = t - nh - 1
        return remote(lp.at[u], late.at[h, u], gh_s.at[u, dh], gh_r.at[u, dh], to)

    def late_piece(t, dh):
        return late.at[(h + hi_n - dh) % hi_n, t - nh - 1] if dh else lp.at[t - nh - 1]

    def late_arrives(t, dh):
        u = t - nh - 1
        return remote(lp.at[u], late_piece(t, dh), gh_s.at[u, dh], gh_r.at[u, dh], mate)

    def give_late(t, dh):
        source = (h + hi_n - dh) % hi_n
        return remote(
            late_piece(t, dh), theirs.at[t, source], th_s.at[t, dh], th_r.at[t, dh], mate
        )

    def load_late(t, dh):
        source = (h + hi_n - dh) % hi_n
        return pltpu.make_async_copy(late_piece(t, dh), wm.at[t % 2, c, source], ld.at[t % 2])

    def first_over_hi(dh):
        to = (h + dh) % hi_n
        return remote(first.at[to], rx0.at[dh - 1], fi_s.at[dh], fi_r.at[dh], (to, c, r, q))

    def give_o():
        return remote(oh, ob, o_s, o_r, (h, 1 - c, r, q))

    def load_own(src, at):
        return pltpu.make_async_copy(src, wm.at[at, c], ld.at[at])

    def load_theirs(t, at):
        return pltpu.make_async_copy(theirs.at[t], wm.at[at, 1 - c], ld.at[2 + at])
    own_x = pltpu.make_async_copy(xa.at[c * (n // 2) + q], x, x_s)
    slot = step % 2
    last = n - 1

    def to_mate(at):
        return remote(buf.at[at, 1 - c], rcv.at[at], buf_s.at[at], buf_r.at[at], mate)

    def out_to_mate():
        return remote(bo.at[1 - c], rcvo, bo_s, bo_r, mate)

    @pl.when(step == 0)
    def _():
        own_x.start()
        own_o.start()
        load_own(near.at[:, 0], 0).start()

        @pl.when(c == r)
        def _():
            own_dy.start()

        @pl.when(c != r)
        def _():
            swapped_dy.start()

        barrier = pltpu.get_barrier_semaphore()
        friends = [mate]
        friends += [((h + dh) % hi_n, c, r, q) for dh in range(1, hi_n)]
        for to in friends:
            pl.semaphore_signal(barrier, inc=1, device_id=to, device_id_type=MESH)
        pl.semaphore_wait(barrier, len(friends))
        for t in range(nh + 1, n):
            for dh in range(1, hi_n):
                late_hi(t, dh).start()
        give_o().start()
        for t in range(nh + 1):
            give(t).start()
        for t in range(nh + 1, n):
            give_late(t, 0).start()
        own_x.wait()
        own_o.wait()
        own_dy.wait()
        give_o().wait_recv()
        for s in range(n):
            for w in range(wide):
                wo[s, w * rw : (w + 1) * rw] = jnp.where(c == w % 2, oa[w // 2, s], ob[w // 2, s])
        give(0).wait_recv()
        load_theirs(0, 0).start()
        hid[...] = x[...].astype(F32)

        def project(s, carry):
            hid[...] += nn(ai[s], wo[s])
            return carry

        lax.fori_loop(0, n, project, 0)
        total = hid[...]
        inv = lax.rsqrt(jnp.mean(total * total, axis=-1, keepdims=True) + EPSILON)
        n2[...] = (total * inv * g2[...]).astype(BF)
        acc_o[...] = jnp.zeros_like(acc_o)
        acc_g[...] = jnp.zeros_like(acc_g)

    @pl.when(step < n)
    def _():
        @pl.when(step > 1)
        def _():
            to_mate(slot).wait_send()

        load_own(near.at[:, 0], slot).wait()
        load_theirs(0, slot).wait()

        def weight(j):
            return jnp.concatenate([wm[slot, w % 2, w // 2, j] for w in range(wide)], axis=1)

        def put(j, grad):
            low = grad.astype(BF)
            for w in range(wide):
                buf[slot, w % 2, w // 2, j] = low[:, w * dw : (w + 1) * dw]

        gate = nt(n2[...], weight(0))
        up = nt(n2[...], weight(1))
        sig = jax.nn.sigmoid(gate)
        silu = gate * sig
        inner = (silu * up).astype(BF)
        grad_inner = nt(dy[...], weight(2))
        for t in range(1, nh + 1):
            @pl.when(step == t - 1)
            def _():
                load_own(block_of(t), t % 2).start()
                give(t).wait_recv()
                load_theirs(t, t % 2).start()

        for t in range(nh + 1, n):
            @pl.when(step == t - 1)
            def _():
                load_late(t, 0).start()
                for dh in range(1, hi_n):
                    late_arrives(t, dh).wait_recv()
                    give_late(t, dh).start()
                    load_late(t, dh).start()

        grad_gate = (grad_inner * up * sig * (1.0 + gate * (1.0 - sig))).astype(BF)
        grad_up = (grad_inner * silu).astype(BF)
        acc_o[...] += nn(inner, weight(2))
        acc_g[...] += nn(grad_gate, weight(0)) + nn(grad_up, weight(1))
        put(0, tn(grad_gate, n2[...]))
        put(1, tn(grad_up, n2[...]))
        put(2, tn(inner, dy[...]))

    @pl.when(step == last)
    def _():
        hidden = hid[...]
        lo[...] = (hidden + acc_o[...]).astype(BF)
        inv = lax.rsqrt(jnp.mean(hidden * hidden, axis=-1, keepdims=True) + EPSILON)
        grad_n = acc_g[...]
        gg2[...] = jnp.sum((grad_n * hidden * inv).reshape(-1, 8, width), axis=0)
        scaled = grad_n * g2[...]
        dot = jnp.sum(scaled * hidden, axis=-1, keepdims=True)
        grad_h = dy[...].astype(F32) + scaled * inv - hidden * (inv * inv * inv * dot / width)
        gh[...] = grad_h
        low = grad_h.astype(BF)

        def project_back(s, carry):
            ga[s] = nt(low, wo[s]).astype(BF)
            grad_wo = tn(ai[s], low).astype(BF)
            for w in range(wide):
                bo[w % 2, w // 2, s] = grad_wo[w * rw : (w + 1) * rw]
            return carry

        lax.fori_loop(0, n, project_back, 0)

    @pl.when(step > 0)
    def _():
        before = (step + 1) % 2
        to_mate(before).wait_recv()
        for a in range(hi_n):
            for j in range(3):
                total = buf[before, c, a, j].astype(F32) + rcv[before, a, j].astype(F32)
                dsum[a, 0, j] = total.astype(BF)

    @pl.when(step == 1)
    def _():
        first[...] = dsum[:, 0]
        for dh in range(1, hi_n):
            first_over_hi(dh).start()

    for t in range(nh + 1, n):
        @pl.when(step == t - 1)
        def _():
            for dh in range(hi_n):
                give_late(t, dh).wait_recv()
            load_theirs(t, t % 2).start()

    @pl.when(step < n)
    def _():
        to_mate(slot).start()

    @pl.when(step == last)
    def _():
        out_to_mate().start()

    @pl.when(step == n)
    def _():
        out_to_mate().wait_recv()
        for a in range(hi_n):
            for s in range(n):
                total = bo[c, a, s].astype(F32) + rcvo[a, s].astype(F32)
                dosum[a, s] = total.astype(BF)
        out_to_mate().wait_send()
        to_mate(0).wait_send()
        to_mate(1).wait_send()
        give_o().wait_send()
        for dh in range(1, hi_n):
            first_over_hi(dh).wait_send()
            first_over_hi(dh).wait_recv()
        for t in range(nh + 1):
            give(t).wait_send()
        for t in range(nh + 1, n):
            for dh in range(hi_n):
                give_late(t, dh).wait_send()
            for dh in range(1, hi_n):
                late_hi(t, dh).wait_send()


def feed_forward(xa, gout, dy_in, near, far, lp, oh, ai, g2):
    n, tok, sw = ai.shape
    nh = n // 2
    width = gout.shape[1]
    hi_n, _, _, ffs, dw = near.shape
    wide = 2 * hi_n
    rw = sw // wide

    def whole(*shape):
        return pl.BlockSpec(shape, lambda i: (0,) * len(shape))

    def fixed(*shape):
        return pl.BlockSpec(
            shape, lambda i: (0,) * len(shape), pipeline_mode=pl.Buffered(1)
        )

    return pl.pallas_call(
        mlp_kernel,
        out_shape=(
            jax.ShapeDtypeStruct((tok, width), BF),
            jax.ShapeDtypeStruct((tok, width), F32),
            jax.ShapeDtypeStruct((n, tok, sw), BF),
            jax.ShapeDtypeStruct((hi_n, n, 3, ffs, dw), BF),
            jax.ShapeDtypeStruct((hi_n, n, rw, width), BF),
            jax.ShapeDtypeStruct((8, width), F32),
            jax.ShapeDtypeStruct((n, hi_n, 3, ffs, dw), BF),
            jax.ShapeDtypeStruct((hi_n, max(nh - 1, 1), 3, ffs, dw), BF),
            jax.ShapeDtypeStruct((max(hi_n - 1, 1), 3, ffs, dw), BF),
        ),
        grid_spec=pl.GridSpec(
            grid=(n + 1,),
            in_specs=[ANY] * 7 + [fixed(n, tok, sw), fixed(1, width)],
            out_specs=(
                whole(tok, width),
                whole(tok, width),
                whole(n, tok, sw),
                pl.BlockSpec(
                    (hi_n, 1, 3, ffs, dw), lambda i: (0, jnp.maximum(i - 1, 0), 0, 0, 0)
                ),
                whole(hi_n, n, rw, width),
                whole(8, width),
                ANY,
                ANY,
                ANY,
            ),
            scratch_shapes=[
                pltpu.VMEM((tok, width), BF),
                pltpu.VMEM((tok, width), BF),
                pltpu.VMEM((tok, width), F32),
                pltpu.VMEM((tok, width), BF),
                pltpu.VMEM((tok, width), F32),
                pltpu.VMEM((tok, width), F32),
                pltpu.VMEM((2, 2, hi_n, 3, ffs, dw), BF),
                pltpu.VMEM((2, hi_n, 3, ffs, dw), BF),
                pltpu.VMEM((2, hi_n, n, rw, width), BF),
                pltpu.VMEM((hi_n, n, rw, width), BF),
                pltpu.VMEM((2, 2, hi_n, 3, ffs, dw), BF),
                pltpu.VMEM((n, sw, width), BF),
                pltpu.VMEM((hi_n, n, rw, width), BF),
                pltpu.VMEM((hi_n, n, rw, width), BF),
                pltpu.VMEM((hi_n, 3, ffs, dw), BF),
                DMA, DMA((2,)), DMA((2,)), DMA, DMA,
                DMA((6,)), DMA((n, hi_n)), DMA((n, hi_n)), DMA, DMA,
                DMA((max(nh - 1, 1), hi_n)), DMA((max(nh - 1, 1), hi_n)),
                DMA((hi_n,)), DMA((hi_n,)),
            ],
        ),
        name="feed_forward",
        compiler_params=pltpu.CompilerParams(
            dimension_semantics=("arbitrary",),
            collective_id=4,
            has_side_effects=True,
            vmem_limit_bytes=VMEM_MAX,
        ),
        cost_estimate=pl.CostEstimate(
            flops=18 * tok * width * ffs * n, bytes_accessed=40 << 20, transcendentals=tok * ffs * n
        ),
    )(xa, gout, dy_in, near, far, lp, oh, ai, g2)


def backward_kernel(
    sizes, block, ga, ds, dos, lo, rx0, xa, ws, g1, lo_c, lo_s, hi_c, hi_s, seg, qi, ki, mi, ao, lse, gh,
    gg2, squares, values_sq,
    gv, gi, fin, og, total_small, lo_in, rx, rxo, zr,
    do, normed, dq, dk, dv, dcat, gow, gnp, rcv, rcv2, gis, part, zs, zos, do_part, rf,
    dwq, gg1, zo, sm, s1, s2, r1, r2, own, mine,
    do_s, do_r, gv_s, gv_r, co_s, co_r, pe_s, pe_r, gi_s, gi_r, loc,
    rx_s, rx_r, rxo_s, rxo_r, ly_s, ly_r, ld, z_s, z_r, zo_s, zo_r,
    a_s, a_r, b_s, b_r, c_s, c_r, d_s, d_r, e_s, e_r, f_s, f_r, m_s, m_r,
):
    hi_n, _, _, nh = sizes
    n = 2 * nh
    h, c, r, q = coords()
    p = c * nh + q
    row_len, sw = qi.shape
    width = xa.shape[1]
    tok = row_len // n
    short = row_len // 2
    pw = lo_c.shape[1]
    pairs = sw // pw
    halves = pw // HEAD_DIM
    same = c == r
    mate = (h, 1 - c, r, q)
    swap_to = (h, r, c, q)
    zed = r * nh + q
    greet_plane(sizes, True, 2)

    order = list(range(nh + 1, n)) + [nh] + list(range(1, nh)) + [0]

    def over_hi(dh, i):
        to = (h + dh) % hi_n
        return remote(
            ds.at[to, i], rx.at[dh - 1, i], rx_s.at[dh, i], rx_r.at[dh, i], (to, c, r, q)
        )

    def out_over_hi(dh):
        to = (h + dh) % hi_n
        return remote(dos.at[to], rxo.at[dh - 1], rxo_s.at[dh], rxo_r.at[dh], (to, c, r, q))

    def send_lo():
        return remote(lo, lo_in, ly_s, ly_r, swap_to)

    def over_z(t):
        if t > nh:
            return remote(zs.at[t], rf.at[t - nh - 1], z_s.at[t], z_r.at[t], (h, c, r, (q + t) % nh))
        to = (h, c, 1 - r, q) if t == nh else (h, c, r, (q + t) % nh)
        return remote(zs.at[t], zr.at[t], z_s.at[t], z_r.at[t], to)

    def out_over_z(i):
        return remote(zos.at[i], zo.at[zed], zo_s.at[i], zo_r.at[zed], (h, c, i // nh, i % nh))

    def keep_z():
        return pltpu.make_async_copy(zs.at[0], zr.at[0], z_s.at[0])

    def keep_out_z(i):
        return pltpu.make_async_copy(zos.at[i], zo.at[i], zo_s.at[i])

    def load_chunk(i):
        copies = [pltpu.make_async_copy(ds.at[h, i], part.at[0], ld.at[0])]
        for dh in range(1, hi_n):
            source = rx.at[dh - 1, i] if i else rx0.at[dh - 1]
            copies.append(pltpu.make_async_copy(source, part.at[dh], ld.at[dh]))
        return copies

    def reduce_chunk(i):
        if i:
            for dh in range(1, hi_n):
                over_hi(dh, i).wait_recv()
        for copy in load_chunk(i):
            copy.start()
        if i == nh:
            for t in range(nh + 1, n):
                over_z(t).wait_recv()
        for copy in load_chunk(i):
            copy.wait()

        def add(j, carry):
            total = part[0, j].astype(F32)
            for dh in range(1, hi_n):
                total = total + part[dh, j].astype(F32)
            if i == nh:
                for t in range(nh - 1):
                    total = total + rf[t, j].astype(F32)
            zs[i, j] = total.astype(BF)
            return carry

        lax.fori_loop(0, 3, add, 0)
        if i:
            over_z(i).start()
        else:
            keep_z().start()

    own_out = pltpu.make_async_copy(dos.at[h], zos, ld.at[0])

    def reduce_out():
        own_out.start()
        own_out.wait()
        for dh in range(1, hi_n):
            out_over_hi(dh).wait_recv()
            copy = pltpu.make_async_copy(rxo.at[dh - 1], do_part, ld.at[dh])
            copy.start()
            copy.wait()
            zos[...] = (zos[...].astype(F32) + do_part[...].astype(F32)).astype(BF)
        for i in range(n):
            @pl.when(zed != i)
            def _():
                out_over_z(i).start()

            @pl.when(zed == i)
            def _():
                keep_out_z(i).start()

    def send_do(s, pair):
        lanes = lane_window(pair, pw, sw)
        to = (h, s // nh, r, s % nh)
        return remote(
            ga.at[s, :, lanes], do.at[p, :, lanes], do_s.at[pair, s], do_r.at[pair, p], to
        )

    def do_arrives(s, pair):
        lanes = lane_window(pair, pw, sw)
        return remote(
            ga.at[s, :, lanes], do.at[s, :, lanes], do_s.at[pair, s], do_r.at[pair, s], mate
        )

    keep_do = pltpu.make_async_copy(ga.at[p], do.at[p], loc.at[0])
    for pair in range(pairs):
        for s in range(n):
            @pl.when(p != s)
            def _():
                send_do(s, pair).start()

    keep_do.start()
    for dh in range(1, hi_n):
        out_over_hi(dh).start()
    for i in order[:-1]:
        for dh in range(1, hi_n):
            over_hi(dh, i).start()

    @pl.when(c != r)
    def _():
        send_lo().start()

    br = 256

    def norm(i, carry):
        rows = pl.ds(pl.multiple_of(i * br, br), br)
        xf = xa[rows, :].astype(F32)
        inv = lax.rsqrt(jnp.mean(xf * xf, axis=-1, keepdims=True) + EPSILON)
        normed[rows, :] = (xf * inv * g1[...]).astype(BF)
        return carry

    lax.fori_loop(0, row_len // br, norm, 0)
    keep_do.wait()

    flag = seg[0:1, 0:1]
    bias = flag * -1e30
    blocks = row_len // block
    per = block // tok
    causal = lax.broadcasted_iota(jnp.int32, (block, block), 0) >= lax.broadcasted_iota(
        jnp.int32, (block, block), 1
    )

    def gv_at(s, pair):
        if len(gv.shape) == 3:
            return gv.at[s]
        return gv.at[:, pl.ds(pl.multiple_of(s * sw + pair * pw, pw), pw)]

    def send_gv(b, pair):
        lanes = lane_window(pair, pw, sw)
        to = (h, r, b // nh, b % nh)
        return remote(
            gow.at[b, :, lanes], gv_at(p, pair), gv_s.at[pair, b], gv_r.at[pair, p], to
        )

    def keep_gv(pair):
        lanes = lane_window(pair, pw, sw)
        return pltpu.make_async_copy(gow.at[p, :, lanes], gv_at(p, pair), loc.at[1 + pair])

    def early(pair, i):
        if pairs < 2 or blocks < 4:
            return 0

        @pl.when(pair == 0)
        def _():
            if i == blocks - 2:
                reduce_out()
                reduce_chunk(order[0])

        @pl.when(pair == 1)
        def _():
            if i == 1:
                reduce_chunk(order[1])

        return 2

    def pair_step(pair, carry):
        for s in range(n):
            @pl.when(p != s)
            def _():
                do_arrives(s, pair).wait_recv()

        lanes = lane_window(pair, pw, sw)
        dk[...] = jnp.zeros_like(dk)
        dv[...] = jnp.zeros_like(dv)
        for i in range(blocks):
            rows = pl.ds(i * block, block)
            pieces = [[] for _ in range(i + 1)]
            dq_parts = []
            do_rows = [do[i * per + t, :, lanes] for t in range(per)]
            do_i = do_rows[0] if per == 1 else jnp.concatenate(do_rows, axis=0)
            ao_rows = [ao[i * per + t, :, lanes] for t in range(per)]
            ao_i = ao_rows[0] if per == 1 else jnp.concatenate(ao_rows, axis=0)
            product = do_i.astype(F32) * ao_i.astype(F32)
            for half in range(halves):
                cols = slice(half * HEAD_DIM, (half + 1) * HEAD_DIM)
                qh = qi[rows, lanes][:, cols]
                doh = do_i[:, cols]
                delta = jnp.sum(product[:, cols], axis=-1, keepdims=True)
                level = lse[pair, rows, half : half + 1]
                acc = 0.0
                for j in range(i + 1):
                    kj = ki[pl.ds(j * block, block), lanes][:, cols]
                    vj = mi[pl.ds(j * block, block), lanes][:, cols]
                    crossing = i * block >= short and j * block < short
                    score = masked(nt(qh, kj), i == j, crossing, causal, bias)
                    prob = jnp.exp(score - level)
                    grad_prob = nt(doh, vj)
                    grad_score = (prob * (grad_prob - delta)).astype(BF)
                    acc = acc + nn(grad_score, kj)
                    pieces[j].append((tn(grad_score, qh), tn(prob.astype(BF), doh)))
                dq_parts.append(acc * HEAD_DIM**-0.5)
            dq[rows, :] = dq_parts[0] if halves == 1 else jnp.concatenate(dq_parts, axis=1)
            for j in range(i + 1):
                at = pl.ds(j * block, block)
                if halves == 1:
                    dk[at, :] += pieces[j][0][0]
                    dv[at, :] += pieces[j][0][1]
                else:
                    dk[at, :] += jnp.concatenate([t[0] for t in pieces[j]], axis=1)
                    dv[at, :] += jnp.concatenate([t[1] for t in pieces[j]], axis=1)
            early(pair, i)
        first = first_lanes(br, pw)

        def finish(i, inner_carry):
            rows = pl.ds(pl.multiple_of(i * br, br), br)
            ct, st = rope_rows(lo_c, lo_s, hi_c, hi_s, flag, i, br)
            a = dq[rows, :]
            b = dk[rows, :]
            dcat[0, rows, lanes] = (a * ct - rotate_lanes(a, first) * st).astype(BF)
            dcat[1, rows, lanes] = (b * ct - rotate_lanes(b, first) * st).astype(BF)
            dcat[2, rows, lanes] = (0.5 * dv[rows, :].astype(BF).astype(F32)).astype(BF)
            return inner_carry

        lax.fori_loop(0, row_len // br, finish, 0)
        for b in range(n):
            gow[b, :, lanes] = dcat[2, pl.ds(b * tok, tok), lanes]

            @pl.when(jnp.logical_or(c != r, p != b))
            def _():
                send_gv(b, pair).start()

        @pl.when(same)
        def _():
            keep_gv(pair).start()

        return carry

    lax.fori_loop(0, pairs, pair_step, 0)
    rest = order[2:] if pairs > 1 and blocks > 3 else order
    if len(rest) == n:
        reduce_out()

    ck = min(256, tok)
    half_rows = row_len // 2
    n_half = half_rows // ck
    n_blk = tok // ck

    def partial(base, k):
        rows = pl.ds(pl.multiple_of(base + k * ck, ck), ck)
        total = nn(dcat[0, rows, :], ws[:sw, :])
        for t in range(1, 3):
            total = total + nn(dcat[t, rows, :], ws[t * sw : (t + 1) * sw, :])
        gnp[rows, :] = total.astype(BF)

    def to_mate(k):
        rows = pl.ds(pl.multiple_of((1 - c) * half_rows + k * ck, ck), ck)
        here = pl.ds(pl.multiple_of(k * ck, ck), ck)
        return remote(gnp.at[rows], rcv.at[here], co_s.at[k], co_r.at[k], mate)

    def first_half(k, carry):
        partial((1 - c) * half_rows, k)
        to_mate(k).start()
        return carry

    lax.fori_loop(0, n_half, first_half, 0)
    for i in rest[:-1]:
        reduce_chunk(i)


    def own_rows(d):
        return ((q + d) % nh) * tok

    def to_peer(d, k):
        rows = pl.ds(pl.multiple_of(c * half_rows + own_rows(d) + k * ck, ck), ck)
        to = (h, c, r, (q + d) % nh)
        here = pl.ds(pl.multiple_of(k * ck, ck), ck)
        return remote(gnp.at[rows], rcv2.at[d - 1, here], pe_s.at[d, k], pe_r.at[d, k], to)

    def second_half(u, carry):
        partial(c * half_rows + own_rows(1 + u // n_blk), u % n_blk)
        return carry

    lax.fori_loop(0, nh * n_blk, second_half, 0)

    for k in range(n_half):
        to_mate(k).wait_recv()

    def added(d, k):
        rows = pl.ds(pl.multiple_of(c * half_rows + own_rows(d) + k * ck, ck), ck)
        theirs = pl.ds(pl.multiple_of(own_rows(d) + k * ck, ck), ck)
        return rows, gnp[rows, :].astype(F32) + rcv[theirs, :].astype(F32)

    def pass_on(u, carry):
        d, k = 1 + u // n_blk, u % n_blk
        rows, total = added(d, k)
        gnp[rows, :] = total.astype(BF)
        to_peer(d, k).start()
        return carry

    lax.fori_loop(0, (nh - 1) * n_blk, pass_on, 0)

    w = 2 * h + c

    def plane_out(dh, dc):
        to = ((h + dh) % hi_n, (c + dc) % 2, r, q)
        return remote(own, og.at[w], c_s.at[dh, dc], c_r.at[dh, dc], to)

    for i in range(n):
        @pl.when(zed != i)
        def _():
            remote(zos.at[i], zo.at[i], zo_s.at[i], zo_r.at[i], mate).wait_recv()

        @pl.when(zed == i)
        def _():
            keep_out_z(i).wait()

    out_rows = zo[0].astype(F32)
    for i in range(1, n):
        out_rows = out_rows + zo[i].astype(F32)
    own[...] = out_rows.astype(BF)
    og[w] = own[...]
    for dh in range(hi_n):
        for dc in range(2):
            if dh or dc:
                plane_out(dh, dc).start()

    cut = 3 * sw // hi_n

    def hi_part(dh):
        to = (h + dh) % hi_n
        return remote(dwq.at[to], r1.at[dh - 1], a_s.at[dh], a_r.at[dh], (to, c, r, q))

    for t in range(3):
        grad = tn(dcat[t], normed[...]).astype(BF)
        for i in range(hi_n):
            begin, end = max(t * sw, i * cut), min((t + 1) * sw, (i + 1) * cut)
            if begin < end:
                dwq[i, begin - i * cut : end - i * cut, :] = grad[begin - t * sw : end - t * sw]
    for dh in range(1, hi_n):
        hi_part(dh).start()

    partner = swap_to
    gg1[...] = jnp.zeros_like(gg1)

    def send_gi(k):
        rows = pl.ds(pl.multiple_of(k * ck, ck), ck)
        return remote(gis.at[rows], gi.at[rows], gi_s.at[k], gi_r.at[k], partner)

    def keep_gi(k):
        rows = pl.ds(pl.multiple_of(k * ck, ck), ck)
        return pltpu.make_async_copy(gis.at[rows], gi.at[rows], gi_s.at[k])

    def last_sums(k, carry):
        rows = pl.ds(pl.multiple_of(k * ck, ck), ck)
        for d in range(1, nh):
            to_peer(d, k).wait_recv()
        _, grad_n = added(0, k)
        for d in range(1, nh):
            grad_n = grad_n + rcv2[d - 1, rows, :].astype(F32)
        here = pl.ds(pl.multiple_of(p * tok + k * ck, ck), ck)
        xf = xa[here, :].astype(F32)
        inv = lax.rsqrt(jnp.mean(xf * xf, axis=-1, keepdims=True) + EPSILON)
        gg1[...] += jnp.sum((grad_n * xf * inv).reshape(-1, 8, width), axis=0)
        scaled = grad_n * g1[...]
        dot = jnp.sum(scaled * xf, axis=-1, keepdims=True)
        gis[rows, :] = (
            gh[rows, :] + scaled * inv - xf * (inv * inv * inv * dot / width)
        ).astype(BF)

        @pl.when(c != r)
        def _():
            send_gi(k).start()

        @pl.when(same)
        def _():
            keep_gi(k).start()

        return carry

    lax.fori_loop(0, n_blk, last_sums, 0)

    def hi_small(dh):
        to = ((h + dh) % hi_n, c, r, q)
        return remote(sm, s1.at[h], b_s.at[dh], b_r.at[dh], to)

    sm[...] = jnp.zeros_like(sm)
    sm[0:1, :] = jnp.sum(gg1[...], axis=0, keepdims=True)
    sm[1:2, :] = jnp.sum(gg2[...], axis=0, keepdims=True)
    sm[2:3, :sw] = jnp.sum(values_sq[...], axis=0, keepdims=True)
    sm[3:4, :sw] = jnp.sum(squares[...], axis=0, keepdims=True)
    for dh in range(1, hi_n):
        hi_small(dh).start()
    s1[h] = sm[...]
    reduce_chunk(rest[-1])
    for dh in range(1, hi_n):
        source = (h + hi_n - dh) % hi_n
        remote(sm, s1.at[source], b_s.at[dh], b_r.at[dh], mate).wait_recv()
    small = s1[0]
    for i in range(1, hi_n):
        small = small + s1[i]
    spot = c * n + zed
    s2[spot] = small

    def plane_small(k):
        dc, dz = k // n, k % n
        z = (zed + dz) % n
        to = (h, (c + dc) % 2, z // nh, z % nh)
        return remote(s2.at[spot], s2.at[spot], d_s.at[k], d_r.at[k], to)

    def small_arrives(k):
        dc, dz = k // n, k % n
        source = ((c + dc) % 2) * n + (zed + n - dz) % n
        return remote(s2.at[source], s2.at[source], d_s.at[k], d_r.at[k], mate)

    for k in range(1, 2 * n):
        plane_small(k).start()

    part_sum = dwq[h].astype(F32)
    for dh in range(1, hi_n):
        hi_part(dh).wait_recv()
        part_sum = part_sum + r1[dh - 1].astype(F32)
    mine[...] = part_sum.astype(BF)
    across = remote(mine, r2, e_s, e_r, (h, c, 1 - r, q))

    @pl.when(c != r)
    def _():
        across.start()

    for k in range(1, 2 * n):
        small_arrives(k).wait_recv()
    whole = s2[0]
    for k in range(1, 2 * n):
        whole = whole + s2[k]
    total_small[...] = whole

    def spread(dh):
        to = ((h + dh) % hi_n, c, r, q)
        return remote(fin.at[h], fin.at[h], f_s.at[dh], f_r.at[dh], to)

    def share(dh):
        source = (h + hi_n - dh) % hi_n
        return remote(fin.at[source], fin.at[source], m_s.at[dh], m_r.at[dh], mate)

    @pl.when(same)
    def _():
        across.wait_recv()
        fin[h] = (mine[...].astype(F32) + r2[...].astype(F32)).astype(BF)
        for dh in range(1, hi_n):
            spread(dh).start()
        share(0).start()
        for dh in range(1, hi_n):
            source = (h + hi_n - dh) % hi_n
            remote(fin.at[h], fin.at[source], f_s.at[dh], f_r.at[dh], mate).wait_recv()
            share(dh).start()

    @pl.when(c != r)
    def _():
        for dh in range(hi_n):
            share(dh).wait_recv()
        across.wait_send()

    @pl.when(same)
    def _():
        for dh in range(1, hi_n):
            spread(dh).wait_send()
        for dh in range(hi_n):
            share(dh).wait_send()

    for k in range(n_blk):
        @pl.when(c != r)
        def _():
            send_gi(k).wait_send()
            send_gi(k).wait_recv()

        @pl.when(same)
        def _():
            keep_gi(k).wait()

    for k in range(n_half):
        to_mate(k).wait_send()
    for d in range(1, nh):
        for k in range(n_blk):
            to_peer(d, k).wait_send()
    for dh in range(hi_n):
        for dc in range(2):
            if dh or dc:
                theirs = 2 * ((h + hi_n - dh) % hi_n) + (c + dc) % 2
                remote(own, og.at[theirs], c_s.at[dh, dc], c_r.at[dh, dc], mate).wait_recv()
                plane_out(dh, dc).wait_send()
    for dh in range(1, hi_n):
        hi_small(dh).wait_send()
        hi_part(dh).wait_send()
    for k in range(1, 2 * n):
        plane_small(k).wait_send()

    def drain(pair, carry):
        lanes = lane_window(pair, pw, sw)
        for b in range(n):
            @pl.when(p != b)
            def _():
                send_do(b, pair).wait_send()

            @pl.when(jnp.logical_or(c != r, p != b))
            def _():
                send_gv(b, pair).wait_send()
                remote(
                    gow.at[b, :, lanes], gv_at(b, pair), gv_s.at[pair, b], gv_r.at[pair, b], mate
                ).wait_recv()

        @pl.when(same)
        def _():
            keep_gv(pair).wait()

        return carry

    lax.fori_loop(0, pairs, drain, 0)

    @pl.when(c != r)
    def _():
        send_lo().wait_send()
        send_lo().wait_recv()

    for dh in range(1, hi_n):
        out_over_hi(dh).wait_send()
        for i in order[:-1]:
            over_hi(dh, i).wait_send()
    for i in range(n):
        @pl.when(zed != i)
        def _():
            out_over_z(i).wait_send()

    keep_z().wait()
    for t in range(1, n):
        over_z(t).wait_send()
        if t <= nh:
            over_z(t).wait_recv()


def attention_backward(sizes, ga, ds, dos, lo, rx0, xa, ws, g1, tables, seg, *saved):
    _, _, _, nh = sizes
    n, tok, sw = ga.shape
    row_len, width = xa.shape
    pw = tables[0].shape[1]
    pairs = sw // pw
    block = max(tok, 512)
    ck = min(256, tok)
    n_half = row_len // 2 // ck
    n_blk = tok // ck
    hi_n = sizes[0]
    _, _, _, ffs, dw = ds.shape
    rw = dos.shape[2]
    others = max(hi_n - 1, 1)
    cut = 3 * sw // hi_n
    return pl.pallas_call(
        functools.partial(backward_kernel, sizes, block),
        out_shape=(
            jax.ShapeDtypeStruct((n, tok, sw) if sw % 128 else (tok, width), BF),
            jax.ShapeDtypeStruct((tok, width), BF),
            jax.ShapeDtypeStruct((hi_n, cut, width), BF),
            jax.ShapeDtypeStruct((2 * hi_n, rw, width), BF),
            jax.ShapeDtypeStruct((8, width), F32),
            jax.ShapeDtypeStruct((tok, width), BF),
            jax.ShapeDtypeStruct((others, n, 3, ffs, dw), BF),
            jax.ShapeDtypeStruct((others, n, rw, width), BF),
            jax.ShapeDtypeStruct((nh + 1, 3, ffs, dw), BF),
        ),
        in_specs=[ANY] * 5 + [VM] * 17,
        out_specs=(ANY, ANY, VM, VM, VM) + (ANY,) * 4,
        scratch_shapes=[
            pltpu.VMEM((n, tok, sw), BF),
            pltpu.VMEM((row_len, width), BF),
            pltpu.VMEM((row_len, pw), F32),
            pltpu.VMEM((row_len, pw), F32),
            pltpu.VMEM((row_len, pw), F32),
            pltpu.VMEM((3, row_len, sw), BF),
            pltpu.VMEM((n, tok, sw), BF),
            pltpu.VMEM((row_len, width), BF),
            pltpu.VMEM((row_len // 2, width), BF),
            pltpu.VMEM((max(nh - 1, 1), tok, width), BF),
            pltpu.VMEM((tok, width), BF),
            pltpu.VMEM((hi_n, 3, ffs, dw), BF),
            pltpu.VMEM((n, 3, ffs, dw), BF),
            pltpu.VMEM((n, rw, width), BF),
            pltpu.VMEM((n, rw, width), BF),
            pltpu.VMEM((max(nh - 1, 1), 3, ffs, dw), BF),
            pltpu.VMEM((hi_n, cut, width), BF),
            pltpu.VMEM((8, width), F32),
            pltpu.VMEM((n, rw, width), BF),
            pltpu.VMEM((8, width), F32),
            pltpu.VMEM((hi_n, 8, width), F32),
            pltpu.VMEM((2 * n, 8, width), F32),
            pltpu.VMEM((others, cut, width), BF),
            pltpu.VMEM((cut, width), BF),
            pltpu.VMEM((rw, width), BF),
            pltpu.VMEM((cut, width), BF),
            DMA((pairs, n)), DMA((pairs, n)),
            DMA((pairs, n)), DMA((pairs, n)),
            DMA((n_half,)), DMA((n_half,)),
            DMA((nh, n_blk)), DMA((nh, n_blk)),
            DMA((n_blk,)), DMA((n_blk,)),
            DMA((1 + pairs,)),
            DMA((hi_n, n)), DMA((hi_n, n)),
            DMA((hi_n,)), DMA((hi_n,)),
            DMA, DMA,
            DMA((hi_n,)),
            DMA((n,)), DMA((n,)),
            DMA((n,)), DMA((n,)),
            DMA((hi_n,)), DMA((hi_n,)),
            DMA((hi_n,)), DMA((hi_n,)),
            DMA((hi_n, 2)), DMA((hi_n, 2)),
            DMA((2 * n,)), DMA((2 * n,)),
            DMA, DMA,
            DMA((hi_n,)), DMA((hi_n,)),
            DMA((hi_n,)), DMA((hi_n,)),
        ],
        name="attention_backward",
        compiler_params=pltpu.CompilerParams(
            collective_id=3, has_side_effects=True, vmem_limit_bytes=VMEM_MAX
        ),
        cost_estimate=pl.CostEstimate(
            flops=60 << 30, bytes_accessed=24 << 20, transcendentals=row_len * row_len * sw // 128
        ),
    )(ga, ds, dos, lo, rx0, xa, ws, g1, *tables, seg, *saved)


def per_device(sizes, layer_in, value_first, seg_start, gain_one, w_qkv, w_out, gain_two, w_mlp, grad_out):
    hi_n, _, _, nh = sizes
    n = 2 * nh
    wide = 2 * hi_n
    tok, width = layer_in.shape
    sw = w_qkv.shape[1]
    row_len = n * tok
    h, c, r, q = coords()

    w_mlp_t = jnp.transpose(w_mlp, (1, 2, 0))
    sg = jnp.full((8, 128), seg_start[1].astype(F32))
    w_cut = w_qkv.reshape(hi_n, 3 * sw // hi_n, width)
    wo_cut = w_out.reshape(wide, sw // wide, width)
    v_cut = value_first.reshape(tok, n, sw).transpose(1, 0, 2) if sw % 128 else value_first
    xa, ws, so, near, cross, oz = exchange_inputs(sizes, layer_in, w_cut, sg, w_mlp_t, wo_cut)
    ws = ws.reshape(3 * sw, width)

    tables = rope_parts(row_len, min(sw, 128))
    g1 = gain_one.reshape(1, width)
    g2 = gain_two.reshape(1, width)
    xr = xa.reshape(row_len, width)
    ai, dy_in, far, late, oh, qo, ko, mo, ao, lse, squares, values_sq = attention_forward(
        sizes, v_cut, grad_out, cross, oz, xr, ws, g1, tables, so
    )
    lo, gh, ga, ds, dos, gg2, _, _, rx0 = feed_forward(xa, grad_out, dy_in, near, far, late, oh, ai, g2)
    gv, gi, fin, og, sums, lo_in, _, _, zr = attention_backward(
        sizes, ga, ds, dos, lo, rx0, xr, ws, g1, tables, so, qo, ko, mo, ao, lse, gh, gg2, squares, values_sq
    )

    layer_out = jnp.where(c == r, lo, lo_in)
    grad_value_first = (gv.transpose(1, 0, 2).reshape(tok, width) if sw % 128 else gv).astype(F32)
    grad_in = gi.astype(F32)
    grad_w_mlp = jnp.transpose(jnp.sum(zr.astype(F32), axis=0), (2, 0, 1))
    grad_w_out = og.reshape(sw, width).astype(F32)
    grad_w_qkv = fin.reshape(3, sw, width).astype(F32)
    entries = tok * width * wide * n
    value_norms = jnp.sqrt(jnp.sum(sums[2:4], axis=1) / entries)
    return (
        layer_out,
        grad_in,
        grad_value_first,
        sums[0],
        grad_w_qkv,
        grad_w_out,
        sums[1],
        grad_w_mlp,
        value_norms,
    )


def solution(mesh):
    wide, narrow = mesh.shape["wide"], mesh.shape["narrow"]
    sizes = (wide // 2, 2, 2, narrow // 2)
    fine = Mesh(mesh.devices.reshape(sizes), AXES)
    w_axes, n_axes = ("hi", "core"), ("zh", "zq")
    rows = P(AXES, None)
    return jax.shard_map(
        functools.partial(per_device, sizes),
        mesh=fine,
        in_specs=(
            rows,
            rows,
            P(w_axes),
            P(),
            P(None, n_axes, None),
            P(n_axes, None),
            P(),
            P(w_axes, None, n_axes),
            rows,
        ),
        out_specs=(
            rows,
            rows,
            rows,
            P(),
            P(None, n_axes, None),
            P(n_axes, None),
            P(),
            P(w_axes, None, n_axes),
            P(),
        ),
        check_vma=False,
    )
```

```python
import functools

import jax
import jax.numpy as jnp
import numpy as np
from jax import lax
from jax.experimental import pallas as pl
from jax.experimental.pallas import tpu as pltpu
from jax.sharding import Mesh, PartitionSpec as P

HEAD_DIM = 64
EPSILON = 1e-06
BF = jnp.bfloat16
F32 = jnp.float32
AXES = ("hi", "core", "zh", "zq")
MESH = pl.DeviceIdType.MESH
ANY = pl.BlockSpec(memory_space=pl.ANY)
VM = pl.BlockSpec(memory_space=pltpu.VMEM)
VMEM_MAX = 62 << 20
DMA = pltpu.SemaphoreType.DMA


def nn(a, b):
    return lax.dot_general(a, b, (((1,), (0,)), ((), ())), preferred_element_type=F32)


def nt(a, b):
    return lax.dot_general(a, b, (((1,), (1,)), ((), ())), preferred_element_type=F32)


def tn(a, b):
    return lax.dot_general(a, b, (((0,), (0,)), ((), ())), preferred_element_type=F32)


def coords():
    return tuple(lax.axis_index(name) for name in AXES)


def remote(src, dst, send, recv, to):
    return pltpu.make_async_remote_copy(
        src_ref=src, dst_ref=dst, send_sem=send, recv_sem=recv, device_id=to, device_id_type=MESH
    )


def hi_to(h, dh, hi_n):
    if hi_n % 2:
        return (h + dh) % hi_n
    half = hi_n // 2
    return (h // 2 + dh // 2) % half * 2 + (h + dh) % 2


def hi_from(h, dh, hi_n):
    if hi_n % 2:
        return (h + hi_n - dh) % hi_n
    half = hi_n // 2
    return (h // 2 + half - dh // 2) % half * 2 + (h + dh) % 2


def greet_plane(sizes, with_hi, cores=1):
    hi_n, _, _, nh = sizes
    h, c, r, q = coords()
    barrier = pltpu.get_barrier_semaphore()
    count = 0
    for dc in range(2):
        for dr in range(2):
            for dq in range(nh):
                if dc or dr or dq:
                    to = (h, (c + dc) % 2, (r + dr) % 2, (q + dq) % nh)
                    pl.semaphore_signal(barrier, inc=1, device_id=to, device_id_type=MESH)
                    count += 1
    if with_hi:
        for dh in range(1, hi_n):
            for dc in range(cores):
                to = (hi_to(h, dh, hi_n), (c + dc) % 2, r, q)
                pl.semaphore_signal(barrier, inc=1, device_id=to, device_id_type=MESH)
                count += 1
    pl.semaphore_wait(barrier, count)


def rotate_lanes(values, first):
    width = values.shape[1]
    if width < 128:
        return jnp.concatenate([values[:, 32:], values[:, :32]], axis=1)
    return jnp.where(
        first, pltpu.roll(values, width - 32, 1), pltpu.roll(values, 32, 1)
    )


def first_lanes(rows, width):
    lane = lax.broadcasted_iota(jnp.int32, (rows, width), 1)
    return lane % HEAD_DIM < HEAD_DIM // 2


def lane_window(pair, pw, sw):
    return slice(0, sw) if pw == sw else pl.ds(pl.multiple_of(pair * pw, pw), pw)


def rope_rows(lo_c, lo_s, hi_c, hi_s, flag, i, rows):
    step = lo_c.shape[0]
    half = hi_c.shape[0] // 2
    cos, sin = [], []
    for u in range(rows // step):
        k = i * (rows // step) + u
        far, near = pl.ds(k, 1), pl.ds(k % half, 1)
        ch = hi_c[near, :] * flag + hi_c[far, :] * (1.0 - flag)
        sh = hi_s[near, :] * flag + hi_s[far, :] * (1.0 - flag)
        cos.append(lo_c[...] * ch - lo_s[...] * sh)
        sin.append(lo_s[...] * ch + lo_c[...] * sh)
    cos = jnp.concatenate(cos, axis=0)
    sin = jnp.concatenate(sin, axis=0)
    return cos, jnp.where(first_lanes(rows, cos.shape[1]), -sin, sin)


def rope_parts(row_len, pw):
    half = HEAD_DIM // 2
    frequency = 10000.0 ** (-2.0 * np.arange(half) / HEAD_DIM)
    frequency = np.tile(frequency, pw // half)[None, :]
    lo = np.arange(64)[:, None] * frequency
    hi = 64.0 * np.arange(row_len // 64)[:, None] * frequency
    return tuple(jnp.asarray(t, F32) for t in (np.cos(lo), np.sin(lo), np.cos(hi), np.sin(hi)))


def columns_of(ref, s, start, size, sw):
    if len(ref.shape) == 3:
        return ref.at[s]
    start = s * sw + start
    start = start if isinstance(start, int) else pl.multiple_of(start, size)
    return ref.at[:, pl.ds(start, size)]


def tiled(table, width):
    times = width // table.shape[1]
    return table if times == 1 else jnp.concatenate([table] * times, axis=1)


def exchange_kernel(
    sizes, chunks, x, w, sg, wt, wo, xa, ws, so, g1, cross, oz,
    xs, wb, sb, tb, ob,
    swap_s, swap_r, peer_s, peer_r, core_s, core_r, w_s, w_r, wh_s, wh_r, sg_s, sg_r, loc,
    oz_s, oz_r, gp_s, gp_r, gh_s, gh_r, cr_s, cr_r,
):
    hi_n, _, _, nh = sizes
    n = 2 * nh
    h, c, r, q = coords()
    p = c * nh + q
    zed = r * nh + q
    partner_p = r * nh + q
    rows = x.shape[0] // chunks
    same = c == r
    other = c != r
    partner = (h, r, c, q)
    mate = (h, 1 - c, r, q)
    greet_plane(sizes, True)

    def part(k):
        return pl.ds(k * rows, rows)

    def swap_x(k):
        return remote(x.at[part(k)], xa.at[partner_p, part(k)], swap_s.at[k], swap_r.at[k], partner)

    def own_arrives(k):
        return remote(x.at[part(k)], xa.at[p, part(k)], swap_s.at[k], swap_r.at[k], partner)

    def push_peer(src, k, dq):
        to = (h, c, r, (q + dq) % nh)
        return remote(src, xa.at[p, part(k)], peer_s.at[dq, k], peer_r.at[dq, k], to)

    def push_mate(src, k, dq):
        block = c * nh + (q + nh - dq) % nh
        return remote(src, xa.at[block, part(k)], core_s.at[dq, k], core_r.at[dq, k], mate)

    def send_w():
        return remote(w.at[h], ws.at[h], w_s, w_r, partner)

    def spread_w(dh):
        to = (hi_to(h, dh, hi_n), c, r, q)
        return remote(ws.at[h], ws.at[h], wh_s.at[dh], wh_r.at[dh], to)

    def send_sg():
        return remote(sg, so, sg_s, sg_r, partner)

    def shard_peer(dq):
        to = (h, c, r, (q + dq) % nh)
        return remote(wt, g1.at[h, (nh - dq) % nh], gp_s.at[dq], gp_r.at[dq], to)

    def shard_hi(src, dh, t):
        to = (hi_to(h, dh, hi_n), c, r, q)
        return remote(src, g1.at[h, t], gh_s.at[dh, t], gh_r.at[dh, t], to)

    def shard_cross():
        return remote(wt, cross, cr_s, cr_r, (h, c, 1 - r, q))

    def rows_z(dz):
        z = (zed + dz) % n
        return remote(
            wo.at[2 * h + c], oz.at[zed], oz_s.at[dz], oz_r.at[dz], (h, c, z // nh, z % nh)
        )

    def from_hi(dh):
        return hi_from(h, dh, hi_n)

    local = [
        (pltpu.make_async_copy(wt, tb, loc.at[0]), pltpu.make_async_copy(tb, g1.at[h, 0], loc.at[5])),
        (
            pltpu.make_async_copy(wo.at[2 * h + c], ob, loc.at[1]),
            pltpu.make_async_copy(ob, oz.at[zed], loc.at[6]),
        ),
    ]
    local_same = [
        (pltpu.make_async_copy(x, xs, loc.at[2]), pltpu.make_async_copy(xs, xa.at[p], loc.at[7])),
        (pltpu.make_async_copy(w, wb, loc.at[3]), pltpu.make_async_copy(wb, ws, loc.at[8])),
        (pltpu.make_async_copy(sg, sb, loc.at[4]), pltpu.make_async_copy(sb, so, loc.at[9])),
    ]

    @pl.when(other)
    def _():
        send_sg().start()
        send_w().start()
        for k in range(chunks):
            swap_x(k).start()

    @pl.when(same)
    def _():
        for k in range(chunks):
            for dq in range(1, nh):
                push_peer(x.at[part(k)], k, dq).start()
            push_mate(x.at[part(k)], k, 0).start()
        for get, _ in local_same:
            get.start()

    for dq in range(1, nh):
        shard_peer(dq).start()
    for dh in range(1, hi_n):
        shard_hi(wt, dh, 0).start()
    for dz in range(1, n):
        rows_z(dz).start()
    shard_cross().start()
    for get, _ in local:
        get.start()

    @pl.when(other)
    def _():
        send_w().wait_recv()
        for dh in range(1, hi_n):
            spread_w(dh).start()

    for dq in range(1, nh):
        remote(wt, g1.at[h, (nh - dq) % nh], gp_s.at[dq], gp_r.at[dq], mate).wait_recv()
        t = (nh - dq) % nh
        for dh in range(1, hi_n):
            shard_hi(g1.at[h, t], dh, t).start()

    @pl.when(other)
    def _():
        for k in range(chunks):
            own_arrives(k).wait_recv()
            for dq in range(1, nh):
                push_peer(xa.at[p, part(k)], k, dq).start()
            push_mate(xa.at[p, part(k)], k, 0).start()

    for get, put in local:
        get.wait()
        put.start()

    @pl.when(same)
    def _():
        for get, put in local_same:
            get.wait()
            put.start()

    for k in range(chunks):
        for dq in range(1, nh):
            block = c * nh + (q + nh - dq) % nh
            remote(
                x.at[part(k)], xa.at[block, part(k)], peer_s.at[dq, k], peer_r.at[dq, k], mate
            ).wait_recv()
            push_mate(xa.at[block, part(k)], k, dq).start()

    for k in range(chunks):
        for dq in range(nh):
            block = (1 - c) * nh + (q + nh - dq) % nh
            remote(
                x.at[part(k)], xa.at[block, part(k)], core_s.at[dq, k], core_r.at[dq, k], mate
            ).wait_recv()

    @pl.when(other)
    def _():
        send_sg().wait_recv()
        for dh in range(1, hi_n):
            source = from_hi(dh)
            remote(ws.at[source], ws.at[source], wh_s.at[dh], wh_r.at[dh], mate).wait_recv()
        send_sg().wait_send()
        send_w().wait_send()
        for dh in range(1, hi_n):
            spread_w(dh).wait_send()
        for k in range(chunks):
            swap_x(k).wait_send()

    for k in range(chunks):
        for dq in range(1, nh):
            push_peer(x.at[part(k)], k, dq).wait_send()
        for dq in range(nh):
            push_mate(x.at[part(k)], k, dq).wait_send()

    @pl.when(same)
    def _():
        for _, put in local_same:
            put.wait()

    for dq in range(1, nh):
        shard_peer(dq).wait_send()
    for dz in range(1, n):
        z = (zed + n - dz) % n
        remote(wo.at[0], oz.at[z], oz_s.at[dz], oz_r.at[dz], mate).wait_recv()
        rows_z(dz).wait_send()
    for t in range(nh):
        for dh in range(1, hi_n):
            shard_hi(wt, dh, t).wait_send()
            remote(wt, g1.at[from_hi(dh), t], gh_s.at[dh, t], gh_r.at[dh, t], mate).wait_recv()
    shard_cross().wait_recv()
    shard_cross().wait_send()
    for _, put in local:
        put.wait()


def exchange_inputs(sizes, x, w, sg, wt, wo):
    hi_n, _, _, nh = sizes
    n = 2 * nh
    tok, width = x.shape
    chunks = 4 if tok % 64 == 0 else 1
    return pl.pallas_call(
        functools.partial(exchange_kernel, sizes, chunks),
        out_shape=(
            jax.ShapeDtypeStruct((n, tok, width), BF),
            jax.ShapeDtypeStruct(w.shape, BF),
            jax.ShapeDtypeStruct(sg.shape, F32),
            jax.ShapeDtypeStruct((hi_n, nh) + wt.shape, BF),
            jax.ShapeDtypeStruct(wt.shape, BF),
            jax.ShapeDtypeStruct((n,) + wo.shape[1:], BF),
        ),
        in_specs=[ANY] * 5,
        out_specs=(ANY,) * 6,
        scratch_shapes=[
            pltpu.VMEM((tok, width), BF),
            pltpu.VMEM(w.shape, BF),
            pltpu.VMEM(sg.shape, F32),
            pltpu.VMEM(wt.shape, BF),
            pltpu.VMEM(wo.shape[1:], BF),
            DMA((chunks,)), DMA((chunks,)),
            DMA((nh, chunks)), DMA((nh, chunks)),
            DMA((nh, chunks)), DMA((nh, chunks)),
            DMA, DMA,
            DMA((hi_n,)), DMA((hi_n,)),
            DMA, DMA,
            DMA((10,)),
            DMA((n,)), DMA((n,)),
            DMA((nh,)), DMA((nh,)),
            DMA((hi_n, nh)), DMA((hi_n, nh)),
            DMA, DMA,
        ],
        name="exchange_inputs",
        compiler_params=pltpu.CompilerParams(collective_id=1, has_side_effects=True),
        cost_estimate=pl.CostEstimate(flops=0, bytes_accessed=160 << 20, transcendentals=0),
    )(x, w, sg, wt, wo)


def masked(scores, diagonal, crossing, causal, bias):
    if diagonal:
        return jnp.where(causal, scores, -1e30)
    if crossing:
        return scores + bias
    return scores


def forward_kernel(
    sizes, block, v, gout, cross, oz, xa, ws, g1, lo_c, lo_s, hi_c, hi_s, seg,
    ai, dy_in, g2, late, oh, qo, ko, mo, ao, lse, own, vsq,
    va, own_rows, tb, ob,
    att_s, att_r, loc, v_s, v_r, dy_s, dy_r, gp_s, gp_r, gh_s, gh_r, oh_s, oh_r, lc,
):
    hi_n, _, _, nh = sizes
    n = 2 * nh
    h, c, r, q = coords()
    p = c * nh + q
    row_len, sw = qo.shape
    tok = row_len // n
    short = row_len // 2
    pw = lo_c.shape[1]
    pairs = sw // pw
    halves = pw // HEAD_DIM
    mate = (h, 1 - c, r, q)
    other = c != r
    greet_plane(sizes, True)

    def send_v(s, pair):
        lanes = lane_window(pair, pw, sw)
        to = (h, s // nh, c, s % nh)
        spot = r * nh + q
        return remote(
            columns_of(v, s, pair * pw, pw, sw), va.at[spot, :, lanes],
            v_s.at[pair, s], v_r.at[pair, spot], to,
        )

    def v_arrives(b, pair):
        lanes = lane_window(pair, pw, sw)
        return remote(
            columns_of(v, 0, 0, pw, sw), va.at[b, :, lanes], v_s.at[pair, b], v_r.at[pair, b], mate
        )

    def send_dy():
        return remote(gout, dy_in, dy_s, dy_r, (h, r, c, q))

    def shard_hi(dh):
        to = (hi_to(h, dh, hi_n), c, r, q)
        return remote(cross, g2.at[h], gh_s.at[dh], gh_r.at[dh], to)

    def late_peer(dq):
        to = (h, c, r, (q + dq) % nh)
        return remote(cross, late.at[nh - dq - 1], gp_s.at[dq], gp_r.at[dq], to)

    def rows_hi(dh):
        to = (hi_to(h, dh, hi_n), c, r, q)
        return remote(oz, oh.at[h], oh_s.at[dh], oh_r.at[dh], to)

    def from_hi(dh):
        return hi_from(h, dh, hi_n)

    keep_v = pltpu.make_async_copy(columns_of(v, p, 0, sw, sw), va.at[p], lc.at[0])
    local = [
        (pltpu.make_async_copy(cross, tb, lc.at[1]), pltpu.make_async_copy(tb, g2.at[h], lc.at[3])),
        (pltpu.make_async_copy(oz, ob, lc.at[2]), pltpu.make_async_copy(ob, oh.at[h], lc.at[4])),
    ]
    for pair in range(pairs):
        for s in range(n):
            @pl.when(jnp.logical_or(other, p != s))
            def _():
                send_v(s, pair).start()

    @pl.when(c == r)
    def _():
        keep_v.start()

    for dh in range(1, hi_n):
        shard_hi(dh).start()
    for dh in range(1, hi_n):
        rows_hi(dh).start()
    for dq in range(1, nh):
        late_peer(dq).start()

    @pl.when(other)
    def _():
        send_dy().start()

    for get, _ in local:
        get.start()

    br = 256
    own[...] = jnp.zeros_like(own)
    flag = seg[0:1, 0:1]

    def project(i, carry):
        rows = pl.ds(pl.multiple_of(i * br, br), br)
        xf = xa[rows, :].astype(F32)
        inv = lax.rsqrt(jnp.mean(xf * xf, axis=-1, keepdims=True) + EPSILON)
        normed = (xf * inv * g1[...]).astype(BF)
        raw = nt(normed, ws[...])
        first = first_lanes(br, sw)
        ct, st = rope_rows(lo_c, lo_s, hi_c, hi_s, flag, i, br)
        ct, st = tiled(ct, sw), tiled(st, sw)
        q_raw = raw[:, :sw]
        k_raw = raw[:, sw : 2 * sw]
        own_vals = raw[:, 2 * sw :]
        q_rot = (q_raw * ct + rotate_lanes(q_raw, first) * st).astype(BF)
        qo[rows, :] = (q_rot.astype(F32) * HEAD_DIM**-0.5).astype(BF)
        ko[rows, :] = (k_raw * ct + rotate_lanes(k_raw, first) * st).astype(BF)
        own_rows[rows, :] = own_vals
        own[...] += jnp.sum((own_vals * own_vals).reshape(br // 8, 8, sw), axis=0)
        return carry

    lax.fori_loop(0, row_len // br, project, 0)

    for get, put in local:
        get.wait()
        put.start()
    @pl.when(c == r)
    def _():
        keep_v.wait()

    bias = flag * -1e30
    blocks = row_len // block
    per = block // tok
    causal = lax.broadcasted_iota(jnp.int32, (block, block), 0) >= lax.broadcasted_iota(
        jnp.int32, (block, block), 1
    )

    def send(b, pair):
        lanes = lane_window(pair, pw, sw)
        to = (h, b // nh, r, b % nh)
        return remote(
            ao.at[b, :, lanes], ai.at[p, :, lanes], att_s.at[pair, b], att_r.at[pair, p], to
        )

    def keep(pair):
        lanes = lane_window(pair, pw, sw)
        return pltpu.make_async_copy(ao.at[p, :, lanes], ai.at[p, :, lanes], loc.at[pair])

    def pair_step(pair, carry):
        lanes = lane_window(pair, pw, sw)
        for b in range(n):
            @pl.when(jnp.logical_or(other, p != b))
            def _():
                v_arrives(b, pair).wait_recv()

        sums = 0.0
        for b in range(n):
            rows = pl.ds(b * tok, tok)
            values = va[b, :, lanes].astype(F32)
            sums = sums + jnp.sum((values * values).reshape(tok // 8, 8, pw), axis=0)
            mo[rows, lanes] = (0.5 * own_rows[rows, lanes] + 0.5 * values).astype(BF)
        vsq[:, lanes] = sums
        for i in range(blocks):
            outs = []
            rows = pl.ds(i * block, block)
            for half in range(halves):
                cols = slice(half * HEAD_DIM, (half + 1) * HEAD_DIM)
                qh = qo[rows, lanes][:, cols]
                score = []
                for j in range(i + 1):
                    kj = ko[pl.ds(j * block, block), lanes][:, cols]
                    crossing = i * block >= short and j * block < short
                    score.append(masked(nt(qh, kj), i == j, crossing, causal, bias))
                top = functools.reduce(
                    jnp.maximum, [jnp.max(s, axis=-1, keepdims=True) for s in score]
                )
                total = 0.0
                acc = 0.0
                for j in range(i + 1):
                    e = jnp.exp(score[j] - top)
                    total = total + jnp.sum(e, axis=-1, keepdims=True)
                    vj = mo[pl.ds(j * block, block), lanes][:, cols]
                    acc = acc + nn(e.astype(BF), vj)
                outs.append(acc / total)
                lse[pair, rows, half : half + 1] = top + jnp.log(total)
            out = (jnp.concatenate(outs, axis=1) if halves > 1 else outs[0]).astype(BF)
            for t in range(per):
                b = i * per + t
                ao[b, :, lanes] = out[t * tok : (t + 1) * tok]

                @pl.when(p != b)
                def _():
                    send(b, pair).start()

        keep(pair).start()
        return carry

    lax.fori_loop(0, pairs, pair_step, 0)

    def drain(pair, carry):
        lanes = lane_window(pair, pw, sw)
        for b in range(n):
            @pl.when(p != b)
            def _():
                send(b, pair).wait_send()
                remote(
                    ao.at[b, :, lanes], ai.at[b, :, lanes], att_s.at[pair, b], att_r.at[pair, b],
                    (h, 1 - c, r, q),
                ).wait_recv()
        keep(pair).wait()
        return carry

    lax.fori_loop(0, pairs, drain, 0)

    for pair in range(pairs):
        for s in range(n):
            @pl.when(jnp.logical_or(other, p != s))
            def _():
                send_v(s, pair).wait_send()

    for dh in range(1, hi_n):
        rows_hi(dh).wait_send()
        remote(oz, oh.at[from_hi(dh)], oh_s.at[dh], oh_r.at[dh], mate).wait_recv()
        shard_hi(dh).wait_send()
        remote(cross, g2.at[from_hi(dh)], gh_s.at[dh], gh_r.at[dh], mate).wait_recv()
    for dq in range(1, nh):
        late_peer(dq).wait_send()
        late_peer(dq).wait_recv()

    @pl.when(other)
    def _():
        send_dy().wait_send()
        send_dy().wait_recv()

    for _, put in local:
        put.wait()


def attention_forward(sizes, v, gout, cross, oz, xa, ws, g1, tables, seg):
    hi_n, _, _, nh = sizes
    n = 2 * nh
    row_len, width = xa.shape
    sw = ws.shape[0] // 3
    tok = row_len // n
    pw = tables[0].shape[1]
    pairs = sw // pw
    block = max(tok, 512)
    flops = 2 * row_len * width * 3 * sw + 2 * row_len * row_len * sw
    return pl.pallas_call(
        functools.partial(forward_kernel, sizes, block),
        out_shape=(
            jax.ShapeDtypeStruct((n, tok, sw), BF),
            jax.ShapeDtypeStruct((tok, width), BF),
            jax.ShapeDtypeStruct((hi_n,) + cross.shape, BF),
            jax.ShapeDtypeStruct((max(nh - 1, 1),) + cross.shape, BF),
            jax.ShapeDtypeStruct((hi_n,) + oz.shape, BF),
            jax.ShapeDtypeStruct((row_len, sw), BF),
            jax.ShapeDtypeStruct((row_len, sw), BF),
            jax.ShapeDtypeStruct((row_len, sw), BF),
            jax.ShapeDtypeStruct((n, tok, sw), BF),
            jax.ShapeDtypeStruct((pairs, row_len, pw // HEAD_DIM), F32),
            jax.ShapeDtypeStruct((8, sw), F32),
            jax.ShapeDtypeStruct((8, sw), F32),
        ),
        in_specs=[ANY] * 4 + [VM] * 8,
        out_specs=(ANY,) * 5 + (VM,) * 7,
        scratch_shapes=[
            pltpu.VMEM((n, tok, sw), BF),
            pltpu.VMEM((row_len, sw), F32),
            pltpu.VMEM(cross.shape, BF),
            pltpu.VMEM(oz.shape, BF),
            DMA((pairs, n)), DMA((pairs, n)), DMA((pairs,)),
            DMA((pairs, n)), DMA((pairs, n)),
            DMA, DMA,
            DMA((nh,)), DMA((nh,)),
            DMA((hi_n,)), DMA((hi_n,)),
            DMA((hi_n,)), DMA((hi_n,)),
            DMA((5,)),
        ],
        name="attention_forward",
        compiler_params=pltpu.CompilerParams(
            collective_id=2, has_side_effects=True, vmem_limit_bytes=VMEM_MAX
        ),
        cost_estimate=pl.CostEstimate(
            flops=4 * flops, bytes_accessed=16 << 20, transcendentals=row_len * row_len * sw // 128
        ),
    )(v, gout, cross, oz, xa, ws, g1, *tables, seg)


def mlp_kernel(
    xa, gout, dy_in, near, far, lp, oh, ai, g2, lo, gh, ga, dsum, dosum, gg2, theirs, late, rx0,
    x, dy, hid, n2, acc_o, acc_g, buf, rcv, bo, rcvo, wm, wo, oa, ob, first,
    x_s, buf_s, buf_r, bo_s, bo_r, ld, th_s, th_r, o_s, o_r, gh_s, gh_r, fi_s, fi_r,
):
    step = pl.program_id(0)
    n = ai.shape[0]
    nh = n // 2
    hi_n = wm.shape[2]
    wide = 2 * hi_n
    width = x.shape[1]
    dw = width // wide
    rw = bo.shape[3]
    h, c, r, q = coords()
    own_dy = pltpu.make_async_copy(gout, dy, ld.at[4])
    swapped_dy = pltpu.make_async_copy(dy_in, dy, ld.at[4])
    own_o = pltpu.make_async_copy(oh, oa, ld.at[5])

    mate = (h, 1 - c, r, q)

    def block_of(t):
        return near.at[:, t] if t < nh else far

    def give(t):
        return remote(block_of(t), theirs.at[t], th_s.at[t, 0], th_r.at[t, 0], mate)

    def late_hi(t, dh):
        to = (hi_to(h, dh, hi_n), c, r, q)
        u = t - nh - 1
        return remote(lp.at[u], late.at[h, u], gh_s.at[u, dh], gh_r.at[u, dh], to)

    def late_piece(t, dh):
        return late.at[hi_from(h, dh, hi_n), t - nh - 1] if dh else lp.at[t - nh - 1]

    def late_arrives(t, dh):
        u = t - nh - 1
        return remote(lp.at[u], late_piece(t, dh), gh_s.at[u, dh], gh_r.at[u, dh], mate)

    def give_late(t, dh):
        source = hi_from(h, dh, hi_n)
        return remote(
            late_piece(t, dh), theirs.at[t, source], th_s.at[t, dh], th_r.at[t, dh], mate
        )

    def load_late(t, dh):
        source = hi_from(h, dh, hi_n)
        return pltpu.make_async_copy(late_piece(t, dh), wm.at[t % 2, c, source], ld.at[t % 2])

    def first_over_hi(dh):
        to = hi_to(h, dh, hi_n)
        return remote(first.at[to], rx0.at[dh - 1], fi_s.at[dh], fi_r.at[dh], (to, c, r, q))

    def give_o():
        return remote(oh, ob, o_s, o_r, (h, 1 - c, r, q))

    def load_own(src, at):
        return pltpu.make_async_copy(src, wm.at[at, c], ld.at[at])

    def load_theirs(t, at):
        return pltpu.make_async_copy(theirs.at[t], wm.at[at, 1 - c], ld.at[2 + at])
    own_x = pltpu.make_async_copy(xa.at[c * (n // 2) + q], x, x_s)
    slot = step % 2
    last = n - 1

    def to_mate(at):
        return remote(buf.at[at, 1 - c], rcv.at[at], buf_s.at[at], buf_r.at[at], mate)

    def out_to_mate():
        return remote(bo.at[1 - c], rcvo, bo_s, bo_r, mate)

    @pl.when(step == 0)
    def _():
        own_x.start()
        own_o.start()
        load_own(near.at[:, 0], 0).start()

        @pl.when(c == r)
        def _():
            own_dy.start()

        @pl.when(c != r)
        def _():
            swapped_dy.start()

        barrier = pltpu.get_barrier_semaphore()
        friends = [mate]
        friends += [(hi_to(h, dh, hi_n), c, r, q) for dh in range(1, hi_n)]
        for to in friends:
            pl.semaphore_signal(barrier, inc=1, device_id=to, device_id_type=MESH)
        pl.semaphore_wait(barrier, len(friends))
        for t in range(nh + 1, n):
            for dh in range(1, hi_n):
                late_hi(t, dh).start()
        give_o().start()
        for t in range(nh + 1):
            give(t).start()
        for t in range(nh + 1, n):
            give_late(t, 0).start()
        own_x.wait()
        own_o.wait()
        own_dy.wait()
        give_o().wait_recv()
        for s in range(n):
            for w in range(wide):
                wo[s, w * rw : (w + 1) * rw] = jnp.where(c == w % 2, oa[w // 2, s], ob[w // 2, s])
        give(0).wait_recv()
        load_theirs(0, 0).start()
        hid[...] = x[...].astype(F32)

        def project(s, carry):
            hid[...] += nn(ai[s], wo[s])
            return carry

        lax.fori_loop(0, n, project, 0)
        total = hid[...]
        inv = lax.rsqrt(jnp.mean(total * total, axis=-1, keepdims=True) + EPSILON)
        n2[...] = (total * inv * g2[...]).astype(BF)
        acc_o[...] = jnp.zeros_like(acc_o)
        acc_g[...] = jnp.zeros_like(acc_g)

    @pl.when(step < n)
    def _():
        @pl.when(step > 1)
        def _():
            to_mate(slot).wait_send()

        load_own(near.at[:, 0], slot).wait()
        load_theirs(0, slot).wait()

        def weight(j):
            return jnp.concatenate([wm[slot, w % 2, w // 2, j] for w in range(wide)], axis=1)

        def put(j, grad):
            low = grad.astype(BF)
            for w in range(wide):
                buf[slot, w % 2, w // 2, j] = low[:, w * dw : (w + 1) * dw]

        gate = nt(n2[...], weight(0))
        up = nt(n2[...], weight(1))
        sig = jax.nn.sigmoid(gate)
        silu = gate * sig
        inner = (silu * up).astype(BF)
        grad_inner = nt(dy[...], weight(2))
        for t in range(1, nh + 1):
            @pl.when(step == t - 1)
            def _():
                load_own(block_of(t), t % 2).start()
                give(t).wait_recv()
                load_theirs(t, t % 2).start()

        for t in range(nh + 1, n):
            @pl.when(step == t - 1)
            def _():
                load_late(t, 0).start()
                for dh in range(1, hi_n):
                    late_arrives(t, dh).wait_recv()
                    give_late(t, dh).start()
                    load_late(t, dh).start()

        grad_gate = (grad_inner * up * sig * (1.0 + gate * (1.0 - sig))).astype(BF)
        grad_up = (grad_inner * silu).astype(BF)
        acc_o[...] += nn(inner, weight(2))
        acc_g[...] += nn(grad_gate, weight(0)) + nn(grad_up, weight(1))
        put(0, tn(grad_gate, n2[...]))
        put(1, tn(grad_up, n2[...]))
        put(2, tn(inner, dy[...]))

    @pl.when(step == last)
    def _():
        hidden = hid[...]
        lo[...] = (hidden + acc_o[...]).astype(BF)
        inv = lax.rsqrt(jnp.mean(hidden * hidden, axis=-1, keepdims=True) + EPSILON)
        grad_n = acc_g[...]
        gg2[...] = jnp.sum((grad_n * hidden * inv).reshape(-1, 8, width), axis=0)
        scaled = grad_n * g2[...]
        dot = jnp.sum(scaled * hidden, axis=-1, keepdims=True)
        grad_h = dy[...].astype(F32) + scaled * inv - hidden * (inv * inv * inv * dot / width)
        gh[...] = grad_h
        low = grad_h.astype(BF)

        def project_back(s, carry):
            ga[s] = nt(low, wo[s]).astype(BF)
            grad_wo = tn(ai[s], low).astype(BF)
            for w in range(wide):
                bo[w % 2, w // 2, s] = grad_wo[w * rw : (w + 1) * rw]
            return carry

        lax.fori_loop(0, n, project_back, 0)

    @pl.when(step > 0)
    def _():
        before = (step + 1) % 2
        to_mate(before).wait_recv()
        for a in range(hi_n):
            for j in range(3):
                total = buf[before, c, a, j].astype(F32) + rcv[before, a, j].astype(F32)
                dsum[a, 0, j] = total.astype(BF)

    @pl.when(step == 1)
    def _():
        first[...] = dsum[:, 0]
        for dh in range(1, hi_n):
            first_over_hi(dh).start()

    for t in range(nh + 1, n):
        @pl.when(step == t - 1)
        def _():
            for dh in range(hi_n):
                give_late(t, dh).wait_recv()
            load_theirs(t, t % 2).start()

    @pl.when(step < n)
    def _():
        to_mate(slot).start()

    @pl.when(step == last)
    def _():
        out_to_mate().start()

    @pl.when(step == n)
    def _():
        out_to_mate().wait_recv()
        for a in range(hi_n):
            for s in range(n):
                total = bo[c, a, s].astype(F32) + rcvo[a, s].astype(F32)
                dosum[a, s] = total.astype(BF)
        out_to_mate().wait_send()
        to_mate(0).wait_send()
        to_mate(1).wait_send()
        give_o().wait_send()
        for dh in range(1, hi_n):
            first_over_hi(dh).wait_send()
            first_over_hi(dh).wait_recv()
        for t in range(nh + 1):
            give(t).wait_send()
        for t in range(nh + 1, n):
            for dh in range(hi_n):
                give_late(t, dh).wait_send()
            for dh in range(1, hi_n):
                late_hi(t, dh).wait_send()


def feed_forward(xa, gout, dy_in, near, far, lp, oh, ai, g2):
    n, tok, sw = ai.shape
    nh = n // 2
    width = gout.shape[1]
    hi_n, _, _, ffs, dw = near.shape
    wide = 2 * hi_n
    rw = sw // wide

    def whole(*shape):
        return pl.BlockSpec(shape, lambda i: (0,) * len(shape))

    def fixed(*shape):
        return pl.BlockSpec(
            shape, lambda i: (0,) * len(shape), pipeline_mode=pl.Buffered(1)
        )

    return pl.pallas_call(
        mlp_kernel,
        out_shape=(
            jax.ShapeDtypeStruct((tok, width), BF),
            jax.ShapeDtypeStruct((tok, width), F32),
            jax.ShapeDtypeStruct((n, tok, sw), BF),
            jax.ShapeDtypeStruct((hi_n, n, 3, ffs, dw), BF),
            jax.ShapeDtypeStruct((hi_n, n, rw, width), BF),
            jax.ShapeDtypeStruct((8, width), F32),
            jax.ShapeDtypeStruct((n, hi_n, 3, ffs, dw), BF),
            jax.ShapeDtypeStruct((hi_n, max(nh - 1, 1), 3, ffs, dw), BF),
            jax.ShapeDtypeStruct((max(hi_n - 1, 1), 3, ffs, dw), BF),
        ),
        grid_spec=pl.GridSpec(
            grid=(n + 1,),
            in_specs=[ANY] * 7 + [fixed(n, tok, sw), fixed(1, width)],
            out_specs=(
                whole(tok, width),
                whole(tok, width),
                whole(n, tok, sw),
                pl.BlockSpec(
                    (hi_n, 1, 3, ffs, dw), lambda i: (0, jnp.maximum(i - 1, 0), 0, 0, 0)
                ),
                whole(hi_n, n, rw, width),
                whole(8, width),
                ANY,
                ANY,
                ANY,
            ),
            scratch_shapes=[
                pltpu.VMEM((tok, width), BF),
                pltpu.VMEM((tok, width), BF),
                pltpu.VMEM((tok, width), F32),
                pltpu.VMEM((tok, width), BF),
                pltpu.VMEM((tok, width), F32),
                pltpu.VMEM((tok, width), F32),
                pltpu.VMEM((2, 2, hi_n, 3, ffs, dw), BF),
                pltpu.VMEM((2, hi_n, 3, ffs, dw), BF),
                pltpu.VMEM((2, hi_n, n, rw, width), BF),
                pltpu.VMEM((hi_n, n, rw, width), BF),
                pltpu.VMEM((2, 2, hi_n, 3, ffs, dw), BF),
                pltpu.VMEM((n, sw, width), BF),
                pltpu.VMEM((hi_n, n, rw, width), BF),
                pltpu.VMEM((hi_n, n, rw, width), BF),
                pltpu.VMEM((hi_n, 3, ffs, dw), BF),
                DMA, DMA((2,)), DMA((2,)), DMA, DMA,
                DMA((6,)), DMA((n, hi_n)), DMA((n, hi_n)), DMA, DMA,
                DMA((max(nh - 1, 1), hi_n)), DMA((max(nh - 1, 1), hi_n)),
                DMA((hi_n,)), DMA((hi_n,)),
            ],
        ),
        name="feed_forward",
        compiler_params=pltpu.CompilerParams(
            dimension_semantics=("arbitrary",),
            collective_id=4,
            has_side_effects=True,
            vmem_limit_bytes=VMEM_MAX,
        ),
        cost_estimate=pl.CostEstimate(
            flops=18 * tok * width * ffs * n, bytes_accessed=40 << 20, transcendentals=tok * ffs * n
        ),
    )(xa, gout, dy_in, near, far, lp, oh, ai, g2)


def backward_kernel(
    sizes, block, ga, ds, dos, lo, rx0, xa, ws, g1, lo_c, lo_s, hi_c, hi_s, seg, qi, ki, mi, ao, lse, gh,
    gg2, squares, values_sq,
    gv, gi, fin, og, total_small, lo_in, rx, rxo, zr,
    do, normed, dq, dk, dv, dcat, gow, gnp, rcv, rcv2, gis, part, zs, zos, do_part, rf,
    dwq, gg1, zo, sm, s1, s2, r1, r2, own, mine,
    do_s, do_r, gv_s, gv_r, co_s, co_r, pe_s, pe_r, gi_s, gi_r, loc,
    rx_s, rx_r, rxo_s, rxo_r, ly_s, ly_r, ld, z_s, z_r, zo_s, zo_r,
    a_s, a_r, b_s, b_r, c_s, c_r, d_s, d_r, e_s, e_r, f_s, f_r, m_s, m_r,
):
    hi_n, _, _, nh = sizes
    n = 2 * nh
    h, c, r, q = coords()
    p = c * nh + q
    row_len, sw = qi.shape
    width = xa.shape[1]
    tok = row_len // n
    short = row_len // 2
    pw = lo_c.shape[1]
    pairs = sw // pw
    halves = pw // HEAD_DIM
    same = c == r
    mate = (h, 1 - c, r, q)
    swap_to = (h, r, c, q)
    zed = r * nh + q
    greet_plane(sizes, True, 2)

    order = list(range(nh + 1, n)) + [nh] + list(range(1, nh)) + [0]

    def over_hi(dh, i):
        to = hi_to(h, dh, hi_n)
        return remote(
            ds.at[to, i], rx.at[dh - 1, i], rx_s.at[dh, i], rx_r.at[dh, i], (to, c, r, q)
        )

    def out_over_hi(dh):
        to = hi_to(h, dh, hi_n)
        return remote(dos.at[to], rxo.at[dh - 1], rxo_s.at[dh], rxo_r.at[dh], (to, c, r, q))

    def send_lo():
        return remote(lo, lo_in, ly_s, ly_r, swap_to)

    def over_z(t):
        if t > nh:
            return remote(zs.at[t], rf.at[t - nh - 1], z_s.at[t], z_r.at[t], (h, c, r, (q + t) % nh))
        to = (h, c, 1 - r, q) if t == nh else (h, c, r, (q + t) % nh)
        return remote(zs.at[t], zr.at[t], z_s.at[t], z_r.at[t], to)

    def out_over_z(i):
        return remote(zos.at[i], zo.at[zed], zo_s.at[i], zo_r.at[zed], (h, c, i // nh, i % nh))

    def keep_z():
        return pltpu.make_async_copy(zs.at[0], zr.at[0], z_s.at[0])

    def keep_out_z(i):
        return pltpu.make_async_copy(zos.at[i], zo.at[i], zo_s.at[i])

    def load_chunk(i):
        copies = [pltpu.make_async_copy(ds.at[h, i], part.at[0], ld.at[0])]
        for dh in range(1, hi_n):
            source = rx.at[dh - 1, i] if i else rx0.at[dh - 1]
            copies.append(pltpu.make_async_copy(source, part.at[dh], ld.at[dh]))
        return copies

    def reduce_chunk(i):
        if i:
            for dh in range(1, hi_n):
                over_hi(dh, i).wait_recv()
        for copy in load_chunk(i):
            copy.start()
        if i == nh:
            for t in range(nh + 1, n):
                over_z(t).wait_recv()
        for copy in load_chunk(i):
            copy.wait()

        def add(j, carry):
            total = part[0, j].astype(F32)
            for dh in range(1, hi_n):
                total = total + part[dh, j].astype(F32)
            if i == nh:
                for t in range(nh - 1):
                    total = total + rf[t, j].astype(F32)
            zs[i, j] = total.astype(BF)
            return carry

        lax.fori_loop(0, 3, add, 0)
        if i:
            over_z(i).start()
        else:
            keep_z().start()

    own_out = pltpu.make_async_copy(dos.at[h], zos, ld.at[0])

    def reduce_out():
        own_out.start()
        own_out.wait()
        for dh in range(1, hi_n):
            out_over_hi(dh).wait_recv()
            copy = pltpu.make_async_copy(rxo.at[dh - 1], do_part, ld.at[dh])
            copy.start()
            copy.wait()
            zos[...] = (zos[...].astype(F32) + do_part[...].astype(F32)).astype(BF)
        for i in range(n):
            @pl.when(zed != i)
            def _():
                out_over_z(i).start()

            @pl.when(zed == i)
            def _():
                keep_out_z(i).start()

    def send_do(s, pair):
        lanes = lane_window(pair, pw, sw)
        to = (h, s // nh, r, s % nh)
        return remote(
            ga.at[s, :, lanes], do.at[p, :, lanes], do_s.at[pair, s], do_r.at[pair, p], to
        )

    def do_arrives(s, pair):
        lanes = lane_window(pair, pw, sw)
        return remote(
            ga.at[s, :, lanes], do.at[s, :, lanes], do_s.at[pair, s], do_r.at[pair, s], mate
        )

    keep_do = pltpu.make_async_copy(ga.at[p], do.at[p], loc.at[0])
    for pair in range(pairs):
        for s in range(n):
            @pl.when(p != s)
            def _():
                send_do(s, pair).start()

    keep_do.start()
    for dh in range(1, hi_n):
        out_over_hi(dh).start()
    for hops in (range(1, min(3, hi_n)), range(3, hi_n)):
        for i in order[:-1]:
            for dh in hops:
                over_hi(dh, i).start()

    @pl.when(c != r)
    def _():
        send_lo().start()

    br = 256

    def norm(i, carry):
        rows = pl.ds(pl.multiple_of(i * br, br), br)
        xf = xa[rows, :].astype(F32)
        inv = lax.rsqrt(jnp.mean(xf * xf, axis=-1, keepdims=True) + EPSILON)
        normed[rows, :] = (xf * inv * g1[...]).astype(BF)
        return carry

    lax.fori_loop(0, row_len // br, norm, 0)
    keep_do.wait()

    flag = seg[0:1, 0:1]
    bias = flag * -1e30
    blocks = row_len // block
    per = block // tok
    causal = lax.broadcasted_iota(jnp.int32, (block, block), 0) >= lax.broadcasted_iota(
        jnp.int32, (block, block), 1
    )

    def gv_at(s, pair):
        if len(gv.shape) == 3:
            return gv.at[s]
        return gv.at[:, pl.ds(pl.multiple_of(s * sw + pair * pw, pw), pw)]

    def send_gv(b, pair):
        lanes = lane_window(pair, pw, sw)
        to = (h, r, b // nh, b % nh)
        return remote(
            gow.at[b, :, lanes], gv_at(p, pair), gv_s.at[pair, b], gv_r.at[pair, p], to
        )

    def keep_gv(pair):
        lanes = lane_window(pair, pw, sw)
        return pltpu.make_async_copy(gow.at[p, :, lanes], gv_at(p, pair), loc.at[1 + pair])

    def early(pair, i):
        if pairs < 2 or blocks < 4:
            return 0

        if i == blocks - 1:
            @pl.when(pair == 0)
            def _():
                reduce_out()

        if i == 1:
            @pl.when(pair == 1)
            def _():
                reduce_chunk(order[0])

        if i == blocks - 1:
            @pl.when(pair == 1)
            def _():
                reduce_chunk(order[1])

        return 2

    def pair_step(pair, carry):
        for s in range(n):
            @pl.when(p != s)
            def _():
                do_arrives(s, pair).wait_recv()

        lanes = lane_window(pair, pw, sw)
        dk[...] = jnp.zeros_like(dk)
        dv[...] = jnp.zeros_like(dv)
        for i in range(blocks):
            rows = pl.ds(i * block, block)
            pieces = [[] for _ in range(i + 1)]
            dq_parts = []
            do_rows = [do[i * per + t, :, lanes] for t in range(per)]
            do_i = do_rows[0] if per == 1 else jnp.concatenate(do_rows, axis=0)
            ao_rows = [ao[i * per + t, :, lanes] for t in range(per)]
            ao_i = ao_rows[0] if per == 1 else jnp.concatenate(ao_rows, axis=0)
            product = do_i.astype(F32) * ao_i.astype(F32)
            for half in range(halves):
                cols = slice(half * HEAD_DIM, (half + 1) * HEAD_DIM)
                qh = qi[rows, lanes][:, cols]
                doh = do_i[:, cols]
                delta = jnp.sum(product[:, cols], axis=-1, keepdims=True)
                level = lse[pair, rows, half : half + 1]
                acc = 0.0
                for j in range(i + 1):
                    kj = ki[pl.ds(j * block, block), lanes][:, cols]
                    vj = mi[pl.ds(j * block, block), lanes][:, cols]
                    crossing = i * block >= short and j * block < short
                    score = masked(nt(qh, kj), i == j, crossing, causal, bias)
                    prob = jnp.exp(score - level)
                    grad_prob = nt(doh, vj)
                    grad_score = (prob * (grad_prob - delta)).astype(BF)
                    acc = acc + nn(grad_score, kj)
                    pieces[j].append((tn(grad_score, qh), tn(prob.astype(BF), doh)))
                dq_parts.append(acc * HEAD_DIM**-0.5)
            dq[rows, :] = dq_parts[0] if halves == 1 else jnp.concatenate(dq_parts, axis=1)
            for j in range(i + 1):
                at = pl.ds(j * block, block)
                if halves == 1:
                    dk[at, :] += pieces[j][0][0]
                    dv[at, :] += pieces[j][0][1]
                else:
                    dk[at, :] += jnp.concatenate([t[0] for t in pieces[j]], axis=1)
                    dv[at, :] += jnp.concatenate([t[1] for t in pieces[j]], axis=1)
            early(pair, i)
        first = first_lanes(br, pw)

        def finish(i, inner_carry):
            rows = pl.ds(pl.multiple_of(i * br, br), br)
            ct, st = rope_rows(lo_c, lo_s, hi_c, hi_s, flag, i, br)
            a = dq[rows, :]
            b = dk[rows, :]
            dcat[0, rows, lanes] = (a * ct - rotate_lanes(a, first) * st).astype(BF)
            dcat[1, rows, lanes] = (b * ct - rotate_lanes(b, first) * st).astype(BF)
            dcat[2, rows, lanes] = (0.5 * dv[rows, :].astype(BF).astype(F32)).astype(BF)
            return inner_carry

        lax.fori_loop(0, row_len // br, finish, 0)
        for b in range(n):
            gow[b, :, lanes] = dcat[2, pl.ds(b * tok, tok), lanes]

            @pl.when(jnp.logical_or(c != r, p != b))
            def _():
                send_gv(b, pair).start()

        @pl.when(same)
        def _():
            keep_gv(pair).start()

        return carry

    lax.fori_loop(0, pairs, pair_step, 0)
    rest = order[2:] if pairs > 1 and blocks > 3 else order
    if len(rest) == n:
        reduce_out()

    ck = min(256, tok)
    half_rows = row_len // 2
    n_half = half_rows // ck
    n_blk = tok // ck

    def partial(base, k):
        rows = pl.ds(pl.multiple_of(base + k * ck, ck), ck)
        total = nn(dcat[0, rows, :], ws[:sw, :])
        for t in range(1, 3):
            total = total + nn(dcat[t, rows, :], ws[t * sw : (t + 1) * sw, :])
        gnp[rows, :] = total.astype(BF)

    def to_mate(k):
        rows = pl.ds(pl.multiple_of((1 - c) * half_rows + k * ck, ck), ck)
        here = pl.ds(pl.multiple_of(k * ck, ck), ck)
        return remote(gnp.at[rows], rcv.at[here], co_s.at[k], co_r.at[k], mate)

    def first_half(k, carry):
        partial((1 - c) * half_rows, k)
        to_mate(k).start()
        return carry

    lax.fori_loop(0, n_half, first_half, 0)
    for i in rest[:-1]:
        reduce_chunk(i)


    def own_rows(d):
        return ((q + d) % nh) * tok

    def to_peer(d, k):
        rows = pl.ds(pl.multiple_of(c * half_rows + own_rows(d) + k * ck, ck), ck)
        to = (h, c, r, (q + d) % nh)
        here = pl.ds(pl.multiple_of(k * ck, ck), ck)
        return remote(gnp.at[rows], rcv2.at[d - 1, here], pe_s.at[d, k], pe_r.at[d, k], to)

    def second_half(u, carry):
        partial(c * half_rows + own_rows(1 + u // n_blk), u % n_blk)
        return carry

    lax.fori_loop(0, nh * n_blk, second_half, 0)

    for k in range(n_half):
        to_mate(k).wait_recv()

    def added(d, k):
        rows = pl.ds(pl.multiple_of(c * half_rows + own_rows(d) + k * ck, ck), ck)
        theirs = pl.ds(pl.multiple_of(own_rows(d) + k * ck, ck), ck)
        return rows, gnp[rows, :].astype(F32) + rcv[theirs, :].astype(F32)

    def pass_on(u, carry):
        d, k = 1 + u // n_blk, u % n_blk
        rows, total = added(d, k)
        gnp[rows, :] = total.astype(BF)
        to_peer(d, k).start()
        return carry

    lax.fori_loop(0, (nh - 1) * n_blk, pass_on, 0)

    w = 2 * h + c

    def plane_out(dh, dc):
        to = (hi_to(h, dh, hi_n), (c + dc) % 2, r, q)
        return remote(own, og.at[w], c_s.at[dh, dc], c_r.at[dh, dc], to)

    for i in range(n):
        @pl.when(zed != i)
        def _():
            remote(zos.at[i], zo.at[i], zo_s.at[i], zo_r.at[i], mate).wait_recv()

        @pl.when(zed == i)
        def _():
            keep_out_z(i).wait()

    out_rows = zo[0].astype(F32)
    for i in range(1, n):
        out_rows = out_rows + zo[i].astype(F32)
    own[...] = out_rows.astype(BF)
    og[w] = own[...]
    for dh in range(hi_n):
        for dc in range(2):
            if dh or dc:
                plane_out(dh, dc).start()

    cut = 3 * sw // hi_n

    def hi_part(dh):
        to = hi_to(h, dh, hi_n)
        return remote(dwq.at[to], r1.at[dh - 1], a_s.at[dh], a_r.at[dh], (to, c, r, q))

    for t in range(3):
        grad = tn(dcat[t], normed[...]).astype(BF)
        for i in range(hi_n):
            begin, end = max(t * sw, i * cut), min((t + 1) * sw, (i + 1) * cut)
            if begin < end:
                dwq[i, begin - i * cut : end - i * cut, :] = grad[begin - t * sw : end - t * sw]
    for dh in range(1, hi_n):
        hi_part(dh).start()

    partner = swap_to
    gg1[...] = jnp.zeros_like(gg1)

    def send_gi(k):
        rows = pl.ds(pl.multiple_of(k * ck, ck), ck)
        return remote(gis.at[rows], gi.at[rows], gi_s.at[k], gi_r.at[k], partner)

    def keep_gi(k):
        rows = pl.ds(pl.multiple_of(k * ck, ck), ck)
        return pltpu.make_async_copy(gis.at[rows], gi.at[rows], gi_s.at[k])

    def last_sums(k, carry):
        rows = pl.ds(pl.multiple_of(k * ck, ck), ck)
        for d in range(1, nh):
            to_peer(d, k).wait_recv()
        _, grad_n = added(0, k)
        for d in range(1, nh):
            grad_n = grad_n + rcv2[d - 1, rows, :].astype(F32)
        here = pl.ds(pl.multiple_of(p * tok + k * ck, ck), ck)
        xf = xa[here, :].astype(F32)
        inv = lax.rsqrt(jnp.mean(xf * xf, axis=-1, keepdims=True) + EPSILON)
        gg1[...] += jnp.sum((grad_n * xf * inv).reshape(-1, 8, width), axis=0)
        scaled = grad_n * g1[...]
        dot = jnp.sum(scaled * xf, axis=-1, keepdims=True)
        gis[rows, :] = (
            gh[rows, :] + scaled * inv - xf * (inv * inv * inv * dot / width)
        ).astype(BF)

        @pl.when(c != r)
        def _():
            send_gi(k).start()

        @pl.when(same)
        def _():
            keep_gi(k).start()

        return carry

    lax.fori_loop(0, n_blk, last_sums, 0)

    def hi_small(dh):
        to = (hi_to(h, dh, hi_n), c, r, q)
        return remote(sm, s1.at[h], b_s.at[dh], b_r.at[dh], to)

    sm[...] = jnp.zeros_like(sm)
    sm[0:1, :] = jnp.sum(gg1[...], axis=0, keepdims=True)
    sm[1:2, :] = jnp.sum(gg2[...], axis=0, keepdims=True)
    sm[2:3, :sw] = jnp.sum(values_sq[...], axis=0, keepdims=True)
    sm[3:4, :sw] = jnp.sum(squares[...], axis=0, keepdims=True)
    for dh in range(1, hi_n):
        hi_small(dh).start()
    s1[h] = sm[...]
    reduce_chunk(rest[-1])
    for dh in range(1, hi_n):
        source = hi_from(h, dh, hi_n)
        remote(sm, s1.at[source], b_s.at[dh], b_r.at[dh], mate).wait_recv()
    small = s1[0]
    for i in range(1, hi_n):
        small = small + s1[i]
    spot = c * n + zed
    s2[spot] = small

    def plane_small(k):
        dc, dz = k // n, k % n
        z = (zed + dz) % n
        to = (h, (c + dc) % 2, z // nh, z % nh)
        return remote(s2.at[spot], s2.at[spot], d_s.at[k], d_r.at[k], to)

    def small_arrives(k):
        dc, dz = k // n, k % n
        source = ((c + dc) % 2) * n + (zed + n - dz) % n
        return remote(s2.at[source], s2.at[source], d_s.at[k], d_r.at[k], mate)

    for k in range(1, 2 * n):
        plane_small(k).start()

    part_sum = dwq[h].astype(F32)
    for dh in range(1, hi_n):
        hi_part(dh).wait_recv()
        part_sum = part_sum + r1[dh - 1].astype(F32)
    mine[...] = part_sum.astype(BF)
    across = remote(mine, r2, e_s, e_r, (h, c, 1 - r, q))

    @pl.when(c != r)
    def _():
        across.start()

    for k in range(1, 2 * n):
        small_arrives(k).wait_recv()
    whole = s2[0]
    for k in range(1, 2 * n):
        whole = whole + s2[k]
    total_small[...] = whole

    def spread(dh):
        to = (hi_to(h, dh, hi_n), c, r, q)
        return remote(fin.at[h], fin.at[h], f_s.at[dh], f_r.at[dh], to)

    def share(dh):
        source = hi_from(h, dh, hi_n)
        return remote(fin.at[source], fin.at[source], m_s.at[dh], m_r.at[dh], mate)

    @pl.when(same)
    def _():
        across.wait_recv()
        fin[h] = (mine[...].astype(F32) + r2[...].astype(F32)).astype(BF)
        for dh in range(1, hi_n):
            spread(dh).start()
        share(0).start()
        for dh in range(1, hi_n):
            source = hi_from(h, dh, hi_n)
            remote(fin.at[h], fin.at[source], f_s.at[dh], f_r.at[dh], mate).wait_recv()
            share(dh).start()

    @pl.when(c != r)
    def _():
        for dh in range(hi_n):
            share(dh).wait_recv()
        across.wait_send()

    @pl.when(same)
    def _():
        for dh in range(1, hi_n):
            spread(dh).wait_send()
        for dh in range(hi_n):
            share(dh).wait_send()

    for k in range(n_blk):
        @pl.when(c != r)
        def _():
            send_gi(k).wait_send()
            send_gi(k).wait_recv()

        @pl.when(same)
        def _():
            keep_gi(k).wait()

    for k in range(n_half):
        to_mate(k).wait_send()
    for d in range(1, nh):
        for k in range(n_blk):
            to_peer(d, k).wait_send()
    for dh in range(hi_n):
        for dc in range(2):
            if dh or dc:
                theirs = 2 * hi_from(h, dh, hi_n) + (c + dc) % 2
                remote(own, og.at[theirs], c_s.at[dh, dc], c_r.at[dh, dc], mate).wait_recv()
                plane_out(dh, dc).wait_send()
    for dh in range(1, hi_n):
        hi_small(dh).wait_send()
        hi_part(dh).wait_send()
    for k in range(1, 2 * n):
        plane_small(k).wait_send()

    def drain(pair, carry):
        lanes = lane_window(pair, pw, sw)
        for b in range(n):
            @pl.when(p != b)
            def _():
                send_do(b, pair).wait_send()

            @pl.when(jnp.logical_or(c != r, p != b))
            def _():
                send_gv(b, pair).wait_send()
                remote(
                    gow.at[b, :, lanes], gv_at(b, pair), gv_s.at[pair, b], gv_r.at[pair, b], mate
                ).wait_recv()

        @pl.when(same)
        def _():
            keep_gv(pair).wait()

        return carry

    lax.fori_loop(0, pairs, drain, 0)

    @pl.when(c != r)
    def _():
        send_lo().wait_send()
        send_lo().wait_recv()

    for dh in range(1, hi_n):
        out_over_hi(dh).wait_send()
        for i in order[:-1]:
            over_hi(dh, i).wait_send()
    for i in range(n):
        @pl.when(zed != i)
        def _():
            out_over_z(i).wait_send()

    keep_z().wait()
    for t in range(1, n):
        over_z(t).wait_send()
        if t <= nh:
            over_z(t).wait_recv()


def attention_backward(sizes, ga, ds, dos, lo, rx0, xa, ws, g1, tables, seg, *saved):
    _, _, _, nh = sizes
    n, tok, sw = ga.shape
    row_len, width = xa.shape
    pw = tables[0].shape[1]
    pairs = sw // pw
    block = max(tok, 512)
    ck = min(256, tok)
    n_half = row_len // 2 // ck
    n_blk = tok // ck
    hi_n = sizes[0]
    _, _, _, ffs, dw = ds.shape
    rw = dos.shape[2]
    others = max(hi_n - 1, 1)
    cut = 3 * sw // hi_n
    return pl.pallas_call(
        functools.partial(backward_kernel, sizes, block),
        out_shape=(
            jax.ShapeDtypeStruct((n, tok, sw) if sw % 128 else (tok, width), BF),
            jax.ShapeDtypeStruct((tok, width), BF),
            jax.ShapeDtypeStruct((hi_n, cut, width), BF),
            jax.ShapeDtypeStruct((2 * hi_n, rw, width), BF),
            jax.ShapeDtypeStruct((8, width), F32),
            jax.ShapeDtypeStruct((tok, width), BF),
            jax.ShapeDtypeStruct((others, n, 3, ffs, dw), BF),
            jax.ShapeDtypeStruct((others, n, rw, width), BF),
            jax.ShapeDtypeStruct((nh + 1, 3, ffs, dw), BF),
        ),
        in_specs=[ANY] * 5 + [VM] * 17,
        out_specs=(ANY, ANY, VM, VM, VM) + (ANY,) * 4,
        scratch_shapes=[
            pltpu.VMEM((n, tok, sw), BF),
            pltpu.VMEM((row_len, width), BF),
            pltpu.VMEM((row_len, pw), F32),
            pltpu.VMEM((row_len, pw), F32),
            pltpu.VMEM((row_len, pw), F32),
            pltpu.VMEM((3, row_len, sw), BF),
            pltpu.VMEM((n, tok, sw), BF),
            pltpu.VMEM((row_len, width), BF),
            pltpu.VMEM((row_len // 2, width), BF),
            pltpu.VMEM((max(nh - 1, 1), tok, width), BF),
            pltpu.VMEM((tok, width), BF),
            pltpu.VMEM((hi_n, 3, ffs, dw), BF),
            pltpu.VMEM((n, 3, ffs, dw), BF),
            pltpu.VMEM((n, rw, width), BF),
            pltpu.VMEM((n, rw, width), BF),
            pltpu.VMEM((max(nh - 1, 1), 3, ffs, dw), BF),
            pltpu.VMEM((hi_n, cut, width), BF),
            pltpu.VMEM((8, width), F32),
            pltpu.VMEM((n, rw, width), BF),
            pltpu.VMEM((8, width), F32),
            pltpu.VMEM((hi_n, 8, width), F32),
            pltpu.VMEM((2 * n, 8, width), F32),
            pltpu.VMEM((others, cut, width), BF),
            pltpu.VMEM((cut, width), BF),
            pltpu.VMEM((rw, width), BF),
            pltpu.VMEM((cut, width), BF),
            DMA((pairs, n)), DMA((pairs, n)),
            DMA((pairs, n)), DMA((pairs, n)),
            DMA((n_half,)), DMA((n_half,)),
            DMA((nh, n_blk)), DMA((nh, n_blk)),
            DMA((n_blk,)), DMA((n_blk,)),
            DMA((1 + pairs,)),
            DMA((hi_n, n)), DMA((hi_n, n)),
            DMA((hi_n,)), DMA((hi_n,)),
            DMA, DMA,
            DMA((hi_n,)),
            DMA((n,)), DMA((n,)),
            DMA((n,)), DMA((n,)),
            DMA((hi_n,)), DMA((hi_n,)),
            DMA((hi_n,)), DMA((hi_n,)),
            DMA((hi_n, 2)), DMA((hi_n, 2)),
            DMA((2 * n,)), DMA((2 * n,)),
            DMA, DMA,
            DMA((hi_n,)), DMA((hi_n,)),
            DMA((hi_n,)), DMA((hi_n,)),
        ],
        name="attention_backward",
        compiler_params=pltpu.CompilerParams(
            collective_id=3, has_side_effects=True, vmem_limit_bytes=VMEM_MAX
        ),
        cost_estimate=pl.CostEstimate(
            flops=60 << 30, bytes_accessed=24 << 20, transcendentals=row_len * row_len * sw // 128
        ),
    )(ga, ds, dos, lo, rx0, xa, ws, g1, *tables, seg, *saved)


def per_device(sizes, layer_in, value_first, seg_start, gain_one, w_qkv, w_out, gain_two, w_mlp, grad_out):
    hi_n, _, _, nh = sizes
    n = 2 * nh
    wide = 2 * hi_n
    tok, width = layer_in.shape
    sw = w_qkv.shape[1]
    row_len = n * tok
    h, c, r, q = coords()

    w_mlp_t = jnp.transpose(w_mlp, (1, 2, 0))
    sg = jnp.full((8, 128), seg_start[1].astype(F32))
    w_cut = w_qkv.reshape(hi_n, 3 * sw // hi_n, width)
    wo_cut = w_out.reshape(wide, sw // wide, width)
    v_cut = value_first.reshape(tok, n, sw).transpose(1, 0, 2) if sw % 128 else value_first
    xa, ws, so, near, cross, oz = exchange_inputs(sizes, layer_in, w_cut, sg, w_mlp_t, wo_cut)
    ws = ws.reshape(3 * sw, width)

    tables = rope_parts(row_len, min(sw, 128))
    g1 = gain_one.reshape(1, width)
    g2 = gain_two.reshape(1, width)
    xr = xa.reshape(row_len, width)
    ai, dy_in, far, late, oh, qo, ko, mo, ao, lse, squares, values_sq = attention_forward(
        sizes, v_cut, grad_out, cross, oz, xr, ws, g1, tables, so
    )
    lo, gh, ga, ds, dos, gg2, _, _, rx0 = feed_forward(xa, grad_out, dy_in, near, far, late, oh, ai, g2)
    gv, gi, fin, og, sums, lo_in, _, _, zr = attention_backward(
        sizes, ga, ds, dos, lo, rx0, xr, ws, g1, tables, so, qo, ko, mo, ao, lse, gh, gg2, squares, values_sq
    )

    layer_out = jnp.where(c == r, lo, lo_in)
    grad_value_first = (gv.transpose(1, 0, 2).reshape(tok, width) if sw % 128 else gv).astype(F32)
    grad_in = gi.astype(F32)
    grad_w_mlp = jnp.transpose(jnp.sum(zr.astype(F32), axis=0), (2, 0, 1))
    grad_w_out = og.reshape(sw, width).astype(F32)
    grad_w_qkv = fin.reshape(3, sw, width).astype(F32)
    entries = tok * width * wide * n
    value_norms = jnp.sqrt(jnp.sum(sums[2:4], axis=1) / entries)
    return (
        layer_out,
        grad_in,
        grad_value_first,
        sums[0],
        grad_w_qkv,
        grad_w_out,
        sums[1],
        grad_w_mlp,
        value_norms,
    )


def solution(mesh):
    wide, narrow = mesh.shape["wide"], mesh.shape["narrow"]
    sizes = (wide // 2, 2, 2, narrow // 2)
    fine = Mesh(mesh.devices.reshape(sizes), AXES)
    w_axes, n_axes = ("hi", "core"), ("zh", "zq")
    rows = P(AXES, None)
    return jax.shard_map(
        functools.partial(per_device, sizes),
        mesh=fine,
        in_specs=(
            rows,
            rows,
            P(w_axes),
            P(),
            P(None, n_axes, None),
            P(n_axes, None),
            P(),
            P(w_axes, None, n_axes),
            rows,
        ),
        out_specs=(
            rows,
            rows,
            rows,
            P(),
            P(None, n_axes, None),
            P(n_axes, None),
            P(),
            P(w_axes, None, n_axes),
            P(),
        ),
        check_vma=False,
    )
```

```python
import functools

import jax
import jax.numpy as jnp
import numpy as np
from jax import lax
from jax.experimental import pallas as pl
from jax.experimental.pallas import tpu as pltpu
from jax.sharding import Mesh, PartitionSpec as P

HEAD_DIM = 64
EPSILON = 1e-06
BF = jnp.bfloat16
F32 = jnp.float32
AXES = ("hi", "core", "zh", "zq")
MESH = pl.DeviceIdType.MESH
ANY = pl.BlockSpec(memory_space=pl.ANY)
VM = pl.BlockSpec(memory_space=pltpu.VMEM)
VMEM_MAX = 62 << 20
DMA = pltpu.SemaphoreType.DMA


def nn(a, b):
    return lax.dot_general(a, b, (((1,), (0,)), ((), ())), preferred_element_type=F32)


def nt(a, b):
    return lax.dot_general(a, b, (((1,), (1,)), ((), ())), preferred_element_type=F32)


def tn(a, b):
    return lax.dot_general(a, b, (((0,), (0,)), ((), ())), preferred_element_type=F32)


def coords():
    return tuple(lax.axis_index(name) for name in AXES)


def remote(src, dst, send, recv, to):
    return pltpu.make_async_remote_copy(
        src_ref=src, dst_ref=dst, send_sem=send, recv_sem=recv, device_id=to, device_id_type=MESH
    )


def hi_to(h, dh, hi_n):
    if hi_n % 2:
        return (h + dh) % hi_n
    half = hi_n // 2
    return (h // 2 + dh // 2) % half * 2 + (h + dh) % 2


def hi_from(h, dh, hi_n):
    if hi_n % 2:
        return (h + hi_n - dh) % hi_n
    half = hi_n // 2
    return (h // 2 + half - dh // 2) % half * 2 + (h + dh) % 2


def greet_plane(sizes, with_hi, cores=1):
    hi_n, _, _, nh = sizes
    h, c, r, q = coords()
    barrier = pltpu.get_barrier_semaphore()
    count = 0
    for dc in range(2):
        for dr in range(2):
            for dq in range(nh):
                if dc or dr or dq:
                    to = (h, (c + dc) % 2, (r + dr) % 2, (q + dq) % nh)
                    pl.semaphore_signal(barrier, inc=1, device_id=to, device_id_type=MESH)
                    count += 1
    if with_hi:
        for dh in range(1, hi_n):
            for dc in range(cores):
                to = (hi_to(h, dh, hi_n), (c + dc) % 2, r, q)
                pl.semaphore_signal(barrier, inc=1, device_id=to, device_id_type=MESH)
                count += 1
    pl.semaphore_wait(barrier, count)


def rotate_lanes(values, first):
    width = values.shape[1]
    if width < 128:
        return jnp.concatenate([values[:, 32:], values[:, :32]], axis=1)
    return jnp.where(
        first, pltpu.roll(values, width - 32, 1), pltpu.roll(values, 32, 1)
    )


def first_lanes(rows, width):
    lane = lax.broadcasted_iota(jnp.int32, (rows, width), 1)
    return lane % HEAD_DIM < HEAD_DIM // 2


def lane_window(pair, pw, sw):
    return slice(0, sw) if pw == sw else pl.ds(pl.multiple_of(pair * pw, pw), pw)


def rope_rows(lo_c, lo_s, hi_c, hi_s, flag, i, rows):
    step = lo_c.shape[0]
    half = hi_c.shape[0] // 2
    cos, sin = [], []
    for u in range(rows // step):
        k = i * (rows // step) + u
        far, near = pl.ds(k, 1), pl.ds(k % half, 1)
        ch = hi_c[near, :] * flag + hi_c[far, :] * (1.0 - flag)
        sh = hi_s[near, :] * flag + hi_s[far, :] * (1.0 - flag)
        cos.append(lo_c[...] * ch - lo_s[...] * sh)
        sin.append(lo_s[...] * ch + lo_c[...] * sh)
    cos = jnp.concatenate(cos, axis=0)
    sin = jnp.concatenate(sin, axis=0)
    return cos, jnp.where(first_lanes(rows, cos.shape[1]), -sin, sin)


def rope_parts(row_len, pw):
    half = HEAD_DIM // 2
    frequency = 10000.0 ** (-2.0 * np.arange(half) / HEAD_DIM)
    frequency = np.tile(frequency, pw // half)[None, :]
    lo = np.arange(64)[:, None] * frequency
    hi = 64.0 * np.arange(row_len // 64)[:, None] * frequency
    return tuple(jnp.asarray(t, F32) for t in (np.cos(lo), np.sin(lo), np.cos(hi), np.sin(hi)))


def columns_of(ref, s, start, size, sw):
    if len(ref.shape) == 3:
        return ref.at[s]
    start = s * sw + start
    start = start if isinstance(start, int) else pl.multiple_of(start, size)
    return ref.at[:, pl.ds(start, size)]


def tiled(table, width):
    times = width // table.shape[1]
    return table if times == 1 else jnp.concatenate([table] * times, axis=1)


def exchange_kernel(
    sizes, chunks, x, w, sg, wt, wo, xa, ws, so, g1, cross, oz,
    xs, wb, sb, tb, ob,
    swap_s, swap_r, peer_s, peer_r, core_s, core_r, w_s, w_r, wh_s, wh_r, sg_s, sg_r, loc,
    oz_s, oz_r, gp_s, gp_r, gh_s, gh_r, cr_s, cr_r,
):
    hi_n, _, _, nh = sizes
    n = 2 * nh
    h, c, r, q = coords()
    p = c * nh + q
    zed = r * nh + q
    partner_p = r * nh + q
    rows = x.shape[0] // chunks
    same = c == r
    other = c != r
    partner = (h, r, c, q)
    mate = (h, 1 - c, r, q)
    greet_plane(sizes, True)

    def part(k):
        return pl.ds(k * rows, rows)

    def swap_x(k):
        return remote(x.at[part(k)], xa.at[partner_p, part(k)], swap_s.at[k], swap_r.at[k], partner)

    def own_arrives(k):
        return remote(x.at[part(k)], xa.at[p, part(k)], swap_s.at[k], swap_r.at[k], partner)

    def push_peer(src, k, dq):
        to = (h, c, r, (q + dq) % nh)
        return remote(src, xa.at[p, part(k)], peer_s.at[dq, k], peer_r.at[dq, k], to)

    def push_mate(src, k, dq):
        block = c * nh + (q + nh - dq) % nh
        return remote(src, xa.at[block, part(k)], core_s.at[dq, k], core_r.at[dq, k], mate)

    def send_w():
        return remote(w.at[h], ws.at[h], w_s, w_r, partner)

    def spread_w(dh):
        to = (hi_to(h, dh, hi_n), c, r, q)
        return remote(ws.at[h], ws.at[h], wh_s.at[dh], wh_r.at[dh], to)

    def send_sg():
        return remote(sg, so, sg_s, sg_r, partner)

    def shard_peer(dq):
        to = (h, c, r, (q + dq) % nh)
        return remote(wt, g1.at[h, (nh - dq) % nh], gp_s.at[dq], gp_r.at[dq], to)

    def shard_hi(src, dh, t):
        to = (hi_to(h, dh, hi_n), c, r, q)
        return remote(src, g1.at[h, t], gh_s.at[dh, t], gh_r.at[dh, t], to)

    def shard_cross():
        return remote(wt, cross, cr_s, cr_r, (h, c, 1 - r, q))

    def rows_z(dz):
        z = (zed + dz) % n
        return remote(
            wo.at[2 * h + c], oz.at[zed], oz_s.at[dz], oz_r.at[dz], (h, c, z // nh, z % nh)
        )

    def from_hi(dh):
        return hi_from(h, dh, hi_n)

    local = [
        (pltpu.make_async_copy(wt, tb, loc.at[0]), pltpu.make_async_copy(tb, g1.at[h, 0], loc.at[5])),
        (
            pltpu.make_async_copy(wo.at[2 * h + c], ob, loc.at[1]),
            pltpu.make_async_copy(ob, oz.at[zed], loc.at[6]),
        ),
    ]
    local_same = [
        (pltpu.make_async_copy(x, xs, loc.at[2]), pltpu.make_async_copy(xs, xa.at[p], loc.at[7])),
        (pltpu.make_async_copy(w, wb, loc.at[3]), pltpu.make_async_copy(wb, ws, loc.at[8])),
        (pltpu.make_async_copy(sg, sb, loc.at[4]), pltpu.make_async_copy(sb, so, loc.at[9])),
    ]

    @pl.when(other)
    def _():
        send_sg().start()
        send_w().start()
        for k in range(chunks):
            swap_x(k).start()

    @pl.when(same)
    def _():
        for k in range(chunks):
            for dq in range(1, nh):
                push_peer(x.at[part(k)], k, dq).start()
            push_mate(x.at[part(k)], k, 0).start()
        for get, _ in local_same:
            get.start()

    for dq in range(1, nh):
        shard_peer(dq).start()
    for dh in range(1, hi_n):
        shard_hi(wt, dh, 0).start()
    for dz in range(1, n):
        rows_z(dz).start()
    shard_cross().start()
    for get, _ in local:
        get.start()

    @pl.when(other)
    def _():
        send_w().wait_recv()
        for dh in range(1, hi_n):
            spread_w(dh).start()

    for dq in range(1, nh):
        remote(wt, g1.at[h, (nh - dq) % nh], gp_s.at[dq], gp_r.at[dq], mate).wait_recv()
        t = (nh - dq) % nh
        for dh in range(1, hi_n):
            shard_hi(g1.at[h, t], dh, t).start()

    @pl.when(other)
    def _():
        for k in range(chunks):
            own_arrives(k).wait_recv()
            for dq in range(1, nh):
                push_peer(xa.at[p, part(k)], k, dq).start()
            push_mate(xa.at[p, part(k)], k, 0).start()

    for get, put in local:
        get.wait()
        put.start()

    @pl.when(same)
    def _():
        for get, put in local_same:
            get.wait()
            put.start()

    for k in range(chunks):
        for dq in range(1, nh):
            block = c * nh + (q + nh - dq) % nh
            remote(
                x.at[part(k)], xa.at[block, part(k)], peer_s.at[dq, k], peer_r.at[dq, k], mate
            ).wait_recv()
            push_mate(xa.at[block, part(k)], k, dq).start()

    for k in range(chunks):
        for dq in range(nh):
            block = (1 - c) * nh + (q + nh - dq) % nh
            remote(
                x.at[part(k)], xa.at[block, part(k)], core_s.at[dq, k], core_r.at[dq, k], mate
            ).wait_recv()

    @pl.when(other)
    def _():
        send_sg().wait_recv()
        for dh in range(1, hi_n):
            source = from_hi(dh)
            remote(ws.at[source], ws.at[source], wh_s.at[dh], wh_r.at[dh], mate).wait_recv()
        send_sg().wait_send()
        send_w().wait_send()
        for dh in range(1, hi_n):
            spread_w(dh).wait_send()
        for k in range(chunks):
            swap_x(k).wait_send()

    for k in range(chunks):
        for dq in range(1, nh):
            push_peer(x.at[part(k)], k, dq).wait_send()
        for dq in range(nh):
            push_mate(x.at[part(k)], k, dq).wait_send()

    @pl.when(same)
    def _():
        for _, put in local_same:
            put.wait()

    for dq in range(1, nh):
        shard_peer(dq).wait_send()
    for dz in range(1, n):
        z = (zed + n - dz) % n
        remote(wo.at[0], oz.at[z], oz_s.at[dz], oz_r.at[dz], mate).wait_recv()
        rows_z(dz).wait_send()
    for t in range(nh):
        for dh in range(1, hi_n):
            shard_hi(wt, dh, t).wait_send()
            remote(wt, g1.at[from_hi(dh), t], gh_s.at[dh, t], gh_r.at[dh, t], mate).wait_recv()
    shard_cross().wait_recv()
    shard_cross().wait_send()
    for _, put in local:
        put.wait()


def exchange_inputs(sizes, x, w, sg, wt, wo):
    hi_n, _, _, nh = sizes
    n = 2 * nh
    tok, width = x.shape
    chunks = 4 if tok % 64 == 0 else 1
    return pl.pallas_call(
        functools.partial(exchange_kernel, sizes, chunks),
        out_shape=(
            jax.ShapeDtypeStruct((n, tok, width), BF),
            jax.ShapeDtypeStruct(w.shape, BF),
            jax.ShapeDtypeStruct(sg.shape, F32),
            jax.ShapeDtypeStruct((hi_n, nh) + wt.shape, BF),
            jax.ShapeDtypeStruct(wt.shape, BF),
            jax.ShapeDtypeStruct((n,) + wo.shape[1:], BF),
        ),
        in_specs=[ANY] * 5,
        out_specs=(ANY,) * 6,
        scratch_shapes=[
            pltpu.VMEM((tok, width), BF),
            pltpu.VMEM(w.shape, BF),
            pltpu.VMEM(sg.shape, F32),
            pltpu.VMEM(wt.shape, BF),
            pltpu.VMEM(wo.shape[1:], BF),
            DMA((chunks,)), DMA((chunks,)),
            DMA((nh, chunks)), DMA((nh, chunks)),
            DMA((nh, chunks)), DMA((nh, chunks)),
            DMA, DMA,
            DMA((hi_n,)), DMA((hi_n,)),
            DMA, DMA,
            DMA((10,)),
            DMA((n,)), DMA((n,)),
            DMA((nh,)), DMA((nh,)),
            DMA((hi_n, nh)), DMA((hi_n, nh)),
            DMA, DMA,
        ],
        name="exchange_inputs",
        compiler_params=pltpu.CompilerParams(collective_id=1, has_side_effects=True),
        cost_estimate=pl.CostEstimate(flops=0, bytes_accessed=160 << 20, transcendentals=0),
    )(x, w, sg, wt, wo)


def masked(scores, diagonal, crossing, causal, bias):
    if diagonal:
        return jnp.where(causal, scores, -1e30)
    if crossing:
        return scores + bias
    return scores


def forward_kernel(
    sizes, block, v, gout, cross, oz, xa, ws, g1, lo_c, lo_s, hi_c, hi_s, seg,
    ai, dy_in, g2, late, oh, qo, ko, mo, ao, lse, own, vsq,
    va, own_rows, tb, ob,
    att_s, att_r, loc, v_s, v_r, dy_s, dy_r, gp_s, gp_r, gh_s, gh_r, oh_s, oh_r, lc,
):
    hi_n, _, _, nh = sizes
    n = 2 * nh
    h, c, r, q = coords()
    p = c * nh + q
    row_len, sw = qo.shape
    tok = row_len // n
    short = row_len // 2
    pw = lo_c.shape[1]
    pairs = sw // pw
    halves = pw // HEAD_DIM
    mate = (h, 1 - c, r, q)
    other = c != r
    greet_plane(sizes, True)

    def send_v(s, pair):
        lanes = lane_window(pair, pw, sw)
        to = (h, s // nh, c, s % nh)
        spot = r * nh + q
        return remote(
            columns_of(v, s, pair * pw, pw, sw), va.at[spot, :, lanes],
            v_s.at[pair, s], v_r.at[pair, spot], to,
        )

    def v_arrives(b, pair):
        lanes = lane_window(pair, pw, sw)
        return remote(
            columns_of(v, 0, 0, pw, sw), va.at[b, :, lanes], v_s.at[pair, b], v_r.at[pair, b], mate
        )

    def send_dy():
        return remote(gout, dy_in, dy_s, dy_r, (h, r, c, q))

    def shard_hi(dh):
        to = (hi_to(h, dh, hi_n), c, r, q)
        return remote(cross, g2.at[h], gh_s.at[dh], gh_r.at[dh], to)

    def late_peer(dq):
        to = (h, c, r, (q + dq) % nh)
        return remote(cross, late.at[nh - dq - 1], gp_s.at[dq], gp_r.at[dq], to)

    def rows_hi(dh):
        to = (hi_to(h, dh, hi_n), c, r, q)
        return remote(oz, oh.at[h], oh_s.at[dh], oh_r.at[dh], to)

    def from_hi(dh):
        return hi_from(h, dh, hi_n)

    keep_v = pltpu.make_async_copy(columns_of(v, p, 0, sw, sw), va.at[p], lc.at[0])
    local = [
        (pltpu.make_async_copy(cross, tb, lc.at[1]), pltpu.make_async_copy(tb, g2.at[h], lc.at[3])),
        (pltpu.make_async_copy(oz, ob, lc.at[2]), pltpu.make_async_copy(ob, oh.at[h], lc.at[4])),
    ]
    for pair in range(pairs):
        for s in range(n):
            @pl.when(jnp.logical_or(other, p != s))
            def _():
                send_v(s, pair).start()

    @pl.when(c == r)
    def _():
        keep_v.start()

    for dh in range(1, hi_n):
        shard_hi(dh).start()
    for dh in range(1, hi_n):
        rows_hi(dh).start()
    for dq in range(1, nh):
        late_peer(dq).start()

    @pl.when(other)
    def _():
        send_dy().start()

    for get, _ in local:
        get.start()

    br = 256
    own[...] = jnp.zeros_like(own)
    flag = seg[0:1, 0:1]

    def project(i, carry):
        rows = pl.ds(pl.multiple_of(i * br, br), br)
        xf = xa[rows, :].astype(F32)
        inv = lax.rsqrt(jnp.mean(xf * xf, axis=-1, keepdims=True) + EPSILON)
        normed = (xf * inv * g1[...]).astype(BF)
        raw = nt(normed, ws[...])
        first = first_lanes(br, sw)
        ct, st = rope_rows(lo_c, lo_s, hi_c, hi_s, flag, i, br)
        ct, st = tiled(ct, sw), tiled(st, sw)
        q_raw = raw[:, :sw]
        k_raw = raw[:, sw : 2 * sw]
        own_vals = raw[:, 2 * sw :]
        q_rot = (q_raw * ct + rotate_lanes(q_raw, first) * st).astype(BF)
        qo[rows, :] = (q_rot.astype(F32) * HEAD_DIM**-0.5).astype(BF)
        ko[rows, :] = (k_raw * ct + rotate_lanes(k_raw, first) * st).astype(BF)
        own_rows[rows, :] = own_vals
        own[...] += jnp.sum((own_vals * own_vals).reshape(br // 8, 8, sw), axis=0)
        return carry

    lax.fori_loop(0, row_len // br, project, 0)

    for get, put in local:
        get.wait()
        put.start()
    @pl.when(c == r)
    def _():
        keep_v.wait()

    bias = flag * -1e30
    blocks = row_len // block
    per = block // tok
    causal = lax.broadcasted_iota(jnp.int32, (block, block), 0) >= lax.broadcasted_iota(
        jnp.int32, (block, block), 1
    )

    def send(b, pair):
        lanes = lane_window(pair, pw, sw)
        to = (h, b // nh, r, b % nh)
        return remote(
            ao.at[b, :, lanes], ai.at[p, :, lanes], att_s.at[pair, b], att_r.at[pair, p], to
        )

    def keep(pair):
        lanes = lane_window(pair, pw, sw)
        return pltpu.make_async_copy(ao.at[p, :, lanes], ai.at[p, :, lanes], loc.at[pair])

    def pair_step(pair, carry):
        lanes = lane_window(pair, pw, sw)
        for b in range(n):
            @pl.when(jnp.logical_or(other, p != b))
            def _():
                v_arrives(b, pair).wait_recv()

        sums = 0.0
        for b in range(n):
            rows = pl.ds(b * tok, tok)
            values = va[b, :, lanes].astype(F32)
            sums = sums + jnp.sum((values * values).reshape(tok // 8, 8, pw), axis=0)
            mo[rows, lanes] = (0.5 * own_rows[rows, lanes] + 0.5 * values).astype(BF)
        vsq[:, lanes] = sums
        for i in range(blocks):
            outs = []
            rows = pl.ds(i * block, block)
            for half in range(halves):
                cols = slice(half * HEAD_DIM, (half + 1) * HEAD_DIM)
                qh = qo[rows, lanes][:, cols]
                score = []
                for j in range(i + 1):
                    kj = ko[pl.ds(j * block, block), lanes][:, cols]
                    crossing = i * block >= short and j * block < short
                    score.append(masked(nt(qh, kj), i == j, crossing, causal, bias))
                top = functools.reduce(
                    jnp.maximum, [jnp.max(s, axis=-1, keepdims=True) for s in score]
                )
                total = 0.0
                acc = 0.0
                for j in range(i + 1):
                    e = jnp.exp(score[j] - top)
                    total = total + jnp.sum(e, axis=-1, keepdims=True)
                    vj = mo[pl.ds(j * block, block), lanes][:, cols]
                    acc = acc + nn(e.astype(BF), vj)
                outs.append(acc / total)
                lse[pair, rows, half : half + 1] = top + jnp.log(total)
            out = (jnp.concatenate(outs, axis=1) if halves > 1 else outs[0]).astype(BF)
            for t in range(per):
                b = i * per + t
                ao[b, :, lanes] = out[t * tok : (t + 1) * tok]

                @pl.when(p != b)
                def _():
                    send(b, pair).start()

        keep(pair).start()
        return carry

    lax.fori_loop(0, pairs, pair_step, 0)

    def drain(pair, carry):
        lanes = lane_window(pair, pw, sw)
        for b in range(n):
            @pl.when(p != b)
            def _():
                send(b, pair).wait_send()
                remote(
                    ao.at[b, :, lanes], ai.at[b, :, lanes], att_s.at[pair, b], att_r.at[pair, b],
                    (h, 1 - c, r, q),
                ).wait_recv()
        keep(pair).wait()
        return carry

    lax.fori_loop(0, pairs, drain, 0)

    for pair in range(pairs):
        for s in range(n):
            @pl.when(jnp.logical_or(other, p != s))
            def _():
                send_v(s, pair).wait_send()

    for dh in range(1, hi_n):
        rows_hi(dh).wait_send()
        remote(oz, oh.at[from_hi(dh)], oh_s.at[dh], oh_r.at[dh], mate).wait_recv()
        shard_hi(dh).wait_send()
        remote(cross, g2.at[from_hi(dh)], gh_s.at[dh], gh_r.at[dh], mate).wait_recv()
    for dq in range(1, nh):
        late_peer(dq).wait_send()
        late_peer(dq).wait_recv()

    @pl.when(other)
    def _():
        send_dy().wait_send()
        send_dy().wait_recv()

    for _, put in local:
        put.wait()


def attention_forward(sizes, v, gout, cross, oz, xa, ws, g1, tables, seg):
    hi_n, _, _, nh = sizes
    n = 2 * nh
    row_len, width = xa.shape
    sw = ws.shape[0] // 3
    tok = row_len // n
    pw = tables[0].shape[1]
    pairs = sw // pw
    block = max(tok, 512)
    flops = 2 * row_len * width * 3 * sw + 2 * row_len * row_len * sw
    return pl.pallas_call(
        functools.partial(forward_kernel, sizes, block),
        out_shape=(
            jax.ShapeDtypeStruct((n, tok, sw), BF),
            jax.ShapeDtypeStruct((tok, width), BF),
            jax.ShapeDtypeStruct((hi_n,) + cross.shape, BF),
            jax.ShapeDtypeStruct((max(nh - 1, 1),) + cross.shape, BF),
            jax.ShapeDtypeStruct((hi_n,) + oz.shape, BF),
            jax.ShapeDtypeStruct((row_len, sw), BF),
            jax.ShapeDtypeStruct((row_len, sw), BF),
            jax.ShapeDtypeStruct((row_len, sw), BF),
            jax.ShapeDtypeStruct((n, tok, sw), BF),
            jax.ShapeDtypeStruct((pairs, row_len, pw // HEAD_DIM), F32),
            jax.ShapeDtypeStruct((8, sw), F32),
            jax.ShapeDtypeStruct((8, sw), F32),
        ),
        in_specs=[ANY] * 4 + [VM] * 8,
        out_specs=(ANY,) * 5 + (VM,) * 7,
        scratch_shapes=[
            pltpu.VMEM((n, tok, sw), BF),
            pltpu.VMEM((row_len, sw), F32),
            pltpu.VMEM(cross.shape, BF),
            pltpu.VMEM(oz.shape, BF),
            DMA((pairs, n)), DMA((pairs, n)), DMA((pairs,)),
            DMA((pairs, n)), DMA((pairs, n)),
            DMA, DMA,
            DMA((nh,)), DMA((nh,)),
            DMA((hi_n,)), DMA((hi_n,)),
            DMA((hi_n,)), DMA((hi_n,)),
            DMA((5,)),
        ],
        name="attention_forward",
        compiler_params=pltpu.CompilerParams(
            collective_id=2, has_side_effects=True, vmem_limit_bytes=VMEM_MAX
        ),
        cost_estimate=pl.CostEstimate(
            flops=4 * flops, bytes_accessed=16 << 20, transcendentals=row_len * row_len * sw // 128
        ),
    )(v, gout, cross, oz, xa, ws, g1, *tables, seg)


def mlp_kernel(
    xa, gout, dy_in, near, far, lp, oh, ai, g2, lo, gh, ga, dsum, dosum, gg2, theirs, late, rx0,
    x, dy, hid, n2, acc_o, acc_g, buf, rcv, bo, rcvo, wm, wo, oa, ob, first,
    x_s, buf_s, buf_r, bo_s, bo_r, ld, th_s, th_r, o_s, o_r, gh_s, gh_r, fi_s, fi_r,
):
    step = pl.program_id(0)
    n = ai.shape[0]
    nh = n // 2
    hi_n = wm.shape[2]
    wide = 2 * hi_n
    width = x.shape[1]
    dw = width // wide
    rw = bo.shape[3]
    h, c, r, q = coords()
    own_dy = pltpu.make_async_copy(gout, dy, ld.at[4])
    swapped_dy = pltpu.make_async_copy(dy_in, dy, ld.at[4])
    own_o = pltpu.make_async_copy(oh, oa, ld.at[5])

    mate = (h, 1 - c, r, q)

    def block_of(t):
        return near.at[:, t] if t < nh else far

    def give(t):
        return remote(block_of(t), theirs.at[t], th_s.at[t, 0], th_r.at[t, 0], mate)

    def late_hi(t, dh):
        to = (hi_to(h, dh, hi_n), c, r, q)
        u = t - nh - 1
        return remote(lp.at[u], late.at[h, u], gh_s.at[u, dh], gh_r.at[u, dh], to)

    def late_piece(t, dh):
        return late.at[hi_from(h, dh, hi_n), t - nh - 1] if dh else lp.at[t - nh - 1]

    def late_arrives(t, dh):
        u = t - nh - 1
        return remote(lp.at[u], late_piece(t, dh), gh_s.at[u, dh], gh_r.at[u, dh], mate)

    def give_late(t, dh):
        source = hi_from(h, dh, hi_n)
        return remote(
            late_piece(t, dh), theirs.at[t, source], th_s.at[t, dh], th_r.at[t, dh], mate
        )

    def load_late(t, dh):
        source = hi_from(h, dh, hi_n)
        return pltpu.make_async_copy(late_piece(t, dh), wm.at[t % 2, c, source], ld.at[t % 2])

    def first_over_hi(dh):
        to = hi_to(h, dh, hi_n)
        return remote(first.at[to], rx0.at[dh - 1], fi_s.at[dh], fi_r.at[dh], (to, c, r, q))

    def give_o():
        return remote(oh, ob, o_s, o_r, (h, 1 - c, r, q))

    def load_own(src, at):
        return pltpu.make_async_copy(src, wm.at[at, c], ld.at[at])

    def load_theirs(t, at):
        return pltpu.make_async_copy(theirs.at[t], wm.at[at, 1 - c], ld.at[2 + at])
    own_x = pltpu.make_async_copy(xa.at[c * (n // 2) + q], x, x_s)
    slot = step % 2
    last = n - 1

    def to_mate(at):
        return remote(buf.at[at, 1 - c], rcv.at[at], buf_s.at[at], buf_r.at[at], mate)

    def out_to_mate():
        return remote(bo.at[1 - c], rcvo, bo_s, bo_r, mate)

    @pl.when(step == 0)
    def _():
        own_x.start()
        own_o.start()
        load_own(near.at[:, 0], 0).start()

        @pl.when(c == r)
        def _():
            own_dy.start()

        @pl.when(c != r)
        def _():
            swapped_dy.start()

        barrier = pltpu.get_barrier_semaphore()
        friends = [mate]
        friends += [(hi_to(h, dh, hi_n), c, r, q) for dh in range(1, hi_n)]
        for to in friends:
            pl.semaphore_signal(barrier, inc=1, device_id=to, device_id_type=MESH)
        pl.semaphore_wait(barrier, len(friends))
        for t in range(nh + 1, n):
            for dh in range(1, hi_n):
                late_hi(t, dh).start()
        give_o().start()
        for t in range(nh + 1):
            give(t).start()
        for t in range(nh + 1, n):
            give_late(t, 0).start()
        own_x.wait()
        own_o.wait()
        own_dy.wait()
        give_o().wait_recv()
        for s in range(n):
            for w in range(wide):
                wo[s, w * rw : (w + 1) * rw] = jnp.where(c == w % 2, oa[w // 2, s], ob[w // 2, s])
        give(0).wait_recv()
        load_theirs(0, 0).start()
        total = x[...].astype(F32)
        for s in range(n):
            total = total + nn(ai[s], wo[s])
        hid[...] = total
        inv = lax.rsqrt(jnp.mean(total * total, axis=-1, keepdims=True) + EPSILON)
        n2[...] = (total * inv * g2[...]).astype(BF)
        acc_o[...] = jnp.zeros_like(acc_o)
        acc_g[...] = jnp.zeros_like(acc_g)

    @pl.when(step < n)
    def _():
        @pl.when(step > 1)
        def _():
            to_mate(slot).wait_send()

        load_own(near.at[:, 0], slot).wait()
        load_theirs(0, slot).wait()

        def weight(j):
            return jnp.concatenate([wm[slot, w % 2, w // 2, j] for w in range(wide)], axis=1)

        def put(j, grad):
            low = grad.astype(BF)
            for w in range(wide):
                buf[slot, w % 2, w // 2, j] = low[:, w * dw : (w + 1) * dw]

        gate = nt(n2[...], weight(0))
        up = nt(n2[...], weight(1))
        sig = jax.nn.sigmoid(gate)
        silu = gate * sig
        inner = (silu * up).astype(BF)
        grad_inner = nt(dy[...], weight(2))
        for t in range(1, nh + 1):
            @pl.when(step == t - 1)
            def _():
                load_own(block_of(t), t % 2).start()
                give(t).wait_recv()
                load_theirs(t, t % 2).start()

        for t in range(nh + 1, n):
            @pl.when(step == t - 1)
            def _():
                load_late(t, 0).start()
                for dh in range(1, hi_n):
                    late_arrives(t, dh).wait_recv()
                    give_late(t, dh).start()
                    load_late(t, dh).start()

        grad_gate = (grad_inner * up * sig * (1.0 + gate * (1.0 - sig))).astype(BF)
        grad_up = (grad_inner * silu).astype(BF)
        acc_o[...] += nn(inner, weight(2))
        acc_g[...] += nn(grad_gate, weight(0)) + nn(grad_up, weight(1))
        put(0, tn(grad_gate, n2[...]))
        put(1, tn(grad_up, n2[...]))
        put(2, tn(inner, dy[...]))

    @pl.when(step == last)
    def _():
        hidden = hid[...]
        lo[...] = (hidden + acc_o[...]).astype(BF)
        inv = lax.rsqrt(jnp.mean(hidden * hidden, axis=-1, keepdims=True) + EPSILON)
        grad_n = acc_g[...]
        gg2[...] = jnp.sum((grad_n * hidden * inv).reshape(-1, 8, width), axis=0)
        scaled = grad_n * g2[...]
        dot = jnp.sum(scaled * hidden, axis=-1, keepdims=True)
        grad_h = dy[...].astype(F32) + scaled * inv - hidden * (inv * inv * inv * dot / width)
        gh[...] = grad_h
        low = grad_h.astype(BF)
        for s in range(n):
            ga[s] = nt(low, wo[s]).astype(BF)
            grad_wo = tn(ai[s], low).astype(BF)
            for w in range(wide):
                bo[w % 2, w // 2, s] = grad_wo[w * rw : (w + 1) * rw]

    @pl.when(step > 0)
    def _():
        before = (step + 1) % 2
        to_mate(before).wait_recv()
        for a in range(hi_n):
            for j in range(3):
                total = buf[before, c, a, j].astype(F32) + rcv[before, a, j].astype(F32)
                dsum[a, 0, j] = total.astype(BF)

    @pl.when(step == 1)
    def _():
        first[...] = dsum[:, 0]
        for dh in range(1, hi_n):
            first_over_hi(dh).start()

    for t in range(nh + 1, n):
        @pl.when(step == t - 1)
        def _():
            for dh in range(hi_n):
                give_late(t, dh).wait_recv()
            load_theirs(t, t % 2).start()

    @pl.when(step < n)
    def _():
        to_mate(slot).start()

    @pl.when(step == last)
    def _():
        out_to_mate().start()

    @pl.when(step == n)
    def _():
        out_to_mate().wait_recv()
        for a in range(hi_n):
            for s in range(n):
                total = bo[c, a, s].astype(F32) + rcvo[a, s].astype(F32)
                dosum[a, s] = total.astype(BF)
        out_to_mate().wait_send()
        to_mate(0).wait_send()
        to_mate(1).wait_send()
        give_o().wait_send()
        for dh in range(1, hi_n):
            first_over_hi(dh).wait_send()
            first_over_hi(dh).wait_recv()
        for t in range(nh + 1):
            give(t).wait_send()
        for t in range(nh + 1, n):
            for dh in range(hi_n):
                give_late(t, dh).wait_send()
            for dh in range(1, hi_n):
                late_hi(t, dh).wait_send()


def feed_forward(xa, gout, dy_in, near, far, lp, oh, ai, g2):
    n, tok, sw = ai.shape
    nh = n // 2
    width = gout.shape[1]
    hi_n, _, _, ffs, dw = near.shape
    wide = 2 * hi_n
    rw = sw // wide

    def whole(*shape):
        return pl.BlockSpec(shape, lambda i: (0,) * len(shape))

    def fixed(*shape):
        return pl.BlockSpec(
            shape, lambda i: (0,) * len(shape), pipeline_mode=pl.Buffered(1)
        )

    return pl.pallas_call(
        mlp_kernel,
        out_shape=(
            jax.ShapeDtypeStruct((tok, width), BF),
            jax.ShapeDtypeStruct((tok, width), F32),
            jax.ShapeDtypeStruct((n, tok, sw), BF),
            jax.ShapeDtypeStruct((hi_n, n, 3, ffs, dw), BF),
            jax.ShapeDtypeStruct((hi_n, n, rw, width), BF),
            jax.ShapeDtypeStruct((8, width), F32),
            jax.ShapeDtypeStruct((n, hi_n, 3, ffs, dw), BF),
            jax.ShapeDtypeStruct((hi_n, max(nh - 1, 1), 3, ffs, dw), BF),
            jax.ShapeDtypeStruct((max(hi_n - 1, 1), 3, ffs, dw), BF),
        ),
        grid_spec=pl.GridSpec(
            grid=(n + 1,),
            in_specs=[ANY] * 7 + [fixed(n, tok, sw), fixed(1, width)],
            out_specs=(
                whole(tok, width),
                whole(tok, width),
                whole(n, tok, sw),
                pl.BlockSpec(
                    (hi_n, 1, 3, ffs, dw), lambda i: (0, jnp.maximum(i - 1, 0), 0, 0, 0)
                ),
                whole(hi_n, n, rw, width),
                whole(8, width),
                ANY,
                ANY,
                ANY,
            ),
            scratch_shapes=[
                pltpu.VMEM((tok, width), BF),
                pltpu.VMEM((tok, width), BF),
                pltpu.VMEM((tok, width), F32),
                pltpu.VMEM((tok, width), BF),
                pltpu.VMEM((tok, width), F32),
                pltpu.VMEM((tok, width), F32),
                pltpu.VMEM((2, 2, hi_n, 3, ffs, dw), BF),
                pltpu.VMEM((2, hi_n, 3, ffs, dw), BF),
                pltpu.VMEM((2, hi_n, n, rw, width), BF),
                pltpu.VMEM((hi_n, n, rw, width), BF),
                pltpu.VMEM((2, 2, hi_n, 3, ffs, dw), BF),
                pltpu.VMEM((n, sw, width), BF),
                pltpu.VMEM((hi_n, n, rw, width), BF),
                pltpu.VMEM((hi_n, n, rw, width), BF),
                pltpu.VMEM((hi_n, 3, ffs, dw), BF),
                DMA, DMA((2,)), DMA((2,)), DMA, DMA,
                DMA((6,)), DMA((n, hi_n)), DMA((n, hi_n)), DMA, DMA,
                DMA((max(nh - 1, 1), hi_n)), DMA((max(nh - 1, 1), hi_n)),
                DMA((hi_n,)), DMA((hi_n,)),
            ],
        ),
        name="feed_forward",
        compiler_params=pltpu.CompilerParams(
            dimension_semantics=("arbitrary",),
            collective_id=4,
            has_side_effects=True,
            vmem_limit_bytes=VMEM_MAX,
        ),
        cost_estimate=pl.CostEstimate(
            flops=18 * tok * width * ffs * n, bytes_accessed=40 << 20, transcendentals=tok * ffs * n
        ),
    )(xa, gout, dy_in, near, far, lp, oh, ai, g2)


def backward_kernel(
    sizes, block, ga, ds, dos, lo, rx0, xa, ws, g1, lo_c, lo_s, hi_c, hi_s, seg, qi, ki, mi, ao, lse, gh,
    gg2, squares, values_sq,
    gv, gi, fin, og, total_small, lo_in, rx, rxo, zr,
    do, normed, dq, dk, dv, dcat, gow, gnp, rcv, rcv2, gis, part, zs, zos, do_part, rf,
    dwq, gg1, zo, sm, s1, s2, r1, r2, own, mine,
    do_s, do_r, gv_s, gv_r, co_s, co_r, pe_s, pe_r, gi_s, gi_r, loc,
    rx_s, rx_r, rxo_s, rxo_r, ly_s, ly_r, ld, z_s, z_r, zo_s, zo_r,
    a_s, a_r, b_s, b_r, c_s, c_r, d_s, d_r, e_s, e_r, f_s, f_r, m_s, m_r,
):
    hi_n, _, _, nh = sizes
    n = 2 * nh
    h, c, r, q = coords()
    p = c * nh + q
    row_len, sw = qi.shape
    width = xa.shape[1]
    tok = row_len // n
    short = row_len // 2
    pw = lo_c.shape[1]
    pairs = sw // pw
    halves = pw // HEAD_DIM
    same = c == r
    mate = (h, 1 - c, r, q)
    swap_to = (h, r, c, q)
    zed = r * nh + q
    greet_plane(sizes, True, 2)

    order = list(range(nh + 1, n)) + [nh] + list(range(1, nh)) + [0]

    def over_hi(dh, i):
        to = hi_to(h, dh, hi_n)
        return remote(
            ds.at[to, i], rx.at[dh - 1, i], rx_s.at[dh, i], rx_r.at[dh, i], (to, c, r, q)
        )

    def out_over_hi(dh):
        to = hi_to(h, dh, hi_n)
        return remote(dos.at[to], rxo.at[dh - 1], rxo_s.at[dh], rxo_r.at[dh], (to, c, r, q))

    def send_lo():
        return remote(lo, lo_in, ly_s, ly_r, swap_to)

    def over_z(t):
        if t > nh:
            return remote(zs.at[t], rf.at[t - nh - 1], z_s.at[t], z_r.at[t], (h, c, r, (q + t) % nh))
        to = (h, c, 1 - r, q) if t == nh else (h, c, r, (q + t) % nh)
        return remote(zs.at[t], zr.at[t], z_s.at[t], z_r.at[t], to)

    def out_over_z(i):
        return remote(zos.at[i], zo.at[zed], zo_s.at[i], zo_r.at[zed], (h, c, i // nh, i % nh))

    def keep_z():
        return pltpu.make_async_copy(zs.at[0], zr.at[0], z_s.at[0])

    def keep_out_z(i):
        return pltpu.make_async_copy(zos.at[i], zo.at[i], zo_s.at[i])

    def load_chunk(i):
        copies = [pltpu.make_async_copy(ds.at[h, i], part.at[0], ld.at[0])]
        for dh in range(1, hi_n):
            source = rx.at[dh - 1, i] if i else rx0.at[dh - 1]
            copies.append(pltpu.make_async_copy(source, part.at[dh], ld.at[dh]))
        return copies

    def reduce_chunk(i):
        if i:
            for dh in range(1, hi_n):
                over_hi(dh, i).wait_recv()
        for copy in load_chunk(i):
            copy.start()
        if i == nh:
            for t in range(nh + 1, n):
                over_z(t).wait_recv()
        for copy in load_chunk(i):
            copy.wait()

        def add(j, carry):
            total = part[0, j].astype(F32)
            for dh in range(1, hi_n):
                total = total + part[dh, j].astype(F32)
            if i == nh:
                for t in range(nh - 1):
                    total = total + rf[t, j].astype(F32)
            zs[i, j] = total.astype(BF)
            return carry

        lax.fori_loop(0, 3, add, 0)
        if i:
            over_z(i).start()
        else:
            keep_z().start()

    own_out = pltpu.make_async_copy(dos.at[h], zos, ld.at[0])

    def reduce_out():
        own_out.start()
        own_out.wait()
        for dh in range(1, hi_n):
            out_over_hi(dh).wait_recv()
            copy = pltpu.make_async_copy(rxo.at[dh - 1], do_part, ld.at[dh])
            copy.start()
            copy.wait()
            zos[...] = (zos[...].astype(F32) + do_part[...].astype(F32)).astype(BF)
        for i in range(n):
            @pl.when(zed != i)
            def _():
                out_over_z(i).start()

            @pl.when(zed == i)
            def _():
                keep_out_z(i).start()

    def send_do(s, pair):
        lanes = lane_window(pair, pw, sw)
        to = (h, s // nh, r, s % nh)
        return remote(
            ga.at[s, :, lanes], do.at[p, :, lanes], do_s.at[pair, s], do_r.at[pair, p], to
        )

    def do_arrives(s, pair):
        lanes = lane_window(pair, pw, sw)
        return remote(
            ga.at[s, :, lanes], do.at[s, :, lanes], do_s.at[pair, s], do_r.at[pair, s], mate
        )

    keep_do = pltpu.make_async_copy(ga.at[p], do.at[p], loc.at[0])
    for pair in range(pairs):
        for s in range(n):
            @pl.when(p != s)
            def _():
                send_do(s, pair).start()

    keep_do.start()
    for dh in range(1, hi_n):
        out_over_hi(dh).start()
    for hops in (range(1, min(3, hi_n)), range(3, hi_n)):
        for i in order[:-1]:
            for dh in hops:
                over_hi(dh, i).start()

    @pl.when(c != r)
    def _():
        send_lo().start()

    br = 256

    def norm(i, carry):
        rows = pl.ds(pl.multiple_of(i * br, br), br)
        xf = xa[rows, :].astype(F32)
        inv = lax.rsqrt(jnp.mean(xf * xf, axis=-1, keepdims=True) + EPSILON)
        normed[rows, :] = (xf * inv * g1[...]).astype(BF)
        return carry

    lax.fori_loop(0, row_len // br, norm, 0)
    keep_do.wait()

    flag = seg[0:1, 0:1]
    bias = flag * -1e30
    blocks = row_len // block
    per = block // tok
    causal = lax.broadcasted_iota(jnp.int32, (block, block), 0) >= lax.broadcasted_iota(
        jnp.int32, (block, block), 1
    )

    def gv_at(s, pair):
        if len(gv.shape) == 3:
            return gv.at[s]
        return gv.at[:, pl.ds(pl.multiple_of(s * sw + pair * pw, pw), pw)]

    def send_gv(b, pair):
        lanes = lane_window(pair, pw, sw)
        to = (h, r, b // nh, b % nh)
        return remote(
            gow.at[b, :, lanes], gv_at(p, pair), gv_s.at[pair, b], gv_r.at[pair, p], to
        )

    def keep_gv(pair):
        lanes = lane_window(pair, pw, sw)
        return pltpu.make_async_copy(gow.at[p, :, lanes], gv_at(p, pair), loc.at[1 + pair])

    def attend(i, pair):
        if i == blocks - 1:
            for s in range(n):
                @pl.when(p != s)
                def _():
                    do_arrives(s, pair).wait_recv()

        lanes = lane_window(pair, pw, sw)
        rows = pl.ds(i * block, block)
        pieces = [[] for _ in range(i + 1)]
        dq_parts = []
        do_rows = [do[i * per + t, :, lanes] for t in range(per)]
        do_i = do_rows[0] if per == 1 else jnp.concatenate(do_rows, axis=0)
        ao_rows = [ao[i * per + t, :, lanes] for t in range(per)]
        ao_i = ao_rows[0] if per == 1 else jnp.concatenate(ao_rows, axis=0)
        product = do_i.astype(F32) * ao_i.astype(F32)
        for half in range(halves):
            cols = slice(half * HEAD_DIM, (half + 1) * HEAD_DIM)
            qh = qi[rows, lanes][:, cols]
            doh = do_i[:, cols]
            delta = jnp.sum(product[:, cols], axis=-1, keepdims=True)
            level = lse[pair, rows, half : half + 1]
            acc = 0.0
            for j in range(i + 1):
                kj = ki[pl.ds(j * block, block), lanes][:, cols]
                vj = mi[pl.ds(j * block, block), lanes][:, cols]
                crossing = i * block >= short and j * block < short
                score = masked(nt(qh, kj), i == j, crossing, causal, bias)
                prob = jnp.exp(score - level)
                grad_prob = nt(doh, vj)
                grad_score = (prob * (grad_prob - delta)).astype(BF)
                acc = acc + nn(grad_score, kj)
                pieces[j].append((tn(grad_score, qh), tn(prob.astype(BF), doh)))
            dq_parts.append(acc * HEAD_DIM**-0.5)
        dq[:, lanes] = dq_parts[0] if halves == 1 else jnp.concatenate(dq_parts, axis=1)
        for j in range(i + 1):
            at = pl.ds(j * block, block)
            if halves == 1:
                dk[at, lanes] += pieces[j][0][0]
                dv[at, lanes] += pieces[j][0][1]
            else:
                dk[at, lanes] += jnp.concatenate([t[0] for t in pieces[j]], axis=1)
                dv[at, lanes] += jnp.concatenate([t[1] for t in pieces[j]], axis=1)

    def rotate_back(i, pair):
        first = first_lanes(br, pw)
        lanes = lane_window(pair, pw, sw)
        for u in range(block // br):
            rows = pl.ds(i * block + u * br, br)
            ct, st = rope_rows(lo_c, lo_s, hi_c, hi_s, flag, i * (block // br) + u, br)
            a = dq[pl.ds(u * br, br), lanes]
            b = dk[rows, lanes]
            dcat[0, rows, lanes] = (a * ct - rotate_lanes(a, first) * st).astype(BF)
            dcat[1, rows, lanes] = (b * ct - rotate_lanes(b, first) * st).astype(BF)
            dcat[2, rows, lanes] = (0.5 * dv[rows, lanes].astype(BF).astype(F32)).astype(BF)

    ck = min(256, tok)
    half_rows = row_len // 2
    n_blk = tok // ck

    def partial(base, k):
        rows = pl.ds(pl.multiple_of(base + k * ck, ck), ck)
        total = nn(dcat[0, rows, :], ws[:sw, :])
        for t in range(1, 3):
            total = total + nn(dcat[t, rows, :], ws[t * sw : (t + 1) * sw, :])
        gnp[rows, :] = total.astype(BF)

    def to_mate(b, k):
        rows = pl.ds(pl.multiple_of(b * tok + k * ck, ck), ck)
        here = pl.ds(pl.multiple_of(b % nh * tok + k * ck, ck), ck)
        return remote(gnp.at[rows], rcv.at[here], co_s.at[b % nh, k], co_r.at[b % nh, k], mate)

    def to_peer(b, d, k):
        rows = pl.ds(pl.multiple_of(b * tok + k * ck, ck), ck)
        here = pl.ds(pl.multiple_of(k * ck, ck), ck)
        to = (h, c, r, b % nh)
        return remote(gnp.at[rows], rcv2.at[d - 1, here], pe_s.at[d, k], pe_r.at[d, k], to)

    def added(b, k):
        rows = pl.ds(pl.multiple_of(b * tok + k * ck, ck), ck)
        theirs = pl.ds(pl.multiple_of(b % nh * tok + k * ck, ck), ck)
        return rows, gnp[rows, :].astype(F32) + rcv[theirs, :].astype(F32)

    def own_heads(b):
        def step(k, carry):
            partial(b * tok, k)

            @pl.when(c != b // nh)
            def _():
                to_mate(b, k).start()

            return carry

        lax.fori_loop(0, n_blk, step, 0)

    def both_cores(b):
        @pl.when(c == b // nh)
        def _():
            def step(k, carry):
                to_mate(b, k).wait_recv()

                @pl.when(q != b % nh)
                def _():
                    rows, total = added(b, k)
                    gnp[rows, :] = total.astype(BF)
                    to_peer(b, (b % nh + nh - q) % nh, k).start()

                return carry

            lax.fori_loop(0, n_blk, step, 0)

    def send_gi(k):
        rows = pl.ds(pl.multiple_of(k * ck, ck), ck)
        return remote(gis.at[rows], gi.at[rows], gi_s.at[k], gi_r.at[k], swap_to)

    def keep_gi(k):
        rows = pl.ds(pl.multiple_of(k * ck, ck), ck)
        return pltpu.make_async_copy(gis.at[rows], gi.at[rows], gi_s.at[k])

    gg1[...] = jnp.zeros_like(gg1)

    def own_tokens(b):
        @pl.when(p == b)
        def _():
            def step(k, carry):
                rows = pl.ds(pl.multiple_of(k * ck, ck), ck)
                for d in range(1, nh):
                    to_peer(b, d, k).wait_recv()
                here, grad_n = added(b, k)
                for d in range(1, nh):
                    grad_n = grad_n + rcv2[d - 1, rows, :].astype(F32)
                xf = xa[here, :].astype(F32)
                inv = lax.rsqrt(jnp.mean(xf * xf, axis=-1, keepdims=True) + EPSILON)
                gg1[...] += jnp.sum((grad_n * xf * inv).reshape(-1, 8, width), axis=0)
                scaled = grad_n * g1[...]
                dot = jnp.sum(scaled * xf, axis=-1, keepdims=True)
                gis[rows, :] = (
                    gh[rows, :] + scaled * inv - xf * (inv * inv * inv * dot / width)
                ).astype(BF)

                @pl.when(c != r)
                def _():
                    send_gi(k).start()

                @pl.when(same)
                def _():
                    keep_gi(k).start()

                return carry

            lax.fori_loop(0, n_blk, step, 0)

    def blocks_of(i):
        return range(i * per, (i + 1) * per) if 0 <= i < blocks else ()

    dk[...] = jnp.zeros_like(dk)
    dv[...] = jnp.zeros_like(dv)
    rest = order
    for i in reversed(range(blocks)):
        def one_pair(pair, carry, i=i):
            attend(i, pair)
            rotate_back(i, pair)
            for b in blocks_of(i):
                lanes = lane_window(pair, pw, sw)
                gow[b, :, lanes] = dcat[2, pl.ds(b * tok, tok), lanes]

                @pl.when(jnp.logical_or(c != r, p != b))
                def _():
                    send_gv(b, pair).start()

            return carry

        lax.fori_loop(0, pairs, one_pair, 0)
        for b in blocks_of(i):
            own_heads(b)
        for b in blocks_of(i + 1):
            both_cores(b)
        for b in blocks_of(i + 2):
            own_tokens(b)
        if i == blocks - 2:
            reduce_out()
            reduce_chunk(order[0])
            rest = order[1:]
    if len(rest) == n:
        reduce_out()

    @pl.when(same)
    def _():
        for pair in range(pairs):
            keep_gv(pair).start()

    for b in blocks_of(0):
        both_cores(b)
    for b in blocks_of(1):
        own_tokens(b)
    reduce_chunk(rest[0])

    w = 2 * h + c

    def plane_out(dh, dc):
        to = (hi_to(h, dh, hi_n), (c + dc) % 2, r, q)
        return remote(own, og.at[w], c_s.at[dh, dc], c_r.at[dh, dc], to)

    for i in range(n):
        @pl.when(zed != i)
        def _():
            remote(zos.at[i], zo.at[i], zo_s.at[i], zo_r.at[i], mate).wait_recv()

        @pl.when(zed == i)
        def _():
            keep_out_z(i).wait()

    out_rows = zo[0].astype(F32)
    for i in range(1, n):
        out_rows = out_rows + zo[i].astype(F32)
    own[...] = out_rows.astype(BF)
    og[w] = own[...]
    for dh in range(hi_n):
        for dc in range(2):
            if dh or dc:
                plane_out(dh, dc).start()

    cut = 3 * sw // hi_n

    def hi_part(dh):
        to = hi_to(h, dh, hi_n)
        return remote(dwq.at[to], r1.at[dh - 1], a_s.at[dh], a_r.at[dh], (to, c, r, q))

    for t in range(3):
        grad = tn(dcat[t], normed[...]).astype(BF)
        for i in range(hi_n):
            begin, end = max(t * sw, i * cut), min((t + 1) * sw, (i + 1) * cut)
            if begin < end:
                dwq[i, begin - i * cut : end - i * cut, :] = grad[begin - t * sw : end - t * sw]
    for dh in range(1, hi_n):
        hi_part(dh).start()

    for i in rest[1:-1]:
        reduce_chunk(i)
    for b in blocks_of(0):
        own_tokens(b)

    def hi_small(dh):
        to = (hi_to(h, dh, hi_n), c, r, q)
        return remote(sm, s1.at[h], b_s.at[dh], b_r.at[dh], to)

    sm[...] = jnp.zeros_like(sm)
    sm[0:1, :] = jnp.sum(gg1[...], axis=0, keepdims=True)
    sm[1:2, :] = jnp.sum(gg2[...], axis=0, keepdims=True)
    sm[2:3, :sw] = jnp.sum(values_sq[...], axis=0, keepdims=True)
    sm[3:4, :sw] = jnp.sum(squares[...], axis=0, keepdims=True)
    for dh in range(1, hi_n):
        hi_small(dh).start()
    s1[h] = sm[...]
    reduce_chunk(rest[-1])
    for dh in range(1, hi_n):
        source = hi_from(h, dh, hi_n)
        remote(sm, s1.at[source], b_s.at[dh], b_r.at[dh], mate).wait_recv()
    small = s1[0]
    for i in range(1, hi_n):
        small = small + s1[i]
    spot = c * n + zed
    s2[spot] = small

    def plane_small(k):
        dc, dz = k // n, k % n
        z = (zed + dz) % n
        to = (h, (c + dc) % 2, z // nh, z % nh)
        return remote(s2.at[spot], s2.at[spot], d_s.at[k], d_r.at[k], to)

    def small_arrives(k):
        dc, dz = k // n, k % n
        source = ((c + dc) % 2) * n + (zed + n - dz) % n
        return remote(s2.at[source], s2.at[source], d_s.at[k], d_r.at[k], mate)

    for k in range(1, 2 * n):
        plane_small(k).start()

    part_sum = dwq[h].astype(F32)
    for dh in range(1, hi_n):
        hi_part(dh).wait_recv()
        part_sum = part_sum + r1[dh - 1].astype(F32)
    mine[...] = part_sum.astype(BF)
    across = remote(mine, r2, e_s, e_r, (h, c, 1 - r, q))

    @pl.when(c != r)
    def _():
        across.start()

    for k in range(1, 2 * n):
        small_arrives(k).wait_recv()
    whole = s2[0]
    for k in range(1, 2 * n):
        whole = whole + s2[k]
    total_small[...] = whole

    def spread(dh):
        to = (hi_to(h, dh, hi_n), c, r, q)
        return remote(fin.at[h], fin.at[h], f_s.at[dh], f_r.at[dh], to)

    def share(dh):
        source = hi_from(h, dh, hi_n)
        return remote(fin.at[source], fin.at[source], m_s.at[dh], m_r.at[dh], mate)

    @pl.when(same)
    def _():
        across.wait_recv()
        fin[h] = (mine[...].astype(F32) + r2[...].astype(F32)).astype(BF)
        for dh in range(1, hi_n):
            spread(dh).start()
        share(0).start()
        for dh in range(1, hi_n):
            source = hi_from(h, dh, hi_n)
            remote(fin.at[h], fin.at[source], f_s.at[dh], f_r.at[dh], mate).wait_recv()
            share(dh).start()

    @pl.when(c != r)
    def _():
        for dh in range(hi_n):
            share(dh).wait_recv()
        across.wait_send()

    @pl.when(same)
    def _():
        for dh in range(1, hi_n):
            spread(dh).wait_send()
        for dh in range(hi_n):
            share(dh).wait_send()

    for k in range(n_blk):
        @pl.when(c != r)
        def _():
            send_gi(k).wait_send()
            send_gi(k).wait_recv()

        @pl.when(same)
        def _():
            keep_gi(k).wait()

    for k in range(n_blk):
        for b in range(nh):
            to_mate(b, k).wait_send()
        for d in range(1, nh):
            to_peer(0, d, k).wait_send()
    for dh in range(hi_n):
        for dc in range(2):
            if dh or dc:
                theirs = 2 * hi_from(h, dh, hi_n) + (c + dc) % 2
                remote(own, og.at[theirs], c_s.at[dh, dc], c_r.at[dh, dc], mate).wait_recv()
                plane_out(dh, dc).wait_send()
    for dh in range(1, hi_n):
        hi_small(dh).wait_send()
        hi_part(dh).wait_send()
    for k in range(1, 2 * n):
        plane_small(k).wait_send()

    def drain(pair, carry):
        lanes = lane_window(pair, pw, sw)
        for b in range(n):
            @pl.when(p != b)
            def _():
                send_do(b, pair).wait_send()

            @pl.when(jnp.logical_or(c != r, p != b))
            def _():
                send_gv(b, pair).wait_send()
                remote(
                    gow.at[b, :, lanes], gv_at(b, pair), gv_s.at[pair, b], gv_r.at[pair, b], mate
                ).wait_recv()

        @pl.when(same)
        def _():
            keep_gv(pair).wait()

        return carry

    lax.fori_loop(0, pairs, drain, 0)

    @pl.when(c != r)
    def _():
        send_lo().wait_send()
        send_lo().wait_recv()

    for dh in range(1, hi_n):
        out_over_hi(dh).wait_send()
        for i in order[:-1]:
            over_hi(dh, i).wait_send()
    for i in range(n):
        @pl.when(zed != i)
        def _():
            out_over_z(i).wait_send()

    keep_z().wait()
    for t in range(1, n):
        over_z(t).wait_send()
        if t <= nh:
            over_z(t).wait_recv()


def attention_backward(sizes, ga, ds, dos, lo, rx0, xa, ws, g1, tables, seg, *saved):
    _, _, _, nh = sizes
    n, tok, sw = ga.shape
    row_len, width = xa.shape
    pw = tables[0].shape[1]
    pairs = sw // pw
    block = max(tok, 512)
    ck = min(256, tok)
    n_blk = tok // ck
    hi_n = sizes[0]
    _, _, _, ffs, dw = ds.shape
    rw = dos.shape[2]
    others = max(hi_n - 1, 1)
    cut = 3 * sw // hi_n
    return pl.pallas_call(
        functools.partial(backward_kernel, sizes, block),
        out_shape=(
            jax.ShapeDtypeStruct((n, tok, sw) if sw % 128 else (tok, width), BF),
            jax.ShapeDtypeStruct((tok, width), BF),
            jax.ShapeDtypeStruct((hi_n, cut, width), BF),
            jax.ShapeDtypeStruct((2 * hi_n, rw, width), BF),
            jax.ShapeDtypeStruct((8, width), F32),
            jax.ShapeDtypeStruct((tok, width), BF),
            jax.ShapeDtypeStruct((others, n, 3, ffs, dw), BF),
            jax.ShapeDtypeStruct((others, n, rw, width), BF),
            jax.ShapeDtypeStruct((nh + 1, 3, ffs, dw), BF),
        ),
        in_specs=[ANY] * 5 + [VM] * 17,
        out_specs=(ANY, ANY, VM, VM, VM) + (ANY,) * 4,
        scratch_shapes=[
            pltpu.VMEM((n, tok, sw), BF),
            pltpu.VMEM((row_len, width), BF),
            pltpu.VMEM((block, sw), F32),
            pltpu.VMEM((row_len, sw), F32),
            pltpu.VMEM((row_len, sw), F32),
            pltpu.VMEM((3, row_len, sw), BF),
            pltpu.VMEM((n, tok, sw), BF),
            pltpu.VMEM((row_len, width), BF),
            pltpu.VMEM((row_len // 2, width), BF),
            pltpu.VMEM((max(nh - 1, 1), tok, width), BF),
            pltpu.VMEM((tok, width), BF),
            pltpu.VMEM((hi_n, 3, ffs, dw), BF),
            pltpu.VMEM((n, 3, ffs, dw), BF),
            pltpu.VMEM((n, rw, width), BF),
            pltpu.VMEM((n, rw, width), BF),
            pltpu.VMEM((max(nh - 1, 1), 3, ffs, dw), BF),
            pltpu.VMEM((hi_n, cut, width), BF),
            pltpu.VMEM((8, width), F32),
            pltpu.VMEM((n, rw, width), BF),
            pltpu.VMEM((8, width), F32),
            pltpu.VMEM((hi_n, 8, width), F32),
            pltpu.VMEM((2 * n, 8, width), F32),
            pltpu.VMEM((others, cut, width), BF),
            pltpu.VMEM((cut, width), BF),
            pltpu.VMEM((rw, width), BF),
            pltpu.VMEM((cut, width), BF),
            DMA((pairs, n)), DMA((pairs, n)),
            DMA((pairs, n)), DMA((pairs, n)),
            DMA((nh, n_blk)), DMA((nh, n_blk)),
            DMA((nh, n_blk)), DMA((nh, n_blk)),
            DMA((n_blk,)), DMA((n_blk,)),
            DMA((1 + pairs,)),
            DMA((hi_n, n)), DMA((hi_n, n)),
            DMA((hi_n,)), DMA((hi_n,)),
            DMA, DMA,
            DMA((hi_n,)),
            DMA((n,)), DMA((n,)),
            DMA((n,)), DMA((n,)),
            DMA((hi_n,)), DMA((hi_n,)),
            DMA((hi_n,)), DMA((hi_n,)),
            DMA((hi_n, 2)), DMA((hi_n, 2)),
            DMA((2 * n,)), DMA((2 * n,)),
            DMA, DMA,
            DMA((hi_n,)), DMA((hi_n,)),
            DMA((hi_n,)), DMA((hi_n,)),
        ],
        name="attention_backward",
        compiler_params=pltpu.CompilerParams(
            collective_id=3, has_side_effects=True, vmem_limit_bytes=VMEM_MAX
        ),
        cost_estimate=pl.CostEstimate(
            flops=60 << 30, bytes_accessed=24 << 20, transcendentals=row_len * row_len * sw // 128
        ),
    )(ga, ds, dos, lo, rx0, xa, ws, g1, *tables, seg, *saved)


def per_device(sizes, layer_in, value_first, seg_start, gain_one, w_qkv, w_out, gain_two, w_mlp, grad_out):
    hi_n, _, _, nh = sizes
    n = 2 * nh
    wide = 2 * hi_n
    tok, width = layer_in.shape
    sw = w_qkv.shape[1]
    row_len = n * tok
    h, c, r, q = coords()

    w_mlp_t = jnp.transpose(w_mlp, (1, 2, 0))
    sg = jnp.full((8, 128), seg_start[1].astype(F32))
    w_cut = w_qkv.reshape(hi_n, 3 * sw // hi_n, width)
    wo_cut = w_out.reshape(wide, sw // wide, width)
    v_cut = value_first.reshape(tok, n, sw).transpose(1, 0, 2) if sw % 128 else value_first
    xa, ws, so, near, cross, oz = exchange_inputs(sizes, layer_in, w_cut, sg, w_mlp_t, wo_cut)
    ws = ws.reshape(3 * sw, width)

    tables = rope_parts(row_len, min(sw, 128))
    g1 = gain_one.reshape(1, width)
    g2 = gain_two.reshape(1, width)
    xr = xa.reshape(row_len, width)
    ai, dy_in, far, late, oh, qo, ko, mo, ao, lse, squares, values_sq = attention_forward(
        sizes, v_cut, grad_out, cross, oz, xr, ws, g1, tables, so
    )
    lo, gh, ga, ds, dos, gg2, _, _, rx0 = feed_forward(xa, grad_out, dy_in, near, far, late, oh, ai, g2)
    gv, gi, fin, og, sums, lo_in, _, _, zr = attention_backward(
        sizes, ga, ds, dos, lo, rx0, xr, ws, g1, tables, so, qo, ko, mo, ao, lse, gh, gg2, squares, values_sq
    )

    layer_out = jnp.where(c == r, lo, lo_in)
    grad_value_first = (gv.transpose(1, 0, 2).reshape(tok, width) if sw % 128 else gv).astype(F32)
    grad_in = gi.astype(F32)
    grad_w_mlp = jnp.transpose(jnp.sum(zr.astype(F32), axis=0), (2, 0, 1))
    grad_w_out = og.reshape(sw, width).astype(F32)
    grad_w_qkv = fin.reshape(3, sw, width).astype(F32)
    entries = tok * width * wide * n
    value_norms = jnp.sqrt(jnp.sum(sums[2:4], axis=1) / entries)
    return (
        layer_out,
        grad_in,
        grad_value_first,
        sums[0],
        grad_w_qkv,
        grad_w_out,
        sums[1],
        grad_w_mlp,
        value_norms,
    )


def solution(mesh):
    wide, narrow = mesh.shape["wide"], mesh.shape["narrow"]
    sizes = (wide // 2, 2, 2, narrow // 2)
    fine = Mesh(mesh.devices.reshape(sizes), AXES)
    w_axes, n_axes = ("hi", "core"), ("zh", "zq")
    rows = P(AXES, None)
    return jax.shard_map(
        functools.partial(per_device, sizes),
        mesh=fine,
        in_specs=(
            rows,
            rows,
            P(w_axes),
            P(),
            P(None, n_axes, None),
            P(n_axes, None),
            P(),
            P(w_axes, None, n_axes),
            rows,
        ),
        out_specs=(
            rows,
            rows,
            rows,
            P(),
            P(None, n_axes, None),
            P(n_axes, None),
            P(),
            P(w_axes, None, n_axes),
            P(),
        ),
        check_vma=False,
    )
```

```python
import functools

import jax
import jax.numpy as jnp
import numpy as np
from jax import lax
from jax.experimental import pallas as pl
from jax.experimental.pallas import tpu as pltpu
from jax.sharding import Mesh, PartitionSpec as P

HEAD_DIM = 64
EPSILON = 1e-06
BF = jnp.bfloat16
F32 = jnp.float32
AXES = ("hi", "core", "zh", "zq")
MESH = pl.DeviceIdType.MESH
ANY = pl.BlockSpec(memory_space=pl.ANY)
VM = pl.BlockSpec(memory_space=pltpu.VMEM)
VMEM_MAX = 62 << 20
DMA = pltpu.SemaphoreType.DMA


def nn(a, b):
    return lax.dot_general(a, b, (((1,), (0,)), ((), ())), preferred_element_type=F32)


def nt(a, b):
    return lax.dot_general(a, b, (((1,), (1,)), ((), ())), preferred_element_type=F32)


def tn(a, b):
    return lax.dot_general(a, b, (((0,), (0,)), ((), ())), preferred_element_type=F32)


def coords():
    return tuple(lax.axis_index(name) for name in AXES)


def remote(src, dst, send, recv, to):
    return pltpu.make_async_remote_copy(
        src_ref=src, dst_ref=dst, send_sem=send, recv_sem=recv, device_id=to, device_id_type=MESH
    )


def hi_to(h, dh, hi_n):
    if hi_n % 2:
        return (h + dh) % hi_n
    half = hi_n // 2
    return (h // 2 + dh // 2) % half * 2 + (h + dh) % 2


def hi_from(h, dh, hi_n):
    if hi_n % 2:
        return (h + hi_n - dh) % hi_n
    half = hi_n // 2
    return (h // 2 + half - dh // 2) % half * 2 + (h + dh) % 2


def greet_plane(sizes, with_hi, cores=1):
    hi_n, _, _, nh = sizes
    h, c, r, q = coords()
    barrier = pltpu.get_barrier_semaphore()
    count = 0
    for dc in range(2):
        for dr in range(2):
            for dq in range(nh):
                if dc or dr or dq:
                    to = (h, (c + dc) % 2, (r + dr) % 2, (q + dq) % nh)
                    pl.semaphore_signal(barrier, inc=1, device_id=to, device_id_type=MESH)
                    count += 1
    if with_hi:
        for dh in range(1, hi_n):
            for dc in range(cores):
                to = (hi_to(h, dh, hi_n), (c + dc) % 2, r, q)
                pl.semaphore_signal(barrier, inc=1, device_id=to, device_id_type=MESH)
                count += 1
    pl.semaphore_wait(barrier, count)


def rotate_lanes(values, first):
    width = values.shape[1]
    if width < 128:
        return jnp.concatenate([values[:, 32:], values[:, :32]], axis=1)
    return jnp.where(
        first, pltpu.roll(values, width - 32, 1), pltpu.roll(values, 32, 1)
    )


def first_lanes(rows, width):
    lane = lax.broadcasted_iota(jnp.int32, (rows, width), 1)
    return lane % HEAD_DIM < HEAD_DIM // 2


def lane_window(pair, pw, sw):
    return slice(0, sw) if pw == sw else pl.ds(pl.multiple_of(pair * pw, pw), pw)


def rope_rows(lo_c, lo_s, hi_c, hi_s, flag, i, rows):
    step = lo_c.shape[0]
    half = hi_c.shape[0] // 2
    cos, sin = [], []
    for u in range(rows // step):
        k = i * (rows // step) + u
        far, near = pl.ds(k, 1), pl.ds(k % half, 1)
        ch = hi_c[near, :] * flag + hi_c[far, :] * (1.0 - flag)
        sh = hi_s[near, :] * flag + hi_s[far, :] * (1.0 - flag)
        cos.append(lo_c[...] * ch - lo_s[...] * sh)
        sin.append(lo_s[...] * ch + lo_c[...] * sh)
    cos = jnp.concatenate(cos, axis=0)
    sin = jnp.concatenate(sin, axis=0)
    return cos, jnp.where(first_lanes(rows, cos.shape[1]), -sin, sin)


def rope_parts(row_len, pw):
    half = HEAD_DIM // 2
    frequency = 10000.0 ** (-2.0 * np.arange(half) / HEAD_DIM)
    frequency = np.tile(frequency, pw // half)[None, :]
    lo = np.arange(64)[:, None] * frequency
    hi = 64.0 * np.arange(row_len // 64)[:, None] * frequency
    return tuple(jnp.asarray(t, F32) for t in (np.cos(lo), np.sin(lo), np.cos(hi), np.sin(hi)))


def columns_of(ref, s, start, size, sw):
    if len(ref.shape) == 3:
        return ref.at[s]
    start = s * sw + start
    start = start if isinstance(start, int) else pl.multiple_of(start, size)
    return ref.at[:, pl.ds(start, size)]


def tiled(table, width):
    times = width // table.shape[1]
    return table if times == 1 else jnp.concatenate([table] * times, axis=1)


def exchange_kernel(
    sizes, chunks, x, w, sg, wt, wo, xa, ws, so, g1, cross, oz,
    xs, wb, sb, tb, ob,
    swap_s, swap_r, peer_s, peer_r, core_s, core_r, w_s, w_r, wh_s, wh_r, sg_s, sg_r, loc,
    oz_s, oz_r, gp_s, gp_r, gh_s, gh_r, cr_s, cr_r,
):
    hi_n, _, _, nh = sizes
    n = 2 * nh
    h, c, r, q = coords()
    p = c * nh + q
    zed = r * nh + q
    partner_p = r * nh + q
    rows = x.shape[0] // chunks
    same = c == r
    other = c != r
    partner = (h, r, c, q)
    mate = (h, 1 - c, r, q)
    greet_plane(sizes, True)

    def part(k):
        return pl.ds(k * rows, rows)

    def swap_x(k):
        return remote(x.at[part(k)], xa.at[partner_p, part(k)], swap_s.at[k], swap_r.at[k], partner)

    def own_arrives(k):
        return remote(x.at[part(k)], xa.at[p, part(k)], swap_s.at[k], swap_r.at[k], partner)

    def push_peer(src, k, dq):
        to = (h, c, r, (q + dq) % nh)
        return remote(src, xa.at[p, part(k)], peer_s.at[dq, k], peer_r.at[dq, k], to)

    def push_mate(src, k, dq):
        block = c * nh + (q + nh - dq) % nh
        return remote(src, xa.at[block, part(k)], core_s.at[dq, k], core_r.at[dq, k], mate)

    def send_w():
        return remote(w.at[h], ws.at[h], w_s, w_r, partner)

    def spread_w(dh):
        to = (hi_to(h, dh, hi_n), c, r, q)
        return remote(ws.at[h], ws.at[h], wh_s.at[dh], wh_r.at[dh], to)

    def send_sg():
        return remote(sg, so, sg_s, sg_r, partner)

    def shard_peer(dq):
        to = (h, c, r, (q + dq) % nh)
        return remote(wt, g1.at[h, (nh - dq) % nh], gp_s.at[dq], gp_r.at[dq], to)

    def shard_hi(src, dh, t):
        to = (hi_to(h, dh, hi_n), c, r, q)
        return remote(src, g1.at[h, t], gh_s.at[dh, t], gh_r.at[dh, t], to)

    def shard_cross():
        return remote(wt, cross, cr_s, cr_r, (h, c, 1 - r, q))

    def rows_z(dz):
        z = (zed + dz) % n
        return remote(
            wo.at[2 * h + c], oz.at[zed], oz_s.at[dz], oz_r.at[dz], (h, c, z // nh, z % nh)
        )

    def from_hi(dh):
        return hi_from(h, dh, hi_n)

    local = [
        (pltpu.make_async_copy(wt, tb, loc.at[0]), pltpu.make_async_copy(tb, g1.at[h, 0], loc.at[5])),
        (
            pltpu.make_async_copy(wo.at[2 * h + c], ob, loc.at[1]),
            pltpu.make_async_copy(ob, oz.at[zed], loc.at[6]),
        ),
    ]
    local_same = [
        (pltpu.make_async_copy(x, xs, loc.at[2]), pltpu.make_async_copy(xs, xa.at[p], loc.at[7])),
        (pltpu.make_async_copy(w, wb, loc.at[3]), pltpu.make_async_copy(wb, ws, loc.at[8])),
        (pltpu.make_async_copy(sg, sb, loc.at[4]), pltpu.make_async_copy(sb, so, loc.at[9])),
    ]

    @pl.when(other)
    def _():
        send_sg().start()
        send_w().start()
        for k in range(chunks):
            swap_x(k).start()

    @pl.when(same)
    def _():
        for k in range(chunks):
            for dq in range(1, nh):
                push_peer(x.at[part(k)], k, dq).start()
            push_mate(x.at[part(k)], k, 0).start()
        for get, _ in local_same:
            get.start()

    for dq in range(1, nh):
        shard_peer(dq).start()
    for dh in range(1, hi_n):
        shard_hi(wt, dh, 0).start()
    for dz in range(1, n):
        rows_z(dz).start()
    shard_cross().start()
    for get, _ in local:
        get.start()

    @pl.when(other)
    def _():
        send_w().wait_recv()
        for dh in range(1, hi_n):
            spread_w(dh).start()

    for dq in range(1, nh):
        remote(wt, g1.at[h, (nh - dq) % nh], gp_s.at[dq], gp_r.at[dq], mate).wait_recv()
        t = (nh - dq) % nh
        for dh in range(1, hi_n):
            shard_hi(g1.at[h, t], dh, t).start()

    @pl.when(other)
    def _():
        for k in range(chunks):
            own_arrives(k).wait_recv()
            for dq in range(1, nh):
                push_peer(xa.at[p, part(k)], k, dq).start()
            push_mate(xa.at[p, part(k)], k, 0).start()

    for get, put in local:
        get.wait()
        put.start()

    @pl.when(same)
    def _():
        for get, put in local_same:
            get.wait()
            put.start()

    for k in range(chunks):
        for dq in range(1, nh):
            block = c * nh + (q + nh - dq) % nh
            remote(
                x.at[part(k)], xa.at[block, part(k)], peer_s.at[dq, k], peer_r.at[dq, k], mate
            ).wait_recv()
            push_mate(xa.at[block, part(k)], k, dq).start()

    for k in range(chunks):
        for dq in range(nh):
            block = (1 - c) * nh + (q + nh - dq) % nh
            remote(
                x.at[part(k)], xa.at[block, part(k)], core_s.at[dq, k], core_r.at[dq, k], mate
            ).wait_recv()

    @pl.when(other)
    def _():
        send_sg().wait_recv()
        for dh in range(1, hi_n):
            source = from_hi(dh)
            remote(ws.at[source], ws.at[source], wh_s.at[dh], wh_r.at[dh], mate).wait_recv()
        send_sg().wait_send()
        send_w().wait_send()
        for dh in range(1, hi_n):
            spread_w(dh).wait_send()
        for k in range(chunks):
            swap_x(k).wait_send()

    for k in range(chunks):
        for dq in range(1, nh):
            push_peer(x.at[part(k)], k, dq).wait_send()
        for dq in range(nh):
            push_mate(x.at[part(k)], k, dq).wait_send()

    @pl.when(same)
    def _():
        for _, put in local_same:
            put.wait()

    for dq in range(1, nh):
        shard_peer(dq).wait_send()
    for dz in range(1, n):
        z = (zed + n - dz) % n
        remote(wo.at[0], oz.at[z], oz_s.at[dz], oz_r.at[dz], mate).wait_recv()
        rows_z(dz).wait_send()
    for t in range(nh):
        for dh in range(1, hi_n):
            shard_hi(wt, dh, t).wait_send()
            remote(wt, g1.at[from_hi(dh), t], gh_s.at[dh, t], gh_r.at[dh, t], mate).wait_recv()
    shard_cross().wait_recv()
    shard_cross().wait_send()
    for _, put in local:
        put.wait()


def exchange_inputs(sizes, x, w, sg, wt, wo):
    hi_n, _, _, nh = sizes
    n = 2 * nh
    tok, width = x.shape
    chunks = 4 if tok % 64 == 0 else 1
    return pl.pallas_call(
        functools.partial(exchange_kernel, sizes, chunks),
        out_shape=(
            jax.ShapeDtypeStruct((n, tok, width), BF),
            jax.ShapeDtypeStruct(w.shape, BF),
            jax.ShapeDtypeStruct(sg.shape, F32),
            jax.ShapeDtypeStruct((hi_n, nh) + wt.shape, BF),
            jax.ShapeDtypeStruct(wt.shape, BF),
            jax.ShapeDtypeStruct((n,) + wo.shape[1:], BF),
        ),
        in_specs=[ANY] * 5,
        out_specs=(ANY,) * 6,
        scratch_shapes=[
            pltpu.VMEM((tok, width), BF),
            pltpu.VMEM(w.shape, BF),
            pltpu.VMEM(sg.shape, F32),
            pltpu.VMEM(wt.shape, BF),
            pltpu.VMEM(wo.shape[1:], BF),
            DMA((chunks,)), DMA((chunks,)),
            DMA((nh, chunks)), DMA((nh, chunks)),
            DMA((nh, chunks)), DMA((nh, chunks)),
            DMA, DMA,
            DMA((hi_n,)), DMA((hi_n,)),
            DMA, DMA,
            DMA((10,)),
            DMA((n,)), DMA((n,)),
            DMA((nh,)), DMA((nh,)),
            DMA((hi_n, nh)), DMA((hi_n, nh)),
            DMA, DMA,
        ],
        name="exchange_inputs",
        compiler_params=pltpu.CompilerParams(collective_id=1, has_side_effects=True),
        cost_estimate=pl.CostEstimate(flops=0, bytes_accessed=160 << 20, transcendentals=0),
    )(x, w, sg, wt, wo)


def masked(scores, diagonal, crossing, causal, bias):
    if diagonal:
        return jnp.where(causal, scores, -1e30)
    if crossing:
        return scores + bias
    return scores


def forward_kernel(
    sizes, block, v, gout, cross, oz, xa, ws, g1, lo_c, lo_s, hi_c, hi_s, seg,
    ai, dy_in, g2, late, oh, qo, ko, mo, ao, lse, own, vsq,
    va, own_rows, tb, ob,
    att_s, att_r, loc, v_s, v_r, dy_s, dy_r, gp_s, gp_r, gh_s, gh_r, oh_s, oh_r, lc,
):
    hi_n, _, _, nh = sizes
    n = 2 * nh
    h, c, r, q = coords()
    p = c * nh + q
    row_len, sw = qo.shape
    tok = row_len // n
    short = row_len // 2
    pw = lo_c.shape[1]
    pairs = sw // pw
    halves = pw // HEAD_DIM
    mate = (h, 1 - c, r, q)
    other = c != r
    greet_plane(sizes, True)

    def send_v(s, pair):
        lanes = lane_window(pair, pw, sw)
        to = (h, s // nh, c, s % nh)
        spot = r * nh + q
        return remote(
            columns_of(v, s, pair * pw, pw, sw), va.at[spot, :, lanes],
            v_s.at[pair, s], v_r.at[pair, spot], to,
        )

    def v_arrives(b, pair):
        lanes = lane_window(pair, pw, sw)
        return remote(
            columns_of(v, 0, 0, pw, sw), va.at[b, :, lanes], v_s.at[pair, b], v_r.at[pair, b], mate
        )

    def send_dy():
        return remote(gout, dy_in, dy_s, dy_r, (h, r, c, q))

    def shard_hi(dh):
        to = (hi_to(h, dh, hi_n), c, r, q)
        return remote(cross, g2.at[h], gh_s.at[dh], gh_r.at[dh], to)

    def late_peer(dq):
        to = (h, c, r, (q + dq) % nh)
        return remote(cross, late.at[nh - dq - 1], gp_s.at[dq], gp_r.at[dq], to)

    def rows_hi(dh):
        to = (hi_to(h, dh, hi_n), c, r, q)
        return remote(oz, oh.at[h], oh_s.at[dh], oh_r.at[dh], to)

    def from_hi(dh):
        return hi_from(h, dh, hi_n)

    keep_v = pltpu.make_async_copy(columns_of(v, p, 0, sw, sw), va.at[p], lc.at[0])
    local = [
        (pltpu.make_async_copy(cross, tb, lc.at[1]), pltpu.make_async_copy(tb, g2.at[h], lc.at[3])),
        (pltpu.make_async_copy(oz, ob, lc.at[2]), pltpu.make_async_copy(ob, oh.at[h], lc.at[4])),
    ]
    for pair in range(pairs):
        for s in range(n):
            @pl.when(jnp.logical_or(other, p != s))
            def _():
                send_v(s, pair).start()

    @pl.when(c == r)
    def _():
        keep_v.start()

    for dh in range(1, hi_n):
        shard_hi(dh).start()
    for dh in range(1, hi_n):
        rows_hi(dh).start()
    for dq in range(1, nh):
        late_peer(dq).start()

    @pl.when(other)
    def _():
        send_dy().start()

    for get, _ in local:
        get.start()

    br = 256
    own[...] = jnp.zeros_like(own)
    flag = seg[0:1, 0:1]

    def project(i, carry):
        rows = pl.ds(pl.multiple_of(i * br, br), br)
        xf = xa[rows, :].astype(F32)
        inv = lax.rsqrt(jnp.mean(xf * xf, axis=-1, keepdims=True) + EPSILON)
        normed = (xf * inv * g1[...]).astype(BF)
        raw = nt(normed, ws[...])
        first = first_lanes(br, sw)
        ct, st = rope_rows(lo_c, lo_s, hi_c, hi_s, flag, i, br)
        ct, st = tiled(ct, sw), tiled(st, sw)
        q_raw = raw[:, :sw]
        k_raw = raw[:, sw : 2 * sw]
        own_vals = raw[:, 2 * sw :]
        q_rot = (q_raw * ct + rotate_lanes(q_raw, first) * st).astype(BF)
        qo[rows, :] = (q_rot.astype(F32) * HEAD_DIM**-0.5).astype(BF)
        ko[rows, :] = (k_raw * ct + rotate_lanes(k_raw, first) * st).astype(BF)
        own_rows[rows, :] = own_vals
        own[...] += jnp.sum((own_vals * own_vals).reshape(br // 8, 8, sw), axis=0)
        return carry

    lax.fori_loop(0, row_len // br, project, 0)

    for get, put in local:
        get.wait()
        put.start()
    @pl.when(c == r)
    def _():
        keep_v.wait()

    bias = flag * -1e30
    blocks = row_len // block
    per = block // tok
    causal = lax.broadcasted_iota(jnp.int32, (block, block), 0) >= lax.broadcasted_iota(
        jnp.int32, (block, block), 1
    )

    def send(b, pair):
        lanes = lane_window(pair, pw, sw)
        to = (h, b // nh, r, b % nh)
        return remote(
            ao.at[b, :, lanes], ai.at[p, :, lanes], att_s.at[pair, b], att_r.at[pair, p], to
        )

    def keep(pair):
        lanes = lane_window(pair, pw, sw)
        return pltpu.make_async_copy(ao.at[p, :, lanes], ai.at[p, :, lanes], loc.at[pair])

    def pair_step(pair, carry):
        lanes = lane_window(pair, pw, sw)
        for b in range(n):
            @pl.when(jnp.logical_or(other, p != b))
            def _():
                v_arrives(b, pair).wait_recv()

        sums = 0.0
        for b in range(n):
            rows = pl.ds(b * tok, tok)
            values = va[b, :, lanes].astype(F32)
            sums = sums + jnp.sum((values * values).reshape(tok // 8, 8, pw), axis=0)
            mo[rows, lanes] = (0.5 * own_rows[rows, lanes] + 0.5 * values).astype(BF)
        vsq[:, lanes] = sums
        for i in range(blocks):
            outs = []
            rows = pl.ds(i * block, block)
            for half in range(halves):
                cols = slice(half * HEAD_DIM, (half + 1) * HEAD_DIM)
                qh = qo[rows, lanes][:, cols]
                score = []
                for j in range(i + 1):
                    kj = ko[pl.ds(j * block, block), lanes][:, cols]
                    crossing = i * block >= short and j * block < short
                    score.append(masked(nt(qh, kj), i == j, crossing, causal, bias))
                top = functools.reduce(
                    jnp.maximum, [jnp.max(s, axis=-1, keepdims=True) for s in score]
                )
                total = 0.0
                acc = 0.0
                for j in range(i + 1):
                    e = jnp.exp(score[j] - top)
                    total = total + jnp.sum(e, axis=-1, keepdims=True)
                    vj = mo[pl.ds(j * block, block), lanes][:, cols]
                    acc = acc + nn(e.astype(BF), vj)
                outs.append(acc / total)
                lse[pair, rows, half : half + 1] = top + jnp.log(total)
            out = (jnp.concatenate(outs, axis=1) if halves > 1 else outs[0]).astype(BF)
            for t in range(per):
                b = i * per + t
                ao[b, :, lanes] = out[t * tok : (t + 1) * tok]

                @pl.when(p != b)
                def _():
                    send(b, pair).start()

        keep(pair).start()
        return carry

    lax.fori_loop(0, pairs, pair_step, 0)

    def drain(pair, carry):
        lanes = lane_window(pair, pw, sw)
        for b in range(n):
            @pl.when(p != b)
            def _():
                send(b, pair).wait_send()
                remote(
                    ao.at[b, :, lanes], ai.at[b, :, lanes], att_s.at[pair, b], att_r.at[pair, b],
                    (h, 1 - c, r, q),
                ).wait_recv()
        keep(pair).wait()
        return carry

    lax.fori_loop(0, pairs, drain, 0)

    for pair in range(pairs):
        for s in range(n):
            @pl.when(jnp.logical_or(other, p != s))
            def _():
                send_v(s, pair).wait_send()

    for dh in range(1, hi_n):
        rows_hi(dh).wait_send()
        remote(oz, oh.at[from_hi(dh)], oh_s.at[dh], oh_r.at[dh], mate).wait_recv()
        shard_hi(dh).wait_send()
        remote(cross, g2.at[from_hi(dh)], gh_s.at[dh], gh_r.at[dh], mate).wait_recv()
    for dq in range(1, nh):
        late_peer(dq).wait_send()
        late_peer(dq).wait_recv()

    @pl.when(other)
    def _():
        send_dy().wait_send()
        send_dy().wait_recv()

    for _, put in local:
        put.wait()


def attention_forward(sizes, v, gout, cross, oz, xa, ws, g1, tables, seg):
    hi_n, _, _, nh = sizes
    n = 2 * nh
    row_len, width = xa.shape
    sw = ws.shape[0] // 3
    tok = row_len // n
    pw = tables[0].shape[1]
    pairs = sw // pw
    block = max(tok, 512)
    flops = 2 * row_len * width * 3 * sw + 2 * row_len * row_len * sw
    return pl.pallas_call(
        functools.partial(forward_kernel, sizes, block),
        out_shape=(
            jax.ShapeDtypeStruct((n, tok, sw), BF),
            jax.ShapeDtypeStruct((tok, width), BF),
            jax.ShapeDtypeStruct((hi_n,) + cross.shape, BF),
            jax.ShapeDtypeStruct((max(nh - 1, 1),) + cross.shape, BF),
            jax.ShapeDtypeStruct((hi_n,) + oz.shape, BF),
            jax.ShapeDtypeStruct((row_len, sw), BF),
            jax.ShapeDtypeStruct((row_len, sw), BF),
            jax.ShapeDtypeStruct((row_len, sw), BF),
            jax.ShapeDtypeStruct((n, tok, sw), BF),
            jax.ShapeDtypeStruct((pairs, row_len, pw // HEAD_DIM), F32),
            jax.ShapeDtypeStruct((8, sw), F32),
            jax.ShapeDtypeStruct((8, sw), F32),
        ),
        in_specs=[ANY] * 4 + [VM] * 8,
        out_specs=(ANY,) * 5 + (VM,) * 7,
        scratch_shapes=[
            pltpu.VMEM((n, tok, sw), BF),
            pltpu.VMEM((row_len, sw), F32),
            pltpu.VMEM(cross.shape, BF),
            pltpu.VMEM(oz.shape, BF),
            DMA((pairs, n)), DMA((pairs, n)), DMA((pairs,)),
            DMA((pairs, n)), DMA((pairs, n)),
            DMA, DMA,
            DMA((nh,)), DMA((nh,)),
            DMA((hi_n,)), DMA((hi_n,)),
            DMA((hi_n,)), DMA((hi_n,)),
            DMA((5,)),
        ],
        name="attention_forward",
        compiler_params=pltpu.CompilerParams(
            collective_id=2, has_side_effects=True, vmem_limit_bytes=VMEM_MAX
        ),
        cost_estimate=pl.CostEstimate(
            flops=4 * flops, bytes_accessed=16 << 20, transcendentals=row_len * row_len * sw // 128
        ),
    )(v, gout, cross, oz, xa, ws, g1, *tables, seg)


def mlp_kernel(
    xa, gout, dy_in, near, far, lp, oh, ai, g2, lo, gh, ga, dsum, dosum, gg2, theirs, late, rx0,
    x, dy, hid, n2, acc_o, acc_g, buf, rcv, bo, rcvo, wm, wo, oa, ob, first,
    x_s, buf_s, buf_r, bo_s, bo_r, ld, th_s, th_r, o_s, o_r, gh_s, gh_r, fi_s, fi_r,
):
    step = pl.program_id(0)
    n = ai.shape[0]
    nh = n // 2
    hi_n = wm.shape[2]
    wide = 2 * hi_n
    width = x.shape[1]
    dw = width // wide
    rw = bo.shape[3]
    h, c, r, q = coords()
    own_dy = pltpu.make_async_copy(gout, dy, ld.at[4])
    swapped_dy = pltpu.make_async_copy(dy_in, dy, ld.at[4])
    own_o = pltpu.make_async_copy(oh, oa, ld.at[5])

    mate = (h, 1 - c, r, q)

    def block_of(t):
        return near.at[:, t] if t < nh else far

    def give(t):
        return remote(block_of(t), theirs.at[t], th_s.at[t, 0], th_r.at[t, 0], mate)

    def late_hi(t, dh):
        to = (hi_to(h, dh, hi_n), c, r, q)
        u = t - nh - 1
        return remote(lp.at[u], late.at[h, u], gh_s.at[u, dh], gh_r.at[u, dh], to)

    def late_piece(t, dh):
        return late.at[hi_from(h, dh, hi_n), t - nh - 1] if dh else lp.at[t - nh - 1]

    def late_arrives(t, dh):
        u = t - nh - 1
        return remote(lp.at[u], late_piece(t, dh), gh_s.at[u, dh], gh_r.at[u, dh], mate)

    def give_late(t, dh):
        source = hi_from(h, dh, hi_n)
        return remote(
            late_piece(t, dh), theirs.at[t, source], th_s.at[t, dh], th_r.at[t, dh], mate
        )

    def load_late(t, dh):
        source = hi_from(h, dh, hi_n)
        return pltpu.make_async_copy(late_piece(t, dh), wm.at[t % 2, c, source], ld.at[t % 2])

    def first_over_hi(dh):
        to = hi_to(h, dh, hi_n)
        return remote(first.at[to], rx0.at[dh - 1], fi_s.at[dh], fi_r.at[dh], (to, c, r, q))

    def give_o():
        return remote(oh, ob, o_s, o_r, (h, 1 - c, r, q))

    def load_own(src, at):
        return pltpu.make_async_copy(src, wm.at[at, c], ld.at[at])

    def load_theirs(t, at):
        return pltpu.make_async_copy(theirs.at[t], wm.at[at, 1 - c], ld.at[2 + at])
    own_x = pltpu.make_async_copy(xa.at[c * (n // 2) + q], x, x_s)
    slot = step % 2
    last = n - 1

    def to_mate(at):
        return remote(buf.at[at, 1 - c], rcv.at[at], buf_s.at[at], buf_r.at[at], mate)

    def out_to_mate():
        return remote(bo.at[1 - c], rcvo, bo_s, bo_r, mate)

    @pl.when(step == 0)
    def _():
        own_x.start()
        own_o.start()
        load_own(near.at[:, 0], 0).start()

        @pl.when(c == r)
        def _():
            own_dy.start()

        @pl.when(c != r)
        def _():
            swapped_dy.start()

        barrier = pltpu.get_barrier_semaphore()
        friends = [mate]
        friends += [(hi_to(h, dh, hi_n), c, r, q) for dh in range(1, hi_n)]
        for to in friends:
            pl.semaphore_signal(barrier, inc=1, device_id=to, device_id_type=MESH)
        pl.semaphore_wait(barrier, len(friends))
        for t in range(nh + 1, n):
            for dh in range(1, hi_n):
                late_hi(t, dh).start()
        give_o().start()
        for t in range(nh + 1):
            give(t).start()
        for t in range(nh + 1, n):
            give_late(t, 0).start()
        own_x.wait()
        own_o.wait()
        own_dy.wait()
        give_o().wait_recv()
        for s in range(n):
            for w in range(wide):
                wo[s, w * rw : (w + 1) * rw] = jnp.where(c == w % 2, oa[w // 2, s], ob[w // 2, s])
        give(0).wait_recv()
        load_theirs(0, 0).start()
        total = x[...].astype(F32)
        for s in range(n):
            total = total + nn(ai[s], wo[s])
        hid[...] = total
        inv = lax.rsqrt(jnp.mean(total * total, axis=-1, keepdims=True) + EPSILON)
        n2[...] = (total * inv * g2[...]).astype(BF)
        acc_o[...] = jnp.zeros_like(acc_o)
        acc_g[...] = jnp.zeros_like(acc_g)

    @pl.when(step < n)
    def _():
        @pl.when(step > 1)
        def _():
            to_mate(slot).wait_send()

        load_own(near.at[:, 0], slot).wait()
        load_theirs(0, slot).wait()

        def weight(j):
            return jnp.concatenate([wm[slot, w % 2, w // 2, j] for w in range(wide)], axis=1)

        def put(j, grad):
            low = grad.astype(BF)
            for w in range(wide):
                buf[slot, w % 2, w // 2, j] = low[:, w * dw : (w + 1) * dw]

        gate = nt(n2[...], weight(0))
        up = nt(n2[...], weight(1))
        sig = jax.nn.sigmoid(gate)
        silu = gate * sig
        inner = (silu * up).astype(BF)
        grad_inner = nt(dy[...], weight(2))
        for t in range(1, nh + 1):
            @pl.when(step == t - 1)
            def _():
                load_own(block_of(t), t % 2).start()
                give(t).wait_recv()
                load_theirs(t, t % 2).start()

        for t in range(nh + 1, n):
            @pl.when(step == t - 1)
            def _():
                load_late(t, 0).start()
                for dh in range(1, hi_n):
                    late_arrives(t, dh).wait_recv()
                    give_late(t, dh).start()
                    load_late(t, dh).start()

        grad_gate = (grad_inner * up * sig * (1.0 + gate * (1.0 - sig))).astype(BF)
        grad_up = (grad_inner * silu).astype(BF)
        acc_o[...] += nn(inner, weight(2))
        acc_g[...] += nn(grad_gate, weight(0)) + nn(grad_up, weight(1))
        put(0, tn(grad_gate, n2[...]))
        put(1, tn(grad_up, n2[...]))
        put(2, tn(inner, dy[...]))

    @pl.when(step == last)
    def _():
        hidden = hid[...]
        lo[...] = (hidden + acc_o[...]).astype(BF)
        inv = lax.rsqrt(jnp.mean(hidden * hidden, axis=-1, keepdims=True) + EPSILON)
        grad_n = acc_g[...]
        gg2[...] = jnp.sum((grad_n * hidden * inv).reshape(-1, 8, width), axis=0)
        scaled = grad_n * g2[...]
        dot = jnp.sum(scaled * hidden, axis=-1, keepdims=True)
        grad_h = dy[...].astype(F32) + scaled * inv - hidden * (inv * inv * inv * dot / width)
        gh[...] = grad_h
        low = grad_h.astype(BF)
        for s in range(n):
            ga[s] = nt(low, wo[s]).astype(BF)
            grad_wo = tn(ai[s], low).astype(BF)
            for w in range(wide):
                bo[w % 2, w // 2, s] = grad_wo[w * rw : (w + 1) * rw]

    @pl.when(step > 0)
    def _():
        before = (step + 1) % 2
        to_mate(before).wait_recv()
        for a in range(hi_n):
            for j in range(3):
                total = buf[before, c, a, j].astype(F32) + rcv[before, a, j].astype(F32)
                dsum[a, 0, j] = total.astype(BF)

    @pl.when(step == 1)
    def _():
        first[...] = dsum[:, 0]
        for dh in range(1, hi_n):
            first_over_hi(dh).start()

    for t in range(nh + 1, n):
        @pl.when(step == t - 1)
        def _():
            for dh in range(hi_n):
                give_late(t, dh).wait_recv()
            load_theirs(t, t % 2).start()

    @pl.when(step < n)
    def _():
        to_mate(slot).start()

    @pl.when(step == last)
    def _():
        out_to_mate().start()

    @pl.when(step == n)
    def _():
        out_to_mate().wait_recv()
        for a in range(hi_n):
            for s in range(n):
                total = bo[c, a, s].astype(F32) + rcvo[a, s].astype(F32)
                dosum[a, s] = total.astype(BF)
        out_to_mate().wait_send()
        to_mate(0).wait_send()
        to_mate(1).wait_send()
        give_o().wait_send()
        for dh in range(1, hi_n):
            first_over_hi(dh).wait_send()
            first_over_hi(dh).wait_recv()
        for t in range(nh + 1):
            give(t).wait_send()
        for t in range(nh + 1, n):
            for dh in range(hi_n):
                give_late(t, dh).wait_send()
            for dh in range(1, hi_n):
                late_hi(t, dh).wait_send()


def feed_forward(xa, gout, dy_in, near, far, lp, oh, ai, g2):
    n, tok, sw = ai.shape
    nh = n // 2
    width = gout.shape[1]
    hi_n, _, _, ffs, dw = near.shape
    wide = 2 * hi_n
    rw = sw // wide

    def whole(*shape):
        return pl.BlockSpec(shape, lambda i: (0,) * len(shape))

    def fixed(*shape):
        return pl.BlockSpec(
            shape, lambda i: (0,) * len(shape), pipeline_mode=pl.Buffered(1)
        )

    return pl.pallas_call(
        mlp_kernel,
        out_shape=(
            jax.ShapeDtypeStruct((tok, width), BF),
            jax.ShapeDtypeStruct((tok, width), F32),
            jax.ShapeDtypeStruct((n, tok, sw), BF),
            jax.ShapeDtypeStruct((hi_n, n, 3, ffs, dw), BF),
            jax.ShapeDtypeStruct((hi_n, n, rw, width), BF),
            jax.ShapeDtypeStruct((8, width), F32),
            jax.ShapeDtypeStruct((n, hi_n, 3, ffs, dw), BF),
            jax.ShapeDtypeStruct((hi_n, max(nh - 1, 1), 3, ffs, dw), BF),
            jax.ShapeDtypeStruct((max(hi_n - 1, 1), 3, ffs, dw), BF),
        ),
        grid_spec=pl.GridSpec(
            grid=(n + 1,),
            in_specs=[ANY] * 7 + [fixed(n, tok, sw), fixed(1, width)],
            out_specs=(
                whole(tok, width),
                whole(tok, width),
                whole(n, tok, sw),
                pl.BlockSpec(
                    (hi_n, 1, 3, ffs, dw), lambda i: (0, jnp.maximum(i - 1, 0), 0, 0, 0)
                ),
                whole(hi_n, n, rw, width),
                whole(8, width),
                ANY,
                ANY,
                ANY,
            ),
            scratch_shapes=[
                pltpu.VMEM((tok, width), BF),
                pltpu.VMEM((tok, width), BF),
                pltpu.VMEM((tok, width), F32),
                pltpu.VMEM((tok, width), BF),
                pltpu.VMEM((tok, width), F32),
                pltpu.VMEM((tok, width), F32),
                pltpu.VMEM((2, 2, hi_n, 3, ffs, dw), BF),
                pltpu.VMEM((2, hi_n, 3, ffs, dw), BF),
                pltpu.VMEM((2, hi_n, n, rw, width), BF),
                pltpu.VMEM((hi_n, n, rw, width), BF),
                pltpu.VMEM((2, 2, hi_n, 3, ffs, dw), BF),
                pltpu.VMEM((n, sw, width), BF),
                pltpu.VMEM((hi_n, n, rw, width), BF),
                pltpu.VMEM((hi_n, n, rw, width), BF),
                pltpu.VMEM((hi_n, 3, ffs, dw), BF),
                DMA, DMA((2,)), DMA((2,)), DMA, DMA,
                DMA((6,)), DMA((n, hi_n)), DMA((n, hi_n)), DMA, DMA,
                DMA((max(nh - 1, 1), hi_n)), DMA((max(nh - 1, 1), hi_n)),
                DMA((hi_n,)), DMA((hi_n,)),
            ],
        ),
        name="feed_forward",
        compiler_params=pltpu.CompilerParams(
            dimension_semantics=("arbitrary",),
            collective_id=4,
            has_side_effects=True,
            vmem_limit_bytes=VMEM_MAX,
        ),
        cost_estimate=pl.CostEstimate(
            flops=18 * tok * width * ffs * n, bytes_accessed=40 << 20, transcendentals=tok * ffs * n
        ),
    )(xa, gout, dy_in, near, far, lp, oh, ai, g2)


def backward_kernel(
    sizes, block, ga, ds, dos, lo, rx0, xa, ws, g1, lo_c, lo_s, hi_c, hi_s, seg, qi, ki, mi, ao, lse, gh,
    gg2, squares, values_sq,
    gv, gi, fin, og, total_small, lo_in, rx, rxo, zr,
    do, normed, dq, dk, dv, dcat, gow, gnp, rcv, rcv2, gis, part, zs, zos, do_part, rf,
    dwq, gg1, zo, sm, s1, s2, r1, r2, own, mine,
    do_s, do_r, gv_s, gv_r, co_s, co_r, pe_s, pe_r, gi_s, gi_r, loc,
    rx_s, rx_r, rxo_s, rxo_r, ly_s, ly_r, ld, z_s, z_r, zo_s, zo_r,
    a_s, a_r, b_s, b_r, c_s, c_r, d_s, d_r, e_s, e_r, f_s, f_r, m_s, m_r,
):
    hi_n, _, _, nh = sizes
    n = 2 * nh
    h, c, r, q = coords()
    p = c * nh + q
    row_len, sw = qi.shape
    width = xa.shape[1]
    tok = row_len // n
    short = row_len // 2
    pw = lo_c.shape[1]
    pairs = sw // pw
    halves = pw // HEAD_DIM
    same = c == r
    mate = (h, 1 - c, r, q)
    swap_to = (h, r, c, q)
    zed = r * nh + q
    greet_plane(sizes, True, 2)

    order = list(range(nh + 1, n)) + [nh] + list(range(1, nh)) + [0]

    def over_hi(dh, i):
        to = hi_to(h, dh, hi_n)
        return remote(
            ds.at[to, i], rx.at[dh - 1, i], rx_s.at[dh, i], rx_r.at[dh, i], (to, c, r, q)
        )

    def out_over_hi(dh):
        to = hi_to(h, dh, hi_n)
        return remote(dos.at[to], rxo.at[dh - 1], rxo_s.at[dh], rxo_r.at[dh], (to, c, r, q))

    def send_lo():
        return remote(lo, lo_in, ly_s, ly_r, swap_to)

    def over_z(t):
        if t > nh:
            return remote(zs.at[t], rf.at[t - nh - 1], z_s.at[t], z_r.at[t], (h, c, r, (q + t) % nh))
        to = (h, c, 1 - r, q) if t == nh else (h, c, r, (q + t) % nh)
        return remote(zs.at[t], zr.at[t], z_s.at[t], z_r.at[t], to)

    def out_over_z(i):
        return remote(zos.at[i], zo.at[zed], zo_s.at[i], zo_r.at[zed], (h, c, i // nh, i % nh))

    def keep_z():
        return pltpu.make_async_copy(zs.at[0], zr.at[0], z_s.at[0])

    def keep_out_z(i):
        return pltpu.make_async_copy(zos.at[i], zo.at[i], zo_s.at[i])

    def load_chunk(i):
        copies = [pltpu.make_async_copy(ds.at[h, i], part.at[0], ld.at[0])]
        for dh in range(1, hi_n):
            source = rx.at[dh - 1, i] if i else rx0.at[dh - 1]
            copies.append(pltpu.make_async_copy(source, part.at[dh], ld.at[dh]))
        return copies

    def reduce_chunk(i):
        if i:
            for dh in range(1, hi_n):
                over_hi(dh, i).wait_recv()
        for copy in load_chunk(i):
            copy.start()
        if i == nh:
            for t in range(nh + 1, n):
                over_z(t).wait_recv()
        for copy in load_chunk(i):
            copy.wait()

        def add(j, carry):
            total = part[0, j].astype(F32)
            for dh in range(1, hi_n):
                total = total + part[dh, j].astype(F32)
            if i == nh:
                for t in range(nh - 1):
                    total = total + rf[t, j].astype(F32)
            zs[i, j] = total.astype(BF)
            return carry

        lax.fori_loop(0, 3, add, 0)
        if i:
            over_z(i).start()
        else:
            keep_z().start()

    own_out = pltpu.make_async_copy(dos.at[h], zos, ld.at[0])

    def reduce_out():
        own_out.start()
        own_out.wait()
        for dh in range(1, hi_n):
            out_over_hi(dh).wait_recv()
            copy = pltpu.make_async_copy(rxo.at[dh - 1], do_part, ld.at[dh])
            copy.start()
            copy.wait()
            zos[...] = (zos[...].astype(F32) + do_part[...].astype(F32)).astype(BF)
        for i in range(n):
            @pl.when(zed != i)
            def _():
                out_over_z(i).start()

            @pl.when(zed == i)
            def _():
                keep_out_z(i).start()

    def send_do(s, pair):
        lanes = lane_window(pair, pw, sw)
        to = (h, s // nh, r, s % nh)
        return remote(
            ga.at[s, :, lanes], do.at[p, :, lanes], do_s.at[pair, s], do_r.at[pair, p], to
        )

    def do_arrives(s, pair):
        lanes = lane_window(pair, pw, sw)
        return remote(
            ga.at[s, :, lanes], do.at[s, :, lanes], do_s.at[pair, s], do_r.at[pair, s], mate
        )

    keep_do = pltpu.make_async_copy(ga.at[p], do.at[p], loc.at[0])
    for pair in range(pairs):
        for s in range(n):
            @pl.when(p != s)
            def _():
                send_do(s, pair).start()

    keep_do.start()
    for dh in range(1, hi_n):
        out_over_hi(dh).start()
    for hops in (range(1, min(3, hi_n)), range(3, hi_n)):
        for i in order[:-1]:
            for dh in hops:
                over_hi(dh, i).start()

    @pl.when(c != r)
    def _():
        send_lo().start()

    br = 256

    def norm(i, carry):
        rows = pl.ds(pl.multiple_of(i * br, br), br)
        xf = xa[rows, :].astype(F32)
        inv = lax.rsqrt(jnp.mean(xf * xf, axis=-1, keepdims=True) + EPSILON)
        normed[rows, :] = (xf * inv * g1[...]).astype(BF)
        return carry

    lax.fori_loop(0, row_len // br, norm, 0)
    keep_do.wait()

    flag = seg[0:1, 0:1]
    bias = flag * -1e30
    blocks = row_len // block
    per = block // tok
    causal = lax.broadcasted_iota(jnp.int32, (block, block), 0) >= lax.broadcasted_iota(
        jnp.int32, (block, block), 1
    )

    def gv_at(s, pair):
        if len(gv.shape) == 3:
            return gv.at[s]
        return gv.at[:, pl.ds(pl.multiple_of(s * sw + pair * pw, pw), pw)]

    def send_gv(b, pair):
        lanes = lane_window(pair, pw, sw)
        to = (h, r, b // nh, b % nh)
        return remote(
            gow.at[b, :, lanes], gv_at(p, pair), gv_s.at[pair, b], gv_r.at[pair, p], to
        )

    def keep_gv(pair):
        lanes = lane_window(pair, pw, sw)
        return pltpu.make_async_copy(gow.at[p, :, lanes], gv_at(p, pair), loc.at[1 + pair])

    def attend(i, pair):
        if i == blocks - 1:
            for s in range(n):
                @pl.when(p != s)
                def _():
                    do_arrives(s, pair).wait_recv()

        lanes = lane_window(pair, pw, sw)
        rows = pl.ds(i * block, block)
        pieces = [[] for _ in range(i + 1)]
        dq_parts = []
        do_rows = [do[i * per + t, :, lanes] for t in range(per)]
        do_i = do_rows[0] if per == 1 else jnp.concatenate(do_rows, axis=0)
        ao_rows = [ao[i * per + t, :, lanes] for t in range(per)]
        ao_i = ao_rows[0] if per == 1 else jnp.concatenate(ao_rows, axis=0)
        product = do_i.astype(F32) * ao_i.astype(F32)
        for half in range(halves):
            cols = slice(half * HEAD_DIM, (half + 1) * HEAD_DIM)
            qh = qi[rows, lanes][:, cols]
            doh = do_i[:, cols]
            delta = jnp.sum(product[:, cols], axis=-1, keepdims=True)
            level = lse[pair, rows, half : half + 1]
            acc = 0.0
            for j in range(i + 1):
                kj = ki[pl.ds(j * block, block), lanes][:, cols]
                vj = mi[pl.ds(j * block, block), lanes][:, cols]
                crossing = i * block >= short and j * block < short
                score = masked(nt(qh, kj), i == j, crossing, causal, bias)
                prob = jnp.exp(score - level)
                grad_prob = nt(doh, vj)
                grad_score = (prob * (grad_prob - delta)).astype(BF)
                acc = acc + nn(grad_score, kj)
                pieces[j].append((tn(grad_score, qh), tn(prob.astype(BF), doh)))
            dq_parts.append(acc * HEAD_DIM**-0.5)
        dq[:, lanes] = dq_parts[0] if halves == 1 else jnp.concatenate(dq_parts, axis=1)
        for j in range(i + 1):
            at = pl.ds(j * block, block)
            if halves == 1:
                dk[at, lanes] += pieces[j][0][0]
                dv[at, lanes] += pieces[j][0][1]
            else:
                dk[at, lanes] += jnp.concatenate([t[0] for t in pieces[j]], axis=1)
                dv[at, lanes] += jnp.concatenate([t[1] for t in pieces[j]], axis=1)

    def rotate_back(i, pair):
        first = first_lanes(br, pw)
        lanes = lane_window(pair, pw, sw)
        for u in range(block // br):
            rows = pl.ds(i * block + u * br, br)
            ct, st = rope_rows(lo_c, lo_s, hi_c, hi_s, flag, i * (block // br) + u, br)
            a = dq[pl.ds(u * br, br), lanes]
            b = dk[rows, lanes]
            dcat[0, rows, lanes] = (a * ct - rotate_lanes(a, first) * st).astype(BF)
            dcat[1, rows, lanes] = (b * ct - rotate_lanes(b, first) * st).astype(BF)
            dcat[2, rows, lanes] = (0.5 * dv[rows, lanes].astype(BF).astype(F32)).astype(BF)

    ck = min(256, tok)
    half_rows = row_len // 2
    n_blk = tok // ck

    def partial(base, k):
        rows = pl.ds(pl.multiple_of(base + k * ck, ck), ck)
        total = nn(dcat[0, rows, :], ws[:sw, :])
        for t in range(1, 3):
            total = total + nn(dcat[t, rows, :], ws[t * sw : (t + 1) * sw, :])
        gnp[rows, :] = total.astype(BF)

    def to_mate(b, k):
        rows = pl.ds(pl.multiple_of(b * tok + k * ck, ck), ck)
        here = pl.ds(pl.multiple_of(b % nh * tok + k * ck, ck), ck)
        return remote(gnp.at[rows], rcv.at[here], co_s.at[b % nh, k], co_r.at[b % nh, k], mate)

    def to_peer(b, d, k):
        rows = pl.ds(pl.multiple_of(b * tok + k * ck, ck), ck)
        here = pl.ds(pl.multiple_of(k * ck, ck), ck)
        to = (h, c, r, b % nh)
        return remote(gnp.at[rows], rcv2.at[d - 1, here], pe_s.at[d, k], pe_r.at[d, k], to)

    def added(b, k):
        rows = pl.ds(pl.multiple_of(b * tok + k * ck, ck), ck)
        theirs = pl.ds(pl.multiple_of(b % nh * tok + k * ck, ck), ck)
        return rows, gnp[rows, :].astype(F32) + rcv[theirs, :].astype(F32)

    def own_heads(b):
        def step(k, carry):
            partial(b * tok, k)

            @pl.when(c != b // nh)
            def _():
                to_mate(b, k).start()

            return carry

        lax.fori_loop(0, n_blk, step, 0)

    def both_cores(b):
        @pl.when(c == b // nh)
        def _():
            def step(k, carry):
                to_mate(b, k).wait_recv()

                @pl.when(q != b % nh)
                def _():
                    rows, total = added(b, k)
                    gnp[rows, :] = total.astype(BF)
                    to_peer(b, (b % nh + nh - q) % nh, k).start()

                return carry

            lax.fori_loop(0, n_blk, step, 0)

    def send_gi(k):
        rows = pl.ds(pl.multiple_of(k * ck, ck), ck)
        return remote(gis.at[rows], gi.at[rows], gi_s.at[k], gi_r.at[k], swap_to)

    def keep_gi(k):
        rows = pl.ds(pl.multiple_of(k * ck, ck), ck)
        return pltpu.make_async_copy(gis.at[rows], gi.at[rows], gi_s.at[k])

    gg1[...] = jnp.zeros_like(gg1)

    def own_tokens(b):
        @pl.when(p == b)
        def _():
            def step(k, carry):
                rows = pl.ds(pl.multiple_of(k * ck, ck), ck)
                for d in range(1, nh):
                    to_peer(b, d, k).wait_recv()
                here, grad_n = added(b, k)
                for d in range(1, nh):
                    grad_n = grad_n + rcv2[d - 1, rows, :].astype(F32)
                xf = xa[here, :].astype(F32)
                inv = lax.rsqrt(jnp.mean(xf * xf, axis=-1, keepdims=True) + EPSILON)
                gg1[...] += jnp.sum((grad_n * xf * inv).reshape(-1, 8, width), axis=0)
                scaled = grad_n * g1[...]
                dot = jnp.sum(scaled * xf, axis=-1, keepdims=True)
                gis[rows, :] = (
                    gh[rows, :] + scaled * inv - xf * (inv * inv * inv * dot / width)
                ).astype(BF)

                @pl.when(c != r)
                def _():
                    send_gi(k).start()

                @pl.when(same)
                def _():
                    keep_gi(k).start()

                return carry

            lax.fori_loop(0, n_blk, step, 0)

    def blocks_of(i):
        return range(i * per, (i + 1) * per) if 0 <= i < blocks else ()

    dk[...] = jnp.zeros_like(dk)
    dv[...] = jnp.zeros_like(dv)
    rest = order
    for i in reversed(range(blocks)):
        def one_pair(pair, carry, i=i):
            attend(i, pair)
            rotate_back(i, pair)
            for b in blocks_of(i):
                lanes = lane_window(pair, pw, sw)
                gow[b, :, lanes] = dcat[2, pl.ds(b * tok, tok), lanes]

                @pl.when(jnp.logical_or(c != r, p != b))
                def _():
                    send_gv(b, pair).start()

            return carry

        lax.fori_loop(0, pairs, one_pair, 0)
        for b in blocks_of(i):
            own_heads(b)
        for b in blocks_of(i + 1):
            both_cores(b)
        for b in blocks_of(i + 2):
            own_tokens(b)
        if i == blocks - 2:
            reduce_out()
        if i == blocks - 3:
            reduce_chunk(order[0])
            rest = order[1:]
    if blocks < 2:
        reduce_out()

    @pl.when(same)
    def _():
        for pair in range(pairs):
            keep_gv(pair).start()

    cut = 3 * sw // hi_n

    def hi_part(dh):
        to = hi_to(h, dh, hi_n)
        return remote(dwq.at[to], r1.at[dh - 1], a_s.at[dh], a_r.at[dh], (to, c, r, q))

    for t in range(3):
        grad = tn(dcat[t], normed[...]).astype(BF)
        for i in range(hi_n):
            begin, end = max(t * sw, i * cut), min((t + 1) * sw, (i + 1) * cut)
            if begin < end:
                dwq[i, begin - i * cut : end - i * cut, :] = grad[begin - t * sw : end - t * sw]
    for dh in range(1, hi_n):
        hi_part(dh).start()

    for b in blocks_of(0):
        both_cores(b)
    for b in blocks_of(1):
        own_tokens(b)
    reduce_chunk(rest[0])

    w = 2 * h + c

    def plane_out(dh, dc):
        to = (hi_to(h, dh, hi_n), (c + dc) % 2, r, q)
        return remote(own, og.at[w], c_s.at[dh, dc], c_r.at[dh, dc], to)

    for i in range(n):
        @pl.when(zed != i)
        def _():
            remote(zos.at[i], zo.at[i], zo_s.at[i], zo_r.at[i], mate).wait_recv()

        @pl.when(zed == i)
        def _():
            keep_out_z(i).wait()

    out_rows = zo[0].astype(F32)
    for i in range(1, n):
        out_rows = out_rows + zo[i].astype(F32)
    own[...] = out_rows.astype(BF)
    og[w] = own[...]
    for dh in range(hi_n):
        for dc in range(2):
            if dh or dc:
                plane_out(dh, dc).start()

    for i in rest[1:-1]:
        reduce_chunk(i)
    for b in blocks_of(0):
        own_tokens(b)

    part_sum = dwq[h].astype(F32)
    for dh in range(1, hi_n):
        hi_part(dh).wait_recv()
        part_sum = part_sum + r1[dh - 1].astype(F32)
    mine[...] = part_sum.astype(BF)
    across = remote(mine, r2, e_s, e_r, (h, c, 1 - r, q))

    @pl.when(c != r)
    def _():
        across.start()

    def hi_small(dh):
        to = (hi_to(h, dh, hi_n), c, r, q)
        return remote(sm, s1.at[h], b_s.at[dh], b_r.at[dh], to)

    sm[...] = jnp.zeros_like(sm)
    sm[0:1, :] = jnp.sum(gg1[...], axis=0, keepdims=True)
    sm[1:2, :] = jnp.sum(gg2[...], axis=0, keepdims=True)
    sm[2:3, :sw] = jnp.sum(values_sq[...], axis=0, keepdims=True)
    sm[3:4, :sw] = jnp.sum(squares[...], axis=0, keepdims=True)
    for dh in range(1, hi_n):
        hi_small(dh).start()
    s1[h] = sm[...]
    reduce_chunk(rest[-1])
    for dh in range(1, hi_n):
        source = hi_from(h, dh, hi_n)
        remote(sm, s1.at[source], b_s.at[dh], b_r.at[dh], mate).wait_recv()
    small = s1[0]
    for i in range(1, hi_n):
        small = small + s1[i]
    spot = c * n + zed
    s2[spot] = small

    def plane_small(k):
        dc, dz = k // n, k % n
        z = (zed + dz) % n
        to = (h, (c + dc) % 2, z // nh, z % nh)
        return remote(s2.at[spot], s2.at[spot], d_s.at[k], d_r.at[k], to)

    def small_arrives(k):
        dc, dz = k // n, k % n
        source = ((c + dc) % 2) * n + (zed + n - dz) % n
        return remote(s2.at[source], s2.at[source], d_s.at[k], d_r.at[k], mate)

    for k in range(1, 2 * n):
        plane_small(k).start()

    for k in range(1, 2 * n):
        small_arrives(k).wait_recv()
    whole = s2[0]
    for k in range(1, 2 * n):
        whole = whole + s2[k]
    total_small[...] = whole

    def spread(dh):
        to = (hi_to(h, dh, hi_n), c, r, q)
        return remote(fin.at[h], fin.at[h], f_s.at[dh], f_r.at[dh], to)

    def share(dh):
        source = hi_from(h, dh, hi_n)
        return remote(fin.at[source], fin.at[source], m_s.at[dh], m_r.at[dh], mate)

    @pl.when(same)
    def _():
        across.wait_recv()
        fin[h] = (mine[...].astype(F32) + r2[...].astype(F32)).astype(BF)
        for dh in range(1, hi_n):
            spread(dh).start()
        share(0).start()
        for dh in range(1, hi_n):
            source = hi_from(h, dh, hi_n)
            remote(fin.at[h], fin.at[source], f_s.at[dh], f_r.at[dh], mate).wait_recv()
            share(dh).start()

    @pl.when(c != r)
    def _():
        for dh in range(hi_n):
            share(dh).wait_recv()
        across.wait_send()

    @pl.when(same)
    def _():
        for dh in range(1, hi_n):
            spread(dh).wait_send()
        for dh in range(hi_n):
            share(dh).wait_send()

    for k in range(n_blk):
        @pl.when(c != r)
        def _():
            send_gi(k).wait_send()
            send_gi(k).wait_recv()

        @pl.when(same)
        def _():
            keep_gi(k).wait()

    for k in range(n_blk):
        for b in range(nh):
            to_mate(b, k).wait_send()
        for d in range(1, nh):
            to_peer(0, d, k).wait_send()
    for dh in range(hi_n):
        for dc in range(2):
            if dh or dc:
                theirs = 2 * hi_from(h, dh, hi_n) + (c + dc) % 2
                remote(own, og.at[theirs], c_s.at[dh, dc], c_r.at[dh, dc], mate).wait_recv()
                plane_out(dh, dc).wait_send()
    for dh in range(1, hi_n):
        hi_small(dh).wait_send()
        hi_part(dh).wait_send()
    for k in range(1, 2 * n):
        plane_small(k).wait_send()

    def drain(pair, carry):
        lanes = lane_window(pair, pw, sw)
        for b in range(n):
            @pl.when(p != b)
            def _():
                send_do(b, pair).wait_send()

            @pl.when(jnp.logical_or(c != r, p != b))
            def _():
                send_gv(b, pair).wait_send()
                remote(
                    gow.at[b, :, lanes], gv_at(b, pair), gv_s.at[pair, b], gv_r.at[pair, b], mate
                ).wait_recv()

        @pl.when(same)
        def _():
            keep_gv(pair).wait()

        return carry

    lax.fori_loop(0, pairs, drain, 0)

    @pl.when(c != r)
    def _():
        send_lo().wait_send()
        send_lo().wait_recv()

    for dh in range(1, hi_n):
        out_over_hi(dh).wait_send()
        for i in order[:-1]:
            over_hi(dh, i).wait_send()
    for i in range(n):
        @pl.when(zed != i)
        def _():
            out_over_z(i).wait_send()

    keep_z().wait()
    for t in range(1, n):
        over_z(t).wait_send()
        if t <= nh:
            over_z(t).wait_recv()


def attention_backward(sizes, ga, ds, dos, lo, rx0, xa, ws, g1, tables, seg, *saved):
    _, _, _, nh = sizes
    n, tok, sw = ga.shape
    row_len, width = xa.shape
    pw = tables[0].shape[1]
    pairs = sw // pw
    block = max(tok, 512)
    ck = min(256, tok)
    n_blk = tok // ck
    hi_n = sizes[0]
    _, _, _, ffs, dw = ds.shape
    rw = dos.shape[2]
    others = max(hi_n - 1, 1)
    cut = 3 * sw // hi_n
    return pl.pallas_call(
        functools.partial(backward_kernel, sizes, block),
        out_shape=(
            jax.ShapeDtypeStruct((n, tok, sw) if sw % 128 else (tok, width), BF),
            jax.ShapeDtypeStruct((tok, width), BF),
            jax.ShapeDtypeStruct((hi_n, cut, width), BF),
            jax.ShapeDtypeStruct((2 * hi_n, rw, width), BF),
            jax.ShapeDtypeStruct((8, width), F32),
            jax.ShapeDtypeStruct((tok, width), BF),
            jax.ShapeDtypeStruct((others, n, 3, ffs, dw), BF),
            jax.ShapeDtypeStruct((others, n, rw, width), BF),
            jax.ShapeDtypeStruct((nh + 1, 3, ffs, dw), BF),
        ),
        in_specs=[ANY] * 5 + [VM] * 17,
        out_specs=(ANY, ANY, VM, VM, VM) + (ANY,) * 4,
        scratch_shapes=[
            pltpu.VMEM((n, tok, sw), BF),
            pltpu.VMEM((row_len, width), BF),
            pltpu.VMEM((block, sw), F32),
            pltpu.VMEM((row_len, sw), F32),
            pltpu.VMEM((row_len, sw), F32),
            pltpu.VMEM((3, row_len, sw), BF),
            pltpu.VMEM((n, tok, sw), BF),
            pltpu.VMEM((row_len, width), BF),
            pltpu.VMEM((row_len // 2, width), BF),
            pltpu.VMEM((max(nh - 1, 1), tok, width), BF),
            pltpu.VMEM((tok, width), BF),
            pltpu.VMEM((hi_n, 3, ffs, dw), BF),
            pltpu.VMEM((n, 3, ffs, dw), BF),
            pltpu.VMEM((n, rw, width), BF),
            pltpu.VMEM((n, rw, width), BF),
            pltpu.VMEM((max(nh - 1, 1), 3, ffs, dw), BF),
            pltpu.VMEM((hi_n, cut, width), BF),
            pltpu.VMEM((8, width), F32),
            pltpu.VMEM((n, rw, width), BF),
            pltpu.VMEM((8, width), F32),
            pltpu.VMEM((hi_n, 8, width), F32),
            pltpu.VMEM((2 * n, 8, width), F32),
            pltpu.VMEM((others, cut, width), BF),
            pltpu.VMEM((cut, width), BF),
            pltpu.VMEM((rw, width), BF),
            pltpu.VMEM((cut, width), BF),
            DMA((pairs, n)), DMA((pairs, n)),
            DMA((pairs, n)), DMA((pairs, n)),
            DMA((nh, n_blk)), DMA((nh, n_blk)),
            DMA((nh, n_blk)), DMA((nh, n_blk)),
            DMA((n_blk,)), DMA((n_blk,)),
            DMA((1 + pairs,)),
            DMA((hi_n, n)), DMA((hi_n, n)),
            DMA((hi_n,)), DMA((hi_n,)),
            DMA, DMA,
            DMA((hi_n,)),
            DMA((n,)), DMA((n,)),
            DMA((n,)), DMA((n,)),
            DMA((hi_n,)), DMA((hi_n,)),
            DMA((hi_n,)), DMA((hi_n,)),
            DMA((hi_n, 2)), DMA((hi_n, 2)),
            DMA((2 * n,)), DMA((2 * n,)),
            DMA, DMA,
            DMA((hi_n,)), DMA((hi_n,)),
            DMA((hi_n,)), DMA((hi_n,)),
        ],
        name="attention_backward",
        compiler_params=pltpu.CompilerParams(
            collective_id=3, has_side_effects=True, vmem_limit_bytes=VMEM_MAX
        ),
        cost_estimate=pl.CostEstimate(
            flops=60 << 30, bytes_accessed=24 << 20, transcendentals=row_len * row_len * sw // 128
        ),
    )(ga, ds, dos, lo, rx0, xa, ws, g1, *tables, seg, *saved)


def per_device(sizes, layer_in, value_first, seg_start, gain_one, w_qkv, w_out, gain_two, w_mlp, grad_out):
    hi_n, _, _, nh = sizes
    n = 2 * nh
    wide = 2 * hi_n
    tok, width = layer_in.shape
    sw = w_qkv.shape[1]
    row_len = n * tok
    h, c, r, q = coords()

    w_mlp_t = jnp.transpose(w_mlp, (1, 2, 0))
    sg = jnp.full((8, 128), seg_start[1].astype(F32))
    w_cut = w_qkv.reshape(hi_n, 3 * sw // hi_n, width)
    wo_cut = w_out.reshape(wide, sw // wide, width)
    v_cut = value_first.reshape(tok, n, sw).transpose(1, 0, 2) if sw % 128 else value_first
    xa, ws, so, near, cross, oz = exchange_inputs(sizes, layer_in, w_cut, sg, w_mlp_t, wo_cut)
    ws = ws.reshape(3 * sw, width)

    tables = rope_parts(row_len, min(sw, 128))
    g1 = gain_one.reshape(1, width)
    g2 = gain_two.reshape(1, width)
    xr = xa.reshape(row_len, width)
    ai, dy_in, far, late, oh, qo, ko, mo, ao, lse, squares, values_sq = attention_forward(
        sizes, v_cut, grad_out, cross, oz, xr, ws, g1, tables, so
    )
    lo, gh, ga, ds, dos, gg2, _, _, rx0 = feed_forward(xa, grad_out, dy_in, near, far, late, oh, ai, g2)
    gv, gi, fin, og, sums, lo_in, _, _, zr = attention_backward(
        sizes, ga, ds, dos, lo, rx0, xr, ws, g1, tables, so, qo, ko, mo, ao, lse, gh, gg2, squares, values_sq
    )

    layer_out = jnp.where(c == r, lo, lo_in)
    grad_value_first = (gv.transpose(1, 0, 2).reshape(tok, width) if sw % 128 else gv).astype(F32)
    grad_in = gi.astype(F32)
    grad_w_mlp = jnp.transpose(jnp.sum(zr.astype(F32), axis=0), (2, 0, 1))
    grad_w_out = og.reshape(sw, width).astype(F32)
    grad_w_qkv = fin.reshape(3, sw, width).astype(F32)
    entries = tok * width * wide * n
    value_norms = jnp.sqrt(jnp.sum(sums[2:4], axis=1) / entries)
    return (
        layer_out,
        grad_in,
        grad_value_first,
        sums[0],
        grad_w_qkv,
        grad_w_out,
        sums[1],
        grad_w_mlp,
        value_norms,
    )


def solution(mesh):
    wide, narrow = mesh.shape["wide"], mesh.shape["narrow"]
    sizes = (wide // 2, 2, 2, narrow // 2)
    fine = Mesh(mesh.devices.reshape(sizes), AXES)
    w_axes, n_axes = ("hi", "core"), ("zh", "zq")
    rows = P(AXES, None)
    return jax.shard_map(
        functools.partial(per_device, sizes),
        mesh=fine,
        in_specs=(
            rows,
            rows,
            P(w_axes),
            P(),
            P(None, n_axes, None),
            P(n_axes, None),
            P(),
            P(w_axes, None, n_axes),
            rows,
        ),
        out_specs=(
            rows,
            rows,
            rows,
            P(),
            P(None, n_axes, None),
            P(n_axes, None),
            P(),
            P(w_axes, None, n_axes),
            P(),
        ),
        check_vma=False,
    )
```
